32 devices in a mesh: dp: 16 (over z, y, core), feat: 2 (over x).
Axes of the slice: x: 2, y: 2, z: 4, core: 2. Of those that a mesh axis runs over, the one named last changes fastest.
Arguments:
- tokens_in: bfloat16 [4, 4096, 768], P(None, ('dp', 'feat')), may hold values from -6 to 6
- out_cotangent: bfloat16 [4, 4096, 768], P(None, ('dp', 'feat')), may hold values from -6 to 6
- segment_ids: int32 [4, 4096], P(None, 'dp'), may hold values from 0 to 3, as said below
- feature_proj: bfloat16 [256, 64], P('feat'), may hold values from -6 to 6
- w_qkv: bfloat16 [768, 2304], P(('dp', 'feat')), may hold values from -1 to 1
- b_qkv: bfloat16 [2304], P(('dp', 'feat')), may hold values from -1.1953125 to 1.1953125
- w_out: bfloat16 [768, 768], P(('dp', 'feat')), may hold values from -1.25 to 1.25
- b_out: bfloat16 [768], P(('dp', 'feat')), may hold values from -1.796875 to 1.796875
- ln1_gain: bfloat16 [768], P(('dp', 'feat')), may hold values from 0.25 to 1.75
- ln1_bias: bfloat16 [768], P(('dp', 'feat')), may hold values from -1.796875 to 1.796875
- w_up: bfloat16 [768, 3072], P(('dp', 'feat')), may hold values from -0.21875 to 0.21875
- b_up: bfloat16 [3072], P(('dp', 'feat')), may hold values from -1.796875 to 1.796875
- w_down: bfloat16 [3072, 768], P(('dp', 'feat')), may hold values from -0.109375 to 0.109375
- b_down: bfloat16 [768], P(('dp', 'feat')), may hold values from -1.796875 to 1.796875
- ln2_gain: bfloat16 [768], P(('dp', 'feat')), may hold values from 0.25 to 1.75
- ln2_bias: bfloat16 [768], P(('dp', 'feat')), may hold values from -1.796875 to 1.796875
Outputs:
- block_out: bfloat16 [4, 4096, 768], P(None, ('dp', 'feat'))
- grad_tokens: float32 [4, 4096, 768], P(None, ('dp', 'feat'))
- grad_w_qkv: float32 [768, 2304], P(('dp', 'feat'))
- grad_b_qkv: float32 [2304], P(('dp', 'feat'))
- grad_w_out: float32 [768, 768], P(('dp', 'feat'))
- grad_b_out: float32 [768], P(('dp', 'feat'))
- grad_ln1_gain: float32 [768], P(('dp', 'feat'))
- grad_ln1_bias: float32 [768], P(('dp', 'feat'))
- grad_w_up: float32 [768, 3072], P(('dp', 'feat'))
- grad_b_up: float32 [3072], P(('dp', 'feat'))
- grad_w_down: float32 [3072, 768], P(('dp', 'feat'))
- grad_b_down: float32 [768], P(('dp', 'feat'))
- grad_ln2_gain: float32 [768], P(('dp', 'feat'))
- grad_ln2_bias: float32 [768], P(('dp', 'feat'))
The draws below stay inside these ranges and needn't reach their ends.
Inputs may be any that keep to these rules, and one draw needn't show every extreme that they name: `segment_ids`: in every block of 256 positions (one index of dp) the ids start at 0 and rise by one at each new segment; every block has 4 segments, one of exactly 252 positions and none longer.
All inputs are finite; a program needn't handle non-finite values.
Results may differ from the reference program's by a relative error of at most 0.018.
Values may be sent and summed in bfloat16 or wider, within the bound.
A program may use at most 256 MiB of HBM per device.

```python
import jax
import jax.numpy as jnp
from jax import lax

D = 768
H = 12
DH = 64
FF = 3072
FEATS = 256
MICRO = 4
SEGS = 4
GROUP = 256
LONG = 252
TOKENS = 4096


def block_values(block_key):
    leftover = GROUP - LONG
    key_cut, key_place = jax.random.split(block_key)
    cut_points = jnp.sort(jax.random.permutation(key_cut, leftover - 1)[:SEGS - 2] + 1).astype(jnp.int32)
    bounds = jnp.concatenate([jnp.zeros((1,), jnp.int32), cut_points, jnp.full((1,), leftover, jnp.int32)])
    pieces = bounds[1:] - bounds[:-1]
    long_slot = jax.random.randint(key_place, (), 0, SEGS)
    slot_index = jnp.arange(SEGS, dtype=jnp.int32)
    slot_low = jnp.clip(slot_index, 0, SEGS - 2)
    slot_high = jnp.clip(slot_index - 1, 0, SEGS - 2)
    lengths = jnp.where(slot_index < long_slot, pieces[slot_low], jnp.where(slot_index == long_slot, LONG, pieces[slot_high]))
    seg_ends = jnp.cumsum(lengths).astype(jnp.int32)
    position = jnp.arange(GROUP, dtype=jnp.int32)
    return jnp.sum((position[:, None] >= seg_ends[None, :SEGS - 1]).astype(jnp.int32), 1)


def draw_segment_ids(key, part):
    blocks = MICRO * (TOKENS // GROUP)
    block_keys = jax.random.split(jax.random.fold_in(key, 7), blocks)
    block_vals = jax.vmap(block_values)(block_keys)
    return block_vals.reshape(MICRO, TOKENS).astype(jnp.int32)


def drawn_values(key, shape, scale):
    values = jnp.clip(jax.random.normal(key, shape, jnp.float32), -6.0, 6.0)
    return values * scale


def draw_tokens_in(key, part):
    values = drawn_values(jax.random.fold_in(key, 11), (MICRO, TOKENS, D), 1.0)
    return values.astype(jnp.bfloat16)


def draw_w_qkv(key, part):
    values = drawn_values(jax.random.fold_in(key, 13), (D, 3 * D), D ** (-0.5))
    return values.astype(jnp.bfloat16)


def draw_feature_proj(key, part):
    values = jnp.clip(jax.random.normal(jax.random.fold_in(key, 17), (FEATS, DH), jnp.float32), -6.0, 6.0)
    return values.astype(jnp.bfloat16)


def levels(key, shape, cuts, smallest, largest):
    loudness = 1.0
    for dim, shards_of in cuts:
        heights = jax.random.uniform(jax.random.fold_in(jax.random.fold_in(key, 6), dim), (shards_of,), jnp.float32, smallest / len(cuts), largest / len(cuts))
        loudness = loudness * jnp.repeat(jnp.exp(heights), shape[dim] // shards_of).reshape((-1,) + (1,) * (len(shape) - 1 - dim))
    return loudness


def scatter_about(key, shape, width, most, cuts=(), held_as=jnp.bfloat16):
    values = jax.random.normal(key, shape, jnp.float32) * width
    if len(cuts) > 0:
        values = levels(key, shape, cuts, -0.22, 0.18) * values
    return jnp.clip(values, min=-most, max=most).astype(held_as)


def setup_inputs(seed: int = 0) -> dict:
    seeds = jax.random.split(jax.random.key(seed), 17)
    tokens_in = draw_tokens_in(jax.random.fold_in(seeds[16], 71), 0)
    out_cotangent = scatter_about(seeds[1], (MICRO, TOKENS, D), 1.0, 6.0, ((1, 32),))
    segment_ids = draw_segment_ids(jax.random.fold_in(seeds[16], 71), 0)
    feature_proj = draw_feature_proj(jax.random.fold_in(seeds[16], 71), 0)
    w_qkv = draw_w_qkv(jax.random.fold_in(seeds[16], 71), 0)
    b_qkv = scatter_about(seeds[5], (3 * D,), 0.2, 1.1953125, ((0, 32),))
    w_out = scatter_about(seeds[6], (D, D), (D // 32) ** -0.5, 1.25, ((0, 32),))
    b_out = scatter_about(seeds[7], (D,), 0.3, 1.796875, ((0, 32),))
    ln1_gain = jnp.clip(1.0 + 0.15 * jax.random.normal(seeds[8], (D,), jnp.float32), 0.25, 1.75).astype(jnp.bfloat16)
    ln1_bias = scatter_about(seeds[9], (D,), 0.3, 1.796875, ((0, 32),))
    w_up = scatter_about(seeds[10], (D, FF), D ** -0.5, 0.21875, ((0, 32),))
    b_up = scatter_about(seeds[11], (FF,), 0.3, 1.796875, ((0, 32),))
    w_down = scatter_about(seeds[12], (FF, D), FF ** -0.5, 0.109375, ((0, 32),))
    b_down = scatter_about(seeds[13], (D,), 0.3, 1.796875, ((0, 32),))
    ln2_gain = jnp.clip(1.0 + 0.15 * jax.random.normal(seeds[14], (D,), jnp.float32), 0.25, 1.75).astype(jnp.bfloat16)
    ln2_bias = scatter_about(seeds[15], (D,), 0.3, 1.796875, ((0, 32),))
    return {"tokens_in": tokens_in, "out_cotangent": out_cotangent, "segment_ids": segment_ids, "feature_proj": feature_proj, "w_qkv": w_qkv, "b_qkv": b_qkv, "w_out": w_out, "b_out": b_out, "ln1_gain": ln1_gain, "ln1_bias": ln1_bias, "w_up": w_up, "b_up": b_up, "w_down": w_down, "b_down": b_down, "ln2_gain": ln2_gain, "ln2_bias": ln2_bias}


EPSILON = 1e-05

@jax.custom_vjp
def low(v):
    return lax.optimization_barrier(v.astype(jnp.bfloat16)).astype(jnp.float32)

@jax.custom_vjp
def low_back(v):
    return v

def low_keep(v):
    return (low(v), None)

def low_pass(kept, grad):
    return (grad,)

def back_keep(v):
    return (v, None)

def back_low(kept, grad):
    return (low(grad),)
low.defvjp(low_keep, low_pass)
low_back.defvjp(back_keep, back_low)

def layer_norm(residual, norm_gain, norm_shift):
    center = residual - lax.optimization_barrier(jnp.mean(residual, -1, keepdims=True))
    spread = lax.optimization_barrier(jnp.mean(center * center, -1, keepdims=True))
    return center * lax.rsqrt(spread + EPSILON) * norm_gain + norm_shift

def feature_map(head_rows, feat_proj):
    feat_scale = DH ** (-0.25)
    proj_arg = feat_scale * jnp.einsum('ghd,md->ghm', head_rows, feat_proj, precision=lax.Precision.HIGHEST)
    proj_arg = proj_arg - 0.5 * feat_scale * feat_scale * lax.optimization_barrier(jnp.sum(head_rows * head_rows, -1, keepdims=True))
    return low(jnp.exp(low_back(proj_arg)) * FEATS ** (-0.5))

def block_forward(tokens, seg_row, feat_proj, params):
    w_qkv, b_qkv, w_out, b_out, ln1_gain, ln1_bias, w_up, b_up, w_down, b_down, ln2_gain, ln2_bias = params
    tok_count = tokens.shape[0]
    qkv_rows = low(low_back(jnp.dot(tokens, w_qkv, precision=lax.Precision.HIGHEST) + b_qkv))
    query_h = qkv_rows[:, :D].reshape(tok_count, H, DH)
    key_h = qkv_rows[:, D:2 * D].reshape(tok_count, H, DH)
    value_h = qkv_rows[:, 2 * D:].reshape(tok_count, H, DH)
    phi_q = feature_map(query_h, feat_proj)
    phi_k = feature_map(key_h, feat_proj)
    member = (seg_row[:, None] == jnp.arange(SEGS, dtype=jnp.int32)[None, :]).astype(tokens.dtype)
    kv_sum = low(low_back(jnp.einsum('gs,ghm,ghe->shme', member, phi_k, value_h, precision=lax.Precision.HIGHEST)))
    z_sum = low(low_back(jnp.einsum('gs,ghm->shm', member, phi_k, precision=lax.Precision.HIGHEST)))
    numer_sum = low_back(jnp.einsum('gs,ghm,shme->ghe', member, phi_q, kv_sum, precision=lax.Precision.HIGHEST))
    denom_sum = low_back(jnp.einsum('gs,ghm,shm->gh', member, phi_q, z_sum, precision=lax.Precision.HIGHEST))
    attended = low((numer_sum / denom_sum[:, :, None]).reshape(tok_count, D))
    branch = low_back(jnp.dot(attended, w_out, precision=lax.Precision.HIGHEST) + b_out)
    hidden_one = layer_norm(tokens + branch, ln1_gain, ln1_bias)
    pre_act = low_back(jnp.dot(low(hidden_one), w_up, precision=lax.Precision.HIGHEST) + b_up)
    act_low = low(jax.nn.gelu(pre_act, approximate=False))
    ffn_out = low_back(jnp.dot(act_low, w_down, precision=lax.Precision.HIGHEST) + b_down)
    return layer_norm(hidden_one + ffn_out, ln2_gain, ln2_bias)

def reference(tokens_in, out_cotangent, segment_ids, feature_proj, w_qkv, b_qkv, w_out, b_out, ln1_gain, ln1_bias, w_up, b_up, w_down, b_down, ln2_gain, ln2_bias):
    blocks = MICRO * (TOKENS // GROUP)
    token_blocks = tokens_in.astype(jnp.float32).reshape(blocks, GROUP, D)
    seg_blocks = segment_ids.reshape(blocks, GROUP).astype(jnp.int32)
    feat_proj = feature_proj.astype(jnp.float32)
    params = tuple((param.astype(jnp.float32) for param in (w_qkv, b_qkv, w_out, b_out, ln1_gain, ln1_bias, w_up, b_up, w_down, b_down, ln2_gain, ln2_bias)))

    def forward(block_tokens, block_params):
        block_step = jax.checkpoint(lambda block_item: block_forward(block_item[0], block_item[1], feat_proj, block_params))
        return lax.map(block_step, (block_tokens, seg_blocks))
    outputs, back_fn = jax.vjp(forward, token_blocks, params)
    grad_blocks, weight_grads = back_fn(out_cotangent.astype(jnp.float32).reshape(blocks, GROUP, D))
    return (outputs.reshape(MICRO, TOKENS, D).astype(jnp.bfloat16), grad_blocks.reshape(MICRO, TOKENS, D), weight_grads[0], weight_grads[1], weight_grads[2], weight_grads[3], weight_grads[4], weight_grads[5], weight_grads[6], weight_grads[7], weight_grads[8], weight_grads[9], weight_grads[10], weight_grads[11])
```

```python
from functools import partial

import jax
import jax.numpy as jnp
from jax import lax
from jax.experimental import pallas as pl
from jax.experimental.pallas import tpu as pltpu
from jax.sharding import PartitionSpec as P

D = 768
H = 12
DH = 64
FEATS = 256
MICRO = 4
SEGS = 4


EPSILON = 1e-05


def layer_norm(residual, norm_gain, norm_shift):
    center = residual - jnp.mean(residual, -1, keepdims=True)
    spread = jnp.mean(center * center, -1, keepdims=True)
    return center * lax.rsqrt(spread + EPSILON) * norm_gain + norm_shift


def cross_dot(left_op, right_op):
    return lax.dot_general(
        left_op, right_op, (((0,), (0,)), ((), ())), preferred_element_type=jnp.float32
    )


def back_dot(left_op, right_op):
    return lax.dot_general(
        left_op, right_op, (((1,), (1,)), ((), ())), preferred_element_type=jnp.float32
    )


def fetch_weights(
    w_qkv, b_qkv, w_out, b_out, ln1_gain, ln1_bias, w_up, b_up, w_down, b_down, ln2_gain, ln2_bias
):
    return (
        lax.all_gather(w_qkv, ("dp", "feat"), axis=0, tiled=True),
        lax.all_gather(b_qkv, ("dp", "feat"), axis=0, tiled=True),
        lax.all_gather(w_out, ("dp", "feat"), axis=0, tiled=True),
        lax.all_gather(b_out, ("dp", "feat"), axis=0, tiled=True),
        lax.all_gather(ln1_gain, ("dp", "feat"), axis=0, tiled=True),
        lax.all_gather(ln1_bias, ("dp", "feat"), axis=0, tiled=True),
        lax.all_gather(w_up, ("dp", "feat"), axis=0, tiled=True),
        lax.all_gather(b_up, ("dp", "feat"), axis=0, tiled=True),
        lax.all_gather(w_down, ("dp", "feat"), axis=0, tiled=True),
        lax.all_gather(b_down, ("dp", "feat"), axis=0, tiled=True),
        lax.all_gather(ln2_gain, ("dp", "feat"), axis=0, tiled=True),
        lax.all_gather(ln2_bias, ("dp", "feat"), axis=0, tiled=True),
    )


def feature_map(head_rows, feat_proj):
    feat_scale = DH ** (-0.25)
    proj_arg = feat_scale * jnp.einsum(
        "ghd,md->ghm", head_rows, feat_proj, preferred_element_type=jnp.float32
    )
    squares = jnp.einsum("ghd,ghd->gh", head_rows, head_rows, preferred_element_type=jnp.float32)
    proj_arg = proj_arg - 0.5 * feat_scale * feat_scale * squares[:, :, None]
    return jnp.exp(proj_arg) * FEATS ** (-0.5)


def feature_back(head_rows, feat_proj, grad_arg):
    feat_scale = DH ** (-0.25)
    proj_back = feat_scale * jnp.einsum(
        "ghm,md->ghd", grad_arg, feat_proj, preferred_element_type=jnp.float32
    )
    arg_total = jnp.sum(grad_arg.astype(jnp.float32), -1, keepdims=True)
    return proj_back - feat_scale * feat_scale * head_rows.astype(jnp.float32) * arg_total


def spread_segments(phi_low, member):
    tok_count, head_count, feat_width = phi_low.shape
    return (phi_low[:, :, None, :] * member[:, None, :, None]).reshape(
        tok_count, head_count, SEGS * feat_width
    )


def fold_segments(grad_wide, member_f):
    tok_count, head_count, wide_dim = grad_wide.shape
    shaped = grad_wide.reshape(tok_count, head_count, SEGS, wide_dim // SEGS)
    return jnp.sum(shaped * member_f[:, None, :, None], 2)


def micro_step(tokens, cotangent, seg_row, feat_proj, weights):
    (
        w_qkv,
        b_qkv,
        w_out,
        b_out,
        ln1_gain,
        ln1_bias,
        w_up,
        b_up,
        w_down,
        b_down,
        ln2_gain,
        ln2_bias,
    ) = weights
    tok_count = tokens.shape[0]
    qkv_rows = jnp.dot(tokens, w_qkv, preferred_element_type=jnp.float32) + b_qkv.astype(
        jnp.float32
    )
    qkv_low = qkv_rows.astype(jnp.bfloat16)
    grouped = lax.all_gather(qkv_low, "feat", axis=0, tiled=True)
    group_rows = grouped.shape[0]
    query_h = grouped[:, :D].reshape(group_rows, H, DH)
    key_h = grouped[:, D : 2 * D].reshape(group_rows, H, DH)
    value_h = grouped[:, 2 * D :].reshape(group_rows, H, DH)
    phi_q = feature_map(query_h, feat_proj)
    phi_k = feature_map(key_h, feat_proj)
    member_f = (seg_row[:, None] == jnp.arange(SEGS, dtype=jnp.int32)[None, :]).astype(jnp.float32)
    member = member_f.astype(jnp.bfloat16)
    wide_q = spread_segments(phi_q.astype(jnp.bfloat16), member)
    wide_k = spread_segments(phi_k.astype(jnp.bfloat16), member)
    ones_col = jnp.ones((group_rows,), jnp.bfloat16)
    kv_part = jnp.einsum("gha,ghe->hae", wide_k, value_h, preferred_element_type=jnp.float32)
    z_part = jnp.einsum("gha,g->ha", wide_k, ones_col, preferred_element_type=jnp.float32)
    kv_low = kv_part.astype(jnp.bfloat16)
    z_low = z_part.astype(jnp.bfloat16)
    numer_part = jnp.einsum(
        "gha,hae->ghe", wide_q, kv_low, preferred_element_type=jnp.float32
    ).reshape(group_rows, D)
    denom_part = jnp.einsum("gha,ha->gh", wide_q, z_low, preferred_element_type=jnp.float32)
    numer_sum, denom_sum = (
        lax.psum_scatter(numer_part, "feat", scatter_dimension=0, tiled=True),
        lax.psum_scatter(denom_part, "feat", scatter_dimension=0, tiled=True),
    )
    numer_h = numer_sum.reshape(tok_count, H, DH)
    att_low = (numer_h / denom_sum[:, :, None]).reshape(tok_count, D).astype(jnp.bfloat16)
    branch = jnp.dot(att_low, w_out, preferred_element_type=jnp.float32) + b_out.astype(jnp.float32)
    hidden_one, ln1_back = jax.vjp(
        layer_norm,
        tokens.astype(jnp.float32) + branch,
        ln1_gain.astype(jnp.float32),
        ln1_bias.astype(jnp.float32),
    )
    hid_low = hidden_one.astype(jnp.bfloat16)
    pre_act = jnp.dot(hid_low, w_up, preferred_element_type=jnp.float32) + b_up.astype(jnp.float32)
    act_val, gelu_back = jax.vjp(partial(jax.nn.gelu, approximate=False), pre_act)
    act_low = act_val.astype(jnp.bfloat16)
    ffn_out = jnp.dot(act_low, w_down, preferred_element_type=jnp.float32) + b_down.astype(
        jnp.float32
    )
    result, ln2_back = jax.vjp(
        layer_norm, hidden_one + ffn_out, ln2_gain.astype(jnp.float32), ln2_bias.astype(jnp.float32)
    )
    grad_r2, grad_gain2, grad_bias2 = ln2_back(cotangent.astype(jnp.float32))
    grad_ffn = grad_r2.astype(jnp.bfloat16)
    grad_bdown = jnp.sum(grad_ffn.astype(jnp.float32), 0)
    grad_wdown = cross_dot(act_low, grad_ffn)
    (grad_act,) = gelu_back(back_dot(grad_ffn, w_down))
    grad_pre = grad_act.astype(jnp.bfloat16)
    grad_bup = jnp.sum(grad_pre.astype(jnp.float32), 0)
    grad_wup = cross_dot(hid_low, grad_pre)
    grad_h1 = grad_r2 + back_dot(grad_pre, w_up)
    grad_r1, grad_gain1, grad_bias1 = ln1_back(grad_h1)
    grad_branch = grad_r1.astype(jnp.bfloat16)
    grad_bout = jnp.sum(grad_branch.astype(jnp.float32), 0)
    grad_wout = cross_dot(att_low, grad_branch)
    grad_att = back_dot(grad_branch, w_out).reshape(tok_count, H, DH)
    grad_num = (grad_att / denom_sum[:, :, None]).reshape(tok_count, D).astype(jnp.bfloat16)
    grad_den = (-jnp.sum(grad_att * numer_h, -1) / (denom_sum * denom_sum)).astype(jnp.bfloat16)
    group_num, group_den = (
        lax.all_gather(grad_num, "feat", axis=0, tiled=True),
        lax.all_gather(grad_den, "feat", axis=0, tiled=True),
    )
    group_num_h = group_num.reshape(group_rows, H, DH)
    grad_kv_part = jnp.einsum(
        "gha,ghe->hae", wide_q, group_num_h, preferred_element_type=jnp.float32
    )
    grad_z_part = jnp.einsum("gha,gh->ha", wide_q, group_den, preferred_element_type=jnp.float32)
    grad_kv = grad_kv_part.astype(jnp.bfloat16)
    grad_z = grad_z_part.astype(jnp.bfloat16)
    wide_gq = jnp.einsum("ghe,hae->gha", group_num_h, kv_low, preferred_element_type=jnp.float32)
    wide_gq = wide_gq + group_den[:, :, None].astype(jnp.float32) * z_low[None].astype(jnp.float32)
    grad_arg_q = (fold_segments(wide_gq, member_f) * phi_q).astype(jnp.bfloat16)
    wide_gk = jnp.einsum(
        "ghe,hae->gha", value_h, grad_kv, preferred_element_type=jnp.float32
    ) + grad_z[None].astype(jnp.float32)
    grad_arg_k = (fold_segments(wide_gk, member_f) * phi_k).astype(jnp.bfloat16)
    grad_value = jnp.einsum("gha,hae->ghe", wide_k, grad_kv, preferred_element_type=jnp.float32)
    grad_query = feature_back(query_h, feat_proj, grad_arg_q)
    grad_key = feature_back(key_h, feat_proj, grad_arg_k)
    grad_group = jnp.concatenate(
        [
            grad_query.reshape(group_rows, D),
            grad_key.reshape(group_rows, D),
            grad_value.reshape(group_rows, D),
        ],
        1,
    )
    grad_qkv = lax.psum_scatter(
        grad_group.astype(jnp.bfloat16), "feat", scatter_dimension=0, tiled=True
    )
    grad_bqkv = jnp.sum(grad_qkv.astype(jnp.float32), 0)
    grad_wqkv = cross_dot(tokens, grad_qkv)
    grad_tokens = grad_r1 + back_dot(grad_qkv, w_qkv)
    grads_now = (
        grad_wqkv,
        grad_bqkv,
        grad_wout,
        grad_bout,
        grad_gain1,
        grad_bias1,
        grad_wup,
        grad_bup,
        grad_wdown,
        grad_bdown,
        grad_gain2,
        grad_bias2,
    )
    return (result.astype(jnp.bfloat16), grad_tokens, grads_now)


def on_device(
    tokens_in,
    out_cotangent,
    segment_ids,
    feature_proj,
    w_qkv,
    b_qkv,
    w_out,
    b_out,
    ln1_gain,
    ln1_bias,
    w_up,
    b_up,
    w_down,
    b_down,
    ln2_gain,
    ln2_bias,
):
    totals = None
    outputs = []
    grad_inputs = []
    for micro_idx in range(MICRO):
        gathered = fetch_weights(
            w_qkv,
            b_qkv,
            w_out,
            b_out,
            ln1_gain,
            ln1_bias,
            w_up,
            b_up,
            w_down,
            b_down,
            ln2_gain,
            ln2_bias,
        )
        result, grad_tokens, grads_now = micro_step(
            tokens_in[micro_idx],
            out_cotangent[micro_idx],
            segment_ids[micro_idx],
            feature_proj,
            gathered,
        )
        outputs.append(result)
        grad_inputs.append(grad_tokens)
        totals = grads_now if totals is None else jax.tree.map(jnp.add, totals, grads_now)
    (
        grad_wqkv,
        grad_bqkv,
        grad_wout,
        grad_bout,
        grad_gain1,
        grad_bias1,
        grad_wup,
        grad_bup,
        grad_wdown,
        grad_bdown,
        grad_gain2,
        grad_bias2,
    ) = totals
    summed = (
        lax.psum_scatter(grad_wqkv, ("dp", "feat"), scatter_dimension=0, tiled=True),
        lax.psum_scatter(grad_bqkv, ("dp", "feat"), scatter_dimension=0, tiled=True),
        lax.psum_scatter(grad_wout, ("dp", "feat"), scatter_dimension=0, tiled=True),
        lax.psum_scatter(grad_bout, ("dp", "feat"), scatter_dimension=0, tiled=True),
        lax.psum_scatter(grad_gain1, ("dp", "feat"), scatter_dimension=0, tiled=True),
        lax.psum_scatter(grad_bias1, ("dp", "feat"), scatter_dimension=0, tiled=True),
        lax.psum_scatter(grad_wup, ("dp", "feat"), scatter_dimension=0, tiled=True),
        lax.psum_scatter(grad_bup, ("dp", "feat"), scatter_dimension=0, tiled=True),
        lax.psum_scatter(grad_wdown, ("dp", "feat"), scatter_dimension=0, tiled=True),
        lax.psum_scatter(grad_bdown, ("dp", "feat"), scatter_dimension=0, tiled=True),
        lax.psum_scatter(grad_gain2, ("dp", "feat"), scatter_dimension=0, tiled=True),
        lax.psum_scatter(grad_bias2, ("dp", "feat"), scatter_dimension=0, tiled=True),
    )
    return (
        jnp.stack(outputs),
        jnp.stack(grad_inputs),
        summed[0],
        summed[1],
        summed[2],
        summed[3],
        summed[4],
        summed[5],
        summed[6],
        summed[7],
        summed[8],
        summed[9],
        summed[10],
        summed[11],
    )


NZ, NY, NC, NX = 4, 2, 2, 2
MESH_ID = pl.DeviceIdType.MESH
BF = jnp.bfloat16
F32 = jnp.float32
SHARE = MICRO // NX


def fits(mesh):
    return mesh.shape["dp"] == NZ * NY * NC and mesh.shape["feat"] == NX


def place():
    i = lax.axis_index("dp")
    return i // (NY * NC), (i // NC) % NY, i % NC, lax.axis_index("feat")


def device(z, y, c, x):
    return (z * (NY * NC) + y * NC + c, x)


def meet(peers):
    barrier = pltpu.get_barrier_semaphore()
    for peer in peers:
        pl.semaphore_signal(barrier, inc=1, device_id=peer, device_id_type=MESH_ID)
    pl.semaphore_wait(barrier, len(peers))


def gather_kernel(count, *refs):
    ins, tok, cot = refs[:count], refs[count], refs[count + 1]
    outs, tok_all, cot_all = refs[count + 2 : 2 * count + 2], refs[2 * count + 2], refs[2 * count + 3]
    lsem, ssem, rsem, xlsem, xssem, xrsem = refs[2 * count + 4 :]
    z, y, c, x = place()
    z_peers = [device(lax.rem(z + k, NZ), y, c, x) for k in (1, 2, 3)]
    y2, x2 = jnp.where(c == 0, 1 - y, y), jnp.where(c == 0, x, 1 - x)
    y3, x3 = jnp.where(c == 0, y, 1 - y), jnp.where(c == 0, 1 - x, x)
    second, third = device(z, y2, c, x2), device(z, y3, c, x3)
    sibling, across = device(z, y, 1 - c, x), device(z, y, c, 1 - x)
    meet(z_peers + [second, third, sibling])

    def send(src, dst, w, s, peer):
        return pltpu.make_async_remote_copy(
            src_ref=src, dst_ref=dst, send_sem=ssem.at[w, s], recv_sem=rsem.at[w, s],
            device_id=peer, device_id_type=MESH_ID,
        )

    def own(w):
        return pltpu.make_async_copy(ins[w], outs[w].at[z, y, c, x], lsem.at[w])

    def swap(n, src, dst):
        there = pltpu.make_async_remote_copy(
            src_ref=src.at[pl.ds((1 - x) * SHARE, SHARE)], dst_ref=dst.at[:, x],
            send_sem=xssem.at[n], recv_sem=xrsem.at[n], device_id=across, device_id_type=MESH_ID,
        )
        here = pltpu.make_async_copy(src.at[pl.ds(x * SHARE, SHARE)], dst.at[:, x], xlsem.at[n])
        return there, here

    def z_copy(w, k):
        return send(ins[w], outs[w].at[z, y, c, x], w, k, z_peers[k])

    for w in range(count):
        own(w).start()

    def phase(w, number):
        out = outs[w]
        four, eight = out.at[:, y, c, x], out.at[:, :, c, x]
        if number == 0:
            for k in range(3):
                z_copy(w, k).start()
        elif number == 1:
            for k in range(3):
                z_copy(w, k).wait_recv()
            own(w).wait()
            send(four, four, w, 3, second).start()
            send(four, four, w, 4, sibling).start()
        elif number == 2:
            send(four, four, w, 3, second).wait_recv()

            @pl.when(c == 0)
            def _():
                part = out.at[:, :, c, x]
                send(part, part, w, 5, third).start()

            @pl.when(c == 1)
            def _():
                part = out.at[:, y, c, :]
                send(part, part, w, 5, third).start()

            part = out.at[:, y2, c, x2]
            send(part, part, w, 6, sibling).start()
        else:
            send(eight, eight, w, 5, third).wait_recv()

            @pl.when(c == 0)
            def _():
                part = out.at[:, :, c, 1 - x]
                send(part, part, w, 7, sibling).start()

            @pl.when(c == 1)
            def _():
                part = out.at[:, 1 - y, c, :]
                send(part, part, w, 7, sibling).start()

    moves = [swap(0, tok, tok_all), swap(1, cot, cot_all)]
    for there, here in moves:
        there.start()
        here.start()
    for step in range(count + 3):
        for w in range(count):
            if 0 <= step - w <= 3:
                phase(w, step - w)
    for there, here in moves:
        there.wait()
        here.wait()
    for w in range(count):
        four, eight = outs[w].at[:, y, c, x], outs[w].at[:, :, c, x]
        for k in range(3):
            z_copy(w, k).wait_send()
        send(four, four, w, 3, second).wait_send()
        send(four, four, w, 4, sibling).wait()
        send(eight, eight, w, 5, third).wait_send()
        send(four, four, w, 6, sibling).wait()
        send(eight, eight, w, 7, sibling).wait()


def gather_all(shards, tok, cot):
    count = len(shards)
    block = jax.ShapeDtypeStruct((SHARE, NX) + tok.shape[1:], tok.dtype)
    anywhere = pl.BlockSpec(memory_space=pl.ANY)
    dma = pltpu.SemaphoreType.DMA
    return pl.pallas_call(
        partial(gather_kernel, count),
        out_shape=[jax.ShapeDtypeStruct((NZ, NY, NC, NX) + s.shape, s.dtype) for s in shards] + [block, block],
        in_specs=[anywhere] * (count + 2),
        out_specs=[anywhere] * (count + 2),
        scratch_shapes=[dma((count,)), dma((count, 8)), dma((count, 8)), dma((2,)), dma((2,)), dma((2,))],
        compiler_params=pltpu.CompilerParams(collective_id=0, has_side_effects=True),
        name="gather_weights",
    )(*shards, tok, cot)


def reduce_kernel(count, *refs):
    parts, y_blk, g_blk = refs[:count], refs[count], refs[count + 1]
    outs, y_got, g_got = refs[count + 2 : 2 * count + 2], refs[2 * count + 2], refs[2 * count + 3]
    scratch = refs[2 * count + 4 :]
    held, got_a = scratch[:count], scratch[count : 2 * count]
    got_b, got_c, got_d = scratch[2 * count : 3 * count], scratch[3 * count : 4 * count], scratch[4 * count : 5 * count]
    stage = scratch[5 * count : 6 * count]
    lsem, ssem, rsem, osem, xssem, xrsem = scratch[6 * count :]
    z, y, c, x = place()
    z_peers = [device(lax.rem(z + k, NZ), y, c, x) for k in (1, 2, 3)]
    first, second = jnp.where(c == 0, x, y), jnp.where(c == 0, y, x)
    to_first = device(z, jnp.where(c == 0, y, 1 - y), c, jnp.where(c == 0, 1 - x, x))
    to_second = device(z, jnp.where(c == 0, 1 - y, y), c, jnp.where(c == 0, x, 1 - x))
    sibling, across = device(z, y, 1 - c, x), device(z, y, c, 1 - x)
    meet(z_peers + [to_first, to_second, sibling])

    def send(src, dst, w, s, peer):
        return pltpu.make_async_remote_copy(
            src_ref=src, dst_ref=dst, send_sem=ssem.at[w, s], recv_sem=rsem.at[w, s],
            device_id=peer, device_id_type=MESH_ID,
        )

    def coords(kind, f, s):
        return f * kind + s * (1 - kind), f * (1 - kind) + s * kind

    def a_copy(w, f, s):
        yy, xx = coords(1 - c, f, s)
        return send(parts[w].at[:, yy, 1 - c, xx], got_a[w].at[f, s], w, 2 * f + s, sibling)

    def load(w, f, s):
        yy, xx = coords(c, f, s)
        return pltpu.make_async_copy(parts[w].at[:, yy, c, xx], held[w].at[f, s], lsem.at[w, 2 * f + s])

    def b_copy(w):
        return send(held[w].at[1 - first], got_b[w], w, 4, to_first)

    def c_copy(w):
        return send(held[w].at[first, 1 - second], got_c[w], w, 5, to_second)

    def d_copy(w, k):
        return send(held[w].at[first, second, lax.rem(z + k + 1, NZ)], got_d[w].at[k], w, 6 + k, z_peers[k])

    def phase(w, number):
        if number == 0:
            for f in range(2):
                for s in range(2):
                    a_copy(w, f, s).start()
                    load(w, f, s).start()
        elif number == 1:
            for f in range(2):
                for s in range(2):
                    load(w, f, s).wait()
                    a_copy(w, f, s).wait_recv()

                    @pl.loop(0, NZ)
                    def _(q):
                        held[w][f, s, q] = held[w][f, s, q] + got_a[w][f, s, q]

            b_copy(w).start()
        elif number == 2:
            b_copy(w).wait_recv()
            for s in range(2):

                @pl.loop(0, NZ)
                def _(q):
                    held[w][first, s, q] = held[w][first, s, q] + got_b[w][s, q]

            c_copy(w).start()
        elif number == 3:
            c_copy(w).wait_recv()

            @pl.loop(0, NZ)
            def _(q):
                held[w][first, second, q] = held[w][first, second, q] + got_c[w][q]

            for k in range(3):
                d_copy(w, k).start()
        else:
            for k in range(3):
                d_copy(w, k).wait_recv()
            total = held[w][first, second, z].astype(F32)
            for k in range(3):
                total = total + got_d[w][k].astype(F32)
            stage[w][...] = total
            pltpu.make_async_copy(stage[w], outs[w], osem.at[w]).start()

    moves = []
    for n, (src, dst) in enumerate(((y_blk, y_got), (g_blk, g_got))):
        moves.append(
            pltpu.make_async_remote_copy(
                src_ref=src.at[:, 1 - x], dst_ref=dst, send_sem=xssem.at[n], recv_sem=xrsem.at[n],
                device_id=across, device_id_type=MESH_ID,
            )
        )
    for move in moves:
        move.start()
    for step in range(count + 4):
        for w in range(count):
            if 0 <= step - w <= 4:
                phase(w, step - w)
    for move in moves:
        move.wait()
    for w in range(count):
        for f in range(2):
            for s in range(2):
                a_copy(w, f, s).wait_send()
        b_copy(w).wait_send()
        c_copy(w).wait_send()
        for k in range(3):
            d_copy(w, k).wait_send()
        pltpu.make_async_copy(stage[w], outs[w], osem.at[w]).wait()


def reduce_all(parts, y_blk, g_blk):
    count = len(parts)
    anywhere = pl.BlockSpec(memory_space=pl.ANY)
    dma = pltpu.SemaphoreType.DMA
    shapes = [(p.shape[4:], p.dtype) for p in parts]
    got = jax.ShapeDtypeStruct((SHARE,) + y_blk.shape[2:], y_blk.dtype)
    scratch = (
        [pltpu.VMEM((2, 2, NZ) + s, d) for s, d in shapes]
        + [pltpu.VMEM((2, 2, NZ) + s, d) for s, d in shapes]
        + [pltpu.VMEM((2, NZ) + s, d) for s, d in shapes]
        + [pltpu.VMEM((NZ,) + s, d) for s, d in shapes]
        + [pltpu.VMEM((NZ - 1,) + s, d) for s, d in shapes]
        + [pltpu.VMEM(s, F32) for s, d in shapes]
        + [dma((count, 4)), dma((count, 9)), dma((count, 9)), dma((count,)), dma((2,)), dma((2,))]
    )
    return pl.pallas_call(
        partial(reduce_kernel, count),
        out_shape=[jax.ShapeDtypeStruct(s, F32) for s, d in shapes] + [got, got],
        in_specs=[anywhere] * (count + 2),
        out_specs=[anywhere] * (count + 2),
        scratch_shapes=scratch,
        compiler_params=pltpu.CompilerParams(collective_id=1, has_side_effects=True, vmem_limit_bytes=60 << 20),
        name="reduce_gradients",
    )(*parts, y_blk, g_blk)


SMALL = (("b_qkv", 3 * D), ("b_out", D), ("g1", D), ("b1", D), ("b_up", 4 * D), ("b_down", D), ("g2", D), ("b2", D))
TILE = (8, 128)
N_DEV = NZ * NY * NC * NX


def pack_small(vectors, lead):
    flat = jnp.concatenate([v.reshape(lead + (-1,)) for v in vectors], -1)
    room = TILE[0] * TILE[1] - flat.shape[-1]
    return jnp.pad(flat, [(0, 0)] * len(lead) + [(0, room)]).reshape(lead + TILE)


def unpack_small(tiles):
    lead = tiles.shape[:-2]
    flat = tiles.reshape(lead + (-1,))
    found, at = [], 0
    for _, size in SMALL:
        width = size // N_DEV
        found.append(flat[..., at : at + width].reshape(-1))
        at += width
    return found


def dot(a, b, ca=1, cb=0):
    return lax.dot_general(a, b, (((ca,), (cb,)), ((), ())), preferred_element_type=F32)


SCALE = DH ** (-0.25)


def features(rows, proj):
    wide = rows.astype(F32)
    arg = SCALE * jnp.einsum("bhtd,md->bhtm", rows, proj, preferred_element_type=F32)
    arg = arg - 0.5 * SCALE * SCALE * jnp.sum(wide * wide, -1, keepdims=True)
    return jnp.exp(arg) * FEATS ** (-0.5)


def features_back(rows, grad, proj):
    back = SCALE * jnp.einsum("bhtm,md->bhtd", grad, proj, preferred_element_type=F32)
    return back - SCALE * SCALE * rows.astype(F32) * jnp.sum(grad.astype(F32), -1, keepdims=True)


def normalize(r):
    center = r - jnp.mean(r, -1, keepdims=True)
    scale = lax.rsqrt(jnp.mean(center * center, -1, keepdims=True) + EPSILON)
    return center * scale, scale


def normalize_back(dy, n, scale, gain):
    g = dy * gain
    return (g - jnp.mean(g, -1, keepdims=True) - n * jnp.mean(g * n, -1, keepdims=True)) * scale


def layer(tok, cot, seg, proj, w_qkv, w_out, w_up, w_down, small):
    blocks, size = seg.shape
    rows = blocks * size
    b_qkv, b_out, g1, b1, b_up, b_down, g2, b2 = [s.astype(F32) for s in small]

    def split(m):
        return m.reshape(blocks, size, H, DH).transpose(0, 2, 1, 3)

    def join(m):
        return m.transpose(0, 2, 1, 3).reshape(rows, D)

    qkv = (dot(tok, w_qkv) + b_qkv).astype(BF)
    q, k, v = (split(qkv[:, n * D : (n + 1) * D]) for n in range(3))
    phi_q, phi_k = features(q, proj).astype(BF), features(k, proj).astype(BF)
    same = (seg[:, :, None] == seg[:, None, :])[:, None]
    score = jnp.einsum("bhtm,bhsm->bhts", phi_q, phi_k, preferred_element_type=F32)
    score = jnp.where(same, score, 0.0).astype(BF)
    num = jnp.einsum("bhts,bhse->bhte", score, v, preferred_element_type=F32)
    den = jnp.sum(score.astype(F32), -1, keepdims=True)
    ratio = num / den
    att = join(ratio).astype(BF)
    n1, s1 = normalize(tok.astype(F32) + dot(att, w_out) + b_out)
    h1 = n1 * g1 + b1
    h1_low = h1.astype(BF)
    a = dot(h1_low, w_up) + b_up
    cdf = 0.5 * (1.0 + lax.erf(a * 2**-0.5))
    z = (a * cdf).astype(BF)
    slope = cdf + a * jnp.exp(-0.5 * a * a) * (0.5 / jnp.pi) ** 0.5
    n2, s2 = normalize(h1 + dot(z, w_down) + b_down)
    out = (n2 * g2 + b2).astype(BF)
    dy = cot.astype(F32)
    dr2 = normalize_back(dy, n2, s2, g2)
    df = dr2.astype(BF)
    da = (dot(df, w_down, 1, 1) * slope).astype(BF)
    dh1 = dr2 + dot(da, w_up, 1, 1)
    dr1 = normalize_back(dh1, n1, s1, g1)
    do = dr1.astype(BF)
    datt = split(dot(do, w_out, 1, 1))
    dnum = (datt / den).astype(BF)
    dden = (-jnp.sum(datt * ratio, -1, keepdims=True) / den).astype(BF)
    dscore = jnp.einsum("bhte,bhse->bhts", dnum, v, preferred_element_type=F32) + dden.astype(F32)
    dscore = jnp.where(same, dscore, 0.0).astype(BF)
    dphi_q = jnp.einsum("bhts,bhsm->bhtm", dscore, phi_k, preferred_element_type=F32)
    dphi_k = jnp.einsum("bhts,bhtm->bhsm", dscore, phi_q, preferred_element_type=F32)
    dv = jnp.einsum("bhts,bhte->bhse", score, dnum, preferred_element_type=F32)
    dq = features_back(q, (dphi_q * phi_q.astype(F32)).astype(BF), proj)
    dk = features_back(k, (dphi_k * phi_k.astype(F32)).astype(BF), proj)
    dqkv = jnp.concatenate([join(dq), join(dk), join(dv)], 1).astype(BF)
    grad_tok = dr1 + dot(dqkv, w_qkv, 1, 1)

    def total(m):
        return jnp.sum(m.astype(F32), 0)

    grads = [dot(tok, dqkv, 0, 0), dot(att, do, 0, 0), dot(h1_low, da, 0, 0), dot(z, df, 0, 0)]
    vectors = [total(dqkv), total(do), total(dh1 * n1), total(dh1), total(da), total(df), total(dy * n2), total(dy)]
    return out, grad_tok, [g.astype(BF) for g in grads], vectors


def fast_device(
    tokens_in, out_cotangent, segment_ids, feature_proj,
    w_qkv, b_qkv, w_out, b_out, ln1_gain, ln1_bias, w_up, b_up, w_down, b_down, ln2_gain, ln2_bias,
):
    x = lax.axis_index("feat")
    small = pack_small([b_qkv, b_out, ln1_gain, ln1_bias, b_up, b_down, ln2_gain, ln2_bias], ())
    *gathered, tok, cot = gather_all([w_qkv, w_out, w_up, w_down, small], tokens_in, out_cotangent)
    proj = lax.all_gather(feature_proj, "feat", axis=0, tiled=True)
    seg = lax.dynamic_slice_in_dim(segment_ids, x * SHARE, SHARE, 0)
    whole = [g.reshape(-1, g.shape[-1]) for g in gathered[:4]]
    out, grad_tok, grads, vectors = layer(
        tok.reshape(-1, D), cot.reshape(-1, D), seg, proj, *whole, unpack_small(gathered[4])
    )
    lead = (NZ, NY, NC, NX)
    shards = [g.reshape(lead + (-1, g.shape[-1])) for g in grads]
    shards.append(pack_small(vectors, (N_DEV,)).reshape(lead + TILE))
    half = (SHARE, NX, -1, D)
    out, grad_tok = out.reshape(half), grad_tok.reshape(half)
    *sums, out_got, grad_got = reduce_all(shards, out, grad_tok.astype(BF))

    def arrange(mine, theirs):
        mine = lax.dynamic_index_in_dim(mine, x, 1, keepdims=False)
        theirs = theirs.astype(mine.dtype)
        return jnp.where(x == 0, jnp.concatenate([mine, theirs]), jnp.concatenate([theirs, mine]))

    vec = unpack_small(sums[4])
    return (
        arrange(out, out_got), arrange(grad_tok, grad_got),
        sums[0], vec[0], sums[1], vec[1], vec[2], vec[3], sums[2], vec[4], sums[3], vec[5], vec[6], vec[7],
    )


def solution(mesh):
    return jax.shard_map(
        fast_device if fits(mesh) else on_device,
        mesh=mesh,
        in_specs=(
            P(None, ("dp", "feat"), None),
            P(None, ("dp", "feat"), None),
            P(None, "dp"),
            P("feat", None),
            P(("dp", "feat"), None),
            P(("dp", "feat")),
            P(("dp", "feat"), None),
            P(("dp", "feat")),
            P(("dp", "feat")),
            P(("dp", "feat")),
            P(("dp", "feat"), None),
            P(("dp", "feat")),
            P(("dp", "feat"), None),
            P(("dp", "feat")),
            P(("dp", "feat")),
            P(("dp", "feat")),
        ),
        out_specs=(
            P(None, ("dp", "feat"), None),
            P(None, ("dp", "feat"), None),
            P(("dp", "feat"), None),
            P(("dp", "feat")),
            P(("dp", "feat"), None),
            P(("dp", "feat")),
            P(("dp", "feat")),
            P(("dp", "feat")),
            P(("dp", "feat"), None),
            P(("dp", "feat")),
            P(("dp", "feat"), None),
            P(("dp", "feat")),
            P(("dp", "feat")),
            P(("dp", "feat")),
        ),
        check_vma=False,
    )
```

```python
from functools import partial

import jax
import jax.numpy as jnp
from jax import lax
from jax.experimental import pallas as pl
from jax.experimental.pallas import tpu as pltpu
from jax.sharding import PartitionSpec as P

D = 768
H = 12
DH = 64
FEATS = 256
MICRO = 4
SEGS = 4


EPSILON = 1e-05


def layer_norm(residual, norm_gain, norm_shift):
    center = residual - jnp.mean(residual, -1, keepdims=True)
    spread = jnp.mean(center * center, -1, keepdims=True)
    return center * lax.rsqrt(spread + EPSILON) * norm_gain + norm_shift


def cross_dot(left_op, right_op):
    return lax.dot_general(
        left_op, right_op, (((0,), (0,)), ((), ())), preferred_element_type=jnp.float32
    )


def back_dot(left_op, right_op):
    return lax.dot_general(
        left_op, right_op, (((1,), (1,)), ((), ())), preferred_element_type=jnp.float32
    )


def fetch_weights(
    w_qkv, b_qkv, w_out, b_out, ln1_gain, ln1_bias, w_up, b_up, w_down, b_down, ln2_gain, ln2_bias
):
    return (
        lax.all_gather(w_qkv, ("dp", "feat"), axis=0, tiled=True),
        lax.all_gather(b_qkv, ("dp", "feat"), axis=0, tiled=True),
        lax.all_gather(w_out, ("dp", "feat"), axis=0, tiled=True),
        lax.all_gather(b_out, ("dp", "feat"), axis=0, tiled=True),
        lax.all_gather(ln1_gain, ("dp", "feat"), axis=0, tiled=True),
        lax.all_gather(ln1_bias, ("dp", "feat"), axis=0, tiled=True),
        lax.all_gather(w_up, ("dp", "feat"), axis=0, tiled=True),
        lax.all_gather(b_up, ("dp", "feat"), axis=0, tiled=True),
        lax.all_gather(w_down, ("dp", "feat"), axis=0, tiled=True),
        lax.all_gather(b_down, ("dp", "feat"), axis=0, tiled=True),
        lax.all_gather(ln2_gain, ("dp", "feat"), axis=0, tiled=True),
        lax.all_gather(ln2_bias, ("dp", "feat"), axis=0, tiled=True),
    )


def feature_map(head_rows, feat_proj):
    feat_scale = DH ** (-0.25)
    proj_arg = feat_scale * jnp.einsum(
        "ghd,md->ghm", head_rows, feat_proj, preferred_element_type=jnp.float32
    )
    squares = jnp.einsum("ghd,ghd->gh", head_rows, head_rows, preferred_element_type=jnp.float32)
    proj_arg = proj_arg - 0.5 * feat_scale * feat_scale * squares[:, :, None]
    return jnp.exp(proj_arg) * FEATS ** (-0.5)


def feature_back(head_rows, feat_proj, grad_arg):
    feat_scale = DH ** (-0.25)
    proj_back = feat_scale * jnp.einsum(
        "ghm,md->ghd", grad_arg, feat_proj, preferred_element_type=jnp.float32
    )
    arg_total = jnp.sum(grad_arg.astype(jnp.float32), -1, keepdims=True)
    return proj_back - feat_scale * feat_scale * head_rows.astype(jnp.float32) * arg_total


def spread_segments(phi_low, member):
    tok_count, head_count, feat_width = phi_low.shape
    return (phi_low[:, :, None, :] * member[:, None, :, None]).reshape(
        tok_count, head_count, SEGS * feat_width
    )


def fold_segments(grad_wide, member_f):
    tok_count, head_count, wide_dim = grad_wide.shape
    shaped = grad_wide.reshape(tok_count, head_count, SEGS, wide_dim // SEGS)
    return jnp.sum(shaped * member_f[:, None, :, None], 2)


def micro_step(tokens, cotangent, seg_row, feat_proj, weights):
    (
        w_qkv,
        b_qkv,
        w_out,
        b_out,
        ln1_gain,
        ln1_bias,
        w_up,
        b_up,
        w_down,
        b_down,
        ln2_gain,
        ln2_bias,
    ) = weights
    tok_count = tokens.shape[0]
    qkv_rows = jnp.dot(tokens, w_qkv, preferred_element_type=jnp.float32) + b_qkv.astype(
        jnp.float32
    )
    qkv_low = qkv_rows.astype(jnp.bfloat16)
    grouped = lax.all_gather(qkv_low, "feat", axis=0, tiled=True)
    group_rows = grouped.shape[0]
    query_h = grouped[:, :D].reshape(group_rows, H, DH)
    key_h = grouped[:, D : 2 * D].reshape(group_rows, H, DH)
    value_h = grouped[:, 2 * D :].reshape(group_rows, H, DH)
    phi_q = feature_map(query_h, feat_proj)
    phi_k = feature_map(key_h, feat_proj)
    member_f = (seg_row[:, None] == jnp.arange(SEGS, dtype=jnp.int32)[None, :]).astype(jnp.float32)
    member = member_f.astype(jnp.bfloat16)
    wide_q = spread_segments(phi_q.astype(jnp.bfloat16), member)
    wide_k = spread_segments(phi_k.astype(jnp.bfloat16), member)
    ones_col = jnp.ones((group_rows,), jnp.bfloat16)
    kv_part = jnp.einsum("gha,ghe->hae", wide_k, value_h, preferred_element_type=jnp.float32)
    z_part = jnp.einsum("gha,g->ha", wide_k, ones_col, preferred_element_type=jnp.float32)
    kv_low = kv_part.astype(jnp.bfloat16)
    z_low = z_part.astype(jnp.bfloat16)
    numer_part = jnp.einsum(
        "gha,hae->ghe", wide_q, kv_low, preferred_element_type=jnp.float32
    ).reshape(group_rows, D)
    denom_part = jnp.einsum("gha,ha->gh", wide_q, z_low, preferred_element_type=jnp.float32)
    numer_sum, denom_sum = (
        lax.psum_scatter(numer_part, "feat", scatter_dimension=0, tiled=True),
        lax.psum_scatter(denom_part, "feat", scatter_dimension=0, tiled=True),
    )
    numer_h = numer_sum.reshape(tok_count, H, DH)
    att_low = (numer_h / denom_sum[:, :, None]).reshape(tok_count, D).astype(jnp.bfloat16)
    branch = jnp.dot(att_low, w_out, preferred_element_type=jnp.float32) + b_out.astype(jnp.float32)
    hidden_one, ln1_back = jax.vjp(
        layer_norm,
        tokens.astype(jnp.float32) + branch,
        ln1_gain.astype(jnp.float32),
        ln1_bias.astype(jnp.float32),
    )
    hid_low = hidden_one.astype(jnp.bfloat16)
    pre_act = jnp.dot(hid_low, w_up, preferred_element_type=jnp.float32) + b_up.astype(jnp.float32)
    act_val, gelu_back = jax.vjp(partial(jax.nn.gelu, approximate=False), pre_act)
    act_low = act_val.astype(jnp.bfloat16)
    ffn_out = jnp.dot(act_low, w_down, preferred_element_type=jnp.float32) + b_down.astype(
        jnp.float32
    )
    result, ln2_back = jax.vjp(
        layer_norm, hidden_one + ffn_out, ln2_gain.astype(jnp.float32), ln2_bias.astype(jnp.float32)
    )
    grad_r2, grad_gain2, grad_bias2 = ln2_back(cotangent.astype(jnp.float32))
    grad_ffn = grad_r2.astype(jnp.bfloat16)
    grad_bdown = jnp.sum(grad_ffn.astype(jnp.float32), 0)
    grad_wdown = cross_dot(act_low, grad_ffn)
    (grad_act,) = gelu_back(back_dot(grad_ffn, w_down))
    grad_pre = grad_act.astype(jnp.bfloat16)
    grad_bup = jnp.sum(grad_pre.astype(jnp.float32), 0)
    grad_wup = cross_dot(hid_low, grad_pre)
    grad_h1 = grad_r2 + back_dot(grad_pre, w_up)
    grad_r1, grad_gain1, grad_bias1 = ln1_back(grad_h1)
    grad_branch = grad_r1.astype(jnp.bfloat16)
    grad_bout = jnp.sum(grad_branch.astype(jnp.float32), 0)
    grad_wout = cross_dot(att_low, grad_branch)
    grad_att = back_dot(grad_branch, w_out).reshape(tok_count, H, DH)
    grad_num = (grad_att / denom_sum[:, :, None]).reshape(tok_count, D).astype(jnp.bfloat16)
    grad_den = (-jnp.sum(grad_att * numer_h, -1) / (denom_sum * denom_sum)).astype(jnp.bfloat16)
    group_num, group_den = (
        lax.all_gather(grad_num, "feat", axis=0, tiled=True),
        lax.all_gather(grad_den, "feat", axis=0, tiled=True),
    )
    group_num_h = group_num.reshape(group_rows, H, DH)
    grad_kv_part = jnp.einsum(
        "gha,ghe->hae", wide_q, group_num_h, preferred_element_type=jnp.float32
    )
    grad_z_part = jnp.einsum("gha,gh->ha", wide_q, group_den, preferred_element_type=jnp.float32)
    grad_kv = grad_kv_part.astype(jnp.bfloat16)
    grad_z = grad_z_part.astype(jnp.bfloat16)
    wide_gq = jnp.einsum("ghe,hae->gha", group_num_h, kv_low, preferred_element_type=jnp.float32)
    wide_gq = wide_gq + group_den[:, :, None].astype(jnp.float32) * z_low[None].astype(jnp.float32)
    grad_arg_q = (fold_segments(wide_gq, member_f) * phi_q).astype(jnp.bfloat16)
    wide_gk = jnp.einsum(
        "ghe,hae->gha", value_h, grad_kv, preferred_element_type=jnp.float32
    ) + grad_z[None].astype(jnp.float32)
    grad_arg_k = (fold_segments(wide_gk, member_f) * phi_k).astype(jnp.bfloat16)
    grad_value = jnp.einsum("gha,hae->ghe", wide_k, grad_kv, preferred_element_type=jnp.float32)
    grad_query = feature_back(query_h, feat_proj, grad_arg_q)
    grad_key = feature_back(key_h, feat_proj, grad_arg_k)
    grad_group = jnp.concatenate(
        [
            grad_query.reshape(group_rows, D),
            grad_key.reshape(group_rows, D),
            grad_value.reshape(group_rows, D),
        ],
        1,
    )
    grad_qkv = lax.psum_scatter(
        grad_group.astype(jnp.bfloat16), "feat", scatter_dimension=0, tiled=True
    )
    grad_bqkv = jnp.sum(grad_qkv.astype(jnp.float32), 0)
    grad_wqkv = cross_dot(tokens, grad_qkv)
    grad_tokens = grad_r1 + back_dot(grad_qkv, w_qkv)
    grads_now = (
        grad_wqkv,
        grad_bqkv,
        grad_wout,
        grad_bout,
        grad_gain1,
        grad_bias1,
        grad_wup,
        grad_bup,
        grad_wdown,
        grad_bdown,
        grad_gain2,
        grad_bias2,
    )
    return (result.astype(jnp.bfloat16), grad_tokens, grads_now)


def on_device(
    tokens_in,
    out_cotangent,
    segment_ids,
    feature_proj,
    w_qkv,
    b_qkv,
    w_out,
    b_out,
    ln1_gain,
    ln1_bias,
    w_up,
    b_up,
    w_down,
    b_down,
    ln2_gain,
    ln2_bias,
):
    totals = None
    outputs = []
    grad_inputs = []
    for micro_idx in range(MICRO):
        gathered = fetch_weights(
            w_qkv,
            b_qkv,
            w_out,
            b_out,
            ln1_gain,
            ln1_bias,
            w_up,
            b_up,
            w_down,
            b_down,
            ln2_gain,
            ln2_bias,
        )
        result, grad_tokens, grads_now = micro_step(
            tokens_in[micro_idx],
            out_cotangent[micro_idx],
            segment_ids[micro_idx],
            feature_proj,
            gathered,
        )
        outputs.append(result)
        grad_inputs.append(grad_tokens)
        totals = grads_now if totals is None else jax.tree.map(jnp.add, totals, grads_now)
    (
        grad_wqkv,
        grad_bqkv,
        grad_wout,
        grad_bout,
        grad_gain1,
        grad_bias1,
        grad_wup,
        grad_bup,
        grad_wdown,
        grad_bdown,
        grad_gain2,
        grad_bias2,
    ) = totals
    summed = (
        lax.psum_scatter(grad_wqkv, ("dp", "feat"), scatter_dimension=0, tiled=True),
        lax.psum_scatter(grad_bqkv, ("dp", "feat"), scatter_dimension=0, tiled=True),
        lax.psum_scatter(grad_wout, ("dp", "feat"), scatter_dimension=0, tiled=True),
        lax.psum_scatter(grad_bout, ("dp", "feat"), scatter_dimension=0, tiled=True),
        lax.psum_scatter(grad_gain1, ("dp", "feat"), scatter_dimension=0, tiled=True),
        lax.psum_scatter(grad_bias1, ("dp", "feat"), scatter_dimension=0, tiled=True),
        lax.psum_scatter(grad_wup, ("dp", "feat"), scatter_dimension=0, tiled=True),
        lax.psum_scatter(grad_bup, ("dp", "feat"), scatter_dimension=0, tiled=True),
        lax.psum_scatter(grad_wdown, ("dp", "feat"), scatter_dimension=0, tiled=True),
        lax.psum_scatter(grad_bdown, ("dp", "feat"), scatter_dimension=0, tiled=True),
        lax.psum_scatter(grad_gain2, ("dp", "feat"), scatter_dimension=0, tiled=True),
        lax.psum_scatter(grad_bias2, ("dp", "feat"), scatter_dimension=0, tiled=True),
    )
    return (
        jnp.stack(outputs),
        jnp.stack(grad_inputs),
        summed[0],
        summed[1],
        summed[2],
        summed[3],
        summed[4],
        summed[5],
        summed[6],
        summed[7],
        summed[8],
        summed[9],
        summed[10],
        summed[11],
    )


NZ, NY, NC, NX = 4, 2, 2, 2
MESH_ID = pl.DeviceIdType.MESH
BF = jnp.bfloat16
F32 = jnp.float32
SHARE = MICRO // NX


def fits(mesh):
    return mesh.shape["dp"] == NZ * NY * NC and mesh.shape["feat"] == NX


def place():
    i = lax.axis_index("dp")
    return i // (NY * NC), (i // NC) % NY, i % NC, lax.axis_index("feat")


def device(z, y, c, x):
    return (z * (NY * NC) + y * NC + c, x)


def meet(peers):
    barrier = pltpu.get_barrier_semaphore()
    for peer in peers:
        pl.semaphore_signal(barrier, inc=1, device_id=peer, device_id_type=MESH_ID)
    pl.semaphore_wait(barrier, len(peers))


def gather_kernel(count, *refs):
    ins, tok, cot = refs[:count], refs[count], refs[count + 1]
    outs, tok_all, cot_all = refs[count + 2 : 2 * count + 2], refs[2 * count + 2], refs[2 * count + 3]
    lsem, ssem, rsem, xlsem, xssem, xrsem = refs[2 * count + 4 :]
    z, y, c, x = place()
    z_peers = [device(lax.rem(z + k, NZ), y, c, x) for k in (1, 2, 3)]
    y2, x2 = jnp.where(c == 0, 1 - y, y), jnp.where(c == 0, x, 1 - x)
    y3, x3 = jnp.where(c == 0, y, 1 - y), jnp.where(c == 0, 1 - x, x)
    second, third = device(z, y2, c, x2), device(z, y3, c, x3)
    sibling, across = device(z, y, 1 - c, x), device(z, y, c, 1 - x)
    meet(z_peers + [second, third, sibling])

    def send(src, dst, w, s, peer):
        return pltpu.make_async_remote_copy(
            src_ref=src, dst_ref=dst, send_sem=ssem.at[w, s], recv_sem=rsem.at[w, s],
            device_id=peer, device_id_type=MESH_ID,
        )

    def own(w):
        return pltpu.make_async_copy(ins[w], outs[w].at[z, y, c, x], lsem.at[w])

    def swap(n, src, dst):
        there = pltpu.make_async_remote_copy(
            src_ref=src.at[pl.ds((1 - x) * SHARE, SHARE)], dst_ref=dst.at[:, x],
            send_sem=xssem.at[n], recv_sem=xrsem.at[n], device_id=across, device_id_type=MESH_ID,
        )
        here = pltpu.make_async_copy(src.at[pl.ds(x * SHARE, SHARE)], dst.at[:, x], xlsem.at[n])
        return there, here

    def z_copy(w, k):
        return send(ins[w], outs[w].at[z, y, c, x], w, k, z_peers[k])

    for w in range(count):
        own(w).start()

    def phase(w, number):
        out = outs[w]
        four, eight = out.at[:, y, c, x], out.at[:, :, c, x]
        if number == 0:
            for k in range(3):
                z_copy(w, k).start()
        elif number == 1:
            for k in range(3):
                z_copy(w, k).wait_recv()
            own(w).wait()
            send(four, four, w, 3, second).start()
            send(four, four, w, 4, sibling).start()
        elif number == 2:
            send(four, four, w, 3, second).wait_recv()

            @pl.when(c == 0)
            def _():
                part = out.at[:, :, c, x]
                send(part, part, w, 5, third).start()

            @pl.when(c == 1)
            def _():
                part = out.at[:, y, c, :]
                send(part, part, w, 5, third).start()

            part = out.at[:, y2, c, x2]
            send(part, part, w, 6, sibling).start()
        else:
            send(eight, eight, w, 5, third).wait_recv()

            @pl.when(c == 0)
            def _():
                part = out.at[:, :, c, 1 - x]
                send(part, part, w, 7, sibling).start()

            @pl.when(c == 1)
            def _():
                part = out.at[:, 1 - y, c, :]
                send(part, part, w, 7, sibling).start()

    moves = [swap(0, tok, tok_all), swap(1, cot, cot_all)]
    for there, here in moves:
        there.start()
        here.start()
    for step in range(count + 3):
        for w in range(count):
            if 0 <= step - w <= 3:
                phase(w, step - w)
    for there, here in moves:
        there.wait()
        here.wait()
    for w in range(count):
        four, eight = outs[w].at[:, y, c, x], outs[w].at[:, :, c, x]
        for k in range(3):
            z_copy(w, k).wait_send()
        send(four, four, w, 3, second).wait_send()
        send(four, four, w, 4, sibling).wait()
        send(eight, eight, w, 5, third).wait_send()
        send(four, four, w, 6, sibling).wait()
        send(eight, eight, w, 7, sibling).wait()


def gather_all(shards, tok, cot):
    count = len(shards)
    block = jax.ShapeDtypeStruct((SHARE, NX) + tok.shape[1:], tok.dtype)
    anywhere = pl.BlockSpec(memory_space=pl.ANY)
    dma = pltpu.SemaphoreType.DMA
    return pl.pallas_call(
        partial(gather_kernel, count),
        out_shape=[jax.ShapeDtypeStruct((NZ, NY, NC, NX) + s.shape, s.dtype) for s in shards] + [block, block],
        in_specs=[anywhere] * (count + 2),
        out_specs=[anywhere] * (count + 2),
        scratch_shapes=[dma((count,)), dma((count, 8)), dma((count, 8)), dma((2,)), dma((2,)), dma((2,))],
        compiler_params=pltpu.CompilerParams(collective_id=0, has_side_effects=True),
        name="gather_weights",
    )(*shards, tok, cot)


def reduce_kernel(count, *refs):
    parts, y_blk, g_blk = refs[:count], refs[count], refs[count + 1]
    outs, y_got, g_got = refs[count + 2 : 2 * count + 2], refs[2 * count + 2], refs[2 * count + 3]
    scratch = refs[2 * count + 4 :]
    held, got_a = scratch[:count], scratch[count : 2 * count]
    got_b, got_c, got_d = scratch[2 * count : 3 * count], scratch[3 * count : 4 * count], scratch[4 * count : 5 * count]
    stage = scratch[5 * count : 6 * count]
    lsem, ssem, rsem, osem, xssem, xrsem = scratch[6 * count :]
    z, y, c, x = place()
    z_peers = [device(lax.rem(z + k, NZ), y, c, x) for k in (1, 2, 3)]
    first, second = jnp.where(c == 0, x, y), jnp.where(c == 0, y, x)
    to_first = device(z, jnp.where(c == 0, y, 1 - y), c, jnp.where(c == 0, 1 - x, x))
    to_second = device(z, jnp.where(c == 0, 1 - y, y), c, jnp.where(c == 0, x, 1 - x))
    sibling, across = device(z, y, 1 - c, x), device(z, y, c, 1 - x)
    meet(z_peers + [to_first, to_second, sibling])

    def send(src, dst, w, s, peer):
        return pltpu.make_async_remote_copy(
            src_ref=src, dst_ref=dst, send_sem=ssem.at[w, s], recv_sem=rsem.at[w, s],
            device_id=peer, device_id_type=MESH_ID,
        )

    def coords(kind, f, s):
        return f * kind + s * (1 - kind), f * (1 - kind) + s * kind

    def a_copy(w, f, s):
        yy, xx = coords(1 - c, f, s)
        return send(parts[w].at[:, yy, 1 - c, xx], got_a[w].at[f, s], w, 2 * f + s, sibling)

    def load(w, f, s):
        yy, xx = coords(c, f, s)
        return pltpu.make_async_copy(parts[w].at[:, yy, c, xx], held[w].at[f, s], lsem.at[w, 2 * f + s])

    def b_copy(w):
        return send(held[w].at[1 - first], got_b[w], w, 4, to_first)

    def c_copy(w):
        return send(held[w].at[first, 1 - second], got_c[w], w, 5, to_second)

    def d_copy(w, k):
        return send(held[w].at[first, second, lax.rem(z + k + 1, NZ)], got_d[w].at[k], w, 6 + k, z_peers[k])

    def phase(w, number):
        if number == 0:
            for f in range(2):
                for s in range(2):
                    a_copy(w, f, s).start()
                    load(w, f, s).start()
        elif number == 1:
            for f in range(2):
                for s in range(2):
                    load(w, f, s).wait()
                    a_copy(w, f, s).wait_recv()

                    @pl.loop(0, NZ)
                    def _(q):
                        held[w][f, s, q] = held[w][f, s, q] + got_a[w][f, s, q]

            b_copy(w).start()
        elif number == 2:
            b_copy(w).wait_recv()
            for s in range(2):

                @pl.loop(0, NZ)
                def _(q):
                    held[w][first, s, q] = held[w][first, s, q] + got_b[w][s, q]

            c_copy(w).start()
        elif number == 3:
            c_copy(w).wait_recv()

            @pl.loop(0, NZ)
            def _(q):
                held[w][first, second, q] = held[w][first, second, q] + got_c[w][q]

            for k in range(3):
                d_copy(w, k).start()
        else:
            for k in range(3):
                d_copy(w, k).wait_recv()
            total = held[w][first, second, z].astype(F32)
            for k in range(3):
                total = total + got_d[w][k].astype(F32)
            stage[w][...] = total
            pltpu.make_async_copy(stage[w], outs[w], osem.at[w]).start()

    moves = []
    for n, (src, dst) in enumerate(((y_blk, y_got), (g_blk, g_got))):
        moves.append(
            pltpu.make_async_remote_copy(
                src_ref=src.at[:, 1 - x], dst_ref=dst, send_sem=xssem.at[n], recv_sem=xrsem.at[n],
                device_id=across, device_id_type=MESH_ID,
            )
        )
    for move in moves:
        move.start()
    for step in range(count + 4):
        for w in range(count):
            if 0 <= step - w <= 4:
                phase(w, step - w)
    for move in moves:
        move.wait()
    for w in range(count):
        for f in range(2):
            for s in range(2):
                a_copy(w, f, s).wait_send()
        b_copy(w).wait_send()
        c_copy(w).wait_send()
        for k in range(3):
            d_copy(w, k).wait_send()
        pltpu.make_async_copy(stage[w], outs[w], osem.at[w]).wait()


def reduce_all(parts, y_blk, g_blk):
    count = len(parts)
    anywhere = pl.BlockSpec(memory_space=pl.ANY)
    dma = pltpu.SemaphoreType.DMA
    shapes = [(p.shape[4:], p.dtype) for p in parts]
    got = jax.ShapeDtypeStruct((SHARE,) + y_blk.shape[2:], y_blk.dtype)
    scratch = (
        [pltpu.VMEM((2, 2, NZ) + s, d) for s, d in shapes]
        + [pltpu.VMEM((2, 2, NZ) + s, d) for s, d in shapes]
        + [pltpu.VMEM((2, NZ) + s, d) for s, d in shapes]
        + [pltpu.VMEM((NZ,) + s, d) for s, d in shapes]
        + [pltpu.VMEM((NZ - 1,) + s, d) for s, d in shapes]
        + [pltpu.VMEM(s, F32) for s, d in shapes]
        + [dma((count, 4)), dma((count, 9)), dma((count, 9)), dma((count,)), dma((2,)), dma((2,))]
    )
    return pl.pallas_call(
        partial(reduce_kernel, count),
        out_shape=[jax.ShapeDtypeStruct(s, F32) for s, d in shapes] + [got, got],
        in_specs=[anywhere] * (count + 2),
        out_specs=[anywhere] * (count + 2),
        scratch_shapes=scratch,
        compiler_params=pltpu.CompilerParams(collective_id=1, has_side_effects=True, vmem_limit_bytes=60 << 20),
        name="reduce_gradients",
    )(*parts, y_blk, g_blk)


SMALL = (("b_qkv", 3 * D), ("b_out", D), ("g1", D), ("b1", D), ("b_up", 4 * D), ("b_down", D), ("g2", D), ("b2", D))
TILE = (8, 128)
N_DEV = NZ * NY * NC * NX


def pack_small(vectors, lead):
    flat = jnp.concatenate([v.reshape(lead + (-1,)) for v in vectors], -1)
    room = TILE[0] * TILE[1] - flat.shape[-1]
    return jnp.pad(flat, [(0, 0)] * len(lead) + [(0, room)]).reshape(lead + TILE)


def unpack_small(tiles):
    lead = tiles.shape[:-2]
    flat = tiles.reshape(lead + (-1,))
    found, at = [], 0
    for _, size in SMALL:
        width = size // N_DEV
        found.append(flat[..., at : at + width].reshape(-1))
        at += width
    return found


ROWS = 512
BLK = 256
PAIRS = D // 128
FF = 4 * D
WIDE = 2 * FEATS
SCALE = DH ** (-0.25)


def dot(a, b, ca=1, cb=0):
    return lax.dot_general(a, b, (((ca,), (cb,)), ((), ())), preferred_element_type=F32)


def half_masks(width):
    lane = lax.broadcasted_iota(jnp.int32, (1, width), 1) % 128
    first = (lane < DH).astype(F32)
    return first.astype(BF), (1.0 - first).astype(BF)


def blocks_of(count, body):
    def step(j, carry):
        body(j)
        return carry

    lax.fori_loop(0, count, step, 0)


def lanes(j, width):
    return pl.ds(pl.multiple_of(j * width, width), width)


class Work:
    def __init__(self, refs):
        self.__dict__.update(refs)

    def setup(self, proj, seg_rows):
        row = lax.broadcasted_iota(jnp.int32, (DH, 128), 0)
        col = lax.broadcasted_iota(jnp.int32, (DH, 128), 1)
        for h in range(2):
            place_in = (col == row + h * DH).astype(BF)
            self.table[pl.ds(h * FEATS, FEATS), 0:128] = dot(proj, place_in).astype(BF)
        feat = lax.broadcasted_iota(jnp.int32, (WIDE, 128), 0) // FEATS
        half = lax.broadcasted_iota(jnp.int32, (WIDE, 128), 1) // DH
        same = (feat == half).astype(F32).astype(BF)
        self.table[:, 128:256] = same
        for b in range(2):
            across = jnp.broadcast_to(seg_rows[b], (BLK, BLK))
            self.mask[b] = (across == jnp.transpose(across)).astype(F32)

    def features(self, rows):
        wide = rows.astype(F32)
        squares = wide * wide
        high = squares.astype(BF)
        low = (squares - high.astype(F32)).astype(BF)
        same = self.table[:, 128:256]
        norm = dot(high, same, 1, 1) + dot(low, same, 1, 1)
        arg = SCALE * dot(rows, self.table[:, 0:128], 1, 1) - (0.5 * SCALE * SCALE) * norm
        return (jnp.exp(arg) * FEATS ** (-0.5)).astype(BF)

    def qkv_block(self, j):
        col = lanes(j, 256)
        full = dot(self.x[...], self.w_qkv[:, col]) + self.b_qkv[:, col]
        self.qkv[:, col] = full.astype(BF)

    def pair(self, i):
        b, p = i // PAIRS, i % PAIRS
        rows = pl.ds(pl.multiple_of(b * BLK, BLK), BLK)
        cols = [pl.ds(pl.multiple_of(n * D + p * 128, 128), 128) for n in range(3)]
        return b, rows, cols

    def attend(self, i):
        b, rows, cols = self.pair(i)
        mask = self.mask[b]
        m0, m1 = half_masks(128)
        phi_q = self.features(self.qkv[rows, cols[0]])
        phi_k = self.features(self.qkv[rows, cols[1]])
        self.phi_q[i] = phi_q
        self.phi_k[i] = phi_k
        v = self.qkv[rows, cols[2]]
        one = jnp.ones((BLK, 128), BF)
        res = None
        for h, m in enumerate((m0, m1)):
            part = slice(h * FEATS, (h + 1) * FEATS)
            score = (dot(phi_q[:, part], phi_k[:, part], 1, 1) * mask).astype(BF)
            term = dot(score, jnp.concatenate([v * m, one * m], 1))
            res = term if res is None else res + term
        inv = 1.0 / res[:, 128:]
        self.inv[rows, cols[0]] = inv
        self.att[rows, cols[0]] = (res[:, :128] * inv).astype(BF)

    def normalize(self, r):
        center = r - jnp.mean(r, -1, keepdims=True)
        scale = lax.rsqrt(jnp.mean(center * center, -1, keepdims=True) + EPSILON)
        return center * scale, scale

    def normalize_back(self, dy, n, scale, gain):
        g = dy * gain
        return (g - jnp.mean(g, -1, keepdims=True) - n * jnp.mean(g * n, -1, keepdims=True)) * scale

    def branch(self):
        for j in range(3):
            col = lanes(j, 256)
            self.n1[:, col] = dot(self.att[...], self.w_out[:, col]) + self.b_out[:, col] + self.x[:, col].astype(F32)

        def rows_of(j):
            row = pl.ds(pl.multiple_of(j * 64, 64), 64)
            n1, s1 = self.normalize(self.n1[row, :])
            self.n1[row, :] = n1
            self.s1[row, :] = s1
            self.h1[row, :] = (n1 * self.g1[...] + self.b1[...]).astype(BF)

        blocks_of(ROWS // 64, rows_of)

    def up_block(self, j):
        col = lanes(j, 256)
        for r in range(0, ROWS, 128):
            row = slice(r, r + 128)
            a = dot(self.h1[row, :], self.w_up[:, col]) + self.b_up[:, col]
            cdf = 0.5 * (1.0 + lax.erf(a * 2**-0.5))
            self.z[row, col] = (a * cdf).astype(BF)
            self.slope[row, col] = (cdf + a * jnp.exp(-0.5 * a * a) * (0.5 / 3.141592653589793) ** 0.5).astype(BF)

    def down(self):
        def block(j):
            col = lanes(j, 256)
            back = self.n1[:, col] * self.g1[:, col] + self.b1[:, col]
            self.dr[:, col] = dot(self.z[...], self.w_down[:, col]) + self.b_down[:, col] + back

        blocks_of(3, block)
        for ref in (self.d_g2, self.d_b2, self.d_b_down):
            ref[...] = jnp.zeros_like(ref)

        def rows_of(j):
            row = pl.ds(pl.multiple_of(j * 64, 64), 64)
            n2, s2 = self.normalize(self.dr[row, :])
            self.y[row, :] = (n2 * self.g2[...] + self.b2[...]).astype(BF)
            dy = self.cot[row, :].astype(F32)
            dr2 = self.normalize_back(dy, n2, s2, self.g2[...])
            self.dr[row, :] = dr2
            df = dr2.astype(BF)
            self.df[row, :] = df
            self.d_g2[...] += jnp.sum(dy * n2, 0, keepdims=True)
            self.d_b2[...] += jnp.sum(dy, 0, keepdims=True)
            self.d_b_down[...] += jnp.sum(df.astype(F32), 0, keepdims=True)

        blocks_of(ROWS // 64, rows_of)

    def down_back(self, j):
        col = lanes(j, 256)
        dz = dot(self.df[...], self.w_down[col, :], 1, 1)
        da = (dz * self.slope[:, col].astype(F32)).astype(BF)
        self.slope[:, col] = da
        self.d_b_up[:, col] = jnp.sum(da.astype(F32), 0, keepdims=True)
        self.w_down[col, :] = dot(self.z[:, col], self.df[...], 0, 0).astype(BF)

    def up_back(self):
        def block(j):
            col = lanes(j, 256)
            self.dr[:, col] += dot(self.slope[...], self.w_up[col, :], 1, 1)

        blocks_of(3, block)
        self.flip[...] = jnp.transpose(self.h1[...])

    def up_grad(self, j):
        col = lanes(j, 256)
        self.w_up[:, col] = dot(self.flip[...], self.slope[:, col]).astype(BF)

    def branch_back(self):
        for ref in (self.d_g1, self.d_b1, self.d_b_out):
            ref[...] = jnp.zeros_like(ref)

        def rows_of(j):
            row = pl.ds(pl.multiple_of(j * 64, 64), 64)
            dh1, n1 = self.dr[row, :], self.n1[row, :]
            dr1 = self.normalize_back(dh1, n1, self.s1[row, :], self.g1[...])
            self.dr[row, :] = dr1
            do = dr1.astype(BF)
            self.df[row, :] = do
            self.d_g1[...] += jnp.sum(dh1 * n1, 0, keepdims=True)
            self.d_b1[...] += jnp.sum(dh1, 0, keepdims=True)
            self.d_b_out[...] += jnp.sum(do.astype(F32), 0, keepdims=True)

        blocks_of(ROWS // 64, rows_of)
        head_r = lax.broadcasted_iota(jnp.int32, (256, 256), 0) // DH
        head_c = lax.broadcasted_iota(jnp.int32, (256, 256), 1) // DH
        same = (head_r == head_c).astype(F32).astype(BF)

        def block(j):
            col = lanes(j, 256)
            datt = dot(self.df[...], self.w_out[col, :], 1, 1)
            inv = self.inv[:, col]
            self.dnum[:, col] = (datt * inv).astype(BF)
            prod = datt * self.att[:, col].astype(F32)
            high = prod.astype(BF)
            low = (prod - high.astype(F32)).astype(BF)
            total = dot(high, same) + dot(low, same)
            self.dden[:, col] = (-total * inv).astype(BF)

        blocks_of(3, block)
        self.flip[...] = jnp.transpose(self.att[...])

        def grad(j):
            col = lanes(j, 256)
            self.w_out[:, col] = dot(self.flip[...], self.df[:, col]).astype(BF)

        blocks_of(3, grad)

    def attend_back(self, i):
        b, rows, cols = self.pair(i)
        mask = self.mask[b]
        m0, m1 = half_masks(256)
        q, k, v = (self.qkv[rows, c] for c in cols)
        dnum, dden = self.dnum[rows, cols[0]], self.dden[rows, cols[0]]
        left = jnp.concatenate([dnum, dden * (1.0 / DH)], 1)
        right = jnp.concatenate([v, jnp.ones((BLK, 128), BF)], 1)
        back_q, back_k, dv = None, None, None
        for h, m in enumerate((m0, m1)):
            part = slice(h * FEATS, (h + 1) * FEATS)
            phi_q, phi_k = self.phi_q[i, :, part], self.phi_k[i, :, part]
            mine = left * m
            dscore = (dot(mine, right, 1, 1) * mask).astype(BF)
            flipped = (dot(right, mine, 1, 1) * mask).astype(BF)
            darg_q = (dot(dscore, phi_k) * phi_q.astype(F32)).astype(BF)
            darg_k = (dot(flipped, phi_q) * phi_k.astype(F32)).astype(BF)
            score = (dot(phi_k, phi_q, 1, 1) * mask).astype(BF)
            table = self.table[part, :]
            terms = dot(darg_q, table), dot(darg_k, table), dot(score, mine[:, :128])
            if h == 0:
                back_q, back_k, dv = terms
            else:
                back_q, back_k, dv = back_q + terms[0], back_k + terms[1], dv + terms[2]
        for n, (rows_in, back) in enumerate(((q, back_q), (k, back_k))):
            grad = SCALE * back[:, :128] - (SCALE * SCALE) * rows_in.astype(F32) * back[:, 128:]
            self.qkv[rows, cols[n]] = grad.astype(BF)
        self.qkv[rows, cols[2]] = dv.astype(BF)

    def tokens_back(self):
        def block(j):
            col = lanes(j, 256)
            self.dr[:, col] += dot(self.qkv[...], self.w_qkv[col, :], 1, 1)

        blocks_of(3, block)
        self.flip[...] = jnp.transpose(self.x[...])

    def qkv_grad(self, j):
        col = lanes(j, 256)
        part = self.qkv[:, col]
        self.d_b_qkv[:, col] = jnp.sum(part.astype(F32), 0, keepdims=True)
        self.w_qkv[:, col] = dot(self.flip[...], part).astype(BF)


VECTORS = ("b_qkv", "b_out", "g1", "b1", "b_up", "b_down", "g2", "b2")
WIDTHS = (3 * D, D, D, D, FF, D, D, D)
SPACE = (
    ("qkv", (ROWS, 3 * D), BF), ("phi_q", (2 * PAIRS, BLK, WIDE), BF), ("phi_k", (2 * PAIRS, BLK, WIDE), BF),
    ("att", (ROWS, D), BF), ("inv", (ROWS, D), F32), ("n1", (ROWS, D), F32), ("s1", (ROWS, 1), F32),
    ("h1", (ROWS, D), BF), ("z", (ROWS, FF), BF), ("slope", (ROWS, FF), BF), ("dr", (ROWS, D), F32),
    ("df", (ROWS, D), BF), ("dnum", (ROWS, D), BF), ("dden", (ROWS, D), BF), ("flip", (D, ROWS), BF),
    ("table", (WIDE, 256), BF), ("mask", (2, BLK, BLK), F32),
)


WEIGHTS = (("w_qkv", (D, 3 * D)), ("w_out", (D, D)), ("w_up", (D, FF)), ("w_down", (FF, D)))


def layer_kernel(*refs):
    it = iter(refs)
    hbm = [next(it) for _ in WEIGHTS]
    named = {n: next(it) for n in ("x", "cot")}
    proj, seg = next(it), next(it)
    named.update({n: next(it) for n in VECTORS})
    grads = [next(it) for _ in WEIGHTS]
    named.update(y=next(it))
    grad_tok = next(it)
    named.update({"d_" + n: next(it) for n in VECTORS})
    named.update({n: next(it) for n, _ in WEIGHTS})
    named.update({n: next(it) for n, _, _ in SPACE})
    sem = next(it)
    work = Work(named)
    loads = [pltpu.make_async_copy(hbm[n], named[w], sem.at[n]) for n, (w, _) in enumerate(WEIGHTS)]
    for load in loads:
        load.start()
    work.setup(proj[...], [seg[b : b + 1, :] for b in range(2)])
    loads[0].wait()
    blocks_of(9, work.qkv_block)
    blocks_of(2 * PAIRS, work.attend)
    loads[1].wait()
    work.branch()
    loads[2].wait()
    blocks_of(12, work.up_block)
    loads[3].wait()
    work.down()
    blocks_of(12, work.down_back)
    work.up_back()
    blocks_of(12, work.up_grad)
    work.branch_back()
    blocks_of(2 * PAIRS, work.attend_back)
    work.tokens_back()
    blocks_of(9, work.qkv_grad)
    grad_tok[...] = work.dr[...]
    stores = [pltpu.make_async_copy(named[w], grads[n], sem.at[n]) for n, (w, _) in enumerate(WEIGHTS)]
    for store in stores:
        store.start()
    for store in stores:
        store.wait()


def layer(tok, cot, seg, proj, weights, small):
    anywhere = pl.BlockSpec(memory_space=pl.ANY)
    vmem = pl.BlockSpec(memory_space=pltpu.VMEM)
    vectors = [s.astype(F32).reshape(1, -1) for s in small]
    shape = jax.ShapeDtypeStruct
    outs = pl.pallas_call(
        layer_kernel,
        out_shape=[shape(s, BF) for _, s in WEIGHTS] + [shape((ROWS, D), BF), shape((ROWS, D), F32)]
        + [shape((1, w), F32) for w in WIDTHS],
        in_specs=[anywhere] * 4 + [vmem] * 12,
        out_specs=[anywhere] * 4 + [vmem] * 10,
        scratch_shapes=[pltpu.VMEM(s, BF) for _, s in WEIGHTS] + [pltpu.VMEM(s, d) for _, s, d in SPACE]
        + [pltpu.SemaphoreType.DMA((4,))],
        compiler_params=pltpu.CompilerParams(vmem_limit_bytes=60 << 20),
        name="layer",
    )(*weights, tok, cot, proj, seg.astype(F32), *vectors)
    return outs[4], outs[5], outs[:4], outs[6:]


def fast_device(
    tokens_in, out_cotangent, segment_ids, feature_proj,
    w_qkv, b_qkv, w_out, b_out, ln1_gain, ln1_bias, w_up, b_up, w_down, b_down, ln2_gain, ln2_bias,
):
    x = lax.axis_index("feat")
    small = pack_small([b_qkv, b_out, ln1_gain, ln1_bias, b_up, b_down, ln2_gain, ln2_bias], ())
    *gathered, tok, cot = gather_all([w_qkv, w_out, w_up, w_down, small], tokens_in, out_cotangent)
    proj = lax.all_gather(feature_proj, "feat", axis=0, tiled=True)
    seg = lax.dynamic_slice_in_dim(segment_ids, x * SHARE, SHARE, 0)
    whole = [g.reshape(-1, g.shape[-1]) for g in gathered[:4]]
    out, grad_tok, grads, vectors = layer(
        tok.reshape(-1, D), cot.reshape(-1, D), seg, proj, whole, unpack_small(gathered[4])
    )
    lead = (NZ, NY, NC, NX)
    shards = [g.reshape(lead + (-1, g.shape[-1])) for g in grads]
    shards.append(pack_small(vectors, (N_DEV,)).reshape(lead + TILE))
    half = (SHARE, NX, -1, D)
    out, grad_tok = out.reshape(half), grad_tok.reshape(half)
    *sums, out_got, grad_got = reduce_all(shards, out, grad_tok.astype(BF))

    def arrange(mine, theirs):
        mine = lax.dynamic_index_in_dim(mine, x, 1, keepdims=False)
        theirs = theirs.astype(mine.dtype)
        return jnp.where(x == 0, jnp.concatenate([mine, theirs]), jnp.concatenate([theirs, mine]))

    vec = unpack_small(sums[4])
    return (
        arrange(out, out_got), arrange(grad_tok, grad_got),
        sums[0], vec[0], sums[1], vec[1], vec[2], vec[3], sums[2], vec[4], sums[3], vec[5], vec[6], vec[7],
    )


def solution(mesh):
    return jax.shard_map(
        fast_device if fits(mesh) else on_device,
        mesh=mesh,
        in_specs=(
            P(None, ("dp", "feat"), None),
            P(None, ("dp", "feat"), None),
            P(None, "dp"),
            P("feat", None),
            P(("dp", "feat"), None),
            P(("dp", "feat")),
            P(("dp", "feat"), None),
            P(("dp", "feat")),
            P(("dp", "feat")),
            P(("dp", "feat")),
            P(("dp", "feat"), None),
            P(("dp", "feat")),
            P(("dp", "feat"), None),
            P(("dp", "feat")),
            P(("dp", "feat")),
            P(("dp", "feat")),
        ),
        out_specs=(
            P(None, ("dp", "feat"), None),
            P(None, ("dp", "feat"), None),
            P(("dp", "feat"), None),
            P(("dp", "feat")),
            P(("dp", "feat"), None),
            P(("dp", "feat")),
            P(("dp", "feat")),
            P(("dp", "feat")),
            P(("dp", "feat"), None),
            P(("dp", "feat")),
            P(("dp", "feat"), None),
            P(("dp", "feat")),
            P(("dp", "feat")),
            P(("dp", "feat")),
        ),
        check_vma=False,
    )
```

```python
from functools import partial

import jax
import jax.numpy as jnp
from jax import lax
from jax.experimental import pallas as pl
from jax.experimental.pallas import tpu as pltpu
from jax.sharding import PartitionSpec as P

D = 768
H = 12
DH = 64
FEATS = 256
MICRO = 4
SEGS = 4


EPSILON = 1e-05


def layer_norm(residual, norm_gain, norm_shift):
    center = residual - jnp.mean(residual, -1, keepdims=True)
    spread = jnp.mean(center * center, -1, keepdims=True)
    return center * lax.rsqrt(spread + EPSILON) * norm_gain + norm_shift


def cross_dot(left_op, right_op):
    return lax.dot_general(
        left_op, right_op, (((0,), (0,)), ((), ())), preferred_element_type=jnp.float32
    )


def back_dot(left_op, right_op):
    return lax.dot_general(
        left_op, right_op, (((1,), (1,)), ((), ())), preferred_element_type=jnp.float32
    )


def fetch_weights(
    w_qkv, b_qkv, w_out, b_out, ln1_gain, ln1_bias, w_up, b_up, w_down, b_down, ln2_gain, ln2_bias
):
    return (
        lax.all_gather(w_qkv, ("dp", "feat"), axis=0, tiled=True),
        lax.all_gather(b_qkv, ("dp", "feat"), axis=0, tiled=True),
        lax.all_gather(w_out, ("dp", "feat"), axis=0, tiled=True),
        lax.all_gather(b_out, ("dp", "feat"), axis=0, tiled=True),
        lax.all_gather(ln1_gain, ("dp", "feat"), axis=0, tiled=True),
        lax.all_gather(ln1_bias, ("dp", "feat"), axis=0, tiled=True),
        lax.all_gather(w_up, ("dp", "feat"), axis=0, tiled=True),
        lax.all_gather(b_up, ("dp", "feat"), axis=0, tiled=True),
        lax.all_gather(w_down, ("dp", "feat"), axis=0, tiled=True),
        lax.all_gather(b_down, ("dp", "feat"), axis=0, tiled=True),
        lax.all_gather(ln2_gain, ("dp", "feat"), axis=0, tiled=True),
        lax.all_gather(ln2_bias, ("dp", "feat"), axis=0, tiled=True),
    )


def feature_map(head_rows, feat_proj):
    feat_scale = DH ** (-0.25)
    proj_arg = feat_scale * jnp.einsum(
        "ghd,md->ghm", head_rows, feat_proj, preferred_element_type=jnp.float32
    )
    squares = jnp.einsum("ghd,ghd->gh", head_rows, head_rows, preferred_element_type=jnp.float32)
    proj_arg = proj_arg - 0.5 * feat_scale * feat_scale * squares[:, :, None]
    return jnp.exp(proj_arg) * FEATS ** (-0.5)


def feature_back(head_rows, feat_proj, grad_arg):
    feat_scale = DH ** (-0.25)
    proj_back = feat_scale * jnp.einsum(
        "ghm,md->ghd", grad_arg, feat_proj, preferred_element_type=jnp.float32
    )
    arg_total = jnp.sum(grad_arg.astype(jnp.float32), -1, keepdims=True)
    return proj_back - feat_scale * feat_scale * head_rows.astype(jnp.float32) * arg_total


def spread_segments(phi_low, member):
    tok_count, head_count, feat_width = phi_low.shape
    return (phi_low[:, :, None, :] * member[:, None, :, None]).reshape(
        tok_count, head_count, SEGS * feat_width
    )


def fold_segments(grad_wide, member_f):
    tok_count, head_count, wide_dim = grad_wide.shape
    shaped = grad_wide.reshape(tok_count, head_count, SEGS, wide_dim // SEGS)
    return jnp.sum(shaped * member_f[:, None, :, None], 2)


def micro_step(tokens, cotangent, seg_row, feat_proj, weights):
    (
        w_qkv,
        b_qkv,
        w_out,
        b_out,
        ln1_gain,
        ln1_bias,
        w_up,
        b_up,
        w_down,
        b_down,
        ln2_gain,
        ln2_bias,
    ) = weights
    tok_count = tokens.shape[0]
    qkv_rows = jnp.dot(tokens, w_qkv, preferred_element_type=jnp.float32) + b_qkv.astype(
        jnp.float32
    )
    qkv_low = qkv_rows.astype(jnp.bfloat16)
    grouped = lax.all_gather(qkv_low, "feat", axis=0, tiled=True)
    group_rows = grouped.shape[0]
    query_h = grouped[:, :D].reshape(group_rows, H, DH)
    key_h = grouped[:, D : 2 * D].reshape(group_rows, H, DH)
    value_h = grouped[:, 2 * D :].reshape(group_rows, H, DH)
    phi_q = feature_map(query_h, feat_proj)
    phi_k = feature_map(key_h, feat_proj)
    member_f = (seg_row[:, None] == jnp.arange(SEGS, dtype=jnp.int32)[None, :]).astype(jnp.float32)
    member = member_f.astype(jnp.bfloat16)
    wide_q = spread_segments(phi_q.astype(jnp.bfloat16), member)
    wide_k = spread_segments(phi_k.astype(jnp.bfloat16), member)
    ones_col = jnp.ones((group_rows,), jnp.bfloat16)
    kv_part = jnp.einsum("gha,ghe->hae", wide_k, value_h, preferred_element_type=jnp.float32)
    z_part = jnp.einsum("gha,g->ha", wide_k, ones_col, preferred_element_type=jnp.float32)
    kv_low = kv_part.astype(jnp.bfloat16)
    z_low = z_part.astype(jnp.bfloat16)
    numer_part = jnp.einsum(
        "gha,hae->ghe", wide_q, kv_low, preferred_element_type=jnp.float32
    ).reshape(group_rows, D)
    denom_part = jnp.einsum("gha,ha->gh", wide_q, z_low, preferred_element_type=jnp.float32)
    numer_sum, denom_sum = (
        lax.psum_scatter(numer_part, "feat", scatter_dimension=0, tiled=True),
        lax.psum_scatter(denom_part, "feat", scatter_dimension=0, tiled=True),
    )
    numer_h = numer_sum.reshape(tok_count, H, DH)
    att_low = (numer_h / denom_sum[:, :, None]).reshape(tok_count, D).astype(jnp.bfloat16)
    branch = jnp.dot(att_low, w_out, preferred_element_type=jnp.float32) + b_out.astype(jnp.float32)
    hidden_one, ln1_back = jax.vjp(
        layer_norm,
        tokens.astype(jnp.float32) + branch,
        ln1_gain.astype(jnp.float32),
        ln1_bias.astype(jnp.float32),
    )
    hid_low = hidden_one.astype(jnp.bfloat16)
    pre_act = jnp.dot(hid_low, w_up, preferred_element_type=jnp.float32) + b_up.astype(jnp.float32)
    act_val, gelu_back = jax.vjp(partial(jax.nn.gelu, approximate=False), pre_act)
    act_low = act_val.astype(jnp.bfloat16)
    ffn_out = jnp.dot(act_low, w_down, preferred_element_type=jnp.float32) + b_down.astype(
        jnp.float32
    )
    result, ln2_back = jax.vjp(
        layer_norm, hidden_one + ffn_out, ln2_gain.astype(jnp.float32), ln2_bias.astype(jnp.float32)
    )
    grad_r2, grad_gain2, grad_bias2 = ln2_back(cotangent.astype(jnp.float32))
    grad_ffn = grad_r2.astype(jnp.bfloat16)
    grad_bdown = jnp.sum(grad_ffn.astype(jnp.float32), 0)
    grad_wdown = cross_dot(act_low, grad_ffn)
    (grad_act,) = gelu_back(back_dot(grad_ffn, w_down))
    grad_pre = grad_act.astype(jnp.bfloat16)
    grad_bup = jnp.sum(grad_pre.astype(jnp.float32), 0)
    grad_wup = cross_dot(hid_low, grad_pre)
    grad_h1 = grad_r2 + back_dot(grad_pre, w_up)
    grad_r1, grad_gain1, grad_bias1 = ln1_back(grad_h1)
    grad_branch = grad_r1.astype(jnp.bfloat16)
    grad_bout = jnp.sum(grad_branch.astype(jnp.float32), 0)
    grad_wout = cross_dot(att_low, grad_branch)
    grad_att = back_dot(grad_branch, w_out).reshape(tok_count, H, DH)
    grad_num = (grad_att / denom_sum[:, :, None]).reshape(tok_count, D).astype(jnp.bfloat16)
    grad_den = (-jnp.sum(grad_att * numer_h, -1) / (denom_sum * denom_sum)).astype(jnp.bfloat16)
    group_num, group_den = (
        lax.all_gather(grad_num, "feat", axis=0, tiled=True),
        lax.all_gather(grad_den, "feat", axis=0, tiled=True),
    )
    group_num_h = group_num.reshape(group_rows, H, DH)
    grad_kv_part = jnp.einsum(
        "gha,ghe->hae", wide_q, group_num_h, preferred_element_type=jnp.float32
    )
    grad_z_part = jnp.einsum("gha,gh->ha", wide_q, group_den, preferred_element_type=jnp.float32)
    grad_kv = grad_kv_part.astype(jnp.bfloat16)
    grad_z = grad_z_part.astype(jnp.bfloat16)
    wide_gq = jnp.einsum("ghe,hae->gha", group_num_h, kv_low, preferred_element_type=jnp.float32)
    wide_gq = wide_gq + group_den[:, :, None].astype(jnp.float32) * z_low[None].astype(jnp.float32)
    grad_arg_q = (fold_segments(wide_gq, member_f) * phi_q).astype(jnp.bfloat16)
    wide_gk = jnp.einsum(
        "ghe,hae->gha", value_h, grad_kv, preferred_element_type=jnp.float32
    ) + grad_z[None].astype(jnp.float32)
    grad_arg_k = (fold_segments(wide_gk, member_f) * phi_k).astype(jnp.bfloat16)
    grad_value = jnp.einsum("gha,hae->ghe", wide_k, grad_kv, preferred_element_type=jnp.float32)
    grad_query = feature_back(query_h, feat_proj, grad_arg_q)
    grad_key = feature_back(key_h, feat_proj, grad_arg_k)
    grad_group = jnp.concatenate(
        [
            grad_query.reshape(group_rows, D),
            grad_key.reshape(group_rows, D),
            grad_value.reshape(group_rows, D),
        ],
        1,
    )
    grad_qkv = lax.psum_scatter(
        grad_group.astype(jnp.bfloat16), "feat", scatter_dimension=0, tiled=True
    )
    grad_bqkv = jnp.sum(grad_qkv.astype(jnp.float32), 0)
    grad_wqkv = cross_dot(tokens, grad_qkv)
    grad_tokens = grad_r1 + back_dot(grad_qkv, w_qkv)
    grads_now = (
        grad_wqkv,
        grad_bqkv,
        grad_wout,
        grad_bout,
        grad_gain1,
        grad_bias1,
        grad_wup,
        grad_bup,
        grad_wdown,
        grad_bdown,
        grad_gain2,
        grad_bias2,
    )
    return (result.astype(jnp.bfloat16), grad_tokens, grads_now)


def on_device(
    tokens_in,
    out_cotangent,
    segment_ids,
    feature_proj,
    w_qkv,
    b_qkv,
    w_out,
    b_out,
    ln1_gain,
    ln1_bias,
    w_up,
    b_up,
    w_down,
    b_down,
    ln2_gain,
    ln2_bias,
):
    totals = None
    outputs = []
    grad_inputs = []
    for micro_idx in range(MICRO):
        gathered = fetch_weights(
            w_qkv,
            b_qkv,
            w_out,
            b_out,
            ln1_gain,
            ln1_bias,
            w_up,
            b_up,
            w_down,
            b_down,
            ln2_gain,
            ln2_bias,
        )
        result, grad_tokens, grads_now = micro_step(
            tokens_in[micro_idx],
            out_cotangent[micro_idx],
            segment_ids[micro_idx],
            feature_proj,
            gathered,
        )
        outputs.append(result)
        grad_inputs.append(grad_tokens)
        totals = grads_now if totals is None else jax.tree.map(jnp.add, totals, grads_now)
    (
        grad_wqkv,
        grad_bqkv,
        grad_wout,
        grad_bout,
        grad_gain1,
        grad_bias1,
        grad_wup,
        grad_bup,
        grad_wdown,
        grad_bdown,
        grad_gain2,
        grad_bias2,
    ) = totals
    summed = (
        lax.psum_scatter(grad_wqkv, ("dp", "feat"), scatter_dimension=0, tiled=True),
        lax.psum_scatter(grad_bqkv, ("dp", "feat"), scatter_dimension=0, tiled=True),
        lax.psum_scatter(grad_wout, ("dp", "feat"), scatter_dimension=0, tiled=True),
        lax.psum_scatter(grad_bout, ("dp", "feat"), scatter_dimension=0, tiled=True),
        lax.psum_scatter(grad_gain1, ("dp", "feat"), scatter_dimension=0, tiled=True),
        lax.psum_scatter(grad_bias1, ("dp", "feat"), scatter_dimension=0, tiled=True),
        lax.psum_scatter(grad_wup, ("dp", "feat"), scatter_dimension=0, tiled=True),
        lax.psum_scatter(grad_bup, ("dp", "feat"), scatter_dimension=0, tiled=True),
        lax.psum_scatter(grad_wdown, ("dp", "feat"), scatter_dimension=0, tiled=True),
        lax.psum_scatter(grad_bdown, ("dp", "feat"), scatter_dimension=0, tiled=True),
        lax.psum_scatter(grad_gain2, ("dp", "feat"), scatter_dimension=0, tiled=True),
        lax.psum_scatter(grad_bias2, ("dp", "feat"), scatter_dimension=0, tiled=True),
    )
    return (
        jnp.stack(outputs),
        jnp.stack(grad_inputs),
        summed[0],
        summed[1],
        summed[2],
        summed[3],
        summed[4],
        summed[5],
        summed[6],
        summed[7],
        summed[8],
        summed[9],
        summed[10],
        summed[11],
    )


NZ, NY, NC, NX = 4, 2, 2, 2
N_DEV = NZ * NY * NC * NX
MESH_ID = pl.DeviceIdType.MESH
BF = jnp.bfloat16
F32 = jnp.float32
SHARE = MICRO // NX
GRID = (NZ, NY, NC)
ALL = slice(None)


def fits(mesh):
    return mesh.shape["dp"] == NZ * NY * NC and mesh.shape["feat"] == NX


class Place:
    def __init__(self):
        i = lax.axis_index("dp")
        self.z, self.y, self.c, self.x = i // (NY * NC), (i // NC) % NY, i % NC, lax.axis_index("feat")
        self.sibling = self.device(c=1 - self.c)
        self.over = {"x": self.device(x=1 - self.x), "y": self.device(y=1 - self.y)}
        self.z_of = [lax.rem(self.z + k, NZ) for k in (1, 2, 3)]
        self.over_z = [self.device(z=z) for z in self.z_of]

    def device(self, **other):
        z, y, c, x = (other.get(n, getattr(self, n)) for n in "zycx")
        return (z * (NY * NC) + y * NC + c, x)

    def meet(self):
        barrier = pltpu.get_barrier_semaphore()
        peers = [self.sibling, self.over["x"], self.over["y"]] + self.over_z
        for peer in peers:
            pl.semaphore_signal(barrier, inc=1, device_id=peer, device_id_type=MESH_ID)
        pl.semaphore_wait(barrier, len(peers))

    def per_class(self, orders, act):
        if orders[0] == orders[1]:
            act(orders[0])
            return
        for c in range(NC):

            @pl.when(self.c == c)
            def _(order=orders[c]):
                act(order)

    def rows(self, grid, x):
        share = grid.shape[3] // NX
        return pl.ds(pl.multiple_of(x * share, 8), share)

    def view(self, grid, cols, spread=(), **at):
        index = [ALL if n in spread else at.get(n, getattr(self, n)) for n in "zyc"]
        rows = ALL if "x" in spread else self.rows(grid, at.get("x", self.x))
        return grid.at[(*index, rows, cols)]


class Copies:
    def __init__(self, send_sems, recv_sems):
        self.send_sems, self.recv_sems = send_sems, recv_sems

    def copy(self, slot, src, dst, peer):
        return pltpu.make_async_remote_copy(
            src_ref=src, dst_ref=dst, send_sem=self.send_sems.at[slot], recv_sem=self.recv_sems.at[slot],
            device_id=peer, device_id_type=MESH_ID,
        )


class Gather(Copies):
    def __init__(self, here, part, src, grid, cols, orders, sems):
        super().__init__(sems[0].at[part], sems[1].at[part])
        self.here, self.grid, self.cols, self.orders = here, grid, cols, orders
        self.src = src.at[ALL, cols]
        self.local = pltpu.make_async_copy(self.src, here.view(grid, cols), sems[2].at[part])

    def phase(self, order, n):
        here, dim = self.here, order[n]
        mine = here.view(self.grid, self.cols, order[:n])
        src = self.src if n == 0 else mine
        if dim == "z":
            return [self.copy(n + k, src, mine, peer) for k, peer in enumerate(here.over_z)]
        slot = n if order.index("z") > n else n + 2
        return [self.copy(slot, src, mine, here.over[dim])]

    def to_sibling(self):
        mine = self.here.view(self.grid, self.cols, "zyx")
        return self.copy(5, mine, mine, self.here.sibling)

    def step(self, n):
        if n == 0:
            self.local.start()
            self.here.per_class(self.orders, lambda order: [c.start() for c in self.phase(order, 0)])
        elif n < 4:
            self.here.per_class(self.orders, lambda order: [c.wait_recv() for c in self.phase(order, n - 1)])
            if n == 1:
                self.local.wait()
            if n < 3:
                self.here.per_class(self.orders, lambda order: [c.start() for c in self.phase(order, n)])
            else:
                self.to_sibling().start()
        else:
            self.to_sibling().wait_recv()

    def drain(self):
        for n in range(3):
            self.here.per_class(self.orders, lambda order, n=n: [c.wait_send() for c in self.phase(order, n)])
        self.to_sibling().wait_send()


class Reduce(Copies):
    def __init__(self, here, part, grid, cols, orders, got, stage, out, sems):
        super().__init__(sems[0].at[part], sems[1].at[part])
        self.here, self.grid, self.cols, self.orders = here, grid, cols, orders
        self.got, self.stage = got, stage
        self.out = pltpu.make_async_copy(stage, out.at[ALL, cols], sems[2].at[part])

    def from_sibling(self):
        here = self.here
        theirs = here.view(self.grid, self.cols, "zyx", c=1 - here.c)
        return self.copy(0, theirs, self.got[0][0], here.sibling)

    def received(self, order, n):
        return self.got[n][self.orders.index(order) % len(self.got[n])]

    def phase(self, order, n):
        here, dim, rest = self.here, order[n], order[n + 1 :]
        got = self.received(order, n + 1)
        if dim == "z":
            return [
                self.copy(1 + n + k, here.view(self.grid, self.cols, rest, z=z), got.at[k], peer)
                for k, (z, peer) in enumerate(zip(here.z_of, here.over_z, strict=True))
            ]
        slot = 1 + n if order.index("z") > n else 3 + n
        place = {dim: 1 - getattr(here, dim)}
        return [self.copy(slot, here.view(self.grid, self.cols, rest, **place), got, here.over[dim])]

    def spot(self, spread, q):
        here, index, inner = self.here, {}, []
        if "y" in spread:
            index["y"] = q % NY
            q = q // NY
        if "z" in spread:
            index["z"] = q
        inner = tuple(index[n] for n in "zy" if n in index)
        rows = ALL if "x" in spread else here.rows(self.grid, here.x)
        return tuple(index.get(n, getattr(here, n)) for n in "zyc") + (rows, self.cols), inner

    def add(self, got, spread, copies=1):
        def one(q):
            index, inner = self.spot(spread, q)
            if copies == 1:
                self.grid[index] = self.grid[index] + got[inner + (ALL, ALL)]
                return
            total = self.grid[index].astype(F32)
            for k in range(copies):
                total = total + got[(k,) + inner + (ALL, ALL)].astype(F32)
            self.grid[index] = total.astype(self.grid.dtype)

        count = (NZ if "z" in spread else 1) * (NY if "y" in spread else 1)
        blocks_of(count, one) if count > 1 else one(0)

    def finish(self, got, copies):
        index, _ = self.spot((), 0)
        total = self.grid[index].astype(F32)
        for k in range(copies):
            total = total + got[((k,) if copies > 1 else ()) + (ALL, ALL)].astype(F32)
        self.stage[...] = total

    def step(self, n):
        if n == 0:
            self.from_sibling().start()
            return
        if n == 1:
            self.from_sibling().wait_recv()
            self.add(self.got[0][0], "zyx")
        else:

            def take(order):
                for c in self.phase(order, n - 2):
                    c.wait_recv()
                copies = 3 if order[n - 2] == "z" else 1
                got = self.received(order, n - 1)
                if n < 4:
                    self.add(got, order[n - 1 :], copies)
                else:
                    self.finish(got, copies)

            self.here.per_class(self.orders, take)
        if n < 4:
            self.here.per_class(self.orders, lambda order: [c.start() for c in self.phase(order, n - 1)])
        else:
            self.out.start()

    def drain(self):
        self.from_sibling().wait_send()
        for n in range(3):
            self.here.per_class(self.orders, lambda order, n=n: [c.wait_send() for c in self.phase(order, n)])
        self.out.wait()


def got_shapes(orders, rows, width):
    first, second = (order_shapes(order, rows, width) for order in orders)
    return [(a,) if a == b else (a, b) for a, b in zip(first, second, strict=True)]


def order_shapes(order, rows, width):

    def block(spread):
        return tuple(dict(z=NZ, y=NY)[n] for n in "zy" if n in spread) + (rows * (NX if "x" in spread else 1), width)

    shapes = [block("zyx")]
    for n, dim in enumerate(order):
        shapes.append(((NZ - 1,) if dim == "z" else ()) + block(order[n + 1 :]))
    return shapes


def blocks_of(count, body, then=()):
    def step(j, carry):
        body(j)
        for at in sorted({at for at, _ in then}):

            @pl.when(j == at)
            def _(at=at):
                for when, act in then:
                    if when == at:
                        act()

        return carry

    lax.fori_loop(0, count, step, 0)


ROWS = 512
BLK = 256
PAIRS = D // 128
FF = 4 * D
WIDE = 2 * FEATS
SCALE = DH ** (-0.25)


def dot(a, b, ca=1, cb=0):
    return lax.dot_general(a, b, (((ca,), (cb,)), ((), ())), preferred_element_type=F32)


def half_masks(width):
    lane = lax.broadcasted_iota(jnp.int32, (1, width), 1) % 128
    first = (lane < DH).astype(F32)
    return first.astype(BF), (1.0 - first).astype(BF)


def lanes(j, width):
    return pl.ds(pl.multiple_of(j * width, width), width)


class Work:
    def __init__(self, refs):
        self.__dict__.update(refs)

    def setup(self, proj, seg_rows):
        row = lax.broadcasted_iota(jnp.int32, (DH, 128), 0)
        col = lax.broadcasted_iota(jnp.int32, (DH, 128), 1)
        for h in range(2):
            place_in = (col == row + h * DH).astype(BF)
            for n in range(NX):
                self.table[pl.ds(h * FEATS + n * 128, 128), 0:128] = dot(proj[n], place_in).astype(BF)
        feat = lax.broadcasted_iota(jnp.int32, (WIDE, 128), 0) // FEATS
        half = lax.broadcasted_iota(jnp.int32, (WIDE, 128), 1) // DH
        same = (feat == half).astype(F32).astype(BF)
        self.table[:, 128:256] = same
        for b in range(2):
            across = jnp.broadcast_to(seg_rows[b], (BLK, BLK))
            self.mask[b] = (across == jnp.transpose(across)).astype(F32)

    def features(self, rows):
        wide = rows.astype(F32)
        squares = wide * wide
        high = squares.astype(BF)
        low = (squares - high.astype(F32)).astype(BF)
        same = self.table[:, 128:256]
        norm = dot(high, same, 1, 1) + dot(low, same, 1, 1)
        arg = SCALE * dot(rows, self.table[:, 0:128], 1, 1) - (0.5 * SCALE * SCALE) * norm
        return (jnp.exp(arg) * FEATS ** (-0.5)).astype(BF)

    def qkv_block(self, j):
        col = lanes(j, 256)
        full = dot(self.x[...], self.w_qkv[:, col]) + self.b_qkv[:, col]
        self.qkv[:, col] = full.astype(BF)

    def pair(self, i):
        b, p = i // PAIRS, i % PAIRS
        rows = pl.ds(pl.multiple_of(b * BLK, BLK), BLK)
        cols = [pl.ds(pl.multiple_of(n * D + p * 128, 128), 128) for n in range(3)]
        return b, rows, cols

    def attend(self, i):
        b, rows, cols = self.pair(i)
        mask = self.mask[b]
        m0, m1 = half_masks(128)
        phi_q = self.features(self.qkv[rows, cols[0]])
        phi_k = self.features(self.qkv[rows, cols[1]])
        self.phi_q[i] = phi_q
        self.phi_k[i] = phi_k
        v = self.qkv[rows, cols[2]]
        one = jnp.ones((BLK, 128), BF)
        res = None
        for h, m in enumerate((m0, m1)):
            part = slice(h * FEATS, (h + 1) * FEATS)
            score = (dot(phi_q[:, part], phi_k[:, part], 1, 1) * mask).astype(BF)
            term = dot(score, jnp.concatenate([v * m, one * m], 1))
            res = term if res is None else res + term
        inv = 1.0 / res[:, 128:]
        self.inv[rows, cols[0]] = inv
        self.att[rows, cols[0]] = (res[:, :128] * inv).astype(BF)

    def normalize(self, r):
        center = r - jnp.mean(r, -1, keepdims=True)
        scale = lax.rsqrt(jnp.mean(center * center, -1, keepdims=True) + EPSILON)
        return center * scale, scale

    def normalize_back(self, dy, n, scale, gain):
        g = dy * gain
        return (g - jnp.mean(g, -1, keepdims=True) - n * jnp.mean(g * n, -1, keepdims=True)) * scale

    def branch(self):
        for j in range(3):
            col = lanes(j, 256)
            self.n1[:, col] = dot(self.att[...], self.w_out[:, col]) + self.b_out[:, col] + self.x[:, col].astype(F32)

        def rows_of(j):
            row = pl.ds(pl.multiple_of(j * 64, 64), 64)
            n1, s1 = self.normalize(self.n1[row, :])
            self.n1[row, :] = n1
            self.s1[row, :] = s1
            self.h1[row, :] = (n1 * self.g1[...] + self.b1[...]).astype(BF)

        blocks_of(ROWS // 64, rows_of)

    def up_block(self, j):
        col = lanes(j, 256)
        for r in range(0, ROWS, 128):
            row = slice(r, r + 128)
            a = dot(self.h1[row, :], self.w_up[:, col]) + self.b_up[:, col]
            cdf = 0.5 * (1.0 + lax.erf(a * 2**-0.5))
            self.z[row, col] = (a * cdf).astype(BF)
            self.slope[row, col] = (cdf + a * jnp.exp(-0.5 * a * a) * (0.5 / 3.141592653589793) ** 0.5).astype(BF)

    def down(self):
        def block(j):
            col = lanes(j, 256)
            back = self.n1[:, col] * self.g1[:, col] + self.b1[:, col]
            self.dr[:, col] = dot(self.z[...], self.w_down[:, col]) + self.b_down[:, col] + back

        blocks_of(3, block)
        for ref in (self.d_g2, self.d_b2, self.d_b_down):
            ref[...] = jnp.zeros_like(ref)

        def rows_of(j):
            row = pl.ds(pl.multiple_of(j * 64, 64), 64)
            n2, s2 = self.normalize(self.dr[row, :])
            self.y[row, :] = (n2 * self.g2[...] + self.b2[...]).astype(BF)
            dy = self.cot[row, :].astype(F32)
            dr2 = self.normalize_back(dy, n2, s2, self.g2[...])
            self.dr[row, :] = dr2
            df = dr2.astype(BF)
            self.df[row, :] = df
            self.d_g2[...] += jnp.sum(dy * n2, 0, keepdims=True)
            self.d_b2[...] += jnp.sum(dy, 0, keepdims=True)
            self.d_b_down[...] += jnp.sum(df.astype(F32), 0, keepdims=True)

        blocks_of(ROWS // 64, rows_of)

    def down_back(self, j):
        col = lanes(j, 256)
        dz = dot(self.df[...], self.w_down[col, :], 1, 1)
        da = (dz * self.slope[:, col].astype(F32)).astype(BF)
        self.slope[:, col] = da
        self.d_b_up[:, col] = jnp.sum(da.astype(F32), 0, keepdims=True)
        self.w_down[col, :] = dot(self.z[:, col], self.df[...], 0, 0).astype(BF)

    def up_back(self):
        def block(j):
            col = lanes(j, 256)
            self.dr[:, col] += dot(self.slope[...], self.w_up[col, :], 1, 1)

        blocks_of(3, block)
        self.flip[...] = jnp.transpose(self.h1[...])

    def up_grad(self, j):
        col = lanes(j, 256)
        self.w_up[:, col] = dot(self.flip[...], self.slope[:, col]).astype(BF)

    def branch_back(self):
        for ref in (self.d_g1, self.d_b1, self.d_b_out):
            ref[...] = jnp.zeros_like(ref)

        def rows_of(j):
            row = pl.ds(pl.multiple_of(j * 64, 64), 64)
            dh1, n1 = self.dr[row, :], self.n1[row, :]
            dr1 = self.normalize_back(dh1, n1, self.s1[row, :], self.g1[...])
            self.dr[row, :] = dr1
            do = dr1.astype(BF)
            self.df[row, :] = do
            self.d_g1[...] += jnp.sum(dh1 * n1, 0, keepdims=True)
            self.d_b1[...] += jnp.sum(dh1, 0, keepdims=True)
            self.d_b_out[...] += jnp.sum(do.astype(F32), 0, keepdims=True)

        blocks_of(ROWS // 64, rows_of)
        head_r = lax.broadcasted_iota(jnp.int32, (256, 256), 0) // DH
        head_c = lax.broadcasted_iota(jnp.int32, (256, 256), 1) // DH
        same = (head_r == head_c).astype(F32).astype(BF)

        def block(j):
            col = lanes(j, 256)
            datt = dot(self.df[...], self.w_out[col, :], 1, 1)
            inv = self.inv[:, col]
            self.dnum[:, col] = (datt * inv).astype(BF)
            prod = datt * self.att[:, col].astype(F32)
            high = prod.astype(BF)
            low = (prod - high.astype(F32)).astype(BF)
            total = dot(high, same) + dot(low, same)
            self.dden[:, col] = (-total * inv).astype(BF)

        blocks_of(3, block)
        self.flip[...] = jnp.transpose(self.att[...])

        def grad(j):
            col = lanes(j, 256)
            self.w_out[:, col] = dot(self.flip[...], self.df[:, col]).astype(BF)

        blocks_of(3, grad)

    def attend_back(self, i):
        b, rows, cols = self.pair(i)
        mask = self.mask[b]
        m0, m1 = half_masks(256)
        q, k, v = (self.qkv[rows, c] for c in cols)
        dnum, dden = self.dnum[rows, cols[0]], self.dden[rows, cols[0]]
        left = jnp.concatenate([dnum, dden * (1.0 / DH)], 1)
        right = jnp.concatenate([v, jnp.ones((BLK, 128), BF)], 1)
        back_q, back_k, dv = None, None, None
        for h, m in enumerate((m0, m1)):
            part = slice(h * FEATS, (h + 1) * FEATS)
            phi_q, phi_k = self.phi_q[i, :, part], self.phi_k[i, :, part]
            mine = left * m
            dscore = (dot(mine, right, 1, 1) * mask).astype(BF)
            flipped = (dot(right, mine, 1, 1) * mask).astype(BF)
            darg_q = (dot(dscore, phi_k) * phi_q.astype(F32)).astype(BF)
            darg_k = (dot(flipped, phi_q) * phi_k.astype(F32)).astype(BF)
            score = (dot(phi_k, phi_q, 1, 1) * mask).astype(BF)
            table = self.table[part, :]
            terms = dot(darg_q, table), dot(darg_k, table), dot(score, mine[:, :128])
            if h == 0:
                back_q, back_k, dv = terms
            else:
                back_q, back_k, dv = back_q + terms[0], back_k + terms[1], dv + terms[2]
        for n, (rows_in, back) in enumerate(((q, back_q), (k, back_k))):
            grad = SCALE * back[:, :128] - (SCALE * SCALE) * rows_in.astype(F32) * back[:, 128:]
            self.qkv[rows, cols[n]] = grad.astype(BF)
        self.qkv[rows, cols[2]] = dv.astype(BF)

    def tokens_back(self):
        def block(j):
            col = lanes(j, 256)
            self.dr[:, col] += dot(self.qkv[...], self.w_qkv[col, :], 1, 1)

        blocks_of(3, block)
        self.flip[...] = jnp.transpose(self.x[...])

    def qkv_grad(self, j):
        col = lanes(j, 256)
        part = self.qkv[:, col]
        self.d_b_qkv[:, col] = jnp.sum(part.astype(F32), 0, keepdims=True)
        self.w_qkv[:, col] = dot(self.flip[...], part).astype(BF)


VECTORS = ("b_qkv", "b_out", "g1", "b1", "b_up", "b_down", "g2", "b2")
WIDTHS = (3 * D, D, D, D, FF, D, D, D)
SPACE = (
    ("qkv", (ROWS, 3 * D), BF), ("phi_q", (2 * PAIRS, BLK, WIDE), BF), ("phi_k", (2 * PAIRS, BLK, WIDE), BF),
    ("att", (ROWS, D), BF), ("inv", (ROWS, D), F32), ("n1", (ROWS, D), F32), ("s1", (ROWS, 1), F32),
    ("h1", (ROWS, D), BF), ("z", (ROWS, FF), BF), ("slope", (ROWS, FF), BF), ("dr", (ROWS, D), F32),
    ("df", (ROWS, D), BF), ("dnum", (ROWS, D), BF), ("dden", (ROWS, D), BF), ("flip", (D, ROWS), BF),
    ("table", (WIDE, 256), BF), ("mask", (2, BLK, BLK), F32),
)


ZYX, ZXY, XYZ, YXZ = tuple("zyx"), tuple("zxy"), tuple("xyz"), tuple("yxz")
SPLIT = (ZYX, ZXY)
SPLIT_BACK = (XYZ, YXZ)
PARTS = {
    "small": ("small", 0, 128, SPLIT, SPLIT_BACK),
    "q": ("w_qkv", 0, D, SPLIT, SPLIT_BACK),
    "k": ("w_qkv", D, D, SPLIT, SPLIT_BACK),
    "v": ("w_qkv", 2 * D, D, SPLIT, SPLIT_BACK),
    "out": ("w_out", 0, D, (ZXY, ZXY), (YXZ, YXZ)),
    "up0": ("w_up", 0, 2 * D, (ZXY, ZXY), (YXZ, YXZ)),
    "up1": ("w_up", 2 * D, 2 * D, SPLIT, SPLIT_BACK),
    "dn0": ("w_down", 0, 384, (ZXY, ZXY), (YXZ, YXZ)),
    "dn1": ("w_down", 384, 384, (XYZ, XYZ), (ZYX, ZYX)),
}
WEIGHTS = (("w_qkv", (D, 3 * D)), ("w_out", (D, D)), ("w_up", (D, FF)), ("w_down", (FF, D)))
TILE = (8, 128)
HALF = (SHARE, NX, ROWS // SHARE // NX, D)


def shard_rows(weight):
    return TILE[0] if weight == "small" else dict(WEIGHTS)[weight][0] // N_DEV


class Swap:
    def __init__(self, here, n, theirs, target, mine, home, sems):
        self.there = pltpu.make_async_remote_copy(
            src_ref=theirs, dst_ref=target, send_sem=sems[0].at[n], recv_sem=sems[1].at[n],
            device_id=here.over["x"], device_id_type=MESH_ID,
        )
        self.here = None if home is None else pltpu.make_async_copy(mine, home, sems[2].at[n])

    def start(self):
        self.there.start()
        if self.here is not None:
            self.here.start()

    def arrive(self):
        self.there.wait_recv()
        if self.here is not None:
            self.here.wait()


def one_hot(width, count):
    at = lax.broadcasted_iota(jnp.int32, (1, count), 1).astype(F32)
    owner = jnp.floor((at + 0.5) * (1.0 / width))
    lane = at - owner * width
    lanes_hot = (lax.broadcasted_iota(jnp.int32, (128, count), 0).astype(F32) == lane).astype(F32).astype(BF)
    owner_hot = (lax.broadcasted_iota(jnp.int32, (N_DEV, count), 0).astype(F32) == owner).astype(F32)
    return lanes_hot, owner_hot


def spread_small(tiles, vectors):
    for width in sorted({v.shape[1] // N_DEV for v in vectors}):
        hot, owner = one_hot(width, width * N_DEV)
        for n, vector in enumerate(vectors):
            if vector.shape[1] == width * N_DEV:
                rows = tiles[pl.ds(n, N_DEV, stride=TILE[0]), :].astype(BF)
                vector[...] = jnp.sum(dot(rows, hot) * owner, 0, keepdims=True)


def collect_small(tiles, vectors):
    for width in sorted({v.shape[1] // N_DEV for v in vectors}):
        hot, owner = one_hot(width, width * N_DEV)
        for n, vector in enumerate(vectors):
            if vector.shape[1] == width * N_DEV:
                full = owner * vector[...]
                high = full.astype(BF)
                low = (full - high.astype(F32)).astype(BF)
                tiles[pl.ds(n, N_DEV, stride=TILE[0]), :] = dot(high, hot, 1, 1) + dot(low, hot, 1, 1)


def layer_kernel(*refs):
    it = iter(refs)
    tok, cot = next(it), next(it)
    local = {w: next(it) for w, _ in WEIGHTS}
    local["small"], proj_in, seg = next(it), next(it), next(it)
    block_out, grad_tok = next(it), next(it)
    outs = {w: next(it) for w, _ in WEIGHTS}
    outs["small"] = next(it)
    ref = {n: next(it) for n, _ in WEIGHTS}
    ref.update({n: next(it) for n, _, _ in SPACE})
    work = Work(ref)
    got = {
        p: [tuple(next(it) for _ in shapes) for shapes in got_shapes(orders, shard_rows(w), width)]
        for p, (w, _, width, _, orders) in PARTS.items()
    }
    stage = {p: next(it) for p in PARTS}
    gather_sems = [next(it) for _ in range(3)]
    reduce_sems = [next(it) for _ in range(3)]
    swap_sems = [next(it) for _ in range(3)]
    out_sems = next(it)

    here = Place()
    here.meet()
    x = here.x
    grids = {w: ref[w].reshape(GRID + (NX * shard_rows(w), ref[w].shape[1])) for w, _ in WEIGHTS}
    grids["small"] = ref["tiles"].reshape(GRID + (NX * TILE[0], TILE[1]))
    into, back = {}, {}
    for n, (p, (w, first, width, order, order_back)) in enumerate(PARTS.items()):
        cols = pl.ds(first, width)
        into[p] = Gather(here, n, local[w], grids[w], cols, order, gather_sems)
        back[p] = Reduce(here, n, grids[w], cols, order_back, got[p], stage[p], outs[w], reduce_sems)

    def halves(r):
        return r.reshape(HALF)

    own, other = pl.ds(x * SHARE, SHARE), pl.ds((1 - x) * SHARE, SHARE)
    swap = {
        "tok": Swap(here, 0, tok.at[other], halves(work.x).at[:, x], tok.at[own], halves(work.x).at[:, x], swap_sems),
        "cot": Swap(here, 1, cot.at[other], halves(work.cot).at[:, x], cot.at[own], halves(work.cot).at[:, x], swap_sems),
        "proj": Swap(here, 2, proj_in, work.proj.at[x], proj_in, work.proj.at[x], swap_sems),
        "y": Swap(here, 3, halves(work.y).at[:, 1 - x], block_out.at[own], halves(work.y).at[:, x], block_out.at[own], swap_sems),
        "grad": Swap(here, 4, work.grad_low, work.grad_got, halves(work.dr).at[:, x], grad_tok.at[own], swap_sems),
    }

    def g(*names):
        for name in names:
            into[name[:-1]].step(int(name[-1]))

    def r(*names):
        for name in names:
            back[name[:-1]].step(int(name[-1]))

    def later(act, plan):
        return [(at, partial(act, *names.split())) for at, names in plan]

    vectors = [getattr(work, n) for n in VECTORS]
    totals = [getattr(work, "d_" + n) for n in VECTORS]

    swap["proj"].start()
    g("small0", "q0", "dn10", "k0")
    swap["tok"].start()
    g("small1", "q1", "dn11", "v0", "small2", "k1", "q2", "out0", "v1", "small3", "k2", "q3", "dn12", "up00")
    swap["proj"].arrive()
    work.setup(work.proj, [seg[pl.ds(SHARE * x + b, 1), :].astype(F32) for b in range(SHARE)])
    g("small4")
    spread_small(ref["tiles"], vectors)
    g("v2", "out1", "k3", "q4", "up10", "v3")
    swap["tok"].arrive()
    g("k4", "out2", "up01", "v4")
    swap["cot"].start()
    blocks_of(9, work.qkv_block, later(g, ((4, "up11 dn00"),)))
    blocks_of(
        2 * PAIRS, work.attend,
        later(g, ((1, "out3"), (2, "up02"), (3, "up12 out4"), (6, "dn01"), (9, "up13"), (11, "up03"))),
    )
    work.branch()
    g("up14", "up04", "dn02")
    blocks_of(12, work.up_block, later(g, ((8, "dn13"),)))
    g("dn03", "dn14", "dn04")
    swap["cot"].arrive()
    work.down()
    for part in into.values():
        part.drain()
    swap["y"].start()
    blocks_of(12, work.down_back)
    r("dn00", "dn10")
    work.up_back()
    r("dn01", "dn11")
    blocks_of(12, work.up_grad, later(r, ((5, "up00"), (11, "up10"))))
    work.branch_back()
    r("up01", "up11", "out0")
    blocks_of(2 * PAIRS, work.attend_back, later(r, ((2, "out1"), (6, "dn02"), (11, "up12"))))
    work.tokens_back()

    def lower(b):
        work.grad_low[b] = halves(work.dr)[b, 1 - x].astype(BF)

    blocks_of(SHARE, lower)
    swap["grad"].start()
    blocks_of(9, work.qkv_grad, later(r, ((2, "q0"), (5, "k0"), (8, "v0"))))
    collect_small(ref["tiles"], totals)
    r("small0", "q1", "k1", "v1", "small1", "dn03", "up02", "dn12", "out2", "up13", "q2", "dn13", "small2", "k2", "up03", "v2")
    r("out3", "dn04", "dn14", "small3", "q3", "k3", "v3", "up04", "up14", "out4", "small4", "q4", "k4", "v4")
    swap["grad"].arrive()

    def raise_(b):
        work.grad_high[b] = work.grad_got[b].astype(F32)

    blocks_of(SHARE, raise_)
    last = pltpu.make_async_copy(work.grad_high, grad_tok.at[other], out_sems.at[0])
    last.start()
    swap["y"].arrive()
    for each in swap.values():
        each.there.wait_send()
    for part in back.values():
        part.drain()
    last.wait()


QUARTER = (SHARE, ROWS // SHARE // NX, D)
SPACE = (
    (("x", (ROWS, D), BF), ("cot", (ROWS, D), BF), ("y", (ROWS, D), BF), ("proj", (NX, FEATS // NX, DH), BF))
    + (("tiles", (N_DEV * TILE[0], TILE[1]), F32), ("grad_low", QUARTER, BF), ("grad_got", QUARTER, BF))
    + (("grad_high", QUARTER, F32),)
    + tuple((n, (1, w), F32) for n, w in zip(VECTORS, WIDTHS))
    + tuple(("d_" + n, (1, w), F32) for n, w in zip(VECTORS, WIDTHS))
    + SPACE
)


def layer(tok, cot, weights, small, proj, seg):
    anywhere = pl.BlockSpec(memory_space=pl.ANY)
    vmem = pl.BlockSpec(memory_space=pltpu.VMEM)
    shape, dma = jax.ShapeDtypeStruct, pltpu.SemaphoreType.DMA
    received, stages = [], []
    for w, _, width, _, orders in PARTS.values():
        kind = F32 if w == "small" else BF
        received += [pltpu.VMEM(s, kind) for shapes in got_shapes(orders, shard_rows(w), width) for s in shapes]
        stages.append(pltpu.VMEM((shard_rows(w), width), F32))
    count = len(PARTS)
    return pl.pallas_call(
        layer_kernel,
        out_shape=[shape(tok.shape, BF), shape(tok.shape, F32)] + [shape(w.shape, F32) for w in weights] + [shape(TILE, F32)],
        in_specs=[anywhere] * 8 + [vmem],
        out_specs=[anywhere] * 7,
        scratch_shapes=[pltpu.VMEM(s, BF) for _, s in WEIGHTS] + [pltpu.VMEM(s, d) for _, s, d in SPACE] + received + stages
        + [dma((count, 6)), dma((count, 6)), dma((count,)), dma((count, 6)), dma((count, 6)), dma((count,))]
        + [dma((5,)), dma((5,)), dma((5,)), dma((1,))],
        compiler_params=pltpu.CompilerParams(collective_id=0, has_side_effects=True, vmem_limit_bytes=61 << 20),
        name="layer",
    )(tok, cot, *weights, small, proj, seg)


def pack_small(vectors):
    rows = [jnp.pad(v.astype(F32).reshape(1, -1), ((n, TILE[0] - 1 - n), (0, TILE[1] - v.shape[0]))) for n, v in enumerate(vectors)]
    total = rows[0]
    for row in rows[1:]:
        total = total + row
    return total


def fast_device(
    tokens_in, out_cotangent, segment_ids, feature_proj,
    w_qkv, b_qkv, w_out, b_out, ln1_gain, ln1_bias, w_up, b_up, w_down, b_down, ln2_gain, ln2_bias,
):
    small = pack_small([b_qkv, b_out, ln1_gain, ln1_bias, b_up, b_down, ln2_gain, ln2_bias])
    out, grad_tok, *sums, tile = layer(
        tokens_in, out_cotangent, [w_qkv, w_out, w_up, w_down], small, feature_proj, segment_ids
    )
    vec = [tile[n, : w // N_DEV] for n, w in enumerate(WIDTHS)]
    return (
        out, grad_tok, sums[0], vec[0], sums[1], vec[1], vec[2], vec[3], sums[2], vec[4], sums[3], vec[5], vec[6], vec[7],
    )


def solution(mesh):
    return jax.shard_map(
        fast_device if fits(mesh) else on_device,
        mesh=mesh,
        in_specs=(
            P(None, ("dp", "feat"), None),
            P(None, ("dp", "feat"), None),
            P(None, "dp"),
            P("feat", None),
            P(("dp", "feat"), None),
            P(("dp", "feat")),
            P(("dp", "feat"), None),
            P(("dp", "feat")),
            P(("dp", "feat")),
            P(("dp", "feat")),
            P(("dp", "feat"), None),
            P(("dp", "feat")),
            P(("dp", "feat"), None),
            P(("dp", "feat")),
            P(("dp", "feat")),
            P(("dp", "feat")),
        ),
        out_specs=(
            P(None, ("dp", "feat"), None),
            P(None, ("dp", "feat"), None),
            P(("dp", "feat"), None),
            P(("dp", "feat")),
            P(("dp", "feat"), None),
            P(("dp", "feat")),
            P(("dp", "feat")),
            P(("dp", "feat")),
            P(("dp", "feat"), None),
            P(("dp", "feat")),
            P(("dp", "feat"), None),
            P(("dp", "feat")),
            P(("dp", "feat")),
            P(("dp", "feat")),
        ),
        check_vma=False,
    )
```

```python
from functools import partial

import jax
import jax.numpy as jnp
from jax import lax
from jax.experimental import pallas as pl
from jax.experimental.pallas import tpu as pltpu
from jax.sharding import PartitionSpec as P

D = 768
H = 12
DH = 64
FEATS = 256
MICRO = 4
SEGS = 4


EPSILON = 1e-05


def layer_norm(residual, norm_gain, norm_shift):
    center = residual - jnp.mean(residual, -1, keepdims=True)
    spread = jnp.mean(center * center, -1, keepdims=True)
    return center * lax.rsqrt(spread + EPSILON) * norm_gain + norm_shift


def cross_dot(left_op, right_op):
    return lax.dot_general(
        left_op, right_op, (((0,), (0,)), ((), ())), preferred_element_type=jnp.float32
    )


def back_dot(left_op, right_op):
    return lax.dot_general(
        left_op, right_op, (((1,), (1,)), ((), ())), preferred_element_type=jnp.float32
    )


def fetch_weights(
    w_qkv, b_qkv, w_out, b_out, ln1_gain, ln1_bias, w_up, b_up, w_down, b_down, ln2_gain, ln2_bias
):
    return (
        lax.all_gather(w_qkv, ("dp", "feat"), axis=0, tiled=True),
        lax.all_gather(b_qkv, ("dp", "feat"), axis=0, tiled=True),
        lax.all_gather(w_out, ("dp", "feat"), axis=0, tiled=True),
        lax.all_gather(b_out, ("dp", "feat"), axis=0, tiled=True),
        lax.all_gather(ln1_gain, ("dp", "feat"), axis=0, tiled=True),
        lax.all_gather(ln1_bias, ("dp", "feat"), axis=0, tiled=True),
        lax.all_gather(w_up, ("dp", "feat"), axis=0, tiled=True),
        lax.all_gather(b_up, ("dp", "feat"), axis=0, tiled=True),
        lax.all_gather(w_down, ("dp", "feat"), axis=0, tiled=True),
        lax.all_gather(b_down, ("dp", "feat"), axis=0, tiled=True),
        lax.all_gather(ln2_gain, ("dp", "feat"), axis=0, tiled=True),
        lax.all_gather(ln2_bias, ("dp", "feat"), axis=0, tiled=True),
    )


def feature_map(head_rows, feat_proj):
    feat_scale = DH ** (-0.25)
    proj_arg = feat_scale * jnp.einsum(
        "ghd,md->ghm", head_rows, feat_proj, preferred_element_type=jnp.float32
    )
    squares = jnp.einsum("ghd,ghd->gh", head_rows, head_rows, preferred_element_type=jnp.float32)
    proj_arg = proj_arg - 0.5 * feat_scale * feat_scale * squares[:, :, None]
    return jnp.exp(proj_arg) * FEATS ** (-0.5)


def feature_back(head_rows, feat_proj, grad_arg):
    feat_scale = DH ** (-0.25)
    proj_back = feat_scale * jnp.einsum(
        "ghm,md->ghd", grad_arg, feat_proj, preferred_element_type=jnp.float32
    )
    arg_total = jnp.sum(grad_arg.astype(jnp.float32), -1, keepdims=True)
    return proj_back - feat_scale * feat_scale * head_rows.astype(jnp.float32) * arg_total


def spread_segments(phi_low, member):
    tok_count, head_count, feat_width = phi_low.shape
    return (phi_low[:, :, None, :] * member[:, None, :, None]).reshape(
        tok_count, head_count, SEGS * feat_width
    )


def fold_segments(grad_wide, member_f):
    tok_count, head_count, wide_dim = grad_wide.shape
    shaped = grad_wide.reshape(tok_count, head_count, SEGS, wide_dim // SEGS)
    return jnp.sum(shaped * member_f[:, None, :, None], 2)


def micro_step(tokens, cotangent, seg_row, feat_proj, weights):
    (
        w_qkv,
        b_qkv,
        w_out,
        b_out,
        ln1_gain,
        ln1_bias,
        w_up,
        b_up,
        w_down,
        b_down,
        ln2_gain,
        ln2_bias,
    ) = weights
    tok_count = tokens.shape[0]
    qkv_rows = jnp.dot(tokens, w_qkv, preferred_element_type=jnp.float32) + b_qkv.astype(
        jnp.float32
    )
    qkv_low = qkv_rows.astype(jnp.bfloat16)
    grouped = lax.all_gather(qkv_low, "feat", axis=0, tiled=True)
    group_rows = grouped.shape[0]
    query_h = grouped[:, :D].reshape(group_rows, H, DH)
    key_h = grouped[:, D : 2 * D].reshape(group_rows, H, DH)
    value_h = grouped[:, 2 * D :].reshape(group_rows, H, DH)
    phi_q = feature_map(query_h, feat_proj)
    phi_k = feature_map(key_h, feat_proj)
    member_f = (seg_row[:, None] == jnp.arange(SEGS, dtype=jnp.int32)[None, :]).astype(jnp.float32)
    member = member_f.astype(jnp.bfloat16)
    wide_q = spread_segments(phi_q.astype(jnp.bfloat16), member)
    wide_k = spread_segments(phi_k.astype(jnp.bfloat16), member)
    ones_col = jnp.ones((group_rows,), jnp.bfloat16)
    kv_part = jnp.einsum("gha,ghe->hae", wide_k, value_h, preferred_element_type=jnp.float32)
    z_part = jnp.einsum("gha,g->ha", wide_k, ones_col, preferred_element_type=jnp.float32)
    kv_low = kv_part.astype(jnp.bfloat16)
    z_low = z_part.astype(jnp.bfloat16)
    numer_part = jnp.einsum(
        "gha,hae->ghe", wide_q, kv_low, preferred_element_type=jnp.float32
    ).reshape(group_rows, D)
    denom_part = jnp.einsum("gha,ha->gh", wide_q, z_low, preferred_element_type=jnp.float32)
    numer_sum, denom_sum = (
        lax.psum_scatter(numer_part, "feat", scatter_dimension=0, tiled=True),
        lax.psum_scatter(denom_part, "feat", scatter_dimension=0, tiled=True),
    )
    numer_h = numer_sum.reshape(tok_count, H, DH)
    att_low = (numer_h / denom_sum[:, :, None]).reshape(tok_count, D).astype(jnp.bfloat16)
    branch = jnp.dot(att_low, w_out, preferred_element_type=jnp.float32) + b_out.astype(jnp.float32)
    hidden_one, ln1_back = jax.vjp(
        layer_norm,
        tokens.astype(jnp.float32) + branch,
        ln1_gain.astype(jnp.float32),
        ln1_bias.astype(jnp.float32),
    )
    hid_low = hidden_one.astype(jnp.bfloat16)
    pre_act = jnp.dot(hid_low, w_up, preferred_element_type=jnp.float32) + b_up.astype(jnp.float32)
    act_val, gelu_back = jax.vjp(partial(jax.nn.gelu, approximate=False), pre_act)
    act_low = act_val.astype(jnp.bfloat16)
    ffn_out = jnp.dot(act_low, w_down, preferred_element_type=jnp.float32) + b_down.astype(
        jnp.float32
    )
    result, ln2_back = jax.vjp(
        layer_norm, hidden_one + ffn_out, ln2_gain.astype(jnp.float32), ln2_bias.astype(jnp.float32)
    )
    grad_r2, grad_gain2, grad_bias2 = ln2_back(cotangent.astype(jnp.float32))
    grad_ffn = grad_r2.astype(jnp.bfloat16)
    grad_bdown = jnp.sum(grad_ffn.astype(jnp.float32), 0)
    grad_wdown = cross_dot(act_low, grad_ffn)
    (grad_act,) = gelu_back(back_dot(grad_ffn, w_down))
    grad_pre = grad_act.astype(jnp.bfloat16)
    grad_bup = jnp.sum(grad_pre.astype(jnp.float32), 0)
    grad_wup = cross_dot(hid_low, grad_pre)
    grad_h1 = grad_r2 + back_dot(grad_pre, w_up)
    grad_r1, grad_gain1, grad_bias1 = ln1_back(grad_h1)
    grad_branch = grad_r1.astype(jnp.bfloat16)
    grad_bout = jnp.sum(grad_branch.astype(jnp.float32), 0)
    grad_wout = cross_dot(att_low, grad_branch)
    grad_att = back_dot(grad_branch, w_out).reshape(tok_count, H, DH)
    grad_num = (grad_att / denom_sum[:, :, None]).reshape(tok_count, D).astype(jnp.bfloat16)
    grad_den = (-jnp.sum(grad_att * numer_h, -1) / (denom_sum * denom_sum)).astype(jnp.bfloat16)
    group_num, group_den = (
        lax.all_gather(grad_num, "feat", axis=0, tiled=True),
        lax.all_gather(grad_den, "feat", axis=0, tiled=True),
    )
    group_num_h = group_num.reshape(group_rows, H, DH)
    grad_kv_part = jnp.einsum(
        "gha,ghe->hae", wide_q, group_num_h, preferred_element_type=jnp.float32
    )
    grad_z_part = jnp.einsum("gha,gh->ha", wide_q, group_den, preferred_element_type=jnp.float32)
    grad_kv = grad_kv_part.astype(jnp.bfloat16)
    grad_z = grad_z_part.astype(jnp.bfloat16)
    wide_gq = jnp.einsum("ghe,hae->gha", group_num_h, kv_low, preferred_element_type=jnp.float32)
    wide_gq = wide_gq + group_den[:, :, None].astype(jnp.float32) * z_low[None].astype(jnp.float32)
    grad_arg_q = (fold_segments(wide_gq, member_f) * phi_q).astype(jnp.bfloat16)
    wide_gk = jnp.einsum(
        "ghe,hae->gha", value_h, grad_kv, preferred_element_type=jnp.float32
    ) + grad_z[None].astype(jnp.float32)
    grad_arg_k = (fold_segments(wide_gk, member_f) * phi_k).astype(jnp.bfloat16)
    grad_value = jnp.einsum("gha,hae->ghe", wide_k, grad_kv, preferred_element_type=jnp.float32)
    grad_query = feature_back(query_h, feat_proj, grad_arg_q)
    grad_key = feature_back(key_h, feat_proj, grad_arg_k)
    grad_group = jnp.concatenate(
        [
            grad_query.reshape(group_rows, D),
            grad_key.reshape(group_rows, D),
            grad_value.reshape(group_rows, D),
        ],
        1,
    )
    grad_qkv = lax.psum_scatter(
        grad_group.astype(jnp.bfloat16), "feat", scatter_dimension=0, tiled=True
    )
    grad_bqkv = jnp.sum(grad_qkv.astype(jnp.float32), 0)
    grad_wqkv = cross_dot(tokens, grad_qkv)
    grad_tokens = grad_r1 + back_dot(grad_qkv, w_qkv)
    grads_now = (
        grad_wqkv,
        grad_bqkv,
        grad_wout,
        grad_bout,
        grad_gain1,
        grad_bias1,
        grad_wup,
        grad_bup,
        grad_wdown,
        grad_bdown,
        grad_gain2,
        grad_bias2,
    )
    return (result.astype(jnp.bfloat16), grad_tokens, grads_now)


def on_device(
    tokens_in,
    out_cotangent,
    segment_ids,
    feature_proj,
    w_qkv,
    b_qkv,
    w_out,
    b_out,
    ln1_gain,
    ln1_bias,
    w_up,
    b_up,
    w_down,
    b_down,
    ln2_gain,
    ln2_bias,
):
    totals = None
    outputs = []
    grad_inputs = []
    for micro_idx in range(MICRO):
        gathered = fetch_weights(
            w_qkv,
            b_qkv,
            w_out,
            b_out,
            ln1_gain,
            ln1_bias,
            w_up,
            b_up,
            w_down,
            b_down,
            ln2_gain,
            ln2_bias,
        )
        result, grad_tokens, grads_now = micro_step(
            tokens_in[micro_idx],
            out_cotangent[micro_idx],
            segment_ids[micro_idx],
            feature_proj,
            gathered,
        )
        outputs.append(result)
        grad_inputs.append(grad_tokens)
        totals = grads_now if totals is None else jax.tree.map(jnp.add, totals, grads_now)
    (
        grad_wqkv,
        grad_bqkv,
        grad_wout,
        grad_bout,
        grad_gain1,
        grad_bias1,
        grad_wup,
        grad_bup,
        grad_wdown,
        grad_bdown,
        grad_gain2,
        grad_bias2,
    ) = totals
    summed = (
        lax.psum_scatter(grad_wqkv, ("dp", "feat"), scatter_dimension=0, tiled=True),
        lax.psum_scatter(grad_bqkv, ("dp", "feat"), scatter_dimension=0, tiled=True),
        lax.psum_scatter(grad_wout, ("dp", "feat"), scatter_dimension=0, tiled=True),
        lax.psum_scatter(grad_bout, ("dp", "feat"), scatter_dimension=0, tiled=True),
        lax.psum_scatter(grad_gain1, ("dp", "feat"), scatter_dimension=0, tiled=True),
        lax.psum_scatter(grad_bias1, ("dp", "feat"), scatter_dimension=0, tiled=True),
        lax.psum_scatter(grad_wup, ("dp", "feat"), scatter_dimension=0, tiled=True),
        lax.psum_scatter(grad_bup, ("dp", "feat"), scatter_dimension=0, tiled=True),
        lax.psum_scatter(grad_wdown, ("dp", "feat"), scatter_dimension=0, tiled=True),
        lax.psum_scatter(grad_bdown, ("dp", "feat"), scatter_dimension=0, tiled=True),
        lax.psum_scatter(grad_gain2, ("dp", "feat"), scatter_dimension=0, tiled=True),
        lax.psum_scatter(grad_bias2, ("dp", "feat"), scatter_dimension=0, tiled=True),
    )
    return (
        jnp.stack(outputs),
        jnp.stack(grad_inputs),
        summed[0],
        summed[1],
        summed[2],
        summed[3],
        summed[4],
        summed[5],
        summed[6],
        summed[7],
        summed[8],
        summed[9],
        summed[10],
        summed[11],
    )


NZ, NY, NC, NX = 4, 2, 2, 2
N_DEV = NZ * NY * NC * NX
MESH_ID = pl.DeviceIdType.MESH
BF = jnp.bfloat16
F32 = jnp.float32
SHARE = MICRO // NX
GRID = (NZ, NY, NC)
ALL = slice(None)


def fits(mesh):
    return mesh.shape["dp"] == NZ * NY * NC and mesh.shape["feat"] == NX


class Place:
    def __init__(self):
        i = lax.axis_index("dp")
        self.z, self.y, self.c, self.x = i // (NY * NC), (i // NC) % NY, i % NC, lax.axis_index("feat")
        self.sibling = self.device(c=1 - self.c)
        self.over = {"x": self.device(x=1 - self.x), "y": self.device(y=1 - self.y)}
        self.z_of = [lax.rem(self.z + k, NZ) for k in (1, 2, 3)]
        self.over_z = [self.device(z=z) for z in self.z_of]

    def device(self, **other):
        z, y, c, x = (other.get(n, getattr(self, n)) for n in "zycx")
        return (z * (NY * NC) + y * NC + c, x)

    def meet(self):
        barrier = pltpu.get_barrier_semaphore()
        peers = [self.sibling, self.over["x"], self.over["y"]] + self.over_z
        for peer in peers:
            pl.semaphore_signal(barrier, inc=1, device_id=peer, device_id_type=MESH_ID)
        pl.semaphore_wait(barrier, len(peers))

    def per_class(self, orders, act):
        if orders[0] == orders[1]:
            act(orders[0])
            return
        for c in range(NC):

            @pl.when(self.c == c)
            def _(order=orders[c]):
                act(order)

    def rows(self, grid, x):
        share = grid.shape[3] // NX
        return pl.ds(pl.multiple_of(x * share, 8), share)

    def view(self, grid, cols, spread=(), **at):
        index = [ALL if n in spread else at.get(n, getattr(self, n)) for n in "zyc"]
        rows = ALL if "x" in spread else self.rows(grid, at.get("x", self.x))
        return grid.at[(*index, rows, cols)]


class Copies:
    def __init__(self, send_sems, recv_sems):
        self.send_sems, self.recv_sems = send_sems, recv_sems

    def copy(self, slot, src, dst, peer):
        return pltpu.make_async_remote_copy(
            src_ref=src, dst_ref=dst, send_sem=self.send_sems.at[slot], recv_sem=self.recv_sems.at[slot],
            device_id=peer, device_id_type=MESH_ID,
        )


class Gather(Copies):
    def __init__(self, here, part, src, grid, cols, orders, sems):
        super().__init__(sems[0].at[part], sems[1].at[part])
        self.here, self.grid, self.cols, self.orders = here, grid, cols, orders
        self.src = src.at[ALL, cols]
        self.local = pltpu.make_async_copy(self.src, here.view(grid, cols), sems[2].at[part])

    def phase(self, order, n):
        here, dim = self.here, order[n]
        mine = here.view(self.grid, self.cols, order[:n])
        src = self.src if n == 0 else mine
        if dim == "z":
            return [self.copy(n + k, src, mine, peer) for k, peer in enumerate(here.over_z)]
        slot = n if order.index("z") > n else n + 2
        return [self.copy(slot, src, mine, here.over[dim])]

    def to_sibling(self):
        mine = self.here.view(self.grid, self.cols, "zyx")
        return self.copy(5, mine, mine, self.here.sibling)

    def step(self, n):
        if n == 0:
            self.local.start()
            self.here.per_class(self.orders, lambda order: [c.start() for c in self.phase(order, 0)])
        elif n < 4:
            self.here.per_class(self.orders, lambda order: [c.wait_recv() for c in self.phase(order, n - 1)])
            if n == 1:
                self.local.wait()
            if n < 3:
                self.here.per_class(self.orders, lambda order: [c.start() for c in self.phase(order, n)])
            else:
                self.to_sibling().start()
        else:
            self.to_sibling().wait_recv()

    def drain(self):
        for n in range(3):
            self.here.per_class(self.orders, lambda order, n=n: [c.wait_send() for c in self.phase(order, n)])
        self.to_sibling().wait_send()


class Reduce(Copies):
    def __init__(self, here, part, grid, cols, orders, got, stage, out, sems):
        super().__init__(sems[0].at[part], sems[1].at[part])
        self.here, self.grid, self.cols, self.orders = here, grid, cols, orders
        self.got, self.stage = got, stage
        self.out = pltpu.make_async_copy(stage, out.at[ALL, cols], sems[2].at[part])

    def from_sibling(self):
        here = self.here
        theirs = here.view(self.grid, self.cols, "zyx", c=1 - here.c)
        return self.copy(0, theirs, self.got[0][0], here.sibling)

    def received(self, order, n):
        return self.got[n][self.orders.index(order) % len(self.got[n])]

    def phase(self, order, n):
        here, dim, rest = self.here, order[n], order[n + 1 :]
        got = self.received(order, n + 1)
        if dim == "z":
            return [
                self.copy(1 + n + k, here.view(self.grid, self.cols, rest, z=z), got.at[k], peer)
                for k, (z, peer) in enumerate(zip(here.z_of, here.over_z, strict=True))
            ]
        slot = 1 + n if order.index("z") > n else 3 + n
        place = {dim: 1 - getattr(here, dim)}
        return [self.copy(slot, here.view(self.grid, self.cols, rest, **place), got, here.over[dim])]

    def spot(self, spread, q):
        here, index, inner = self.here, {}, []
        if "y" in spread:
            index["y"] = q % NY
            q = q // NY
        if "z" in spread:
            index["z"] = q
        inner = tuple(index[n] for n in "zy" if n in index)
        rows = ALL if "x" in spread else here.rows(self.grid, here.x)
        return tuple(index.get(n, getattr(here, n)) for n in "zyc") + (rows, self.cols), inner

    def add(self, got, spread, copies=1):
        def one(q):
            index, inner = self.spot(spread, q)
            if copies == 1:
                self.grid[index] = self.grid[index] + got[inner + (ALL, ALL)]
                return
            total = self.grid[index].astype(F32)
            for k in range(copies):
                total = total + got[(k,) + inner + (ALL, ALL)].astype(F32)
            self.grid[index] = total.astype(self.grid.dtype)

        count = (NZ if "z" in spread else 1) * (NY if "y" in spread else 1)
        blocks_of(count, one) if count > 1 else one(0)

    def finish(self, got, copies):
        index, _ = self.spot((), 0)
        total = self.grid[index].astype(F32)
        for k in range(copies):
            total = total + got[((k,) if copies > 1 else ()) + (ALL, ALL)].astype(F32)
        self.stage[...] = total

    def step(self, n):
        if n == 0:
            self.from_sibling().start()
            return
        if n == 1:
            self.from_sibling().wait_recv()
            self.add(self.got[0][0], "zyx")
        else:

            def take(order):
                for c in self.phase(order, n - 2):
                    c.wait_recv()
                copies = 3 if order[n - 2] == "z" else 1
                got = self.received(order, n - 1)
                if n < 4:
                    self.add(got, order[n - 1 :], copies)
                else:
                    self.finish(got, copies)

            self.here.per_class(self.orders, take)
        if n < 4:
            self.here.per_class(self.orders, lambda order: [c.start() for c in self.phase(order, n - 1)])
        else:
            self.out.start()

    def drain(self):
        self.from_sibling().wait_send()
        for n in range(3):
            self.here.per_class(self.orders, lambda order, n=n: [c.wait_send() for c in self.phase(order, n)])
        self.out.wait()


def got_shapes(orders, rows, width):
    first, second = (order_shapes(order, rows, width) for order in orders)
    return [(a,) if a == b else (a, b) for a, b in zip(first, second, strict=True)]


def order_shapes(order, rows, width):

    def block(spread):
        return tuple(dict(z=NZ, y=NY)[n] for n in "zy" if n in spread) + (rows * (NX if "x" in spread else 1), width)

    shapes = [block("zyx")]
    for n, dim in enumerate(order):
        shapes.append(((NZ - 1,) if dim == "z" else ()) + block(order[n + 1 :]))
    return shapes


def blocks_of(count, body, then=()):
    def step(j, carry):
        body(j)
        for at in sorted({at for at, _ in then}):

            @pl.when(j == at)
            def _(at=at):
                for when, act in then:
                    if when == at:
                        act()

        return carry

    lax.fori_loop(0, count, step, 0)


ROWS = 512
BLK = 256
PAIRS = D // 128
FF = 4 * D
WIDE = 2 * FEATS
SCALE = DH ** (-0.25)


def dot(a, b, ca=1, cb=0):
    return lax.dot_general(a, b, (((ca,), (cb,)), ((), ())), preferred_element_type=F32)


def half_masks(width):
    lane = lax.broadcasted_iota(jnp.int32, (1, width), 1) % 128
    first = (lane < DH).astype(F32)
    return first.astype(BF), (1.0 - first).astype(BF)


def lanes(j, width):
    return pl.ds(pl.multiple_of(j * width, width), width)


class Work:
    def __init__(self, refs):
        self.__dict__.update(refs)

    def setup(self, proj, seg_rows):
        row = lax.broadcasted_iota(jnp.int32, (DH, 128), 0)
        col = lax.broadcasted_iota(jnp.int32, (DH, 128), 1)
        for h in range(2):
            place_in = (col == row + h * DH).astype(BF)
            for n in range(NX):
                self.table[pl.ds(h * FEATS + n * 128, 128), 0:128] = dot(proj[n], place_in).astype(BF)
        feat = lax.broadcasted_iota(jnp.int32, (WIDE, 128), 0) // FEATS
        half = lax.broadcasted_iota(jnp.int32, (WIDE, 128), 1) // DH
        same = (feat == half).astype(F32).astype(BF)
        self.table[:, 128:256] = same
        for b in range(2):
            across = jnp.broadcast_to(seg_rows[b], (BLK, BLK))
            self.mask[b] = (across == jnp.transpose(across)).astype(F32)

    def features(self, rows):
        wide = rows.astype(F32)
        squares = wide * wide
        high = squares.astype(BF)
        low = (squares - high.astype(F32)).astype(BF)
        same = self.table[:, 128:256]
        norm = dot(high, same, 1, 1) + dot(low, same, 1, 1)
        arg = SCALE * dot(rows, self.table[:, 0:128], 1, 1) - (0.5 * SCALE * SCALE) * norm
        return (jnp.exp(arg) * FEATS ** (-0.5)).astype(BF)

    def qkv_block(self, j):
        col = lanes(j, 256)
        full = dot(self.x[...], self.w_qkv[:, col]) + self.b_qkv[:, col]
        self.qkv[:, col] = full.astype(BF)

    def pair(self, i):
        b, p = i // PAIRS, i % PAIRS
        rows = pl.ds(pl.multiple_of(b * BLK, BLK), BLK)
        cols = [pl.ds(pl.multiple_of(n * D + p * 128, 128), 128) for n in range(3)]
        return b, rows, cols

    def attend(self, i):
        b, rows, cols = self.pair(i)
        mask = self.mask[b]
        m0, m1 = half_masks(128)
        phi_q = self.features(self.qkv[rows, cols[0]])
        phi_k = self.features(self.qkv[rows, cols[1]])
        self.phi_q[i] = phi_q
        self.phi_k[i] = phi_k
        v = self.qkv[rows, cols[2]]
        one = jnp.ones((BLK, 128), BF)
        res = None
        for h, m in enumerate((m0, m1)):
            part = slice(h * FEATS, (h + 1) * FEATS)
            score = (dot(phi_q[:, part], phi_k[:, part], 1, 1) * mask).astype(BF)
            term = dot(score, jnp.concatenate([v * m, one * m], 1))
            res = term if res is None else res + term
        inv = 1.0 / res[:, 128:]
        self.inv[rows, cols[0]] = inv
        self.att[rows, cols[0]] = (res[:, :128] * inv).astype(BF)

    def normalize(self, r):
        center = r - jnp.mean(r, -1, keepdims=True)
        scale = lax.rsqrt(jnp.mean(center * center, -1, keepdims=True) + EPSILON)
        return center * scale, scale

    def normalize_back(self, dy, n, scale, gain):
        g = dy * gain
        return (g - jnp.mean(g, -1, keepdims=True) - n * jnp.mean(g * n, -1, keepdims=True)) * scale

    def branch(self):
        for j in range(3):
            col = lanes(j, 256)
            self.n1[:, col] = dot(self.att[...], self.w_out[:, col]) + self.b_out[:, col] + self.x[:, col].astype(F32)

        def rows_of(j):
            row = pl.ds(pl.multiple_of(j * 64, 64), 64)
            n1, s1 = self.normalize(self.n1[row, :])
            self.n1[row, :] = n1
            self.s1[row, :] = s1
            self.h1[row, :] = (n1 * self.g1[...] + self.b1[...]).astype(BF)

        blocks_of(ROWS // 64, rows_of)

    def up_block(self, j):
        col = lanes(j, 256)
        for r in range(0, ROWS, 128):
            row = slice(r, r + 128)
            a = dot(self.h1[row, :], self.w_up[:, col]) + self.b_up[:, col]
            cdf = 0.5 * (1.0 + lax.erf(a * 2**-0.5))
            self.z[row, col] = (a * cdf).astype(BF)
            self.slope[row, col] = (cdf + a * jnp.exp(-0.5 * a * a) * (0.5 / 3.141592653589793) ** 0.5).astype(BF)

    def down_block(self, j):
        col = lanes(j, 256)
        back = self.n1[:, col] * self.g1[:, col] + self.b1[:, col]
        self.dr[:, col] = dot(self.z[...], self.w_down[:, col]) + self.b_down[:, col] + back

    def second_norm(self):
        for ref in (self.d_g2, self.d_b2, self.d_b_down):
            ref[...] = jnp.zeros_like(ref)

        def rows_of(j):
            row = pl.ds(pl.multiple_of(j * 64, 64), 64)
            n2, s2 = self.normalize(self.dr[row, :])
            self.y[row, :] = (n2 * self.g2[...] + self.b2[...]).astype(BF)
            dy = self.cot[row, :].astype(F32)
            dr2 = self.normalize_back(dy, n2, s2, self.g2[...])
            self.dr[row, :] = dr2
            df = dr2.astype(BF)
            self.df[row, :] = df
            self.d_g2[...] += jnp.sum(dy * n2, 0, keepdims=True)
            self.d_b2[...] += jnp.sum(dy, 0, keepdims=True)
            self.d_b_down[...] += jnp.sum(df.astype(F32), 0, keepdims=True)

        blocks_of(ROWS // 64, rows_of)

    def down_back(self, j):
        col = lanes(j, 256)
        dz = dot(self.df[...], self.w_down[col, :], 1, 1)
        da = (dz * self.slope[:, col].astype(F32)).astype(BF)
        self.slope[:, col] = da
        self.d_b_up[:, col] = jnp.sum(da.astype(F32), 0, keepdims=True)

    def down_grad(self, part, j):
        col = lanes(j, 256)
        self.w_down[col, part] = dot(self.z[:, col], self.df[:, part], 0, 0).astype(BF)

    def up_back(self, j):
        col = lanes(j, 256)
        self.dr[:, col] += dot(self.slope[...], self.w_up[col, :], 1, 1)

    def turn(self, name):
        self.flip[...] = jnp.transpose(getattr(self, name)[...])

    def up_grad(self, j):
        col = lanes(j, 256)
        self.w_up[:, col] = dot(self.flip[...], self.slope[:, col]).astype(BF)

    def first_norm_back(self):
        for ref in (self.d_g1, self.d_b1, self.d_b_out):
            ref[...] = jnp.zeros_like(ref)

        def rows_of(j):
            row = pl.ds(pl.multiple_of(j * 64, 64), 64)
            dh1, n1 = self.dr[row, :], self.n1[row, :]
            dr1 = self.normalize_back(dh1, n1, self.s1[row, :], self.g1[...])
            self.dr[row, :] = dr1
            do = dr1.astype(BF)
            self.df[row, :] = do
            self.d_g1[...] += jnp.sum(dh1 * n1, 0, keepdims=True)
            self.d_b1[...] += jnp.sum(dh1, 0, keepdims=True)
            self.d_b_out[...] += jnp.sum(do.astype(F32), 0, keepdims=True)

        blocks_of(ROWS // 64, rows_of)

    def att_back(self, j):
        head_r = lax.broadcasted_iota(jnp.int32, (256, 256), 0) // DH
        head_c = lax.broadcasted_iota(jnp.int32, (256, 256), 1) // DH
        same = (head_r == head_c).astype(F32).astype(BF)
        col = lanes(j, 256)
        datt = dot(self.df[...], self.w_out[col, :], 1, 1)
        inv = self.inv[:, col]
        self.cot[:, col] = (datt * inv).astype(BF)
        prod = datt * self.att[:, col].astype(F32)
        high = prod.astype(BF)
        low = (prod - high.astype(F32)).astype(BF)
        total = dot(high, same) + dot(low, same)
        self.h1[:, col] = (-total * inv).astype(BF)

    def out_grad(self, j):
        col = lanes(j, 256)
        self.w_out[:, col] = dot(self.flip[...], self.df[:, col]).astype(BF)

    def attend_back(self, i):
        b, rows, cols = self.pair(i)
        mask = self.mask[b]
        m0, m1 = half_masks(256)
        q, k, v = (self.qkv[rows, c] for c in cols)
        dnum, dden = self.cot[rows, cols[0]], self.h1[rows, cols[0]]
        left = jnp.concatenate([dnum, dden * (1.0 / DH)], 1)
        right = jnp.concatenate([v, jnp.ones((BLK, 128), BF)], 1)
        back_q, back_k, dv = None, None, None
        for h, m in enumerate((m0, m1)):
            part = slice(h * FEATS, (h + 1) * FEATS)
            phi_q, phi_k = self.phi_q[i, :, part], self.phi_k[i, :, part]
            mine = left * m
            dscore = (dot(mine, right, 1, 1) * mask).astype(BF)
            flipped = (dot(right, mine, 1, 1) * mask).astype(BF)
            darg_q = (dot(dscore, phi_k) * phi_q.astype(F32)).astype(BF)
            darg_k = (dot(flipped, phi_q) * phi_k.astype(F32)).astype(BF)
            score = (dot(phi_k, phi_q, 1, 1) * mask).astype(BF)
            table = self.table[part, :]
            terms = dot(darg_q, table), dot(darg_k, table), dot(score, mine[:, :128])
            if h == 0:
                back_q, back_k, dv = terms
            else:
                back_q, back_k, dv = back_q + terms[0], back_k + terms[1], dv + terms[2]
        for n, (rows_in, back) in enumerate(((q, back_q), (k, back_k))):
            grad = SCALE * back[:, :128] - (SCALE * SCALE) * rows_in.astype(F32) * back[:, 128:]
            self.qkv[rows, cols[n]] = grad.astype(BF)
        self.qkv[rows, cols[2]] = dv.astype(BF)

    def tokens_back(self, j):
        col = lanes(j, 256)
        self.dr[:, col] += dot(self.qkv[...], self.w_qkv[col, :], 1, 1)

    def qkv_grad(self, j):
        col = lanes(j, 256)
        part = self.qkv[:, col]
        self.d_b_qkv[:, col] = jnp.sum(part.astype(F32), 0, keepdims=True)
        self.w_qkv[:, col] = dot(self.flip[...], part).astype(BF)


VECTORS = ("b_qkv", "b_out", "g1", "b1", "b_up", "b_down", "g2", "b2")
WIDTHS = (3 * D, D, D, D, FF, D, D, D)
SPACE = (
    ("qkv", (ROWS, 3 * D), BF), ("phi_q", (2 * PAIRS, BLK, WIDE), BF), ("phi_k", (2 * PAIRS, BLK, WIDE), BF),
    ("att", (ROWS, D), BF), ("inv", (ROWS, D), F32), ("n1", (ROWS, D), F32), ("s1", (ROWS, 1), F32),
    ("h1", (ROWS, D), BF), ("z", (ROWS, FF), BF), ("slope", (ROWS, FF), BF), ("dr", (ROWS, D), F32),
    ("df", (ROWS, D), BF), ("flip", (D, ROWS), BF),
    ("table", (WIDE, 256), BF), ("mask", (2, BLK, BLK), F32),
)


GATHER_PARTS = {
    "small": ("small", 0, 128, ("zyx", "zxy")),
    "q": ("w_qkv", 0, 768, ("zyx", "zyx")),
    "k": ("w_qkv", 768, 768, ("zyx", "zyx")),
    "v": ("w_qkv", 1536, 768, ("zyx", "zyx")),
    "out": ("w_out", 0, 768, ("zyx", "zyx")),
    "up0": ("w_up", 0, 768, ("zyx", "zyx")),
    "up1": ("w_up", 768, 768, ("zxy", "zxy")),
    "up2": ("w_up", 1536, 768, ("xzy", "xzy")),
    "up3": ("w_up", 2304, 768, ("xzy", "xzy")),
    "dn0": ("w_down", 0, 256, ("xzy", "xzy")),
    "dn1": ("w_down", 256, 256, ("zyx", "zyx")),
    "dn2": ("w_down", 512, 256, ("xyz", "xyz")),
}
REDUCE_PARTS = {
    "small": ("small", 0, 128, ("xyz", "yxz")),
    "q": ("w_qkv", 0, 768, ("xyz", "yxz")),
    "k": ("w_qkv", 768, 768, ("yzx", "yzx")),
    "v": ("w_qkv", 1536, 768, ("xyz", "xyz")),
    "out": ("w_out", 0, 768, ("xyz", "yxz")),
    "up0": ("w_up", 0, 1536, ("yzx", "xzy")),
    "up1": ("w_up", 1536, 1536, ("xyz", "yxz")),
    "dn0": ("w_down", 0, 384, ("yzx", "xzy")),
    "dn1": ("w_down", 384, 384, ("xyz", "yxz")),
}
FORWARD = (
    "proj!", "small0", "q0", "tok!", "k0", "v0", "out0", "up20", "small1", "dn00", "proj?", "setup", "q1", "up10",
    "k1", "up00", "q2", "dn10", "dn20", "up30", "up21", "small2", "v1", "dn01", "k2", "out1", "v2", "up11", "q3",
    "out2", "dn21", "up31", "small3", "up01", "q4", "small4", "spread", "dn22", "tok?", "qkv*3", "dn11", "up02", "k3",
    "k4", "qkv*3", "dn12", "up22", "v3", "v4", "cot!", "qkv*2", "up12", "qkv", "att*2", "up23", "att", "dn02", "att",
    "up24", "att", "out3", "att*3", "out4", "up13", "up32", "att*2", "up14", "att", "up03", "att", "branch", "up04",
    "dn03", "upb*5", "dn04", "upb*2", "dn13", "upb*2", "up33", "dn14", "up34", "upb", "dn23", "upb*2", "down*2",
    "dn24", "down", "cot?", "ln2",
)
BACKWARD = (
    "y!", "dz*12", "gdn0*12", "dn00", "gdn1*12", "dn10", "uback", "dn01", "uback*2", "dn11", "flip0", "gup*6", "up00",
    "gup*5", "dn02", "gup", "up10", "nback", "up01", "datt", "up11", "datt*2", "dn12", "flip1", "gout*3", "out0",
    "attb*3", "out1", "attb", "up02", "attb*2", "dn03", "attb*5", "up12", "attb", "tback*2", "dn13", "tback", "lower",
    "flip2", "gqkv", "out2", "gqkv*2", "q0", "dn04", "gqkv", "up03", "gqkv*2", "k0", "gqkv*2", "q1", "up13", "gqkv",
    "v0", "collect", "k1", "out3", "up04", "small0", "v1", "dn14", "small1", "q2", "up14", "k2", "small2", "v2",
    "grad!", "out4", "q3", "small3", "v3", "k3", "q4", "small4", "k4", "v4",
)
WEIGHTS = (("w_qkv", (D, 3 * D)), ("w_out", (D, D)), ("w_up", (D, FF)), ("w_down", (FF, D)))
TILE = (8, 128)
HALF = (SHARE, NX, ROWS // SHARE // NX, D)


def shard_rows(weight):
    return TILE[0] if weight == "small" else dict(WEIGHTS)[weight][0] // N_DEV


class Swap:
    def __init__(self, here, n, theirs, target, mine, home, sems):
        self.there = pltpu.make_async_remote_copy(
            src_ref=theirs, dst_ref=target, send_sem=sems[0].at[n], recv_sem=sems[1].at[n],
            device_id=here.over["x"], device_id_type=MESH_ID,
        )
        self.here = None if home is None else pltpu.make_async_copy(mine, home, sems[2].at[n])

    def start(self):
        self.there.start()
        if self.here is not None:
            self.here.start()

    def arrive(self):
        self.there.wait_recv()
        if self.here is not None:
            self.here.wait()


def one_hot(width, count):
    at = lax.broadcasted_iota(jnp.int32, (1, count), 1).astype(F32)
    owner = jnp.floor((at + 0.5) * (1.0 / width))
    lane = at - owner * width
    lanes_hot = (lax.broadcasted_iota(jnp.int32, (128, count), 0).astype(F32) == lane).astype(F32).astype(BF)
    owner_hot = (lax.broadcasted_iota(jnp.int32, (N_DEV, count), 0).astype(F32) == owner).astype(F32)
    return lanes_hot, owner_hot


def spread_small(tiles, vectors):
    for width in sorted({v.shape[1] // N_DEV for v in vectors}):
        hot, owner = one_hot(width, width * N_DEV)
        for n, vector in enumerate(vectors):
            if vector.shape[1] == width * N_DEV:
                rows = tiles[pl.ds(n, N_DEV, stride=TILE[0]), :].astype(BF)
                vector[...] = jnp.sum(dot(rows, hot) * owner, 0, keepdims=True)


def collect_small(tiles, vectors):
    for width in sorted({v.shape[1] // N_DEV for v in vectors}):
        hot, owner = one_hot(width, width * N_DEV)
        for n, vector in enumerate(vectors):
            if vector.shape[1] == width * N_DEV:
                full = owner * vector[...]
                high = full.astype(BF)
                low = (full - high.astype(F32)).astype(BF)
                tiles[pl.ds(n, N_DEV, stride=TILE[0]), :] = dot(high, hot, 1, 1) + dot(low, hot, 1, 1)


def layer_kernel(*refs):
    it = iter(refs)
    tok, cot = next(it), next(it)
    local = {w: next(it) for w, _ in WEIGHTS}
    local["small"], proj_in, seg = next(it), next(it), next(it)
    block_out, grad_tok = next(it), next(it)
    outs = {w: next(it) for w, _ in WEIGHTS}
    outs["small"] = next(it)
    ref = {n: next(it) for n, _ in WEIGHTS}
    ref.update({n: next(it) for n, _, _ in SPACE})
    work = Work(ref)
    got = {
        p: [tuple(next(it) for _ in shapes) for shapes in got_shapes(orders, shard_rows(w), width)]
        for p, (w, _, width, orders) in REDUCE_PARTS.items()
    }
    stage = {p: next(it) for p in REDUCE_PARTS}
    gather_sems = [next(it) for _ in range(3)]
    reduce_sems = [next(it) for _ in range(3)]
    swap_sems = [next(it) for _ in range(3)]
    out_sems = next(it)

    here = Place()
    here.meet()
    x = here.x
    grids = {w: ref[w].reshape(GRID + (NX * shard_rows(w), ref[w].shape[1])) for w, _ in WEIGHTS}
    grids["small"] = ref["tiles"].reshape(GRID + (NX * TILE[0], TILE[1]))
    into, back = {}, {}
    for n, (p, (w, first, width, orders)) in enumerate(GATHER_PARTS.items()):
        into[p] = Gather(here, n, local[w], grids[w], pl.ds(first, width), orders, gather_sems)
    for n, (p, (w, first, width, orders)) in enumerate(REDUCE_PARTS.items()):
        cols = pl.ds(first, width)
        back[p] = Reduce(here, n, grids[w], cols, orders, got[p], stage[p], outs[w], reduce_sems)

    def halves(r):
        return r.reshape(HALF)

    grad_low, grad_high = halves(work.df).at[0], halves(work.inv).at[0]
    own, other = pl.ds(x * SHARE, SHARE), pl.ds((1 - x) * SHARE, SHARE)
    swap = {
        "tok": Swap(here, 0, tok.at[other], halves(work.x).at[:, x], tok.at[own], halves(work.x).at[:, x], swap_sems),
        "cot": Swap(here, 1, cot.at[other], halves(work.cot).at[:, x], cot.at[own], halves(work.cot).at[:, x], swap_sems),
        "proj": Swap(here, 2, proj_in, work.proj.at[x], proj_in, work.proj.at[x], swap_sems),
        "y": Swap(here, 3, halves(work.y).at[:, 1 - x], block_out.at[own], halves(work.y).at[:, x], block_out.at[own], swap_sems),
        "grad": Swap(here, 4, grad_low, work.grad_got, halves(work.dr).at[:, x], grad_tok.at[own], swap_sems),
    }

    vectors = [getattr(work, n) for n in VECTORS]
    totals = [getattr(work, "d_" + n) for n in VECTORS]

    def setup():
        work.setup(work.proj, [seg[pl.ds(SHARE * x + b, 1), :].astype(F32) for b in range(SHARE)])

    def lower():
        def block(b):
            grad_low[b] = halves(work.dr)[b, 1 - x].astype(BF)

        blocks_of(SHARE, block)

    stages = {
        "setup": (1, setup),
        "spread": (1, lambda: spread_small(ref["tiles"], vectors)),
        "qkv": (9, work.qkv_block),
        "att": (2 * PAIRS, work.attend),
        "branch": (1, work.branch),
        "upb": (12, work.up_block),
        "down": (3, work.down_block),
        "ln2": (1, work.second_norm),
        "dz": (12, work.down_back),
        "uback": (3, work.up_back),
        "flip0": (1, partial(work.turn, "h1")),
        "gup": (12, work.up_grad),
        "nback": (1, work.first_norm_back),
        "datt": (3, work.att_back),
        "flip1": (1, partial(work.turn, "att")),
        "gout": (3, work.out_grad),
        "attb": (2 * PAIRS, work.attend_back),
        "tback": (3, work.tokens_back),
        "lower": (1, lower),
        "flip2": (1, partial(work.turn, "x")),
        "gqkv": (9, work.qkv_grad),
        "collect": (1, lambda: collect_small(ref["tiles"], totals)),
    }
    for p, (w, first, width, _) in REDUCE_PARTS.items():
        if w == "w_down":
            stages["g" + p] = (12, partial(work.down_grad, slice(first, first + width)))

    def act(steps, token):
        if token[-1] == "!":
            swap[token[:-1]].start()
        elif token[-1] == "?":
            swap[token[:-1]].arrive()
        else:
            steps[token[:-1]].step(int(token[-1]))

    def play(tokens, steps):
        tokens = [t.split("*") for t in tokens]
        tokens = [(t[0], int(t[1]) if len(t) > 1 else 1) for t in tokens]
        while tokens:
            name, _ = tokens[0]
            if name not in stages:
                act(steps, name)
                tokens.pop(0)
                continue
            count, body = stages[name]
            n, then = 0, []
            while n < count:
                token, times = tokens.pop(0)
                if token == name:
                    n += times
                else:
                    then.append((n - 1, partial(act, steps, token)))
            if count > 1:
                blocks_of(count, body, then)
            else:
                body()

    play(FORWARD, into)
    for part in into.values():
        part.drain()
    play(BACKWARD, back)
    swap["grad"].arrive()

    def lift(b):
        grad_high[b] = work.grad_got[b].astype(F32)

    blocks_of(SHARE, lift)
    last = pltpu.make_async_copy(grad_high, grad_tok.at[other], out_sems.at[0])
    last.start()
    swap["y"].arrive()
    for each in swap.values():
        each.there.wait_send()
    for part in back.values():
        part.drain()
    last.wait()


QUARTER = (SHARE, ROWS // SHARE // NX, D)
SPACE = (
    (("x", (ROWS, D), BF), ("cot", (ROWS, D), BF), ("y", (ROWS, D), BF), ("proj", (NX, FEATS // NX, DH), BF))
    + (("tiles", (N_DEV * TILE[0], TILE[1]), F32), ("grad_got", QUARTER, BF))
    + tuple((n, (1, w), F32) for n, w in zip(VECTORS, WIDTHS))
    + tuple(("d_" + n, (1, w), F32) for n, w in zip(VECTORS, WIDTHS))
    + SPACE
)


def layer(tok, cot, weights, small, proj, seg):
    anywhere = pl.BlockSpec(memory_space=pl.ANY)
    vmem = pl.BlockSpec(memory_space=pltpu.VMEM)
    shape, dma = jax.ShapeDtypeStruct, pltpu.SemaphoreType.DMA
    received, stages = [], []
    for w, _, width, orders in REDUCE_PARTS.values():
        kind = F32 if w == "small" else BF
        received += [pltpu.VMEM(s, kind) for shapes in got_shapes(orders, shard_rows(w), width) for s in shapes]
        stages.append(pltpu.VMEM((shard_rows(w), width), F32))
    there, back = len(GATHER_PARTS), len(REDUCE_PARTS)
    return pl.pallas_call(
        layer_kernel,
        out_shape=[shape(tok.shape, BF), shape(tok.shape, F32)] + [shape(w.shape, F32) for w in weights] + [shape(TILE, F32)],
        in_specs=[anywhere] * 8 + [vmem],
        out_specs=[anywhere] * 7,
        scratch_shapes=[pltpu.VMEM(s, BF) for _, s in WEIGHTS] + [pltpu.VMEM(s, d) for _, s, d in SPACE] + received + stages
        + [dma((there, 6)), dma((there, 6)), dma((there,)), dma((back, 6)), dma((back, 6)), dma((back,))]
        + [dma((5,)), dma((5,)), dma((5,)), dma((1,))],
        compiler_params=pltpu.CompilerParams(collective_id=0, has_side_effects=True, vmem_limit_bytes=61 << 20),
        name="layer",
    )(tok, cot, *weights, small, proj, seg)


def pack_small(vectors):
    rows = [jnp.pad(v.astype(F32).reshape(1, -1), ((n, TILE[0] - 1 - n), (0, TILE[1] - v.shape[0]))) for n, v in enumerate(vectors)]
    total = rows[0]
    for row in rows[1:]:
        total = total + row
    return total


def fast_device(
    tokens_in, out_cotangent, segment_ids, feature_proj,
    w_qkv, b_qkv, w_out, b_out, ln1_gain, ln1_bias, w_up, b_up, w_down, b_down, ln2_gain, ln2_bias,
):
    small = pack_small([b_qkv, b_out, ln1_gain, ln1_bias, b_up, b_down, ln2_gain, ln2_bias])
    out, grad_tok, *sums, tile = layer(
        tokens_in, out_cotangent, [w_qkv, w_out, w_up, w_down], small, feature_proj, segment_ids
    )
    vec = [tile[n, : w // N_DEV] for n, w in enumerate(WIDTHS)]
    return (
        out, grad_tok, sums[0], vec[0], sums[1], vec[1], vec[2], vec[3], sums[2], vec[4], sums[3], vec[5], vec[6], vec[7],
    )


def solution(mesh):
    return jax.shard_map(
        fast_device if fits(mesh) else on_device,
        mesh=mesh,
        in_specs=(
            P(None, ("dp", "feat"), None),
            P(None, ("dp", "feat"), None),
            P(None, "dp"),
            P("feat", None),
            P(("dp", "feat"), None),
            P(("dp", "feat")),
            P(("dp", "feat"), None),
            P(("dp", "feat")),
            P(("dp", "feat")),
            P(("dp", "feat")),
            P(("dp", "feat"), None),
            P(("dp", "feat")),
            P(("dp", "feat"), None),
            P(("dp", "feat")),
            P(("dp", "feat")),
            P(("dp", "feat")),
        ),
        out_specs=(
            P(None, ("dp", "feat"), None),
            P(None, ("dp", "feat"), None),
            P(("dp", "feat"), None),
            P(("dp", "feat")),
            P(("dp", "feat"), None),
            P(("dp", "feat")),
            P(("dp", "feat")),
            P(("dp", "feat")),
            P(("dp", "feat"), None),
            P(("dp", "feat")),
            P(("dp", "feat"), None),
            P(("dp", "feat")),
            P(("dp", "feat")),
            P(("dp", "feat")),
        ),
        check_vma=False,
    )
```

```python
from functools import partial

import jax
import jax.numpy as jnp
from jax import lax
from jax.experimental import pallas as pl
from jax.experimental.pallas import tpu as pltpu
from jax.sharding import PartitionSpec as P

D = 768
H = 12
DH = 64
FEATS = 256
MICRO = 4
SEGS = 4


EPSILON = 1e-05


def layer_norm(residual, norm_gain, norm_shift):
    center = residual - jnp.mean(residual, -1, keepdims=True)
    spread = jnp.mean(center * center, -1, keepdims=True)
    return center * lax.rsqrt(spread + EPSILON) * norm_gain + norm_shift


def cross_dot(left_op, right_op):
    return lax.dot_general(
        left_op, right_op, (((0,), (0,)), ((), ())), preferred_element_type=jnp.float32
    )


def back_dot(left_op, right_op):
    return lax.dot_general(
        left_op, right_op, (((1,), (1,)), ((), ())), preferred_element_type=jnp.float32
    )


def fetch_weights(
    w_qkv, b_qkv, w_out, b_out, ln1_gain, ln1_bias, w_up, b_up, w_down, b_down, ln2_gain, ln2_bias
):
    return (
        lax.all_gather(w_qkv, ("dp", "feat"), axis=0, tiled=True),
        lax.all_gather(b_qkv, ("dp", "feat"), axis=0, tiled=True),
        lax.all_gather(w_out, ("dp", "feat"), axis=0, tiled=True),
        lax.all_gather(b_out, ("dp", "feat"), axis=0, tiled=True),
        lax.all_gather(ln1_gain, ("dp", "feat"), axis=0, tiled=True),
        lax.all_gather(ln1_bias, ("dp", "feat"), axis=0, tiled=True),
        lax.all_gather(w_up, ("dp", "feat"), axis=0, tiled=True),
        lax.all_gather(b_up, ("dp", "feat"), axis=0, tiled=True),
        lax.all_gather(w_down, ("dp", "feat"), axis=0, tiled=True),
        lax.all_gather(b_down, ("dp", "feat"), axis=0, tiled=True),
        lax.all_gather(ln2_gain, ("dp", "feat"), axis=0, tiled=True),
        lax.all_gather(ln2_bias, ("dp", "feat"), axis=0, tiled=True),
    )


def feature_map(head_rows, feat_proj):
    feat_scale = DH ** (-0.25)
    proj_arg = feat_scale * jnp.einsum(
        "ghd,md->ghm", head_rows, feat_proj, preferred_element_type=jnp.float32
    )
    squares = jnp.einsum("ghd,ghd->gh", head_rows, head_rows, preferred_element_type=jnp.float32)
    proj_arg = proj_arg - 0.5 * feat_scale * feat_scale * squares[:, :, None]
    return jnp.exp(proj_arg) * FEATS ** (-0.5)


def feature_back(head_rows, feat_proj, grad_arg):
    feat_scale = DH ** (-0.25)
    proj_back = feat_scale * jnp.einsum(
        "ghm,md->ghd", grad_arg, feat_proj, preferred_element_type=jnp.float32
    )
    arg_total = jnp.sum(grad_arg.astype(jnp.float32), -1, keepdims=True)
    return proj_back - feat_scale * feat_scale * head_rows.astype(jnp.float32) * arg_total


def spread_segments(phi_low, member):
    tok_count, head_count, feat_width = phi_low.shape
    return (phi_low[:, :, None, :] * member[:, None, :, None]).reshape(
        tok_count, head_count, SEGS * feat_width
    )


def fold_segments(grad_wide, member_f):
    tok_count, head_count, wide_dim = grad_wide.shape
    shaped = grad_wide.reshape(tok_count, head_count, SEGS, wide_dim // SEGS)
    return jnp.sum(shaped * member_f[:, None, :, None], 2)


def micro_step(tokens, cotangent, seg_row, feat_proj, weights):
    (
        w_qkv,
        b_qkv,
        w_out,
        b_out,
        ln1_gain,
        ln1_bias,
        w_up,
        b_up,
        w_down,
        b_down,
        ln2_gain,
        ln2_bias,
    ) = weights
    tok_count = tokens.shape[0]
    qkv_rows = jnp.dot(tokens, w_qkv, preferred_element_type=jnp.float32) + b_qkv.astype(
        jnp.float32
    )
    qkv_low = qkv_rows.astype(jnp.bfloat16)
    grouped = lax.all_gather(qkv_low, "feat", axis=0, tiled=True)
    group_rows = grouped.shape[0]
    query_h = grouped[:, :D].reshape(group_rows, H, DH)
    key_h = grouped[:, D : 2 * D].reshape(group_rows, H, DH)
    value_h = grouped[:, 2 * D :].reshape(group_rows, H, DH)
    phi_q = feature_map(query_h, feat_proj)
    phi_k = feature_map(key_h, feat_proj)
    member_f = (seg_row[:, None] == jnp.arange(SEGS, dtype=jnp.int32)[None, :]).astype(jnp.float32)
    member = member_f.astype(jnp.bfloat16)
    wide_q = spread_segments(phi_q.astype(jnp.bfloat16), member)
    wide_k = spread_segments(phi_k.astype(jnp.bfloat16), member)
    ones_col = jnp.ones((group_rows,), jnp.bfloat16)
    kv_part = jnp.einsum("gha,ghe->hae", wide_k, value_h, preferred_element_type=jnp.float32)
    z_part = jnp.einsum("gha,g->ha", wide_k, ones_col, preferred_element_type=jnp.float32)
    kv_low = kv_part.astype(jnp.bfloat16)
    z_low = z_part.astype(jnp.bfloat16)
    numer_part = jnp.einsum(
        "gha,hae->ghe", wide_q, kv_low, preferred_element_type=jnp.float32
    ).reshape(group_rows, D)
    denom_part = jnp.einsum("gha,ha->gh", wide_q, z_low, preferred_element_type=jnp.float32)
    numer_sum, denom_sum = (
        lax.psum_scatter(numer_part, "feat", scatter_dimension=0, tiled=True),
        lax.psum_scatter(denom_part, "feat", scatter_dimension=0, tiled=True),
    )
    numer_h = numer_sum.reshape(tok_count, H, DH)
    att_low = (numer_h / denom_sum[:, :, None]).reshape(tok_count, D).astype(jnp.bfloat16)
    branch = jnp.dot(att_low, w_out, preferred_element_type=jnp.float32) + b_out.astype(jnp.float32)
    hidden_one, ln1_back = jax.vjp(
        layer_norm,
        tokens.astype(jnp.float32) + branch,
        ln1_gain.astype(jnp.float32),
        ln1_bias.astype(jnp.float32),
    )
    hid_low = hidden_one.astype(jnp.bfloat16)
    pre_act = jnp.dot(hid_low, w_up, preferred_element_type=jnp.float32) + b_up.astype(jnp.float32)
    act_val, gelu_back = jax.vjp(partial(jax.nn.gelu, approximate=False), pre_act)
    act_low = act_val.astype(jnp.bfloat16)
    ffn_out = jnp.dot(act_low, w_down, preferred_element_type=jnp.float32) + b_down.astype(
        jnp.float32
    )
    result, ln2_back = jax.vjp(
        layer_norm, hidden_one + ffn_out, ln2_gain.astype(jnp.float32), ln2_bias.astype(jnp.float32)
    )
    grad_r2, grad_gain2, grad_bias2 = ln2_back(cotangent.astype(jnp.float32))
    grad_ffn = grad_r2.astype(jnp.bfloat16)
    grad_bdown = jnp.sum(grad_ffn.astype(jnp.float32), 0)
    grad_wdown = cross_dot(act_low, grad_ffn)
    (grad_act,) = gelu_back(back_dot(grad_ffn, w_down))
    grad_pre = grad_act.astype(jnp.bfloat16)
    grad_bup = jnp.sum(grad_pre.astype(jnp.float32), 0)
    grad_wup = cross_dot(hid_low, grad_pre)
    grad_h1 = grad_r2 + back_dot(grad_pre, w_up)
    grad_r1, grad_gain1, grad_bias1 = ln1_back(grad_h1)
    grad_branch = grad_r1.astype(jnp.bfloat16)
    grad_bout = jnp.sum(grad_branch.astype(jnp.float32), 0)
    grad_wout = cross_dot(att_low, grad_branch)
    grad_att = back_dot(grad_branch, w_out).reshape(tok_count, H, DH)
    grad_num = (grad_att / denom_sum[:, :, None]).reshape(tok_count, D).astype(jnp.bfloat16)
    grad_den = (-jnp.sum(grad_att * numer_h, -1) / (denom_sum * denom_sum)).astype(jnp.bfloat16)
    group_num, group_den = (
        lax.all_gather(grad_num, "feat", axis=0, tiled=True),
        lax.all_gather(grad_den, "feat", axis=0, tiled=True),
    )
    group_num_h = group_num.reshape(group_rows, H, DH)
    grad_kv_part = jnp.einsum(
        "gha,ghe->hae", wide_q, group_num_h, preferred_element_type=jnp.float32
    )
    grad_z_part = jnp.einsum("gha,gh->ha", wide_q, group_den, preferred_element_type=jnp.float32)
    grad_kv = grad_kv_part.astype(jnp.bfloat16)
    grad_z = grad_z_part.astype(jnp.bfloat16)
    wide_gq = jnp.einsum("ghe,hae->gha", group_num_h, kv_low, preferred_element_type=jnp.float32)
    wide_gq = wide_gq + group_den[:, :, None].astype(jnp.float32) * z_low[None].astype(jnp.float32)
    grad_arg_q = (fold_segments(wide_gq, member_f) * phi_q).astype(jnp.bfloat16)
    wide_gk = jnp.einsum(
        "ghe,hae->gha", value_h, grad_kv, preferred_element_type=jnp.float32
    ) + grad_z[None].astype(jnp.float32)
    grad_arg_k = (fold_segments(wide_gk, member_f) * phi_k).astype(jnp.bfloat16)
    grad_value = jnp.einsum("gha,hae->ghe", wide_k, grad_kv, preferred_element_type=jnp.float32)
    grad_query = feature_back(query_h, feat_proj, grad_arg_q)
    grad_key = feature_back(key_h, feat_proj, grad_arg_k)
    grad_group = jnp.concatenate(
        [
            grad_query.reshape(group_rows, D),
            grad_key.reshape(group_rows, D),
            grad_value.reshape(group_rows, D),
        ],
        1,
    )
    grad_qkv = lax.psum_scatter(
        grad_group.astype(jnp.bfloat16), "feat", scatter_dimension=0, tiled=True
    )
    grad_bqkv = jnp.sum(grad_qkv.astype(jnp.float32), 0)
    grad_wqkv = cross_dot(tokens, grad_qkv)
    grad_tokens = grad_r1 + back_dot(grad_qkv, w_qkv)
    grads_now = (
        grad_wqkv,
        grad_bqkv,
        grad_wout,
        grad_bout,
        grad_gain1,
        grad_bias1,
        grad_wup,
        grad_bup,
        grad_wdown,
        grad_bdown,
        grad_gain2,
        grad_bias2,
    )
    return (result.astype(jnp.bfloat16), grad_tokens, grads_now)


def on_device(
    tokens_in,
    out_cotangent,
    segment_ids,
    feature_proj,
    w_qkv,
    b_qkv,
    w_out,
    b_out,
    ln1_gain,
    ln1_bias,
    w_up,
    b_up,
    w_down,
    b_down,
    ln2_gain,
    ln2_bias,
):
    totals = None
    outputs = []
    grad_inputs = []
    for micro_idx in range(MICRO):
        gathered = fetch_weights(
            w_qkv,
            b_qkv,
            w_out,
            b_out,
            ln1_gain,
            ln1_bias,
            w_up,
            b_up,
            w_down,
            b_down,
            ln2_gain,
            ln2_bias,
        )
        result, grad_tokens, grads_now = micro_step(
            tokens_in[micro_idx],
            out_cotangent[micro_idx],
            segment_ids[micro_idx],
            feature_proj,
            gathered,
        )
        outputs.append(result)
        grad_inputs.append(grad_tokens)
        totals = grads_now if totals is None else jax.tree.map(jnp.add, totals, grads_now)
    (
        grad_wqkv,
        grad_bqkv,
        grad_wout,
        grad_bout,
        grad_gain1,
        grad_bias1,
        grad_wup,
        grad_bup,
        grad_wdown,
        grad_bdown,
        grad_gain2,
        grad_bias2,
    ) = totals
    summed = (
        lax.psum_scatter(grad_wqkv, ("dp", "feat"), scatter_dimension=0, tiled=True),
        lax.psum_scatter(grad_bqkv, ("dp", "feat"), scatter_dimension=0, tiled=True),
        lax.psum_scatter(grad_wout, ("dp", "feat"), scatter_dimension=0, tiled=True),
        lax.psum_scatter(grad_bout, ("dp", "feat"), scatter_dimension=0, tiled=True),
        lax.psum_scatter(grad_gain1, ("dp", "feat"), scatter_dimension=0, tiled=True),
        lax.psum_scatter(grad_bias1, ("dp", "feat"), scatter_dimension=0, tiled=True),
        lax.psum_scatter(grad_wup, ("dp", "feat"), scatter_dimension=0, tiled=True),
        lax.psum_scatter(grad_bup, ("dp", "feat"), scatter_dimension=0, tiled=True),
        lax.psum_scatter(grad_wdown, ("dp", "feat"), scatter_dimension=0, tiled=True),
        lax.psum_scatter(grad_bdown, ("dp", "feat"), scatter_dimension=0, tiled=True),
        lax.psum_scatter(grad_gain2, ("dp", "feat"), scatter_dimension=0, tiled=True),
        lax.psum_scatter(grad_bias2, ("dp", "feat"), scatter_dimension=0, tiled=True),
    )
    return (
        jnp.stack(outputs),
        jnp.stack(grad_inputs),
        summed[0],
        summed[1],
        summed[2],
        summed[3],
        summed[4],
        summed[5],
        summed[6],
        summed[7],
        summed[8],
        summed[9],
        summed[10],
        summed[11],
    )


NZ, NY, NC, NX = 4, 2, 2, 2
N_DEV = NZ * NY * NC * NX
MESH_ID = pl.DeviceIdType.MESH
BF = jnp.bfloat16
F32 = jnp.float32
SHARE = MICRO // NX
GRID = (NZ, NY, NC)
ALL = slice(None)


def fits(mesh):
    return mesh.shape["dp"] == NZ * NY * NC and mesh.shape["feat"] == NX


class Place:
    def __init__(self):
        i = lax.axis_index("dp")
        self.z, self.y, self.c, self.x = i // (NY * NC), (i // NC) % NY, i % NC, lax.axis_index("feat")
        self.sibling = self.device(c=1 - self.c)
        self.over = {"x": self.device(x=1 - self.x), "y": self.device(y=1 - self.y)}
        self.z_of = [lax.rem(self.z + k, NZ) for k in (1, 2, 3)]
        self.over_z = [self.device(z=z) for z in self.z_of]

    def device(self, **other):
        z, y, c, x = (other.get(n, getattr(self, n)) for n in "zycx")
        return (z * (NY * NC) + y * NC + c, x)

    def meet(self):
        barrier = pltpu.get_barrier_semaphore()
        peers = [self.sibling, self.over["x"], self.over["y"]] + self.over_z
        for peer in peers:
            pl.semaphore_signal(barrier, inc=1, device_id=peer, device_id_type=MESH_ID)
        pl.semaphore_wait(barrier, len(peers))

    def per_class(self, orders, act):
        if orders[0] == orders[1]:
            act(orders[0])
            return
        for c in range(NC):

            @pl.when(self.c == c)
            def _(order=orders[c]):
                act(order)

    def rows(self, grid, x):
        share = grid.shape[3] // NX
        return pl.ds(pl.multiple_of(x * share, 8), share)

    def view(self, grid, cols, spread=(), **at):
        index = [ALL if n in spread else at.get(n, getattr(self, n)) for n in "zyc"]
        rows = ALL if "x" in spread else self.rows(grid, at.get("x", self.x))
        return grid.at[(*index, rows, cols)]


class Copies:
    def __init__(self, send_sems, recv_sems):
        self.send_sems, self.recv_sems = send_sems, recv_sems

    def copy(self, slot, src, dst, peer):
        return pltpu.make_async_remote_copy(
            src_ref=src, dst_ref=dst, send_sem=self.send_sems.at[slot], recv_sem=self.recv_sems.at[slot],
            device_id=peer, device_id_type=MESH_ID,
        )


class Gather(Copies):
    def __init__(self, here, part, src, grid, cols, orders, sems):
        super().__init__(sems[0].at[part], sems[1].at[part])
        self.here, self.grid, self.cols, self.orders = here, grid, cols, orders
        self.src = src.at[ALL, cols]
        self.local = pltpu.make_async_copy(self.src, here.view(grid, cols), sems[2].at[part])

    def phase(self, order, n):
        here, dim = self.here, order[n]
        mine = here.view(self.grid, self.cols, order[:n])
        src = self.src if n == 0 else mine
        if dim == "z":
            return [self.copy(n + k, src, mine, peer) for k, peer in enumerate(here.over_z)]
        slot = n if order.index("z") > n else n + 2
        return [self.copy(slot, src, mine, here.over[dim])]

    def to_sibling(self):
        mine = self.here.view(self.grid, self.cols, "zyx")
        return self.copy(5, mine, mine, self.here.sibling)

    def step(self, n):
        if n == 0:
            self.local.start()
            self.here.per_class(self.orders, lambda order: [c.start() for c in self.phase(order, 0)])
        elif n < 4:
            self.here.per_class(self.orders, lambda order: [c.wait_recv() for c in self.phase(order, n - 1)])
            if n == 1:
                self.local.wait()
            if n < 3:
                self.here.per_class(self.orders, lambda order: [c.start() for c in self.phase(order, n)])
            else:
                self.to_sibling().start()
        else:
            self.to_sibling().wait_recv()

    def drain(self):
        for n in range(3):
            self.here.per_class(self.orders, lambda order, n=n: [c.wait_send() for c in self.phase(order, n)])
        self.to_sibling().wait_send()


class Reduce(Copies):
    def __init__(self, here, part, grid, cols, orders, got, stage, out, sems):
        super().__init__(sems[0].at[part], sems[1].at[part])
        self.here, self.grid, self.cols, self.orders = here, grid, cols, orders
        self.got, self.stage = got, stage
        self.out = pltpu.make_async_copy(stage, out, sems[2].at[part])

    def from_sibling(self):
        here = self.here
        theirs = here.view(self.grid, self.cols, "zyx", c=1 - here.c)
        return self.copy(0, theirs, self.got[0][0], here.sibling)

    def received(self, order, n):
        return self.got[n][self.orders.index(order) % len(self.got[n])]

    def phase(self, order, n):
        here, dim, rest = self.here, order[n], order[n + 1 :]
        got = self.received(order, n + 1)
        if dim == "z":
            return [
                self.copy(1 + n + k, here.view(self.grid, self.cols, rest, z=z), got.at[k], peer)
                for k, (z, peer) in enumerate(zip(here.z_of, here.over_z, strict=True))
            ]
        slot = 1 + n if order.index("z") > n else 3 + n
        place = {dim: 1 - getattr(here, dim)}
        return [self.copy(slot, here.view(self.grid, self.cols, rest, **place), got, here.over[dim])]

    def spot(self, spread, q):
        here, index, inner = self.here, {}, []
        if "y" in spread:
            index["y"] = q % NY
            q = q // NY
        if "z" in spread:
            index["z"] = q
        inner = tuple(index[n] for n in "zy" if n in index)
        rows = ALL if "x" in spread else here.rows(self.grid, here.x)
        return tuple(index.get(n, getattr(here, n)) for n in "zyc") + (rows, self.cols), inner

    def add(self, got, spread, copies=1):
        def one(q):
            index, inner = self.spot(spread, q)
            if copies == 1:
                self.grid[index] = self.grid[index] + got[inner + (ALL, ALL)]
                return
            total = self.grid[index].astype(F32)
            for k in range(copies):
                total = total + got[(k,) + inner + (ALL, ALL)].astype(F32)
            self.grid[index] = total.astype(self.grid.dtype)

        count = (NZ if "z" in spread else 1) * (NY if "y" in spread else 1)
        blocks_of(count, one) if count > 1 else one(0)

    def finish(self, got, copies):
        index, _ = self.spot((), 0)
        total = self.grid[index].astype(F32)
        for k in range(copies):
            total = total + got[((k,) if copies > 1 else ()) + (ALL, ALL)].astype(F32)
        self.stage[...] = total

    def step(self, n):
        if n == 0:
            self.from_sibling().start()
            return
        if n == 1:
            self.from_sibling().wait_recv()
            self.add(self.got[0][0], "zyx")
        else:

            def take(order):
                for c in self.phase(order, n - 2):
                    c.wait_recv()
                copies = 3 if order[n - 2] == "z" else 1
                got = self.received(order, n - 1)
                if n < 4:
                    self.add(got, order[n - 1 :], copies)
                else:
                    self.finish(got, copies)

            self.here.per_class(self.orders, take)
        if n < 4:
            self.here.per_class(self.orders, lambda order: [c.start() for c in self.phase(order, n - 1)])
        else:
            self.out.start()

    def drain(self):
        self.from_sibling().wait_send()
        for n in range(3):
            self.here.per_class(self.orders, lambda order, n=n: [c.wait_send() for c in self.phase(order, n)])
        self.out.wait()


def got_shapes(orders, rows, width):
    first, second = (order_shapes(order, rows, width) for order in orders)
    return [(a,) if a == b else (a, b) for a, b in zip(first, second, strict=True)]


def order_shapes(order, rows, width):

    def block(spread):
        return tuple(dict(z=NZ, y=NY)[n] for n in "zy" if n in spread) + (rows * (NX if "x" in spread else 1), width)

    shapes = [block("zyx")]
    for n, dim in enumerate(order):
        shapes.append(((NZ - 1,) if dim == "z" else ()) + block(order[n + 1 :]))
    return shapes


def blocks_of(count, body, then=()):
    def step(j, carry):
        body(j)
        for at in sorted({at for at, _ in then}):

            @pl.when(j == at)
            def _(at=at):
                for when, act in then:
                    if when == at:
                        act()

        return carry

    lax.fori_loop(0, count, step, 0)


ROWS = 512
BLK = 256
PAIRS = D // 128
FF = 4 * D
WIDE = 2 * FEATS
SCALE = DH ** (-0.25)


def dot(a, b, ca=1, cb=0):
    return lax.dot_general(a, b, (((ca,), (cb,)), ((), ())), preferred_element_type=F32)


def half_masks(width):
    lane = lax.broadcasted_iota(jnp.int32, (1, width), 1) % 128
    first = (lane < DH).astype(F32)
    return first.astype(BF), (1.0 - first).astype(BF)


def lanes(j, width):
    return pl.ds(pl.multiple_of(j * width, width), width)


class Work:
    def __init__(self, refs):
        self.__dict__.update(refs)

    def setup(self, proj, seg_rows):
        row = lax.broadcasted_iota(jnp.int32, (DH, 128), 0)
        col = lax.broadcasted_iota(jnp.int32, (DH, 128), 1)
        for h in range(2):
            place_in = (col == row + h * DH).astype(BF)
            for n in range(NX):
                self.table[pl.ds(h * FEATS + n * 128, 128), 0:128] = dot(proj[n], place_in, 0, 0).astype(BF)
        feat = lax.broadcasted_iota(jnp.int32, (WIDE, 128), 0) // FEATS
        half = lax.broadcasted_iota(jnp.int32, (WIDE, 128), 1) // DH
        same = (feat == half).astype(F32).astype(BF)
        self.table[:, 128:256] = same
        self.flip[D:, :] = jnp.ones((16, ROWS), BF)
        for b in range(2):
            across = jnp.broadcast_to(seg_rows[b], (BLK, BLK))
            self.mask[b] = (across == jnp.transpose(across)).astype(F32)

    def features(self, rows):
        wide = rows.astype(F32)
        squares = wide * wide
        high = squares.astype(BF)
        low = (squares - high.astype(F32)).astype(BF)
        same = self.table[:, 128:256]
        norm = dot(high, same, 1, 1) + dot(low, same, 1, 1)
        arg = SCALE * dot(rows, self.table[:, 0:128], 1, 1) - (0.5 * SCALE * SCALE) * norm
        return (jnp.exp(arg) * FEATS ** (-0.5)).astype(BF)

    def qkv_block(self, j):
        col = lanes(j, 256)
        full = dot(self.x[...], self.w_qkv[:, col]) + self.b_qkv[:, col]
        self.qkv[:, col] = full.astype(BF)

    def pair(self, i):
        b, p = i // PAIRS, i % PAIRS
        rows = pl.ds(pl.multiple_of(b * BLK, BLK), BLK)
        cols = [pl.ds(pl.multiple_of(n * D + p * 128, 128), 128) for n in range(3)]
        return b, rows, cols

    def attend(self, i):
        b, rows, cols = self.pair(i)
        mask = self.mask[b]
        m0, m1 = half_masks(128)
        phi_q = self.features(self.qkv[rows, cols[0]])
        phi_k = self.features(self.qkv[rows, cols[1]])
        self.phi_q[i] = phi_q
        self.phi_k[i] = phi_k
        v = self.qkv[rows, cols[2]]
        one = jnp.ones((BLK, 128), BF)
        res = None
        for h, m in enumerate((m0, m1)):
            part = slice(h * FEATS, (h + 1) * FEATS)
            score = (dot(phi_q[:, part], phi_k[:, part], 1, 1) * mask).astype(BF)
            term = dot(score, jnp.concatenate([v * m, one * m], 1))
            res = term if res is None else res + term
        inv = 1.0 / res[:, 128:]
        self.inv[rows, cols[0]] = inv
        self.att[rows, cols[0]] = (res[:, :128] * inv).astype(BF)

    def normalize(self, r):
        center = r - jnp.mean(r, -1, keepdims=True)
        scale = lax.rsqrt(jnp.mean(center * center, -1, keepdims=True) + EPSILON)
        return center * scale, scale

    def normalize_back(self, dy, n, scale, gain):
        g = dy * gain
        return (g - jnp.mean(g, -1, keepdims=True) - n * jnp.mean(g * n, -1, keepdims=True)) * scale

    def branch(self):
        for j in range(3):
            col = lanes(j, 256)
            self.n1[:, col] = dot(self.att[...], self.w_out[:, col]) + self.b_out[:, col] + self.x[:, col].astype(F32)

        def rows_of(j):
            row = pl.ds(pl.multiple_of(j * 64, 64), 64)
            n1, s1 = self.normalize(self.n1[row, :])
            self.n1[row, :] = n1
            self.s1[row, :] = s1
            self.h1[row, :] = (n1 * self.g1[...] + self.b1[...]).astype(BF)

        blocks_of(ROWS // 64, rows_of)

    def up_block(self, j):
        col = lanes(j, 256)
        for r in range(0, ROWS, 128):
            row = slice(r, r + 128)
            a = dot(self.h1[row, :], self.w_up[:, col]) + self.b_up[:, col]
            cdf = 0.5 * (1.0 + lax.erf(a * 2**-0.5))
            self.z[row, col] = (a * cdf).astype(BF)
            self.slope[row, col] = (cdf + a * jnp.exp(-0.5 * a * a) * (0.5 / 3.141592653589793) ** 0.5).astype(BF)

    def down_block(self, j):
        col = lanes(j, 256)
        back = self.n1[:, col] * self.g1[:, col] + self.b1[:, col]
        self.dr[:, col] = dot(self.z[...], self.w_down[:, col]) + self.b_down[:, col] + back

    def second_norm(self):
        for ref in (self.d_g2, self.d_b2, self.d_b_down):
            ref[...] = jnp.zeros_like(ref)

        def rows_of(j):
            row = pl.ds(pl.multiple_of(j * 64, 64), 64)
            n2, s2 = self.normalize(self.dr[row, :])
            self.y[row, :] = (n2 * self.g2[...] + self.b2[...]).astype(BF)
            dy = self.cot[row, :].astype(F32)
            dr2 = self.normalize_back(dy, n2, s2, self.g2[...])
            self.dr[row, :] = dr2
            df = dr2.astype(BF)
            self.df[row, :] = df
            self.d_g2[...] += jnp.sum(dy * n2, 0, keepdims=True)
            self.d_b2[...] += jnp.sum(dy, 0, keepdims=True)
            self.d_b_down[...] += jnp.sum(df.astype(F32), 0, keepdims=True)

        blocks_of(ROWS // 64, rows_of)

    def down_back(self, j):
        col = lanes(j, 256)
        dz = dot(self.df[...], self.w_down[col, :], 1, 1)
        da = (dz * self.slope[:, col].astype(F32)).astype(BF)
        self.slope[:, col] = da

    def down_grad(self, into, part, j):
        col = lanes(j, D)
        into[col, :] = dot(self.z[:, col], self.df[:, part], 0, 0).astype(BF)

    def up_back(self, j):
        col = lanes(j, 256)
        self.dr[:, col] += dot(self.slope[...], self.w_up[col, :], 1, 1)

    def turn(self, name):
        self.flip[0:D, :] = jnp.transpose(getattr(self, name)[...])

    def weight_grad(self, weight, bias, col, grad):
        full = dot(self.flip[...], grad)
        weight[:, col] = full[0:D].astype(BF)
        bias[:, col] = full[D : D + 1]

    def up_grad(self, j):
        col = lanes(j, 256)
        self.weight_grad(self.w_up, self.d_b_up, col, self.slope[:, col])

    def first_norm_back(self):
        for ref in (self.d_g1, self.d_b1):
            ref[...] = jnp.zeros_like(ref)

        def rows_of(j):
            row = pl.ds(pl.multiple_of(j * 64, 64), 64)
            dh1, n1 = self.dr[row, :], self.n1[row, :]
            dr1 = self.normalize_back(dh1, n1, self.s1[row, :], self.g1[...])
            self.dr[row, :] = dr1
            self.df[row, :] = dr1.astype(BF)
            self.d_g1[...] += jnp.sum(dh1 * n1, 0, keepdims=True)
            self.d_b1[...] += jnp.sum(dh1, 0, keepdims=True)

        blocks_of(ROWS // 64, rows_of)

    def att_back(self, j):
        head_r = lax.broadcasted_iota(jnp.int32, (256, 256), 0) // DH
        head_c = lax.broadcasted_iota(jnp.int32, (256, 256), 1) // DH
        same = (head_r == head_c).astype(F32).astype(BF)
        col = lanes(j, 256)
        datt = dot(self.df[...], self.w_out[col, :], 1, 1)
        inv = self.inv[:, col]
        self.cot[:, col] = (datt * inv).astype(BF)
        prod = datt * self.att[:, col].astype(F32)
        high = prod.astype(BF)
        low = (prod - high.astype(F32)).astype(BF)
        total = dot(high, same) + dot(low, same)
        self.h1[:, col] = (-total * inv).astype(BF)

    def out_grad(self, j):
        col = lanes(j, 256)
        self.weight_grad(self.w_out, self.d_b_out, col, self.df[:, col])

    def attend_back(self, i):
        b, rows, cols = self.pair(i)
        mask = self.mask[b]
        m0, m1 = half_masks(256)
        q, k, v = (self.qkv[rows, c] for c in cols)
        dnum, dden = self.cot[rows, cols[0]], self.h1[rows, cols[0]]
        left = jnp.concatenate([dnum, dden * (1.0 / DH)], 1)
        right = jnp.concatenate([v, jnp.ones((BLK, 128), BF)], 1)
        back_q, back_k, dv = None, None, None
        for h, m in enumerate((m0, m1)):
            part = slice(h * FEATS, (h + 1) * FEATS)
            phi_q, phi_k = self.phi_q[i, :, part], self.phi_k[i, :, part]
            mine = left * m
            dscore = (dot(mine, right, 1, 1) * mask).astype(BF)
            flipped = (dot(right, mine, 1, 1) * mask).astype(BF)
            darg_q = (dot(dscore, phi_k) * phi_q.astype(F32)).astype(BF)
            darg_k = (dot(flipped, phi_q) * phi_k.astype(F32)).astype(BF)
            score = (dot(phi_k, phi_q, 1, 1) * mask).astype(BF)
            table = self.table[part, :]
            terms = dot(darg_q, table), dot(darg_k, table), dot(score, mine[:, :128])
            if h == 0:
                back_q, back_k, dv = terms
            else:
                back_q, back_k, dv = back_q + terms[0], back_k + terms[1], dv + terms[2]
        for n, (rows_in, back) in enumerate(((q, back_q), (k, back_k))):
            grad = SCALE * back[:, :128] - (SCALE * SCALE) * rows_in.astype(F32) * back[:, 128:]
            self.qkv[rows, cols[n]] = grad.astype(BF)
        self.qkv[rows, cols[2]] = dv.astype(BF)

    def tokens_back(self, j):
        col = lanes(j, 256)
        self.dr[:, col] += dot(self.qkv[...], self.w_qkv[col, :], 1, 1)

    def qkv_grad(self, j):
        col = lanes(j, 256)
        self.weight_grad(self.w_qkv, self.d_b_qkv, col, self.qkv[:, col])


VECTORS = ("b_qkv", "b_out", "g1", "b1", "b_up", "b_down", "g2", "b2")
WIDTHS = (3 * D, D, D, D, FF, D, D, D)
SPACE = (
    ("qkv", (ROWS, 3 * D), BF), ("phi_q", (2 * PAIRS, BLK, WIDE), BF), ("phi_k", (2 * PAIRS, BLK, WIDE), BF),
    ("att", (ROWS, D), BF), ("inv", (ROWS, D), F32), ("n1", (ROWS, D), F32), ("s1", (ROWS, 1), F32),
    ("h1", (ROWS, D), BF), ("z", (ROWS, FF), BF), ("slope", (ROWS, FF), BF), ("dr", (ROWS, D), F32),
    ("df", (ROWS, D), BF), ("flip", (D + 16, ROWS), BF),
    ("table", (WIDE, 256), BF), ("mask", (2, BLK, BLK), F32),
)


GATHER_PARTS = {
    "small": ("small", 0, 128, ("zyx", "zxy")),
    "q": ("w_qkv", 0, 768, ("zyx", "zyx")),
    "k": ("w_qkv", 768, 768, ("zxy", "zxy")),
    "v": ("w_qkv", 1536, 768, ("xzy", "xzy")),
    "out": ("w_out", 0, 768, ("zyx", "zyx")),
    "up0": ("w_up", 0, 768, ("zyx", "zxy")),
    "up1": ("w_up", 768, 768, ("xzy", "xzy")),
    "up2": ("w_up", 1536, 768, ("zyx", "zxy")),
    "up3": ("w_up", 2304, 768, ("xzy", "yzx")),
    "dn0": ("w_down", 0, 256, ("zyx", "zxy")),
    "dn1": ("w_down", 256, 256, ("xyz", "yxz")),
    "dn2": ("w_down", 512, 256, ("zyx", "zxy")),
}
REDUCE_PARTS = {
    "small": ("small", 0, 128, ("xyz", "xyz"), "small", 0),
    "q": ("w_qkv", 0, 768, ("xyz", "xyz"), "w_qkv", 0),
    "k": ("w_qkv", 768, 768, ("yzx", "yzx"), "w_qkv", 768),
    "v": ("w_qkv", 1536, 768, ("xyz", "xyz"), "w_qkv", 1536),
    "out": ("w_out", 0, 768, ("yxz", "yxz"), "w_out", 0),
    "up0": ("w_up", 0, 1024, ("yxz", "yxz"), "w_up", 0),
    "up1": ("w_up", 1024, 1024, ("yxz", "yxz"), "w_up", 1024),
    "up2": ("w_up", 2048, 1024, ("xyz", "xyz"), "w_up", 2048),
    "dn0": ("spare", 0, 256, ("yxz", "yxz"), "w_down", 0),
    "dn1": ("w_down", 256, 256, ("xzy", "xzy"), "w_down", 256),
    "dn2": ("w_down", 512, 256, ("zyx", "zyx"), "w_down", 512),
}
FORWARD = (
    "proj!", "small0", "k0", "v0", "q0", "out0", "tok!", "up10", "small1", "proj?", "setup", "v1", "k1", "q1", "up20",
    "up30", "out1", "dn10", "up11", "small2", "q2", "k2", "cot!", "up31", "out2", "dn11", "small3", "v2", "small4",
    "spread", "up21", "q3", "k3", "q4", "tok?", "qkv*3", "k4", "up00", "qkv*2", "up12", "qkv", "v3", "v4", "dn00",
    "qkv", "up32", "qkv*2", "att*2", "dn20", "att", "out3", "up01", "att", "up13", "dn12", "att", "out4", "up22",
    "att", "up14", "dn01", "att", "up33", "att*2", "up02", "up34", "dn21", "att*2", "up23", "att", "branch", "up24",
    "dn02", "up03", "dn22", "up04", "upb*8", "dn03", "upb*4", "dn13", "dn04", "down", "dn23", "dn14", "down", "dn24",
    "down", "cot?", "ln2",
)
BACKWARD = (
    "y!", "gdn0*4", "dn00", "dz*7", "dn01", "dz*5", "gdn1*4", "dn10", "gdn2*4", "dn20", "uback", "dn11", "uback",
    "dn21", "uback", "dn02", "flip0", "gup*4", "up00", "gup*4", "up10", "gup*3", "up01", "gup", "up20", "nback",
    "up11", "dn12", "datt", "up21", "datt*2", "dn03", "flip1", "gout*3", "out0", "attb*3", "out1", "up02", "attb",
    "dn22", "attb*2", "up22", "attb*4", "up12", "up03", "attb", "dn13", "attb", "tback*3", "lower", "up13", "dn04",
    "out2", "flip2", "gqkv*3", "q0", "gqkv", "dn23", "gqkv*2", "k0", "gqkv*2", "q1", "out3", "up04", "gqkv", "v0",
    "k1", "dn24", "up23", "collect", "small0", "v1", "up14", "dn14", "small1", "out4", "q2", "k2", "up24", "q3",
    "grad!", "v2", "small2", "k3", "v3", "small3", "q4", "k4", "v4", "small4",
)
WEIGHTS = (("w_qkv", (D, 3 * D)), ("w_out", (D, D)), ("w_up", (D, FF)), ("w_down", (FF, D)))
TILE = (8, 128)
SPARE = 256
HALF = (SHARE, NX, ROWS // SHARE // NX, D)


def shard_rows(weight):
    return TILE[0] if weight == "small" else dict(WEIGHTS)[weight][0] // N_DEV


class Swap:
    def __init__(self, here, n, theirs, target, mine, home, sems):
        self.there = pltpu.make_async_remote_copy(
            src_ref=theirs, dst_ref=target, send_sem=sems[0].at[n], recv_sem=sems[1].at[n],
            device_id=here.over["x"], device_id_type=MESH_ID,
        )
        self.here = None if home is None else pltpu.make_async_copy(mine, home, sems[2].at[n])

    def start(self):
        self.there.start()
        if self.here is not None:
            self.here.start()

    def arrive(self):
        self.there.wait_recv()
        if self.here is not None:
            self.here.wait()


def one_hot(width, count):
    at = lax.broadcasted_iota(jnp.int32, (1, count), 1).astype(F32)
    owner = jnp.floor((at + 0.5) * (1.0 / width))
    lane = at - owner * width
    lanes_hot = (lax.broadcasted_iota(jnp.int32, (128, count), 0).astype(F32) == lane).astype(F32).astype(BF)
    owner_hot = (lax.broadcasted_iota(jnp.int32, (N_DEV, count), 0).astype(F32) == owner).astype(F32)
    return lanes_hot, owner_hot


def spread_small(tiles, vectors):
    for width in sorted({v.shape[1] // N_DEV for v in vectors}):
        hot, owner = one_hot(width, width * N_DEV)
        for n, vector in enumerate(vectors):
            if vector.shape[1] == width * N_DEV:
                rows = tiles[pl.ds(n, N_DEV, stride=TILE[0]), :].astype(BF)
                vector[...] = jnp.sum(dot(rows, hot) * owner, 0, keepdims=True)


def collect_small(tiles, vectors):
    for width in sorted({v.shape[1] // N_DEV for v in vectors}):
        hot, owner = one_hot(width, width * N_DEV)
        for n, vector in enumerate(vectors):
            if vector.shape[1] == width * N_DEV:
                full = owner * vector[...]
                high = full.astype(BF)
                low = (full - high.astype(F32)).astype(BF)
                tiles[pl.ds(n, N_DEV, stride=TILE[0]), :] = dot(high, hot, 1, 1) + dot(low, hot, 1, 1)


def layer_kernel(*refs):
    it = iter(refs)
    tok, cot = next(it), next(it)
    local = {w: next(it) for w, _ in WEIGHTS}
    own_vectors = [next(it) for _ in VECTORS]
    proj_in, seg = next(it), next(it)
    block_out, grad_tok = next(it), next(it)
    outs = {w: next(it) for w, _ in WEIGHTS}
    outs["small"] = next(it)
    ref = {n: next(it) for n, _ in WEIGHTS}
    ref.update({n: next(it) for n, _, _ in SPACE})
    work = Work(ref)
    got = {
        p: [tuple(next(it) for _ in shapes) for shapes in got_shapes(orders, shard_rows(w), width)]
        for p, (_, _, width, orders, w, _) in REDUCE_PARTS.items()
    }
    stage = {p: next(it) for p in REDUCE_PARTS}
    gather_sems = [next(it) for _ in range(3)]
    reduce_sems = [next(it) for _ in range(3)]
    swap_sems = [next(it) for _ in range(3)]
    out_sems, vector_sems = next(it), next(it)

    vector_loads = [pltpu.make_async_copy(v, ref["in_" + n], vector_sems.at[k]) for k, (n, v) in enumerate(zip(VECTORS, own_vectors))]
    for load in vector_loads:
        load.start()
    here = Place()
    here.meet()
    local["small"] = ref["tile"]
    ref["tile"][...] = jnp.zeros(TILE, F32)
    for k, (n, load) in enumerate(zip(VECTORS, vector_loads)):
        load.wait()
        width = ref["in_" + n].shape[0]
        ref["tile"][k : k + 1, 0:width] = ref["in_" + n][...].astype(F32).reshape(1, width)
    x = here.x
    grids = {w: ref[w].reshape(GRID + (NX * shard_rows(w), ref[w].shape[1])) for w, _ in WEIGHTS}
    grids["spare"] = ref["spare"].reshape(GRID + (NX * shard_rows("w_down"), SPARE))
    grids["small"] = ref["tiles"].reshape(GRID + (NX * TILE[0], TILE[1]))
    into, back = {}, {}
    for n, (p, (w, first, width, orders)) in enumerate(GATHER_PARTS.items()):
        into[p] = Gather(here, n, local[w], grids[w], pl.ds(first, width), orders, gather_sems)
    for n, (p, (a, first, width, orders, w, at)) in enumerate(REDUCE_PARTS.items()):
        out = outs[w].at[ALL, pl.ds(at, width)]
        back[p] = Reduce(here, n, grids[a], pl.ds(first, width), orders, got[p], stage[p], out, reduce_sems)

    def halves(r):
        return r.reshape(HALF)

    grad_low, grad_high = halves(work.df).at[0], halves(work.inv).at[0]
    own, other = pl.ds(x * SHARE, SHARE), pl.ds((1 - x) * SHARE, SHARE)
    swap = {
        "tok": Swap(here, 0, tok.at[other], halves(work.x).at[:, x], tok.at[own], halves(work.x).at[:, x], swap_sems),
        "cot": Swap(here, 1, cot.at[other], halves(work.cot).at[:, x], cot.at[own], halves(work.cot).at[:, x], swap_sems),
        "proj": Swap(here, 2, proj_in, work.proj.at[x], proj_in, work.proj.at[x], swap_sems),
        "y": Swap(here, 3, halves(work.y).at[:, 1 - x], block_out.at[own], halves(work.y).at[:, x], block_out.at[own], swap_sems),
        "grad": Swap(here, 4, grad_low, work.grad_got, halves(work.dr).at[:, x], grad_tok.at[own], swap_sems),
    }

    vectors = [getattr(work, n) for n in VECTORS]
    totals = [getattr(work, "d_" + n) for n in VECTORS]

    def setup():
        work.setup(work.proj, [seg[pl.ds(SHARE * x + b, 1), :].astype(F32) for b in range(SHARE)])

    def lower():
        def block(b):
            grad_low[b] = halves(work.dr)[b, 1 - x].astype(BF)

        blocks_of(SHARE, block)

    stages = {
        "setup": (1, setup),
        "spread": (1, lambda: spread_small(ref["tiles"], vectors)),
        "qkv": (9, work.qkv_block),
        "att": (2 * PAIRS, work.attend),
        "branch": (1, work.branch),
        "upb": (12, work.up_block),
        "down": (3, work.down_block),
        "ln2": (1, work.second_norm),
        "dz": (12, work.down_back),
        "uback": (3, work.up_back),
        "flip0": (1, partial(work.turn, "h1")),
        "gup": (12, work.up_grad),
        "nback": (1, work.first_norm_back),
        "datt": (3, work.att_back),
        "flip1": (1, partial(work.turn, "att")),
        "gout": (3, work.out_grad),
        "attb": (2 * PAIRS, work.attend_back),
        "tback": (3, work.tokens_back),
        "lower": (1, lower),
        "flip2": (1, partial(work.turn, "x")),
        "gqkv": (9, work.qkv_grad),
        "collect": (1, lambda: collect_small(ref["tiles"], totals)),
    }
    for p, (a, first, width, _, w, at) in REDUCE_PARTS.items():
        if w == "w_down":
            into_part = ref[a].at[ALL, pl.ds(first, width)]
            stages["g" + p] = (4, partial(work.down_grad, into_part, slice(at, at + width)))

    def act(steps, token):
        if token[-1] == "!":
            swap[token[:-1]].start()
        elif token[-1] == "?":
            swap[token[:-1]].arrive()
        else:
            steps[token[:-1]].step(int(token[-1]))

    def play(tokens, steps):
        tokens = [t.split("*") for t in tokens]
        tokens = [(t[0], int(t[1]) if len(t) > 1 else 1) for t in tokens]
        while tokens:
            name, _ = tokens[0]
            if name not in stages:
                act(steps, name)
                tokens.pop(0)
                continue
            count, body = stages[name]
            n, then = 0, []
            while n < count:
                token, times = tokens.pop(0)
                if token == name:
                    n += times
                else:
                    then.append((n - 1, partial(act, steps, token)))
            if count > 1:
                blocks_of(count, body, then)
            else:
                body()

    play(FORWARD, into)
    for part in into.values():
        part.drain()
    play(BACKWARD, back)
    swap["grad"].arrive()

    def lift(b):
        grad_high[b] = work.grad_got[b].astype(F32)

    blocks_of(SHARE, lift)
    last = pltpu.make_async_copy(grad_high, grad_tok.at[other], out_sems.at[0])
    last.start()
    swap["y"].arrive()
    for each in swap.values():
        each.there.wait_send()
    for part in back.values():
        part.drain()
    last.wait()


QUARTER = (SHARE, ROWS // SHARE // NX, D)
SPACE = (
    (("x", (ROWS, D), BF), ("cot", (ROWS, D), BF), ("y", (ROWS, D), BF), ("proj", (NX, DH, FEATS // NX), BF))
    + (("spare", (FF, SPARE), BF), ("tile", TILE, F32))
    + tuple(("in_" + n, (w // N_DEV,), BF) for n, w in zip(VECTORS, WIDTHS))
    + (("tiles", (N_DEV * TILE[0], TILE[1]), F32), ("grad_got", QUARTER, BF))
    + tuple((n, (1, w), F32) for n, w in zip(VECTORS, WIDTHS))
    + tuple(("d_" + n, (1, w), F32) for n, w in zip(VECTORS, WIDTHS))
    + SPACE
)


def layer(tok, cot, weights, vectors, proj, seg):
    anywhere = pl.BlockSpec(memory_space=pl.ANY)
    vmem = pl.BlockSpec(memory_space=pltpu.VMEM)
    shape, dma = jax.ShapeDtypeStruct, pltpu.SemaphoreType.DMA
    received, stages = [], []
    for _, _, width, orders, w, _ in REDUCE_PARTS.values():
        kind = F32 if w == "small" else BF
        received += [pltpu.VMEM(s, kind) for shapes in got_shapes(orders, shard_rows(w), width) for s in shapes]
        stages.append(pltpu.VMEM((shard_rows(w), width), F32))
    there, back = len(GATHER_PARTS), len(REDUCE_PARTS)
    return pl.pallas_call(
        layer_kernel,
        out_shape=[shape(tok.shape, BF), shape(tok.shape, F32)] + [shape(w.shape, F32) for w in weights] + [shape(TILE, F32)],
        in_specs=[anywhere] * 15 + [vmem],
        out_specs=[anywhere] * 7,
        scratch_shapes=[pltpu.VMEM(s, BF) for _, s in WEIGHTS] + [pltpu.VMEM(s, d) for _, s, d in SPACE] + received + stages
        + [dma((there, 6)), dma((there, 6)), dma((there,)), dma((back, 6)), dma((back, 6)), dma((back,))]
        + [dma((5,)), dma((5,)), dma((5,)), dma((1,)), dma((len(VECTORS),))],
        compiler_params=pltpu.CompilerParams(collective_id=0, has_side_effects=True, vmem_limit_bytes=61 << 20),
        name="layer",
    )(tok, cot, *weights, *vectors, proj, seg)


def finish_kernel(count, *refs):
    ins, tile, outs = refs[:count], refs[count], refs[count + 1 : 2 * count + 1]
    rows, spaces, sems = refs[2 * count + 1 : -count - 1], refs[-count - 1 : -1], refs[-1]
    loads = [pltpu.make_async_copy(a, b, sems.at[0, n]) for n, (a, b) in enumerate(zip(ins, spaces))]
    stores = [pltpu.make_async_copy(a, b, sems.at[1, n]) for n, (a, b) in enumerate(zip(spaces, outs))]
    for load in loads:
        load.start()
    for n, row in enumerate(rows):
        row[...] = tile[n, 0 : row.shape[0]]
    for load, store in zip(loads, stores):
        load.wait()
        store.start()
    for store in stores:
        store.wait()


def finish(arrays, tile):
    anywhere = pl.BlockSpec(memory_space=pl.ANY)
    vmem = pl.BlockSpec(memory_space=pltpu.VMEM)
    count = len(arrays)
    return pl.pallas_call(
        partial(finish_kernel, count),
        out_shape=[jax.ShapeDtypeStruct(a.shape, a.dtype) for a in arrays]
        + [jax.ShapeDtypeStruct((w // N_DEV,), F32) for w in WIDTHS],
        in_specs=[anywhere] * count + [vmem],
        out_specs=[anywhere] * count + [vmem] * len(WIDTHS),
        scratch_shapes=[pltpu.VMEM(a.shape, a.dtype) for a in arrays] + [pltpu.SemaphoreType.DMA((2, count))],
        name="finish",
    )(*arrays, tile)


def fast_device(
    tokens_in, out_cotangent, segment_ids, feature_proj,
    w_qkv, b_qkv, w_out, b_out, ln1_gain, ln1_bias, w_up, b_up, w_down, b_down, ln2_gain, ln2_bias,
):
    *arrays, tile = layer(
        tokens_in, out_cotangent, [w_qkv, w_out, w_up, w_down],
        [b_qkv, b_out, ln1_gain, ln1_bias, b_up, b_down, ln2_gain, ln2_bias], feature_proj.T, segment_ids,
    )
    out, grad_tok, g_qkv, g_out, g_up, g_down, *vec = finish(arrays, tile)
    return out, grad_tok, g_qkv, vec[0], g_out, vec[1], vec[2], vec[3], g_up, vec[4], g_down, vec[5], vec[6], vec[7]


def solution(mesh):
    return jax.shard_map(
        fast_device if fits(mesh) else on_device,
        mesh=mesh,
        in_specs=(
            P(None, ("dp", "feat"), None),
            P(None, ("dp", "feat"), None),
            P(None, "dp"),
            P("feat", None),
            P(("dp", "feat"), None),
            P(("dp", "feat")),
            P(("dp", "feat"), None),
            P(("dp", "feat")),
            P(("dp", "feat")),
            P(("dp", "feat")),
            P(("dp", "feat"), None),
            P(("dp", "feat")),
            P(("dp", "feat"), None),
            P(("dp", "feat")),
            P(("dp", "feat")),
            P(("dp", "feat")),
        ),
        out_specs=(
            P(None, ("dp", "feat"), None),
            P(None, ("dp", "feat"), None),
            P(("dp", "feat"), None),
            P(("dp", "feat")),
            P(("dp", "feat"), None),
            P(("dp", "feat")),
            P(("dp", "feat")),
            P(("dp", "feat")),
            P(("dp", "feat"), None),
            P(("dp", "feat")),
            P(("dp", "feat"), None),
            P(("dp", "feat")),
            P(("dp", "feat")),
            P(("dp", "feat")),
        ),
        check_vma=False,
    )
```

```python
from functools import partial

import jax
import jax.numpy as jnp
from jax import lax
from jax.experimental import pallas as pl
from jax.experimental.pallas import tpu as pltpu
from jax.sharding import PartitionSpec as P

D = 768
H = 12
DH = 64
FEATS = 256
MICRO = 4
SEGS = 4


EPSILON = 1e-05


def layer_norm(residual, norm_gain, norm_shift):
    center = residual - jnp.mean(residual, -1, keepdims=True)
    spread = jnp.mean(center * center, -1, keepdims=True)
    return center * lax.rsqrt(spread + EPSILON) * norm_gain + norm_shift


def cross_dot(left_op, right_op):
    return lax.dot_general(
        left_op, right_op, (((0,), (0,)), ((), ())), preferred_element_type=jnp.float32
    )


def back_dot(left_op, right_op):
    return lax.dot_general(
        left_op, right_op, (((1,), (1,)), ((), ())), preferred_element_type=jnp.float32
    )


def fetch_weights(
    w_qkv, b_qkv, w_out, b_out, ln1_gain, ln1_bias, w_up, b_up, w_down, b_down, ln2_gain, ln2_bias
):
    return (
        lax.all_gather(w_qkv, ("dp", "feat"), axis=0, tiled=True),
        lax.all_gather(b_qkv, ("dp", "feat"), axis=0, tiled=True),
        lax.all_gather(w_out, ("dp", "feat"), axis=0, tiled=True),
        lax.all_gather(b_out, ("dp", "feat"), axis=0, tiled=True),
        lax.all_gather(ln1_gain, ("dp", "feat"), axis=0, tiled=True),
        lax.all_gather(ln1_bias, ("dp", "feat"), axis=0, tiled=True),
        lax.all_gather(w_up, ("dp", "feat"), axis=0, tiled=True),
        lax.all_gather(b_up, ("dp", "feat"), axis=0, tiled=True),
        lax.all_gather(w_down, ("dp", "feat"), axis=0, tiled=True),
        lax.all_gather(b_down, ("dp", "feat"), axis=0, tiled=True),
        lax.all_gather(ln2_gain, ("dp", "feat"), axis=0, tiled=True),
        lax.all_gather(ln2_bias, ("dp", "feat"), axis=0, tiled=True),
    )


def feature_map(head_rows, feat_proj):
    feat_scale = DH ** (-0.25)
    proj_arg = feat_scale * jnp.einsum(
        "ghd,md->ghm", head_rows, feat_proj, preferred_element_type=jnp.float32
    )
    squares = jnp.einsum("ghd,ghd->gh", head_rows, head_rows, preferred_element_type=jnp.float32)
    proj_arg = proj_arg - 0.5 * feat_scale * feat_scale * squares[:, :, None]
    return jnp.exp(proj_arg) * FEATS ** (-0.5)


def feature_back(head_rows, feat_proj, grad_arg):
    feat_scale = DH ** (-0.25)
    proj_back = feat_scale * jnp.einsum(
        "ghm,md->ghd", grad_arg, feat_proj, preferred_element_type=jnp.float32
    )
    arg_total = jnp.sum(grad_arg.astype(jnp.float32), -1, keepdims=True)
    return proj_back - feat_scale * feat_scale * head_rows.astype(jnp.float32) * arg_total


def spread_segments(phi_low, member):
    tok_count, head_count, feat_width = phi_low.shape
    return (phi_low[:, :, None, :] * member[:, None, :, None]).reshape(
        tok_count, head_count, SEGS * feat_width
    )


def fold_segments(grad_wide, member_f):
    tok_count, head_count, wide_dim = grad_wide.shape
    shaped = grad_wide.reshape(tok_count, head_count, SEGS, wide_dim // SEGS)
    return jnp.sum(shaped * member_f[:, None, :, None], 2)


def micro_step(tokens, cotangent, seg_row, feat_proj, weights):
    (
        w_qkv,
        b_qkv,
        w_out,
        b_out,
        ln1_gain,
        ln1_bias,
        w_up,
        b_up,
        w_down,
        b_down,
        ln2_gain,
        ln2_bias,
    ) = weights
    tok_count = tokens.shape[0]
    qkv_rows = jnp.dot(tokens, w_qkv, preferred_element_type=jnp.float32) + b_qkv.astype(
        jnp.float32
    )
    qkv_low = qkv_rows.astype(jnp.bfloat16)
    grouped = lax.all_gather(qkv_low, "feat", axis=0, tiled=True)
    group_rows = grouped.shape[0]
    query_h = grouped[:, :D].reshape(group_rows, H, DH)
    key_h = grouped[:, D : 2 * D].reshape(group_rows, H, DH)
    value_h = grouped[:, 2 * D :].reshape(group_rows, H, DH)
    phi_q = feature_map(query_h, feat_proj)
    phi_k = feature_map(key_h, feat_proj)
    member_f = (seg_row[:, None] == jnp.arange(SEGS, dtype=jnp.int32)[None, :]).astype(jnp.float32)
    member = member_f.astype(jnp.bfloat16)
    wide_q = spread_segments(phi_q.astype(jnp.bfloat16), member)
    wide_k = spread_segments(phi_k.astype(jnp.bfloat16), member)
    ones_col = jnp.ones((group_rows,), jnp.bfloat16)
    kv_part = jnp.einsum("gha,ghe->hae", wide_k, value_h, preferred_element_type=jnp.float32)
    z_part = jnp.einsum("gha,g->ha", wide_k, ones_col, preferred_element_type=jnp.float32)
    kv_low = kv_part.astype(jnp.bfloat16)
    z_low = z_part.astype(jnp.bfloat16)
    numer_part = jnp.einsum(
        "gha,hae->ghe", wide_q, kv_low, preferred_element_type=jnp.float32
    ).reshape(group_rows, D)
    denom_part = jnp.einsum("gha,ha->gh", wide_q, z_low, preferred_element_type=jnp.float32)
    numer_sum, denom_sum = (
        lax.psum_scatter(numer_part, "feat", scatter_dimension=0, tiled=True),
        lax.psum_scatter(denom_part, "feat", scatter_dimension=0, tiled=True),
    )
    numer_h = numer_sum.reshape(tok_count, H, DH)
    att_low = (numer_h / denom_sum[:, :, None]).reshape(tok_count, D).astype(jnp.bfloat16)
    branch = jnp.dot(att_low, w_out, preferred_element_type=jnp.float32) + b_out.astype(jnp.float32)
    hidden_one, ln1_back = jax.vjp(
        layer_norm,
        tokens.astype(jnp.float32) + branch,
        ln1_gain.astype(jnp.float32),
        ln1_bias.astype(jnp.float32),
    )
    hid_low = hidden_one.astype(jnp.bfloat16)
    pre_act = jnp.dot(hid_low, w_up, preferred_element_type=jnp.float32) + b_up.astype(jnp.float32)
    act_val, gelu_back = jax.vjp(partial(jax.nn.gelu, approximate=False), pre_act)
    act_low = act_val.astype(jnp.bfloat16)
    ffn_out = jnp.dot(act_low, w_down, preferred_element_type=jnp.float32) + b_down.astype(
        jnp.float32
    )
    result, ln2_back = jax.vjp(
        layer_norm, hidden_one + ffn_out, ln2_gain.astype(jnp.float32), ln2_bias.astype(jnp.float32)
    )
    grad_r2, grad_gain2, grad_bias2 = ln2_back(cotangent.astype(jnp.float32))
    grad_ffn = grad_r2.astype(jnp.bfloat16)
    grad_bdown = jnp.sum(grad_ffn.astype(jnp.float32), 0)
    grad_wdown = cross_dot(act_low, grad_ffn)
    (grad_act,) = gelu_back(back_dot(grad_ffn, w_down))
    grad_pre = grad_act.astype(jnp.bfloat16)
    grad_bup = jnp.sum(grad_pre.astype(jnp.float32), 0)
    grad_wup = cross_dot(hid_low, grad_pre)
    grad_h1 = grad_r2 + back_dot(grad_pre, w_up)
    grad_r1, grad_gain1, grad_bias1 = ln1_back(grad_h1)
    grad_branch = grad_r1.astype(jnp.bfloat16)
    grad_bout = jnp.sum(grad_branch.astype(jnp.float32), 0)
    grad_wout = cross_dot(att_low, grad_branch)
    grad_att = back_dot(grad_branch, w_out).reshape(tok_count, H, DH)
    grad_num = (grad_att / denom_sum[:, :, None]).reshape(tok_count, D).astype(jnp.bfloat16)
    grad_den = (-jnp.sum(grad_att * numer_h, -1) / (denom_sum * denom_sum)).astype(jnp.bfloat16)
    group_num, group_den = (
        lax.all_gather(grad_num, "feat", axis=0, tiled=True),
        lax.all_gather(grad_den, "feat", axis=0, tiled=True),
    )
    group_num_h = group_num.reshape(group_rows, H, DH)
    grad_kv_part = jnp.einsum(
        "gha,ghe->hae", wide_q, group_num_h, preferred_element_type=jnp.float32
    )
    grad_z_part = jnp.einsum("gha,gh->ha", wide_q, group_den, preferred_element_type=jnp.float32)
    grad_kv = grad_kv_part.astype(jnp.bfloat16)
    grad_z = grad_z_part.astype(jnp.bfloat16)
    wide_gq = jnp.einsum("ghe,hae->gha", group_num_h, kv_low, preferred_element_type=jnp.float32)
    wide_gq = wide_gq + group_den[:, :, None].astype(jnp.float32) * z_low[None].astype(jnp.float32)
    grad_arg_q = (fold_segments(wide_gq, member_f) * phi_q).astype(jnp.bfloat16)
    wide_gk = jnp.einsum(
        "ghe,hae->gha", value_h, grad_kv, preferred_element_type=jnp.float32
    ) + grad_z[None].astype(jnp.float32)
    grad_arg_k = (fold_segments(wide_gk, member_f) * phi_k).astype(jnp.bfloat16)
    grad_value = jnp.einsum("gha,hae->ghe", wide_k, grad_kv, preferred_element_type=jnp.float32)
    grad_query = feature_back(query_h, feat_proj, grad_arg_q)
    grad_key = feature_back(key_h, feat_proj, grad_arg_k)
    grad_group = jnp.concatenate(
        [
            grad_query.reshape(group_rows, D),
            grad_key.reshape(group_rows, D),
            grad_value.reshape(group_rows, D),
        ],
        1,
    )
    grad_qkv = lax.psum_scatter(
        grad_group.astype(jnp.bfloat16), "feat", scatter_dimension=0, tiled=True
    )
    grad_bqkv = jnp.sum(grad_qkv.astype(jnp.float32), 0)
    grad_wqkv = cross_dot(tokens, grad_qkv)
    grad_tokens = grad_r1 + back_dot(grad_qkv, w_qkv)
    grads_now = (
        grad_wqkv,
        grad_bqkv,
        grad_wout,
        grad_bout,
        grad_gain1,
        grad_bias1,
        grad_wup,
        grad_bup,
        grad_wdown,
        grad_bdown,
        grad_gain2,
        grad_bias2,
    )
    return (result.astype(jnp.bfloat16), grad_tokens, grads_now)


def on_device(
    tokens_in,
    out_cotangent,
    segment_ids,
    feature_proj,
    w_qkv,
    b_qkv,
    w_out,
    b_out,
    ln1_gain,
    ln1_bias,
    w_up,
    b_up,
    w_down,
    b_down,
    ln2_gain,
    ln2_bias,
):
    totals = None
    outputs = []
    grad_inputs = []
    for micro_idx in range(MICRO):
        gathered = fetch_weights(
            w_qkv,
            b_qkv,
            w_out,
            b_out,
            ln1_gain,
            ln1_bias,
            w_up,
            b_up,
            w_down,
            b_down,
            ln2_gain,
            ln2_bias,
        )
        result, grad_tokens, grads_now = micro_step(
            tokens_in[micro_idx],
            out_cotangent[micro_idx],
            segment_ids[micro_idx],
            feature_proj,
            gathered,
        )
        outputs.append(result)
        grad_inputs.append(grad_tokens)
        totals = grads_now if totals is None else jax.tree.map(jnp.add, totals, grads_now)
    (
        grad_wqkv,
        grad_bqkv,
        grad_wout,
        grad_bout,
        grad_gain1,
        grad_bias1,
        grad_wup,
        grad_bup,
        grad_wdown,
        grad_bdown,
        grad_gain2,
        grad_bias2,
    ) = totals
    summed = (
        lax.psum_scatter(grad_wqkv, ("dp", "feat"), scatter_dimension=0, tiled=True),
        lax.psum_scatter(grad_bqkv, ("dp", "feat"), scatter_dimension=0, tiled=True),
        lax.psum_scatter(grad_wout, ("dp", "feat"), scatter_dimension=0, tiled=True),
        lax.psum_scatter(grad_bout, ("dp", "feat"), scatter_dimension=0, tiled=True),
        lax.psum_scatter(grad_gain1, ("dp", "feat"), scatter_dimension=0, tiled=True),
        lax.psum_scatter(grad_bias1, ("dp", "feat"), scatter_dimension=0, tiled=True),
        lax.psum_scatter(grad_wup, ("dp", "feat"), scatter_dimension=0, tiled=True),
        lax.psum_scatter(grad_bup, ("dp", "feat"), scatter_dimension=0, tiled=True),
        lax.psum_scatter(grad_wdown, ("dp", "feat"), scatter_dimension=0, tiled=True),
        lax.psum_scatter(grad_bdown, ("dp", "feat"), scatter_dimension=0, tiled=True),
        lax.psum_scatter(grad_gain2, ("dp", "feat"), scatter_dimension=0, tiled=True),
        lax.psum_scatter(grad_bias2, ("dp", "feat"), scatter_dimension=0, tiled=True),
    )
    return (
        jnp.stack(outputs),
        jnp.stack(grad_inputs),
        summed[0],
        summed[1],
        summed[2],
        summed[3],
        summed[4],
        summed[5],
        summed[6],
        summed[7],
        summed[8],
        summed[9],
        summed[10],
        summed[11],
    )


NZ, NY, NC, NX = 4, 2, 2, 2
N_DEV = NZ * NY * NC * NX
MESH_ID = pl.DeviceIdType.MESH
BF = jnp.bfloat16
F32 = jnp.float32
SHARE = MICRO // NX
GRID = (NZ, NY, NC)
ALL = slice(None)


def fits(mesh):
    return mesh.shape["dp"] == NZ * NY * NC and mesh.shape["feat"] == NX


class Place:
    def __init__(self):
        i = lax.axis_index("dp")
        self.z, self.y, self.c, self.x = i // (NY * NC), (i // NC) % NY, i % NC, lax.axis_index("feat")
        self.sibling = self.device(c=1 - self.c)
        self.over = {"x": self.device(x=1 - self.x), "y": self.device(y=1 - self.y)}
        z = self.z
        self.to = {1: z <= 2, -1: z >= 1, 2: z <= 1, -2: z >= 2}
        self.had = {1: z >= 1, -1: z <= 2, 2: z >= 2, -2: z <= 1}

    def device(self, **other):
        z, y, c, x = (other.get(n, getattr(self, n)) for n in "zycx")
        return (z * (NY * NC) + y * NC + c, x)

    def meet(self):
        barrier = pltpu.get_barrier_semaphore()
        peers = [self.sibling, self.over["x"], self.over["y"]] + [self.device(z=lax.rem(self.z + k, NZ)) for k in (1, 2, 3)]
        for peer in peers:
            pl.semaphore_signal(barrier, inc=1, device_id=peer, device_id_type=MESH_ID)
        pl.semaphore_wait(barrier, len(peers))

    def per_class(self, orders, act):
        if orders[0] == orders[1]:
            act(orders[0])
            return
        for c in range(NC):

            @pl.when(self.c == c)
            def _(order=orders[c]):
                act(order)

    def rows(self, grid, x):
        share = grid.shape[3] // NX
        return pl.ds(pl.multiple_of(x * share, 8), share)

    def view(self, grid, cols, spread=(), **at):
        index = [ALL if n in spread else at.get(n, getattr(self, n)) for n in "zyc"]
        rows = ALL if "x" in spread else self.rows(grid, at.get("x", self.x))
        return grid.at[(*index, rows, cols)]


class Copies:
    def __init__(self, send_sems, recv_sems):
        self.send_sems, self.recv_sems = send_sems, recv_sems

    def copy(self, slot, src, dst, peer, sent=None):
        return pltpu.make_async_remote_copy(
            src_ref=src, dst_ref=dst, send_sem=self.send_sems.at[slot if sent is None else sent],
            recv_sem=self.recv_sems.at[slot], device_id=peer, device_id_type=MESH_ID,
        )


MOVES = (1, -1, 2, -2)


def stretch(order):
    return "".join("zZ" if n == "z" else n for n in order)


class Gather(Copies):
    def __init__(self, here, part, src, grid, cols, orders, sems):
        super().__init__(sems[0].at[part], sems[1].at[part])
        self.here, self.grid, self.cols, self.orders = here, grid, cols, tuple(stretch(o) for o in orders)
        self.src = src.at[ALL, cols]
        self.local = pltpu.make_async_copy(self.src, here.view(grid, cols), sems[2].at[part])

    def phase(self, order, n):
        here, dim = self.here, order[n]
        mine = here.view(self.grid, self.cols, order[:n].replace("Z", "").replace("z", "" if dim == "Z" else "z"))
        src = self.src if n == 0 else mine
        if dim == "z":
            return [
                (here.to[k], here.had[k], self.copy(s, src, mine, here.device(z=lax.rem(here.z + k + NZ, NZ))))
                for s, k in enumerate(MOVES)
            ]
        if dim == "Z":
            inner = (here.z == 1) | (here.z == 2)
            outer = (here.z == 0) | (here.z == 3)
            far = here.view(self.grid, self.cols, order[: n - 1], z=jnp.where(inner, 6 - 3 * here.z, 3 - here.z))
            return [(inner, outer, self.copy(4, far, far, here.device(z=jnp.where(inner, 3 * here.z - 3, 3 - here.z))))]
        return [(None, None, self.copy(5 + "xy".index(dim), src, mine, here.over[dim]))]

    def to_sibling(self):
        mine = self.here.view(self.grid, self.cols, "zyx")
        return self.copy(7, mine, mine, self.here.sibling)

    def step(self, n):
        here, last = self.here, len(self.orders[0])
        if n == 0:
            self.local.start()
            here.per_class(self.orders, lambda order: run_all("start", self.phase(order, 0)))
        elif n <= last:
            here.per_class(self.orders, lambda order: run_all("wait_recv", self.phase(order, n - 1)))
            if n == 1:
                self.local.wait()
            if n < last:
                here.per_class(self.orders, lambda order: run_all("start", self.phase(order, n)))
            else:
                self.to_sibling().start()
        else:
            self.to_sibling().wait_recv()

    def drain(self):
        for n in range(len(self.orders[0])):
            self.here.per_class(self.orders, lambda order, n=n: run_all("wait_send", self.phase(order, n)))
        self.to_sibling().wait_send()


def run_all(what, copies):
    for sends, gets, copy in copies:
        when(gets if what == "wait_recv" else sends, getattr(copy, what))


def when(condition, act):
    if condition is None:
        act()
        return

    @pl.when(condition)
    def _():
        act()


class Reduce(Copies):
    def __init__(self, here, part, grid, cols, orders, got, stage, out, sems):
        super().__init__(sems[0].at[part], sems[1].at[part])
        self.here, self.grid, self.cols, self.orders = here, grid, cols, tuple(stretch(o) for o in orders)
        self.got, self.stage = got, stage
        self.out = pltpu.make_async_copy(stage, out, sems[2].at[part])

    def from_sibling(self):
        here = self.here
        theirs = here.view(self.grid, self.cols, "zyx", c=1 - here.c)
        return self.copy(0, theirs, self.got[0][0], here.sibling)

    def received(self, order, n):
        at = order.replace("Z", "").index(order[n].lower()) + 1
        return self.got[at][self.orders.index(order) % len(self.got[at])]

    def phase(self, order, n):
        here, dim, rest = self.here, order[n], order[n + 1 :].replace("Z", "")
        got, z = self.received(order, n), here.z
        if dim == "z":
            aim = {1: z + 1, -1: z - 1, 2: 2, -2: 1}
            ends = {1: here.to[1], -1: here.to[-1], 2: z == 0, -2: z == 3}
            copies = [
                (ends[k], None, self.copy(3 + s, here.view(self.grid, self.cols, rest, z=aim[k]), got.at[s], here.device(z=aim[k])))
                for s, k in enumerate(MOVES)
            ]
            near = {2: (z == 0, 3, 1), -2: (z == 3, 0, 2)}
            first = [
                (near[k][0], None, self.copy(
                    3 + s, here.view(self.grid, self.cols, rest, z=near[k][1]), got.at[s], here.device(z=near[k][2]), 5 + s
                ))
                for s, k in enumerate(MOVES) if k in near
            ]
            return first + copies
        if dim == "Z":
            end = {2: (z == 1, 3), -2: (z == 2, 0)}
            return [
                (end[k][0], None, self.copy(3 + s, here.view(self.grid, self.cols, rest, z=end[k][1]), got.at[s], here.device(z=end[k][1])))
                for s, k in enumerate(MOVES) if k in end
            ]
        place = {dim: 1 - getattr(here, dim)}
        return [(None, None, self.copy(1 + "xy".index(dim), here.view(self.grid, self.cols, rest, **place), got, here.over[dim]))]

    def arrivals(self, order, n):
        here, got = self.here, self.received(order, n)
        if order[n] != "Z":
            (_, _, copy), = self.phase(order, n)
            return [(None, copy.wait_recv, got)]
        mine = here.view(self.grid, self.cols, order[n + 1 :])
        return [
            (here.had[k], self.copy(3 + s, mine, got.at[s], here.sibling).wait_recv, got.at[s]) for s, k in enumerate(MOVES)
        ]

    def spot(self, spread, q, z=None):
        here, index, inner = self.here, {} if z is None else {"z": z}, {}
        if "y" in spread:
            index["y"] = inner["y"] = q % NY
            q = q // NY
        if "z" in spread:
            index["z"] = inner["z"] = q
        rows = ALL if "x" in spread else here.rows(self.grid, here.x)
        return tuple(index.get(n, getattr(here, n)) for n in "zyc") + (rows, self.cols), tuple(inner[n] for n in "zy" if n in inner)

    def add(self, got, spread, z=None):
        def one(q):
            index, inner = self.spot(spread, q, z)
            self.grid[index] = self.grid[index] + got[inner + (ALL, ALL)]

        count = (NZ if "z" in spread else 1) * (NY if "y" in spread else 1)
        blocks_of(count, one) if count > 1 else one(0)

    def take(self, order, n):
        if order[n] == "z":
            return
        here, final = self.here, n == len(order) - 1
        if final:
            self.stage[...] = self.grid[self.spot((), 0)[0]].astype(F32)
        for condition, wait, got in self.arrivals(order, n):

            def one(wait=wait, got=got):
                wait()
                if final:
                    self.stage[...] += got[...].astype(F32)
                else:
                    self.add(got, order[n + 1 :].replace("Z", ""))

            when(condition, one)

    def send(self, order, n):
        copies = self.phase(order, n)
        if order[n] == "Z":
            got, rest = self.received(order, n), order[n + 1 :]
            for (condition, _, copy), (slot, end) in zip(copies, ((2, 3), (3, 0)), strict=True):

                def pass_on(copy=copy, slot=slot, end=end):
                    copy.wait_recv()
                    self.add(got.at[slot], rest, z=end)
                    copy.start()

                when(condition, pass_on)
        else:
            run_all("start", copies)

    def step(self, n):
        here, last = self.here, len(self.orders[0])
        if n == 0:
            self.from_sibling().start()
        elif n == 1:
            self.from_sibling().wait_recv()
            self.add(self.got[0][0], "zyx")
        else:
            here.per_class(self.orders, lambda order: self.take(order, n - 2))
        if 0 < n <= last:
            here.per_class(self.orders, lambda order: self.send(order, n - 1))
        elif n > last:
            self.out.start()

    def drain(self):
        self.from_sibling().wait_send()
        for n in range(len(self.orders[0])):
            self.here.per_class(self.orders, lambda order, n=n: run_all("wait_send", self.phase(order, n)))
        self.out.wait()


def got_shapes(orders, rows, width):
    first, second = (order_shapes(order, rows, width) for order in orders)
    return [(a,) if a == b else (a, b) for a, b in zip(first, second, strict=True)]


def order_shapes(order, rows, width):

    def block(spread):
        return tuple(dict(z=NZ, y=NY)[n] for n in "zy" if n in spread) + (rows * (NX if "x" in spread else 1), width)

    shapes = [block("zyx")]
    for n, dim in enumerate(order):
        shapes.append(((len(MOVES),) if dim == "z" else ()) + block(order[n + 1 :]))
    return shapes


def blocks_of(count, body, then=()):
    def step(j, carry):
        body(j)
        for at in sorted({at for at, _ in then}):

            @pl.when(j == at)
            def _(at=at):
                for when, act in then:
                    if when == at:
                        act()

        return carry

    lax.fori_loop(0, count, step, 0)


ROWS = 512
BLK = 256
PAIRS = D // 128
FF = 4 * D
WIDE = 2 * FEATS
SCALE = DH ** (-0.25)


def dot(a, b, ca=1, cb=0):
    return lax.dot_general(a, b, (((ca,), (cb,)), ((), ())), preferred_element_type=F32)


def half_masks(width):
    lane = lax.broadcasted_iota(jnp.int32, (1, width), 1) % 128
    first = (lane < DH).astype(F32)
    return first.astype(BF), (1.0 - first).astype(BF)


def lanes(j, width):
    return pl.ds(pl.multiple_of(j * width, width), width)


class Work:
    def __init__(self, refs):
        self.__dict__.update(refs)

    def setup(self, proj, seg_rows):
        row = lax.broadcasted_iota(jnp.int32, (DH, 128), 0)
        col = lax.broadcasted_iota(jnp.int32, (DH, 128), 1)
        for h in range(2):
            place_in = (col == row + h * DH).astype(BF)
            for n in range(NX):
                self.table[pl.ds(h * FEATS + n * 128, 128), 0:128] = dot(proj[n], place_in, 0, 0).astype(BF)
        feat = lax.broadcasted_iota(jnp.int32, (WIDE, 128), 0) // FEATS
        half = lax.broadcasted_iota(jnp.int32, (WIDE, 128), 1) // DH
        same = (feat == half).astype(F32).astype(BF)
        self.table[:, 128:256] = same
        self.flip[D:, :] = jnp.ones((16, ROWS), BF)
        for b in range(2):
            across = jnp.broadcast_to(seg_rows[b], (BLK, BLK))
            self.mask[b] = (across == jnp.transpose(across)).astype(F32)

    def features(self, rows):
        wide = rows.astype(F32)
        squares = wide * wide
        high = squares.astype(BF)
        low = (squares - high.astype(F32)).astype(BF)
        same = self.table[:, 128:256]
        norm = dot(high, same, 1, 1) + dot(low, same, 1, 1)
        arg = SCALE * dot(rows, self.table[:, 0:128], 1, 1) - (0.5 * SCALE * SCALE) * norm
        return (jnp.exp(arg) * FEATS ** (-0.5)).astype(BF)

    def qkv_block(self, j):
        col = lanes(j, D)
        full = dot(self.x[...], self.w_qkv[:, col]) + self.b_qkv[:, col]
        self.qkv[:, col] = full.astype(BF)

    def pair(self, i):
        b, p = i // PAIRS, i % PAIRS
        rows = pl.ds(pl.multiple_of(b * BLK, BLK), BLK)
        cols = [pl.ds(pl.multiple_of(n * D + p * 128, 128), 128) for n in range(3)]
        return b, rows, cols

    def attend(self, i):
        b, rows, cols = self.pair(i)
        mask = self.mask[b]
        m0, m1 = half_masks(128)
        phi_q = self.features(self.qkv[rows, cols[0]])
        phi_k = self.features(self.qkv[rows, cols[1]])
        self.phi_q[i] = phi_q
        self.phi_k[i] = phi_k
        v = self.qkv[rows, cols[2]]
        one = jnp.ones((BLK, 128), BF)
        res = None
        for h, m in enumerate((m0, m1)):
            part = slice(h * FEATS, (h + 1) * FEATS)
            score = (dot(phi_q[:, part], phi_k[:, part], 1, 1) * mask).astype(BF)
            term = dot(score, jnp.concatenate([v * m, one * m], 1))
            res = term if res is None else res + term
        inv = 1.0 / res[:, 128:]
        self.inv[rows, cols[0]] = inv
        self.att[rows, cols[0]] = (res[:, :128] * inv).astype(BF)

    def normalize(self, r):
        center = r - jnp.mean(r, -1, keepdims=True)
        scale = lax.rsqrt(jnp.mean(center * center, -1, keepdims=True) + EPSILON)
        return center * scale, scale

    def normalize_back(self, dy, n, scale, gain):
        g = dy * gain
        return (g - jnp.mean(g, -1, keepdims=True) - n * jnp.mean(g * n, -1, keepdims=True)) * scale

    def branch(self):
        for j in range(3):
            col = lanes(j, 256)
            self.n1[:, col] = dot(self.att[...], self.w_out[:, col]) + self.b_out[:, col] + self.x[:, col].astype(F32)

        def rows_of(j):
            row = pl.ds(pl.multiple_of(j * 128, 128), 128)
            n1, s1 = self.normalize(self.n1[row, :])
            self.n1[row, :] = n1
            self.s1[row, :] = s1
            self.h1[row, :] = (n1 * self.g1[...] + self.b1[...]).astype(BF)

        blocks_of(ROWS // 128, rows_of)

    def up_block(self, j):
        col = lanes(j, 256)
        for r in range(0, ROWS, 128):
            row = slice(r, r + 128)
            a = dot(self.h1[row, :], self.w_up[:, col]) + self.b_up[:, col]
            cdf = 0.5 * (1.0 + lax.erf(a * 2**-0.5))
            self.z[row, col] = (a * cdf).astype(BF)
            self.slope[row, col] = (cdf + a * jnp.exp(-0.5 * a * a) * (0.5 / 3.141592653589793) ** 0.5).astype(BF)

    def down_block(self, j):
        col = lanes(j, 256)
        back = self.n1[:, col] * self.g1[:, col] + self.b1[:, col]
        self.dr[:, col] = dot(self.z[...], self.w_down[:, col]) + self.b_down[:, col] + back

    def second_norm(self):
        self.d_g2[...] = jnp.zeros_like(self.d_g2)

        def rows_of(j):
            row = pl.ds(pl.multiple_of(j * 128, 128), 128)
            n2, s2 = self.normalize(self.dr[row, :])
            self.y[row, :] = (n2 * self.g2[...] + self.b2[...]).astype(BF)
            dy = self.cot[row, :].astype(F32)
            dr2 = self.normalize_back(dy, n2, s2, self.g2[...])
            self.dr[row, :] = dr2
            self.df[row, :] = dr2.astype(BF)
            self.d_g2[...] += jnp.sum(dy * n2, 0, keepdims=True)

        blocks_of(ROWS // 128, rows_of)

    def second_sums(self):
        ones = self.flip[D:, :]
        self.d_b2[...] = dot(ones, self.cot[...])[0:1]
        self.d_b_down[...] = dot(ones, self.df[...])[0:1]

    def down_back(self, j):
        col = lanes(j, 1024)
        dz = dot(self.df[...], self.w_down[col, :], 1, 1)
        self.slope[:, col] = (dz * self.slope[:, col].astype(F32)).astype(BF)

    def down_grad(self, into, part, j):
        col = lanes(j, D)
        into[col, :] = dot(self.z[:, col], self.df[:, part], 0, 0).astype(BF)

    def up_back(self, j):
        col = lanes(j, 384)
        self.dr[:, col] += dot(self.slope[...], self.w_up[col, :], 1, 1)

    def turn(self, name):
        self.flip[0:D, :] = jnp.transpose(getattr(self, name)[...])

    def weight_grad(self, weight, bias, col, grad):
        full = dot(self.flip[...], grad)
        weight[:, col] = full[0:D].astype(BF)
        bias[:, col] = full[D : D + 1]

    def up_grad(self, j):
        col = lanes(j, 512)
        self.weight_grad(self.w_up, self.d_b_up, col, self.slope[:, col])

    def first_norm_back(self):
        for ref in (self.d_g1, self.d_b1):
            ref[...] = jnp.zeros_like(ref)

        def rows_of(j):
            row = pl.ds(pl.multiple_of(j * 128, 128), 128)
            dh1, n1 = self.dr[row, :], self.n1[row, :]
            dr1 = self.normalize_back(dh1, n1, self.s1[row, :], self.g1[...])
            self.dr[row, :] = dr1
            self.df[row, :] = dr1.astype(BF)
            self.d_g1[...] += jnp.sum(dh1 * n1, 0, keepdims=True)
            self.d_b1[...] += jnp.sum(dh1, 0, keepdims=True)

        blocks_of(ROWS // 128, rows_of)

    def att_back(self, j):
        head_r = lax.broadcasted_iota(jnp.int32, (256, 256), 0) // DH
        head_c = lax.broadcasted_iota(jnp.int32, (256, 256), 1) // DH
        same = (head_r == head_c).astype(F32).astype(BF)
        col = lanes(j, 256)
        datt = dot(self.df[...], self.w_out[col, :], 1, 1)
        inv = self.inv[:, col]
        self.cot[:, col] = (datt * inv).astype(BF)
        prod = datt * self.att[:, col].astype(F32)
        high = prod.astype(BF)
        low = (prod - high.astype(F32)).astype(BF)
        total = dot(high, same) + dot(low, same)
        self.h1[:, col] = (-total * inv).astype(BF)

    def out_grad(self):
        col = slice(0, D)
        self.weight_grad(self.w_out, self.d_b_out, col, self.df[:, col])

    def attend_back(self, i):
        b, rows, cols = self.pair(i)
        mask = self.mask[b]
        m0, m1 = half_masks(256)
        q, k, v = (self.qkv[rows, c] for c in cols)
        dnum, dden = self.cot[rows, cols[0]], self.h1[rows, cols[0]]
        left = jnp.concatenate([dnum, dden * (1.0 / DH)], 1)
        right = jnp.concatenate([v, jnp.ones((BLK, 128), BF)], 1)
        back_q, back_k, dv = None, None, None
        for h, m in enumerate((m0, m1)):
            part = slice(h * FEATS, (h + 1) * FEATS)
            phi_q, phi_k = self.phi_q[i, :, part], self.phi_k[i, :, part]
            mine = left * m
            dscore = (dot(mine, right, 1, 1) * mask).astype(BF)
            flipped = (dot(right, mine, 1, 1) * mask).astype(BF)
            darg_q = (dot(dscore, phi_k) * phi_q.astype(F32)).astype(BF)
            darg_k = (dot(flipped, phi_q) * phi_k.astype(F32)).astype(BF)
            score = (dot(phi_k, phi_q, 1, 1) * mask).astype(BF)
            table = self.table[part, :]
            terms = dot(darg_q, table), dot(darg_k, table), dot(score, mine[:, :128])
            if h == 0:
                back_q, back_k, dv = terms
            else:
                back_q, back_k, dv = back_q + terms[0], back_k + terms[1], dv + terms[2]
        for n, (rows_in, back) in enumerate(((q, back_q), (k, back_k))):
            grad = SCALE * back[:, :128] - (SCALE * SCALE) * rows_in.astype(F32) * back[:, 128:]
            self.qkv[rows, cols[n]] = grad.astype(BF)
        self.qkv[rows, cols[2]] = dv.astype(BF)

    def tokens_back(self, j):
        col = lanes(j, 384)
        self.dr[:, col] += dot(self.qkv[...], self.w_qkv[col, :], 1, 1)

    def qkv_grad(self, j):
        col = lanes(j, D)
        self.weight_grad(self.w_qkv, self.d_b_qkv, col, self.qkv[:, col])


VECTORS = ("b_qkv", "b_out", "g1", "b1", "b_up", "b_down", "g2", "b2")
WIDTHS = (3 * D, D, D, D, FF, D, D, D)
SPACE = (
    ("qkv", (ROWS, 3 * D), BF), ("phi_q", (2 * PAIRS, BLK, WIDE), BF), ("phi_k", (2 * PAIRS, BLK, WIDE), BF),
    ("att", (ROWS, D), BF), ("inv", (ROWS, D), F32), ("n1", (ROWS, D), F32), ("s1", (ROWS, 1), F32),
    ("h1", (ROWS, D), BF), ("z", (ROWS, FF), BF), ("slope", (ROWS, FF), BF), ("dr", (ROWS, D), F32),
    ("df", (ROWS, D), BF), ("flip", (D + 16, ROWS), BF),
    ("table", (WIDE, 256), BF), ("mask", (2, BLK, BLK), F32),
)


GATHER_PARTS = {
    "small": ("small", 0, 128, ("zyx", "zxy")),
    "q": ("w_qkv", 0, 768, ("zyx", "zxy")),
    "k": ("w_qkv", 768, 768, ("zxy", "zxy")),
    "v": ("w_qkv", 1536, 768, ("zxy", "zxy")),
    "out": ("w_out", 0, 768, ("xzy", "yzx")),
    "up0": ("w_up", 0, 1024, ("zyx", "zxy")),
    "up1": ("w_up", 1024, 1024, ("xzy", "yzx")),
    "up2": ("w_up", 2048, 1024, ("xzy", "yzx")),
    "dn0": ("w_down", 0, 256, ("xyz", "xyz")),
    "dn1": ("w_down", 256, 256, ("zyx", "zxy")),
    "dn2": ("w_down", 512, 256, ("xzy", "yzx")),
}
REDUCE_PARTS = {
    "small": ("small", 0, 128, ("xyz", "yxz"), "small", 0),
    "q": ("w_qkv", 0, 768, ("xyz", "yxz"), "w_qkv", 0),
    "k": ("w_qkv", 768, 768, ("xyz", "yxz"), "w_qkv", 768),
    "v": ("w_qkv", 1536, 768, ("xyz", "yxz"), "w_qkv", 1536),
    "out": ("w_out", 0, 768, ("xyz", "yxz"), "w_out", 0),
    "up0": ("w_up", 0, 1024, ("xyz", "yxz"), "w_up", 0),
    "up1": ("w_up", 1024, 1024, ("xyz", "xyz"), "w_up", 1024),
    "up2": ("w_up", 2048, 1024, ("yxz", "yxz"), "w_up", 2048),
    "dn0": ("spare", 0, 256, ("xyz", "yxz"), "w_down", 0),
    "dn1": ("w_down", 256, 256, ("zxy", "zxy"), "w_down", 256),
    "dn2": ("w_down", 512, 256, ("yzx", "xzy"), "w_down", 512),
}
FORWARD = (
    "proj!", "small0", "tok!", "q0", "out0", "up10", "k0", "proj?", "setup", "small1", "q1", "v0", "small2", "up00",
    "q2", "k1", "v1", "dn10", "up20", "dn20", "out1", "k2", "up11", "small3", "v2", "up01", "q3", "up21", "dn21",
    "dn11", "k3", "small4", "dn00", "small5", "spread", "cot!", "v3", "out2", "up02", "q4", "dn01", "k4", "q5",
    "tok?", "qkv", "up12", "k5", "qkv", "v4", "dn12", "up22", "v5", "out3", "qkv", "att", "up03", "up13", "dn02",
    "att*2", "up23", "dn13", "att", "dn22", "att", "out4", "att*3", "out5", "att", "up04", "att*3", "up05", "dn23",
    "branch", "up14", "upb*3", "dn03", "upb", "up24", "up15", "upb*4", "up25", "upb*3", "dn14", "dn04", "upb", "dn15",
    "dn24", "dn05", "down*2", "dn25", "down", "cot?", "ln2",
)
BACKWARD = (
    "y!", "gdn0*4", "dn00", "sums", "dz*3", "dn01", "gdn1*4", "dn10", "gdn2*4", "dn20", "uback", "dn11", "uback",
    "dn21", "flip0", "gup", "dn02", "gup", "up00", "gup*2", "up10", "gup*2", "up20", "up01", "dn22", "nback", "up11",
    "dn03", "up21", "datt*3", "flip1", "gout", "out0", "attb", "dn12", "up02", "attb", "out1", "attb*4", "dn23",
    "attb*2", "up12", "up22", "attb", "dn04", "up03", "attb*3", "tback", "dn13", "out2", "tback", "dn24", "lower",
    "flip2", "gqkv", "q0", "dn05", "gqkv", "k0", "up13", "up23", "gqkv", "dn14", "q1", "up04", "k1", "out3", "v0",
    "dn25", "collect", "dn15", "small0", "up14", "v1", "small1", "q2", "up24", "up05", "k2", "out4", "up15", "up25",
    "small2", "v2", "out5", "q3", "grad!", "k3", "small3", "v3", "q4", "k4", "small4", "v4", "k5", "small5", "q5",
    "v5",
)
WEIGHTS = (("w_qkv", (D, 3 * D)), ("w_out", (D, D)), ("w_up", (D, FF)), ("w_down", (FF, D)))
TILE = (8, 128)
SPARE = 256
HALF = (SHARE, NX, ROWS // SHARE // NX, D)


def shard_rows(weight):
    return TILE[0] if weight == "small" else dict(WEIGHTS)[weight][0] // N_DEV


class Swap:
    def __init__(self, here, n, theirs, target, mine, home, sems):
        self.there = pltpu.make_async_remote_copy(
            src_ref=theirs, dst_ref=target, send_sem=sems[0].at[n], recv_sem=sems[1].at[n],
            device_id=here.over["x"], device_id_type=MESH_ID,
        )
        self.here = None if home is None else pltpu.make_async_copy(mine, home, sems[2].at[n])

    def start(self):
        self.there.start()
        if self.here is not None:
            self.here.start()

    def arrive(self):
        self.there.wait_recv()
        if self.here is not None:
            self.here.wait()


def one_hot(width, count):
    at = lax.broadcasted_iota(jnp.int32, (1, count), 1).astype(F32)
    owner = jnp.floor((at + 0.5) * (1.0 / width))
    lane = at - owner * width
    lanes_hot = (lax.broadcasted_iota(jnp.int32, (128, count), 0).astype(F32) == lane).astype(F32).astype(BF)
    owner_hot = (lax.broadcasted_iota(jnp.int32, (N_DEV, count), 0).astype(F32) == owner).astype(F32)
    return lanes_hot, owner_hot


def spread_small(tiles, vectors):
    for width in sorted({v.shape[1] // N_DEV for v in vectors}):
        hot, owner = one_hot(width, width * N_DEV)
        for n, vector in enumerate(vectors):
            if vector.shape[1] == width * N_DEV:
                rows = tiles[pl.ds(n, N_DEV, stride=TILE[0]), :].astype(BF)
                vector[...] = jnp.sum(dot(rows, hot) * owner, 0, keepdims=True)


def collect_small(tiles, vectors):
    for width in sorted({v.shape[1] // N_DEV for v in vectors}):
        hot, owner = one_hot(width, width * N_DEV)
        for n, vector in enumerate(vectors):
            if vector.shape[1] == width * N_DEV:
                full = owner * vector[...]
                high = full.astype(BF)
                low = (full - high.astype(F32)).astype(BF)
                tiles[pl.ds(n, N_DEV, stride=TILE[0]), :] = dot(high, hot, 1, 1) + dot(low, hot, 1, 1)


def layer_kernel(*refs):
    it = iter(refs)
    tok, cot = next(it), next(it)
    local = {w: next(it) for w, _ in WEIGHTS}
    own_vectors = [next(it) for _ in VECTORS]
    proj_in, seg = next(it), next(it)
    block_out, grad_own, grad_got = next(it), next(it), next(it)
    outs = {w: next(it) for w, _ in WEIGHTS}
    outs["small"] = next(it)
    ref = {n: next(it) for n, _ in WEIGHTS}
    ref.update({n: next(it) for n, _, _ in SPACE})
    work = Work(ref)
    got = {
        p: [tuple(next(it) for _ in shapes) for shapes in got_shapes(orders, shard_rows(w), width)]
        for p, (_, _, width, orders, w, _) in REDUCE_PARTS.items()
    }
    stage = {p: next(it) for p in REDUCE_PARTS}
    gather_sems = [next(it) for _ in range(3)]
    reduce_sems = [next(it) for _ in range(3)]
    swap_sems = [next(it) for _ in range(3)]
    vector_sems = next(it)

    vector_loads = [pltpu.make_async_copy(v, ref["in_" + n], vector_sems.at[k]) for k, (n, v) in enumerate(zip(VECTORS, own_vectors))]
    for load in vector_loads:
        load.start()
    here = Place()
    here.meet()
    local["small"] = ref["tile"]
    ref["tile"][...] = jnp.zeros(TILE, F32)
    for k, (n, load) in enumerate(zip(VECTORS, vector_loads)):
        load.wait()
        width = ref["in_" + n].shape[0]
        ref["tile"][k : k + 1, 0:width] = ref["in_" + n][...].astype(F32).reshape(1, width)
    x = here.x
    grids = {w: ref[w].reshape(GRID + (NX * shard_rows(w), ref[w].shape[1])) for w, _ in WEIGHTS}
    grids["spare"] = ref["spare"].reshape(GRID + (NX * shard_rows("w_down"), SPARE))
    grids["small"] = ref["tiles"].reshape(GRID + (NX * TILE[0], TILE[1]))
    into, back = {}, {}
    for n, (p, (w, first, width, orders)) in enumerate(GATHER_PARTS.items()):
        into[p] = Gather(here, n, local[w], grids[w], pl.ds(first, width), orders, gather_sems)
    for n, (p, (a, first, width, orders, w, at)) in enumerate(REDUCE_PARTS.items()):
        out = outs[w].at[ALL, pl.ds(at, width)]
        back[p] = Reduce(here, n, grids[a], pl.ds(first, width), orders, got[p], stage[p], out, reduce_sems)

    def halves(r):
        return r.reshape(HALF)

    grad_low = halves(work.df).at[0]
    own, other = pl.ds(x * SHARE, SHARE), pl.ds((1 - x) * SHARE, SHARE)
    swap = {
        "tok": Swap(here, 0, tok.at[other], halves(work.x).at[:, x], tok.at[own], halves(work.x).at[:, x], swap_sems),
        "cot": Swap(here, 1, cot.at[other], halves(work.cot).at[:, x], cot.at[own], halves(work.cot).at[:, x], swap_sems),
        "proj": Swap(here, 2, proj_in, work.proj.at[x], proj_in, work.proj.at[x], swap_sems),
        "y": Swap(here, 3, halves(work.y).at[:, 1 - x], block_out.at[own], halves(work.y).at[:, x], block_out.at[own], swap_sems),
        "grad": Swap(here, 4, grad_low, grad_got, halves(work.dr).at[:, x], grad_own, swap_sems),
    }

    vectors = [getattr(work, n) for n in VECTORS]
    totals = [getattr(work, "d_" + n) for n in VECTORS]

    def setup():
        work.setup(work.proj, [seg[pl.ds(SHARE * x + b, 1), :].astype(F32) for b in range(SHARE)])

    def lower():
        def block(b):
            grad_low[b] = halves(work.dr)[b, 1 - x].astype(BF)

        blocks_of(SHARE, block)

    stages = {
        "setup": (1, setup),
        "spread": (1, lambda: spread_small(ref["tiles"], vectors)),
        "qkv": (3, work.qkv_block),
        "att": (2 * PAIRS, work.attend),
        "branch": (1, work.branch),
        "upb": (12, work.up_block),
        "down": (3, work.down_block),
        "ln2": (1, work.second_norm),
        "sums": (1, work.second_sums),
        "dz": (3, work.down_back),
        "uback": (2, work.up_back),
        "flip0": (1, partial(work.turn, "h1")),
        "gup": (6, work.up_grad),
        "nback": (1, work.first_norm_back),
        "datt": (3, work.att_back),
        "flip1": (1, partial(work.turn, "att")),
        "gout": (1, work.out_grad),
        "attb": (2 * PAIRS, work.attend_back),
        "tback": (2, work.tokens_back),
        "lower": (1, lower),
        "flip2": (1, partial(work.turn, "x")),
        "gqkv": (3, work.qkv_grad),
        "collect": (1, lambda: collect_small(ref["tiles"], totals)),
    }
    for p, (a, first, width, _, w, at) in REDUCE_PARTS.items():
        if w == "w_down":
            into_part = ref[a].at[ALL, pl.ds(first, width)]
            stages["g" + p] = (4, partial(work.down_grad, into_part, slice(at, at + width)))

    def act(steps, token):
        if token[-1] == "!":
            swap[token[:-1]].start()
        elif token[-1] == "?":
            swap[token[:-1]].arrive()
        else:
            steps[token[:-1]].step(int(token[-1]))

    def play(tokens, steps):
        tokens = [t.split("*") for t in tokens]
        tokens = [(t[0], int(t[1]) if len(t) > 1 else 1) for t in tokens]
        while tokens:
            name, _ = tokens[0]
            if name not in stages:
                act(steps, name)
                tokens.pop(0)
                continue
            count, body = stages[name]
            n, then = 0, []
            while n < count:
                token, times = tokens.pop(0)
                if token == name:
                    n += times
                else:
                    then.append((n - 1, partial(act, steps, token)))
            if count > 1:
                blocks_of(count, body, then)
            else:
                body()

    play(FORWARD, into)
    for part in into.values():
        part.drain()
    play(BACKWARD, back)
    swap["grad"].arrive()
    swap["y"].arrive()
    for each in swap.values():
        each.there.wait_send()
    for part in back.values():
        part.drain()


QUARTER = (SHARE, ROWS // SHARE // NX, D)
SPACE = (
    (("x", (ROWS, D), BF), ("cot", (ROWS, D), BF), ("y", (ROWS, D), BF), ("proj", (NX, DH, FEATS // NX), BF))
    + (("spare", (FF, SPARE), BF), ("tile", TILE, F32))
    + tuple(("in_" + n, (w // N_DEV,), BF) for n, w in zip(VECTORS, WIDTHS))
    + (("tiles", (N_DEV * TILE[0], TILE[1]), F32),)
    + tuple((n, (1, w), F32) for n, w in zip(VECTORS, WIDTHS))
    + tuple(("d_" + n, (1, w), F32) for n, w in zip(VECTORS, WIDTHS))
    + SPACE
)


def layer(tok, cot, weights, vectors, proj, seg):
    anywhere = pl.BlockSpec(memory_space=pl.ANY)
    vmem = pl.BlockSpec(memory_space=pltpu.VMEM)
    shape, dma = jax.ShapeDtypeStruct, pltpu.SemaphoreType.DMA
    received, stages = [], []
    for _, _, width, orders, w, _ in REDUCE_PARTS.values():
        kind = F32 if w == "small" else BF
        received += [pltpu.VMEM(s, kind) for shapes in got_shapes(orders, shard_rows(w), width) for s in shapes]
        stages.append(pltpu.VMEM((shard_rows(w), width), F32))
    there, back = len(GATHER_PARTS), len(REDUCE_PARTS)
    return pl.pallas_call(
        layer_kernel,
        out_shape=[shape(tok.shape, BF), shape(QUARTER, F32), shape(QUARTER, BF)]
        + [shape(w.shape, F32) for w in weights] + [shape(TILE, F32)],
        in_specs=[anywhere] * 15 + [vmem],
        out_specs=[anywhere] * 8,
        scratch_shapes=[pltpu.VMEM(s, BF) for _, s in WEIGHTS] + [pltpu.VMEM(s, d) for _, s, d in SPACE] + received + stages
        + [dma((there, 8)), dma((there, 8)), dma((there,)), dma((back, 9)), dma((back, 9)), dma((back,))]
        + [dma((5,)), dma((5,)), dma((5,)), dma((len(VECTORS),))],
        compiler_params=pltpu.CompilerParams(collective_id=0, has_side_effects=True, vmem_limit_bytes=62 << 20),
        name="layer",
    )(tok, cot, *weights, *vectors, proj, seg)


def finish_kernel(count, *refs):
    it = iter(refs)
    ins, own, got, tile = [next(it) for _ in range(count)], next(it), next(it), next(it)
    outs, grad = [next(it) for _ in range(count)], next(it)
    rows = [next(it) for _ in WIDTHS]
    spaces, got_space, grad_space, sems = [next(it) for _ in range(count)], next(it), next(it), next(it)
    x = lax.axis_index("feat")
    here, there = pl.ds(x * SHARE, SHARE), pl.ds((1 - x) * SHARE, SHARE)
    loads = [pltpu.make_async_copy(got, got_space, sems.at[0, count]), pltpu.make_async_copy(own, grad_space.at[here], sems.at[0, count + 1])]
    loads += [pltpu.make_async_copy(a, b, sems.at[0, n]) for n, (a, b) in enumerate(zip(ins, spaces))]
    stores = [pltpu.make_async_copy(a, b, sems.at[1, n]) for n, (a, b) in enumerate(zip(spaces, outs))]
    halves = [pltpu.make_async_copy(grad_space.at[h], grad.at[h], sems.at[1, count + n]) for n, h in enumerate((there, here))]
    for load in loads:
        load.start()
    for n, row in enumerate(rows):
        row[...] = tile[n, 0 : row.shape[0]]
    loads[0].wait()
    grad_space[there] = got_space[...].astype(F32)
    halves[0].start()
    loads[1].wait()
    halves[1].start()
    for load, store in zip(loads[2:], stores):
        load.wait()
        store.start()
    for store in stores + halves:
        store.wait()


def finish(arrays, own, got, tile):
    anywhere = pl.BlockSpec(memory_space=pl.ANY)
    vmem = pl.BlockSpec(memory_space=pltpu.VMEM)
    count = len(arrays)
    whole = (MICRO,) + own.shape[1:]
    return pl.pallas_call(
        partial(finish_kernel, count),
        out_shape=[jax.ShapeDtypeStruct(a.shape, a.dtype) for a in arrays] + [jax.ShapeDtypeStruct(whole, F32)]
        + [jax.ShapeDtypeStruct((w // N_DEV,), F32) for w in WIDTHS],
        in_specs=[anywhere] * (count + 2) + [vmem],
        out_specs=[anywhere] * (count + 1) + [vmem] * len(WIDTHS),
        scratch_shapes=[pltpu.VMEM(a.shape, a.dtype) for a in arrays]
        + [pltpu.VMEM(got.shape, BF), pltpu.VMEM(whole, F32), pltpu.SemaphoreType.DMA((2, count + 2))],
        name="finish",
    )(*arrays, own, got, tile)


def fast_device(
    tokens_in, out_cotangent, segment_ids, feature_proj,
    w_qkv, b_qkv, w_out, b_out, ln1_gain, ln1_bias, w_up, b_up, w_down, b_down, ln2_gain, ln2_bias,
):
    out, own, got, *sums, tile = layer(
        tokens_in, out_cotangent, [w_qkv, w_out, w_up, w_down],
        [b_qkv, b_out, ln1_gain, ln1_bias, b_up, b_down, ln2_gain, ln2_bias], feature_proj.T, segment_ids,
    )
    out, g_qkv, g_out, g_up, g_down, grad_tok, *vec = finish([out, *sums], own, got, tile)
    return out, grad_tok, g_qkv, vec[0], g_out, vec[1], vec[2], vec[3], g_up, vec[4], g_down, vec[5], vec[6], vec[7]


def solution(mesh):
    return jax.shard_map(
        fast_device if fits(mesh) else on_device,
        mesh=mesh,
        in_specs=(
            P(None, ("dp", "feat"), None),
            P(None, ("dp", "feat"), None),
            P(None, "dp"),
            P("feat", None),
            P(("dp", "feat"), None),
            P(("dp", "feat")),
            P(("dp", "feat"), None),
            P(("dp", "feat")),
            P(("dp", "feat")),
            P(("dp", "feat")),
            P(("dp", "feat"), None),
            P(("dp", "feat")),
            P(("dp", "feat"), None),
            P(("dp", "feat")),
            P(("dp", "feat")),
            P(("dp", "feat")),
        ),
        out_specs=(
            P(None, ("dp", "feat"), None),
            P(None, ("dp", "feat"), None),
            P(("dp", "feat"), None),
            P(("dp", "feat")),
            P(("dp", "feat"), None),
            P(("dp", "feat")),
            P(("dp", "feat")),
            P(("dp", "feat")),
            P(("dp", "feat"), None),
            P(("dp", "feat")),
            P(("dp", "feat"), None),
            P(("dp", "feat")),
            P(("dp", "feat")),
            P(("dp", "feat")),
        ),
        check_vma=False,
    )
```

```python
from functools import partial

import jax
import jax.numpy as jnp
from jax import lax
from jax.experimental import pallas as pl
from jax.experimental.pallas import tpu as pltpu
from jax.sharding import PartitionSpec as P

D = 768
H = 12
DH = 64
FEATS = 256
MICRO = 4
SEGS = 4


EPSILON = 1e-05


def layer_norm(residual, norm_gain, norm_shift):
    center = residual - jnp.mean(residual, -1, keepdims=True)
    spread = jnp.mean(center * center, -1, keepdims=True)
    return center * lax.rsqrt(spread + EPSILON) * norm_gain + norm_shift


def cross_dot(left_op, right_op):
    return lax.dot_general(
        left_op, right_op, (((0,), (0,)), ((), ())), preferred_element_type=jnp.float32
    )


def back_dot(left_op, right_op):
    return lax.dot_general(
        left_op, right_op, (((1,), (1,)), ((), ())), preferred_element_type=jnp.float32
    )


def fetch_weights(
    w_qkv, b_qkv, w_out, b_out, ln1_gain, ln1_bias, w_up, b_up, w_down, b_down, ln2_gain, ln2_bias
):
    return (
        lax.all_gather(w_qkv, ("dp", "feat"), axis=0, tiled=True),
        lax.all_gather(b_qkv, ("dp", "feat"), axis=0, tiled=True),
        lax.all_gather(w_out, ("dp", "feat"), axis=0, tiled=True),
        lax.all_gather(b_out, ("dp", "feat"), axis=0, tiled=True),
        lax.all_gather(ln1_gain, ("dp", "feat"), axis=0, tiled=True),
        lax.all_gather(ln1_bias, ("dp", "feat"), axis=0, tiled=True),
        lax.all_gather(w_up, ("dp", "feat"), axis=0, tiled=True),
        lax.all_gather(b_up, ("dp", "feat"), axis=0, tiled=True),
        lax.all_gather(w_down, ("dp", "feat"), axis=0, tiled=True),
        lax.all_gather(b_down, ("dp", "feat"), axis=0, tiled=True),
        lax.all_gather(ln2_gain, ("dp", "feat"), axis=0, tiled=True),
        lax.all_gather(ln2_bias, ("dp", "feat"), axis=0, tiled=True),
    )


def feature_map(head_rows, feat_proj):
    feat_scale = DH ** (-0.25)
    proj_arg = feat_scale * jnp.einsum(
        "ghd,md->ghm", head_rows, feat_proj, preferred_element_type=jnp.float32
    )
    squares = jnp.einsum("ghd,ghd->gh", head_rows, head_rows, preferred_element_type=jnp.float32)
    proj_arg = proj_arg - 0.5 * feat_scale * feat_scale * squares[:, :, None]
    return jnp.exp(proj_arg) * FEATS ** (-0.5)


def feature_back(head_rows, feat_proj, grad_arg):
    feat_scale = DH ** (-0.25)
    proj_back = feat_scale * jnp.einsum(
        "ghm,md->ghd", grad_arg, feat_proj, preferred_element_type=jnp.float32
    )
    arg_total = jnp.sum(grad_arg.astype(jnp.float32), -1, keepdims=True)
    return proj_back - feat_scale * feat_scale * head_rows.astype(jnp.float32) * arg_total


def spread_segments(phi_low, member):
    tok_count, head_count, feat_width = phi_low.shape
    return (phi_low[:, :, None, :] * member[:, None, :, None]).reshape(
        tok_count, head_count, SEGS * feat_width
    )


def fold_segments(grad_wide, member_f):
    tok_count, head_count, wide_dim = grad_wide.shape
    shaped = grad_wide.reshape(tok_count, head_count, SEGS, wide_dim // SEGS)
    return jnp.sum(shaped * member_f[:, None, :, None], 2)


def micro_step(tokens, cotangent, seg_row, feat_proj, weights):
    (
        w_qkv,
        b_qkv,
        w_out,
        b_out,
        ln1_gain,
        ln1_bias,
        w_up,
        b_up,
        w_down,
        b_down,
        ln2_gain,
        ln2_bias,
    ) = weights
    tok_count = tokens.shape[0]
    qkv_rows = jnp.dot(tokens, w_qkv, preferred_element_type=jnp.float32) + b_qkv.astype(
        jnp.float32
    )
    qkv_low = qkv_rows.astype(jnp.bfloat16)
    grouped = lax.all_gather(qkv_low, "feat", axis=0, tiled=True)
    group_rows = grouped.shape[0]
    query_h = grouped[:, :D].reshape(group_rows, H, DH)
    key_h = grouped[:, D : 2 * D].reshape(group_rows, H, DH)
    value_h = grouped[:, 2 * D :].reshape(group_rows, H, DH)
    phi_q = feature_map(query_h, feat_proj)
    phi_k = feature_map(key_h, feat_proj)
    member_f = (seg_row[:, None] == jnp.arange(SEGS, dtype=jnp.int32)[None, :]).astype(jnp.float32)
    member = member_f.astype(jnp.bfloat16)
    wide_q = spread_segments(phi_q.astype(jnp.bfloat16), member)
    wide_k = spread_segments(phi_k.astype(jnp.bfloat16), member)
    ones_col = jnp.ones((group_rows,), jnp.bfloat16)
    kv_part = jnp.einsum("gha,ghe->hae", wide_k, value_h, preferred_element_type=jnp.float32)
    z_part = jnp.einsum("gha,g->ha", wide_k, ones_col, preferred_element_type=jnp.float32)
    kv_low = kv_part.astype(jnp.bfloat16)
    z_low = z_part.astype(jnp.bfloat16)
    numer_part = jnp.einsum(
        "gha,hae->ghe", wide_q, kv_low, preferred_element_type=jnp.float32
    ).reshape(group_rows, D)
    denom_part = jnp.einsum("gha,ha->gh", wide_q, z_low, preferred_element_type=jnp.float32)
    numer_sum, denom_sum = (
        lax.psum_scatter(numer_part, "feat", scatter_dimension=0, tiled=True),
        lax.psum_scatter(denom_part, "feat", scatter_dimension=0, tiled=True),
    )
    numer_h = numer_sum.reshape(tok_count, H, DH)
    att_low = (numer_h / denom_sum[:, :, None]).reshape(tok_count, D).astype(jnp.bfloat16)
    branch = jnp.dot(att_low, w_out, preferred_element_type=jnp.float32) + b_out.astype(jnp.float32)
    hidden_one, ln1_back = jax.vjp(
        layer_norm,
        tokens.astype(jnp.float32) + branch,
        ln1_gain.astype(jnp.float32),
        ln1_bias.astype(jnp.float32),
    )
    hid_low = hidden_one.astype(jnp.bfloat16)
    pre_act = jnp.dot(hid_low, w_up, preferred_element_type=jnp.float32) + b_up.astype(jnp.float32)
    act_val, gelu_back = jax.vjp(partial(jax.nn.gelu, approximate=False), pre_act)
    act_low = act_val.astype(jnp.bfloat16)
    ffn_out = jnp.dot(act_low, w_down, preferred_element_type=jnp.float32) + b_down.astype(
        jnp.float32
    )
    result, ln2_back = jax.vjp(
        layer_norm, hidden_one + ffn_out, ln2_gain.astype(jnp.float32), ln2_bias.astype(jnp.float32)
    )
    grad_r2, grad_gain2, grad_bias2 = ln2_back(cotangent.astype(jnp.float32))
    grad_ffn = grad_r2.astype(jnp.bfloat16)
    grad_bdown = jnp.sum(grad_ffn.astype(jnp.float32), 0)
    grad_wdown = cross_dot(act_low, grad_ffn)
    (grad_act,) = gelu_back(back_dot(grad_ffn, w_down))
    grad_pre = grad_act.astype(jnp.bfloat16)
    grad_bup = jnp.sum(grad_pre.astype(jnp.float32), 0)
    grad_wup = cross_dot(hid_low, grad_pre)
    grad_h1 = grad_r2 + back_dot(grad_pre, w_up)
    grad_r1, grad_gain1, grad_bias1 = ln1_back(grad_h1)
    grad_branch = grad_r1.astype(jnp.bfloat16)
    grad_bout = jnp.sum(grad_branch.astype(jnp.float32), 0)
    grad_wout = cross_dot(att_low, grad_branch)
    grad_att = back_dot(grad_branch, w_out).reshape(tok_count, H, DH)
    grad_num = (grad_att / denom_sum[:, :, None]).reshape(tok_count, D).astype(jnp.bfloat16)
    grad_den = (-jnp.sum(grad_att * numer_h, -1) / (denom_sum * denom_sum)).astype(jnp.bfloat16)
    group_num, group_den = (
        lax.all_gather(grad_num, "feat", axis=0, tiled=True),
        lax.all_gather(grad_den, "feat", axis=0, tiled=True),
    )
    group_num_h = group_num.reshape(group_rows, H, DH)
    grad_kv_part = jnp.einsum(
        "gha,ghe->hae", wide_q, group_num_h, preferred_element_type=jnp.float32
    )
    grad_z_part = jnp.einsum("gha,gh->ha", wide_q, group_den, preferred_element_type=jnp.float32)
    grad_kv = grad_kv_part.astype(jnp.bfloat16)
    grad_z = grad_z_part.astype(jnp.bfloat16)
    wide_gq = jnp.einsum("ghe,hae->gha", group_num_h, kv_low, preferred_element_type=jnp.float32)
    wide_gq = wide_gq + group_den[:, :, None].astype(jnp.float32) * z_low[None].astype(jnp.float32)
    grad_arg_q = (fold_segments(wide_gq, member_f) * phi_q).astype(jnp.bfloat16)
    wide_gk = jnp.einsum(
        "ghe,hae->gha", value_h, grad_kv, preferred_element_type=jnp.float32
    ) + grad_z[None].astype(jnp.float32)
    grad_arg_k = (fold_segments(wide_gk, member_f) * phi_k).astype(jnp.bfloat16)
    grad_value = jnp.einsum("gha,hae->ghe", wide_k, grad_kv, preferred_element_type=jnp.float32)
    grad_query = feature_back(query_h, feat_proj, grad_arg_q)
    grad_key = feature_back(key_h, feat_proj, grad_arg_k)
    grad_group = jnp.concatenate(
        [
            grad_query.reshape(group_rows, D),
            grad_key.reshape(group_rows, D),
            grad_value.reshape(group_rows, D),
        ],
        1,
    )
    grad_qkv = lax.psum_scatter(
        grad_group.astype(jnp.bfloat16), "feat", scatter_dimension=0, tiled=True
    )
    grad_bqkv = jnp.sum(grad_qkv.astype(jnp.float32), 0)
    grad_wqkv = cross_dot(tokens, grad_qkv)
    grad_tokens = grad_r1 + back_dot(grad_qkv, w_qkv)
    grads_now = (
        grad_wqkv,
        grad_bqkv,
        grad_wout,
        grad_bout,
        grad_gain1,
        grad_bias1,
        grad_wup,
        grad_bup,
        grad_wdown,
        grad_bdown,
        grad_gain2,
        grad_bias2,
    )
    return (result.astype(jnp.bfloat16), grad_tokens, grads_now)


def on_device(
    tokens_in,
    out_cotangent,
    segment_ids,
    feature_proj,
    w_qkv,
    b_qkv,
    w_out,
    b_out,
    ln1_gain,
    ln1_bias,
    w_up,
    b_up,
    w_down,
    b_down,
    ln2_gain,
    ln2_bias,
):
    totals = None
    outputs = []
    grad_inputs = []
    for micro_idx in range(MICRO):
        gathered = fetch_weights(
            w_qkv,
            b_qkv,
            w_out,
            b_out,
            ln1_gain,
            ln1_bias,
            w_up,
            b_up,
            w_down,
            b_down,
            ln2_gain,
            ln2_bias,
        )
        result, grad_tokens, grads_now = micro_step(
            tokens_in[micro_idx],
            out_cotangent[micro_idx],
            segment_ids[micro_idx],
            feature_proj,
            gathered,
        )
        outputs.append(result)
        grad_inputs.append(grad_tokens)
        totals = grads_now if totals is None else jax.tree.map(jnp.add, totals, grads_now)
    (
        grad_wqkv,
        grad_bqkv,
        grad_wout,
        grad_bout,
        grad_gain1,
        grad_bias1,
        grad_wup,
        grad_bup,
        grad_wdown,
        grad_bdown,
        grad_gain2,
        grad_bias2,
    ) = totals
    summed = (
        lax.psum_scatter(grad_wqkv, ("dp", "feat"), scatter_dimension=0, tiled=True),
        lax.psum_scatter(grad_bqkv, ("dp", "feat"), scatter_dimension=0, tiled=True),
        lax.psum_scatter(grad_wout, ("dp", "feat"), scatter_dimension=0, tiled=True),
        lax.psum_scatter(grad_bout, ("dp", "feat"), scatter_dimension=0, tiled=True),
        lax.psum_scatter(grad_gain1, ("dp", "feat"), scatter_dimension=0, tiled=True),
        lax.psum_scatter(grad_bias1, ("dp", "feat"), scatter_dimension=0, tiled=True),
        lax.psum_scatter(grad_wup, ("dp", "feat"), scatter_dimension=0, tiled=True),
        lax.psum_scatter(grad_bup, ("dp", "feat"), scatter_dimension=0, tiled=True),
        lax.psum_scatter(grad_wdown, ("dp", "feat"), scatter_dimension=0, tiled=True),
        lax.psum_scatter(grad_bdown, ("dp", "feat"), scatter_dimension=0, tiled=True),
        lax.psum_scatter(grad_gain2, ("dp", "feat"), scatter_dimension=0, tiled=True),
        lax.psum_scatter(grad_bias2, ("dp", "feat"), scatter_dimension=0, tiled=True),
    )
    return (
        jnp.stack(outputs),
        jnp.stack(grad_inputs),
        summed[0],
        summed[1],
        summed[2],
        summed[3],
        summed[4],
        summed[5],
        summed[6],
        summed[7],
        summed[8],
        summed[9],
        summed[10],
        summed[11],
    )


NZ, NY, NC, NX = 4, 2, 2, 2
N_DEV = NZ * NY * NC * NX
MESH_ID = pl.DeviceIdType.MESH
BF = jnp.bfloat16
F32 = jnp.float32
SHARE = MICRO // NX
GRID = (NZ, NY, NC)
ALL = slice(None)


def fits(mesh):
    return mesh.shape["dp"] == NZ * NY * NC and mesh.shape["feat"] == NX


class Place:
    def __init__(self):
        i = lax.axis_index("dp")
        self.z, self.y, self.c, self.x = i // (NY * NC), (i // NC) % NY, i % NC, lax.axis_index("feat")
        self.sibling = self.device(c=1 - self.c)
        self.over = {"x": self.device(x=1 - self.x), "y": self.device(y=1 - self.y)}
        z = self.z
        self.to = {1: z <= 2, -1: z >= 1, 2: z <= 1, -2: z >= 2}
        self.had = {1: z >= 1, -1: z <= 2, 2: z >= 2, -2: z <= 1}

    def device(self, **other):
        z, y, c, x = (other.get(n, getattr(self, n)) for n in "zycx")
        return (z * (NY * NC) + y * NC + c, x)

    def meet(self):
        barrier = pltpu.get_barrier_semaphore()
        peers = [self.sibling, self.over["x"], self.over["y"]] + [self.device(z=lax.rem(self.z + k, NZ)) for k in (1, 2, 3)]
        for peer in peers:
            pl.semaphore_signal(barrier, inc=1, device_id=peer, device_id_type=MESH_ID)
        pl.semaphore_wait(barrier, len(peers))

    def per_class(self, orders, act):
        if orders[0] == orders[1]:
            act(orders[0])
            return
        for c in range(NC):

            @pl.when(self.c == c)
            def _(order=orders[c]):
                act(order)

    def rows(self, grid, x):
        share = grid.shape[3] // NX
        return pl.ds(pl.multiple_of(x * share, 8), share)

    def view(self, grid, cols, spread=(), **at):
        index = [ALL if n in spread else at.get(n, getattr(self, n)) for n in "zyc"]
        rows = ALL if "x" in spread else self.rows(grid, at.get("x", self.x))
        return grid.at[(*index, rows, cols)]


class Copies:
    def __init__(self, send_sems, recv_sems):
        self.send_sems, self.recv_sems = send_sems, recv_sems

    def copy(self, slot, src, dst, peer, sent=None):
        return pltpu.make_async_remote_copy(
            src_ref=src, dst_ref=dst, send_sem=self.send_sems.at[slot if sent is None else sent],
            recv_sem=self.recv_sems.at[slot], device_id=peer, device_id_type=MESH_ID,
        )


MOVES = (1, -1, 2, -2)


def stretch(order):
    return "".join("zZ" if n == "z" else n for n in order)


class Gather(Copies):
    def __init__(self, here, part, src, grid, cols, orders, sems):
        super().__init__(sems[0].at[part], sems[1].at[part])
        self.here, self.grid, self.cols, self.orders = here, grid, cols, tuple(stretch(o) for o in orders)
        self.src = src.at[ALL, cols]
        self.local = pltpu.make_async_copy(self.src, here.view(grid, cols), sems[2].at[part])

    def phase(self, order, n):
        here, dim = self.here, order[n]
        mine = here.view(self.grid, self.cols, order[:n].replace("Z", "").replace("z", "" if dim == "Z" else "z"))
        src = self.src if n == 0 else mine
        if dim == "z":
            return [
                (here.to[k], here.had[k], self.copy(s, src, mine, here.device(z=lax.rem(here.z + k + NZ, NZ))))
                for s, k in enumerate(MOVES)
            ]
        if dim == "Z":
            inner = (here.z == 1) | (here.z == 2)
            outer = (here.z == 0) | (here.z == 3)
            far = here.view(self.grid, self.cols, order[: n - 1], z=jnp.where(inner, 6 - 3 * here.z, 3 - here.z))
            return [(inner, outer, self.copy(4, far, far, here.device(z=jnp.where(inner, 3 * here.z - 3, 3 - here.z))))]
        return [(None, None, self.copy(5 + "xy".index(dim), src, mine, here.over[dim]))]

    def to_sibling(self):
        mine = self.here.view(self.grid, self.cols, "zyx")
        return self.copy(7, mine, mine, self.here.sibling)

    def step(self, n):
        here, last = self.here, len(self.orders[0])
        if n == 0:
            self.local.start()
            here.per_class(self.orders, lambda order: run_all("start", self.phase(order, 0)))
        elif n <= last:
            here.per_class(self.orders, lambda order: run_all("wait_recv", self.phase(order, n - 1)))
            if n == 1:
                self.local.wait()
            if n < last:
                here.per_class(self.orders, lambda order: run_all("start", self.phase(order, n)))
            else:
                self.to_sibling().start()
        else:
            self.to_sibling().wait_recv()

    def drain(self):
        for n in range(len(self.orders[0])):
            self.here.per_class(self.orders, lambda order, n=n: run_all("wait_send", self.phase(order, n)))
        self.to_sibling().wait_send()


def run_all(what, copies):
    for sends, gets, copy in copies:
        when(gets if what == "wait_recv" else sends, getattr(copy, what))


def when(condition, act):
    if condition is None:
        act()
        return

    @pl.when(condition)
    def _():
        act()


class Reduce(Copies):
    def __init__(self, here, part, grid, cols, orders, got, stage, out, sems):
        super().__init__(sems[0].at[part], sems[1].at[part])
        self.here, self.grid, self.cols, self.orders = here, grid, cols, tuple(stretch(o) for o in orders)
        self.got, self.stage = got, stage
        self.out = pltpu.make_async_copy(stage, out, sems[2].at[part])

    def from_sibling(self):
        here = self.here
        theirs = here.view(self.grid, self.cols, "zyx", c=1 - here.c)
        return self.copy(0, theirs, self.got[0][0], here.sibling)

    def received(self, order, n):
        at = order.replace("Z", "").index(order[n].lower()) + 1
        return self.got[at][self.orders.index(order) % len(self.got[at])]

    def phase(self, order, n):
        here, dim, rest = self.here, order[n], order[n + 1 :].replace("Z", "")
        got, z = self.received(order, n), here.z
        if dim == "z":
            aim = {1: z + 1, -1: z - 1, 2: 2, -2: 1}
            ends = {1: here.to[1], -1: here.to[-1], 2: z == 0, -2: z == 3}
            copies = [
                (ends[k], None, self.copy(3 + s, here.view(self.grid, self.cols, rest, z=aim[k]), got.at[s], here.device(z=aim[k])))
                for s, k in enumerate(MOVES)
            ]
            near = {2: (z == 0, 3, 1), -2: (z == 3, 0, 2)}
            first = [
                (near[k][0], None, self.copy(
                    3 + s, here.view(self.grid, self.cols, rest, z=near[k][1]), got.at[s], here.device(z=near[k][2]), 5 + s
                ))
                for s, k in enumerate(MOVES) if k in near
            ]
            return first + copies
        if dim == "Z":
            end = {2: (z == 1, 3), -2: (z == 2, 0)}
            return [
                (end[k][0], None, self.copy(3 + s, here.view(self.grid, self.cols, rest, z=end[k][1]), got.at[s], here.device(z=end[k][1])))
                for s, k in enumerate(MOVES) if k in end
            ]
        place = {dim: 1 - getattr(here, dim)}
        return [(None, None, self.copy(1 + "xy".index(dim), here.view(self.grid, self.cols, rest, **place), got, here.over[dim]))]

    def arrivals(self, order, n):
        here, got = self.here, self.received(order, n)
        if order[n] != "Z":
            (_, _, copy), = self.phase(order, n)
            return [(None, copy.wait_recv, got)]
        mine = here.view(self.grid, self.cols, order[n + 1 :])
        return [
            (here.had[k], self.copy(3 + s, mine, got.at[s], here.sibling).wait_recv, got.at[s]) for s, k in enumerate(MOVES)
        ]

    def spot(self, spread, q, z=None):
        here, index, inner = self.here, {} if z is None else {"z": z}, {}
        if "y" in spread:
            index["y"] = inner["y"] = q % NY
            q = q // NY
        if "z" in spread:
            index["z"] = inner["z"] = q
        rows = ALL if "x" in spread else here.rows(self.grid, here.x)
        return tuple(index.get(n, getattr(here, n)) for n in "zyc") + (rows, self.cols), tuple(inner[n] for n in "zy" if n in inner)

    def add(self, got, spread, z=None):
        def one(q):
            index, inner = self.spot(spread, q, z)
            self.grid[index] = self.grid[index] + got[inner + (ALL, ALL)]

        count = (NZ if "z" in spread else 1) * (NY if "y" in spread else 1)
        blocks_of(count, one) if count > 1 else one(0)

    def take(self, order, n):
        if order[n] == "z":
            return
        here, final = self.here, n == len(order) - 1
        if final:
            self.stage[...] = self.grid[self.spot((), 0)[0]].astype(F32)
        for condition, wait, got in self.arrivals(order, n):

            def one(wait=wait, got=got):
                wait()
                if final:
                    self.stage[...] += got[...].astype(F32)
                else:
                    self.add(got, order[n + 1 :].replace("Z", ""))

            when(condition, one)

    def send(self, order, n):
        copies = self.phase(order, n)
        if order[n] == "Z":
            got, rest = self.received(order, n), order[n + 1 :]
            for (condition, _, copy), (slot, end) in zip(copies, ((2, 3), (3, 0)), strict=True):

                def pass_on(copy=copy, slot=slot, end=end):
                    copy.wait_recv()
                    self.add(got.at[slot], rest, z=end)
                    copy.start()

                when(condition, pass_on)
        else:
            run_all("start", copies)

    def step(self, n):
        here, last = self.here, len(self.orders[0])
        if n == 0:
            self.from_sibling().start()
        elif n == 1:
            self.from_sibling().wait_recv()
            self.add(self.got[0][0], "zyx")
        else:
            here.per_class(self.orders, lambda order: self.take(order, n - 2))
        if 0 < n <= last:
            here.per_class(self.orders, lambda order: self.send(order, n - 1))
        elif n > last:
            self.out.start()

    def drain(self):
        self.from_sibling().wait_send()
        for n in range(len(self.orders[0])):
            self.here.per_class(self.orders, lambda order, n=n: run_all("wait_send", self.phase(order, n)))
        self.out.wait()


def got_shapes(orders, rows, width):
    first, second = (order_shapes(order, rows, width) for order in orders)
    return [(a,) if a == b else (a, b) for a, b in zip(first, second, strict=True)]


def order_shapes(order, rows, width):

    def block(spread):
        return tuple(dict(z=NZ, y=NY)[n] for n in "zy" if n in spread) + (rows * (NX if "x" in spread else 1), width)

    shapes = [block("zyx")]
    for n, dim in enumerate(order):
        shapes.append(((len(MOVES),) if dim == "z" else ()) + block(order[n + 1 :]))
    return shapes


def blocks_of(count, body, then=()):
    def step(j, carry):
        body(j)
        for at in sorted({at for at, _ in then}):

            @pl.when(j == at)
            def _(at=at):
                for when, act in then:
                    if when == at:
                        act()

        return carry

    lax.fori_loop(0, count, step, 0)


ROWS = 512
BLK = 256
PAIRS = D // 128
FF = 4 * D
WIDE = 2 * FEATS
SCALE = DH ** (-0.25)


def dot(a, b, ca=1, cb=0):
    return lax.dot_general(a, b, (((ca,), (cb,)), ((), ())), preferred_element_type=F32)


def half_masks(width):
    lane = lax.broadcasted_iota(jnp.int32, (1, width), 1) % 128
    first = (lane < DH).astype(F32)
    return first.astype(BF), (1.0 - first).astype(BF)


def lanes(j, width):
    return pl.ds(pl.multiple_of(j * width, width), width)


class Work:
    def __init__(self, refs):
        self.__dict__.update(refs)

    def setup(self, proj, seg_rows):
        row = lax.broadcasted_iota(jnp.int32, (DH, 128), 0)
        col = lax.broadcasted_iota(jnp.int32, (DH, 128), 1)
        for h in range(2):
            place_in = (col == row + h * DH).astype(BF)
            for n in range(NX):
                self.table[pl.ds(h * FEATS + n * 128, 128), 0:128] = dot(proj[n], place_in, 0, 0).astype(BF)
        feat = lax.broadcasted_iota(jnp.int32, (WIDE, 128), 0) // FEATS
        half = lax.broadcasted_iota(jnp.int32, (WIDE, 128), 1) // DH
        same = (feat == half).astype(F32).astype(BF)
        self.table[:, 128:256] = same
        self.flip[D:, :] = jnp.ones((16, ROWS), BF)
        for b in range(2):
            across = jnp.broadcast_to(seg_rows[b], (BLK, BLK))
            self.mask[b] = (across == jnp.transpose(across)).astype(F32).astype(BF)

    def features(self, rows):
        wide = rows.astype(F32)
        squares = wide * wide
        high = squares.astype(BF)
        low = (squares - high.astype(F32)).astype(BF)
        same = self.table[:, 128:256]
        norm = dot(high, same, 1, 1) + dot(low, same, 1, 1)
        arg = SCALE * dot(rows, self.table[:, 0:128], 1, 1) - (0.5 * SCALE * SCALE) * norm
        return (jnp.exp(arg) * FEATS ** (-0.5)).astype(BF)

    def qkv_block(self, j):
        col = lanes(j, D)
        full = dot(self.x[...], self.w_qkv[:, col]) + self.b_qkv[:, col]
        self.qkv[:, col] = full.astype(BF)

    def pair(self, i):
        b, p = i // PAIRS, i % PAIRS
        rows = pl.ds(pl.multiple_of(b * BLK, BLK), BLK)
        cols = [pl.ds(pl.multiple_of(n * D + p * 128, 128), 128) for n in range(3)]
        return b, rows, cols

    def attend(self, i):
        b, rows, cols = self.pair(i)
        mask = self.mask[b]
        m0, m1 = half_masks(128)
        phi_q = self.features(self.qkv[rows, cols[0]])
        phi_k = self.features(self.qkv[rows, cols[1]])
        self.phi_q[i] = phi_q
        self.phi_k[i] = phi_k
        v = self.qkv[rows, cols[2]]
        one = jnp.ones((BLK, 128), BF)
        res = None
        for h, m in enumerate((m0, m1)):
            part = slice(h * FEATS, (h + 1) * FEATS)
            score = dot(phi_q[:, part], phi_k[:, part], 1, 1).astype(BF) * mask
            term = dot(score, jnp.concatenate([v * m, one * m], 1))
            res = term if res is None else res + term
        inv = 1.0 / res[:, 128:]
        self.inv[rows, cols[0]] = inv
        self.att[rows, cols[0]] = (res[:, :128] * inv).astype(BF)

    def normalize(self, r):
        center = r - jnp.mean(r, -1, keepdims=True)
        scale = lax.rsqrt(jnp.mean(center * center, -1, keepdims=True) + EPSILON)
        return center * scale, scale

    def normalize_back(self, dy, n, scale, gain):
        g = dy * gain
        return (g - jnp.mean(g, -1, keepdims=True) - n * jnp.mean(g * n, -1, keepdims=True)) * scale

    def branch(self):
        for j in range(3):
            col = lanes(j, 256)
            self.n1[:, col] = dot(self.att[...], self.w_out[:, col]) + self.b_out[:, col] + self.x[:, col].astype(F32)

        def rows_of(j):
            row = pl.ds(pl.multiple_of(j * 128, 128), 128)
            n1, s1 = self.normalize(self.n1[row, :])
            self.n1[row, :] = n1
            self.s1[row, :] = s1
            self.h1[row, :] = (n1 * self.g1[...] + self.b1[...]).astype(BF)

        blocks_of(ROWS // 128, rows_of)

    def up_block(self, j):
        col = lanes(j, 256)
        for r in range(0, ROWS, 128):
            row = slice(r, r + 128)
            a = dot(self.h1[row, :], self.w_up[:, col]) + self.b_up[:, col]
            cdf = 0.5 * (1.0 + lax.erf(a * 2**-0.5))
            self.z[row, col] = (a * cdf).astype(BF)
            self.slope[row, col] = (cdf + a * jnp.exp(-0.5 * a * a) * (0.5 / 3.141592653589793) ** 0.5).astype(BF)

    def down_block(self, j):
        col = lanes(j, 256)
        back = self.n1[:, col] * self.g1[:, col] + self.b1[:, col]
        self.dr[:, col] = dot(self.z[...], self.w_down[:, col]) + self.b_down[:, col] + back

    def second_norm(self):
        self.d_g2[...] = jnp.zeros_like(self.d_g2)

        def rows_of(j):
            row = pl.ds(pl.multiple_of(j * 128, 128), 128)
            n2, s2 = self.normalize(self.dr[row, :])
            self.y[row, :] = (n2 * self.g2[...] + self.b2[...]).astype(BF)
            dy = self.cot[row, :].astype(F32)
            dr2 = self.normalize_back(dy, n2, s2, self.g2[...])
            self.dr[row, :] = dr2
            self.df[row, :] = dr2.astype(BF)
            self.d_g2[...] += jnp.sum(dy * n2, 0, keepdims=True)

        blocks_of(ROWS // 128, rows_of)

    def second_sums(self):
        ones = self.flip[D:, :]
        self.d_b2[...] = dot(ones, self.cot[...])[0:1]
        self.d_b_down[...] = dot(ones, self.df[...])[0:1]

    def down_back(self, j):
        col = lanes(j, 1024)
        dz = dot(self.df[...], self.w_down[col, :], 1, 1)
        self.slope[:, col] = (dz * self.slope[:, col].astype(F32)).astype(BF)

    def down_grad(self, into, part, j):
        col = lanes(j, D)
        into[col, :] = dot(self.z[:, col], self.df[:, part], 0, 0).astype(BF)

    def up_back(self, j):
        col = lanes(j, 384)
        self.dr[:, col] += dot(self.slope[...], self.w_up[col, :], 1, 1)

    def turn(self, name):
        self.flip[0:D, :] = jnp.transpose(getattr(self, name)[...])

    def weight_grad(self, weight, bias, col, grad):
        full = dot(self.flip[...], grad)
        weight[:, col] = full[0:D].astype(BF)
        bias[:, col] = full[D : D + 1]

    def up_grad(self, j):
        col = lanes(j, 512)
        self.weight_grad(self.w_up, self.d_b_up, col, self.slope[:, col])

    def first_norm_back(self):
        for ref in (self.d_g1, self.d_b1):
            ref[...] = jnp.zeros_like(ref)

        def rows_of(j):
            row = pl.ds(pl.multiple_of(j * 128, 128), 128)
            dh1, n1 = self.dr[row, :], self.n1[row, :]
            dr1 = self.normalize_back(dh1, n1, self.s1[row, :], self.g1[...])
            self.dr[row, :] = dr1
            self.df[row, :] = dr1.astype(BF)
            self.d_g1[...] += jnp.sum(dh1 * n1, 0, keepdims=True)
            self.d_b1[...] += jnp.sum(dh1, 0, keepdims=True)

        blocks_of(ROWS // 128, rows_of)

    def att_back(self, j):
        head_r = lax.broadcasted_iota(jnp.int32, (256, 256), 0) // DH
        head_c = lax.broadcasted_iota(jnp.int32, (256, 256), 1) // DH
        same = (head_r == head_c).astype(F32).astype(BF)
        col = lanes(j, 256)
        datt = dot(self.df[...], self.w_out[col, :], 1, 1)
        inv = self.inv[:, col]
        self.cot[:, col] = (datt * inv).astype(BF)
        prod = datt * self.att[:, col].astype(F32)
        high = prod.astype(BF)
        low = (prod - high.astype(F32)).astype(BF)
        total = dot(high, same) + dot(low, same)
        self.h1[:, col] = (-total * inv).astype(BF)

    def out_grad(self):
        col = slice(0, D)
        self.weight_grad(self.w_out, self.d_b_out, col, self.df[:, col])

    def attend_back(self, i):
        b, rows, cols = self.pair(i)
        mask = self.mask[b]
        m0, m1 = half_masks(256)
        q, k, v = (self.qkv[rows, c] for c in cols)
        dnum, dden = self.cot[rows, cols[0]], self.h1[rows, cols[0]]
        left = jnp.concatenate([dnum, dden * (1.0 / DH)], 1)
        right = jnp.concatenate([v, jnp.ones((BLK, 128), BF)], 1)
        back_q, back_k, dv = None, None, None
        for h, m in enumerate((m0, m1)):
            part = slice(h * FEATS, (h + 1) * FEATS)
            phi_q, phi_k = self.phi_q[i, :, part], self.phi_k[i, :, part]
            mine = left * m
            dscore = dot(mine, right, 1, 1).astype(BF) * mask
            flipped = dot(right, mine, 1, 1).astype(BF) * mask
            darg_q = (dot(dscore, phi_k) * phi_q.astype(F32)).astype(BF)
            darg_k = (dot(flipped, phi_q) * phi_k.astype(F32)).astype(BF)
            score = dot(phi_k, phi_q, 1, 1).astype(BF) * mask
            table = self.table[part, :]
            terms = dot(darg_q, table), dot(darg_k, table), dot(score, mine[:, :128])
            if h == 0:
                back_q, back_k, dv = terms
            else:
                back_q, back_k, dv = back_q + terms[0], back_k + terms[1], dv + terms[2]
        for n, (rows_in, back) in enumerate(((q, back_q), (k, back_k))):
            grad = SCALE * back[:, :128] - (SCALE * SCALE) * rows_in.astype(F32) * back[:, 128:]
            self.qkv[rows, cols[n]] = grad.astype(BF)
        self.qkv[rows, cols[2]] = dv.astype(BF)

    def tokens_back(self, j):
        col = lanes(j, 384)
        self.dr[:, col] += dot(self.qkv[...], self.w_qkv[col, :], 1, 1)

    def qkv_grad(self, j):
        col = lanes(j, D)
        self.weight_grad(self.w_qkv, self.d_b_qkv, col, self.qkv[:, col])


VECTORS = ("b_qkv", "b_out", "g1", "b1", "b_up", "b_down", "g2", "b2")
WIDTHS = (3 * D, D, D, D, FF, D, D, D)
SPACE = (
    ("qkv", (ROWS, 3 * D), BF), ("phi_q", (2 * PAIRS, BLK, WIDE), BF), ("phi_k", (2 * PAIRS, BLK, WIDE), BF),
    ("att", (ROWS, D), BF), ("inv", (ROWS, D), F32), ("n1", (ROWS, D), F32), ("s1", (ROWS, 1), F32),
    ("h1", (ROWS, D), BF), ("z", (ROWS, FF), BF), ("slope", (ROWS, FF), BF), ("dr", (ROWS, D), F32),
    ("df", (ROWS, D), BF), ("flip", (D + 16, ROWS), BF),
    ("table", (WIDE, 256), BF), ("mask", (2, BLK, BLK), BF),
)


GATHER_PARTS = {
    "small": ("small", 0, 128, ("zyx", "zxy")),
    "q": ("w_qkv", 0, 768, ("zyx", "zxy")),
    "k": ("w_qkv", 768, 768, ("zxy", "zxy")),
    "v": ("w_qkv", 1536, 768, ("zxy", "zxy")),
    "out": ("w_out", 0, 768, ("xzy", "yzx")),
    "up0": ("w_up", 0, 1024, ("zyx", "zxy")),
    "up1": ("w_up", 1024, 1024, ("xzy", "yzx")),
    "up2": ("w_up", 2048, 1024, ("xzy", "yzx")),
    "dn0": ("w_down", 0, 256, ("xyz", "xyz")),
    "dn1": ("w_down", 256, 256, ("zyx", "zxy")),
    "dn2": ("w_down", 512, 256, ("xzy", "yzx")),
}
REDUCE_PARTS = {
    "small": ("small", 0, 128, ("xyz", "yxz"), "small", 0),
    "q": ("w_qkv", 0, 768, ("xyz", "yxz"), "w_qkv", 0),
    "k": ("w_qkv", 768, 768, ("xyz", "yxz"), "w_qkv", 768),
    "v": ("w_qkv", 1536, 768, ("xyz", "yxz"), "w_qkv", 1536),
    "out": ("w_out", 0, 768, ("yxz", "yxz"), "w_out", 0),
    "up0": ("w_up", 0, 1536, ("yxz", "yxz"), "w_up", 0),
    "up1": ("w_up", 1536, 1536, ("xyz", "xyz"), "w_up", 1536),
    "dn0": ("spare", 0, 384, ("yzx", "xzy"), "w_down", 0),
    "dn1": ("w_down", 384, 384, ("yzx", "xzy"), "w_down", 384),
}
FORWARD = (
    "proj!", "small0", "tok!", "q0", "out0", "up10", "k0", "v0", "small1", "proj?", "setup", "q1", "k1", "small2",
    "up00", "q2", "dn10", "v1", "k2", "up20", "out1", "up11", "small3", "up01", "q3", "v2", "dn11", "dn20", "k3",
    "small4", "up21", "small5", "dn00", "spread", "q4", "out2", "q5", "cot!", "v3", "up02", "tok?", "qkv", "dn21",
    "dn12", "dn01", "k4", "up12", "k5", "qkv", "out3", "v4", "up22", "v5", "qkv", "att", "up03", "att", "up13",
    "dn13", "dn02", "att", "up23", "att", "dn22", "att", "out4", "att*3", "out5", "att", "up04", "att*3", "up05",
    "branch", "up14", "dn23", "upb*2", "dn03", "upb*2", "dn14", "up15", "upb*4", "dn15", "up24", "dn04", "up25",
    "upb*2", "dn24", "upb", "dn05", "upb", "down*2", "dn25", "down", "cot?", "ln2",
)
BACKWARD = (
    "y!", "gdn0*4", "dn00", "sums", "dz*3", "gdn1*2", "dn01", "gdn1*2", "dn10", "uback*2", "flip0", "gup*2", "dn11",
    "gup", "up00", "gup*3", "up10", "nback", "dn02", "up01", "datt*2", "up11", "datt", "flip1", "gout", "out0",
    "dn12", "attb*3", "out1", "attb*2", "dn03", "attb*5", "up02", "attb*2", "up12", "tback*2", "dn13", "lower",
    "flip2", "gqkv", "out2", "q0", "dn04", "gqkv", "k0", "up03", "gqkv", "v0", "q1", "dn14", "k1", "out3", "up13",
    "dn05", "v1", "collect", "up04", "small0", "q2", "dn15", "out4", "small1", "k2", "up14", "v2", "up05", "q3",
    "out5", "small2", "grad!", "k3", "up15", "small3", "v3", "q4", "k4", "small4", "v4", "q5", "k5", "small5", "v5",
)
WEIGHTS = (("w_qkv", (D, 3 * D)), ("w_out", (D, D)), ("w_up", (D, FF)), ("w_down", (FF, D)))
TILE = (8, 128)
SPARE = 384
HALF = (SHARE, NX, ROWS // SHARE // NX, D)


def shard_rows(weight):
    return TILE[0] if weight == "small" else dict(WEIGHTS)[weight][0] // N_DEV


class Swap:
    def __init__(self, here, n, theirs, target, mine, home, sems):
        self.there = pltpu.make_async_remote_copy(
            src_ref=theirs, dst_ref=target, send_sem=sems[0].at[n], recv_sem=sems[1].at[n],
            device_id=here.over["x"], device_id_type=MESH_ID,
        )
        self.here = None if home is None else pltpu.make_async_copy(mine, home, sems[2].at[n])

    def start(self):
        self.there.start()
        if self.here is not None:
            self.here.start()

    def arrive(self):
        self.there.wait_recv()
        if self.here is not None:
            self.here.wait()


def one_hot(width, count):
    at = lax.broadcasted_iota(jnp.int32, (1, count), 1).astype(F32)
    owner = jnp.floor((at + 0.5) * (1.0 / width))
    lane = at - owner * width
    lanes_hot = (lax.broadcasted_iota(jnp.int32, (128, count), 0).astype(F32) == lane).astype(F32).astype(BF)
    owner_hot = (lax.broadcasted_iota(jnp.int32, (N_DEV, count), 0).astype(F32) == owner).astype(F32)
    return lanes_hot, owner_hot


def spread_small(tiles, vectors):
    for width in sorted({v.shape[1] // N_DEV for v in vectors}):
        hot, owner = one_hot(width, width * N_DEV)
        for n, vector in enumerate(vectors):
            if vector.shape[1] == width * N_DEV:
                rows = tiles[pl.ds(n, N_DEV, stride=TILE[0]), :].astype(BF)
                vector[...] = jnp.sum(dot(rows, hot) * owner, 0, keepdims=True)


def collect_small(tiles, vectors):
    for width in sorted({v.shape[1] // N_DEV for v in vectors}):
        hot, owner = one_hot(width, width * N_DEV)
        for n, vector in enumerate(vectors):
            if vector.shape[1] == width * N_DEV:
                full = owner * vector[...]
                high = full.astype(BF)
                low = (full - high.astype(F32)).astype(BF)
                tiles[pl.ds(n, N_DEV, stride=TILE[0]), :] = dot(high, hot, 1, 1) + dot(low, hot, 1, 1)


def layer_kernel(*refs):
    it = iter(refs)
    tok, cot = next(it), next(it)
    local = {w: next(it) for w, _ in WEIGHTS}
    own_vectors = [next(it) for _ in VECTORS]
    proj_in, seg = next(it), next(it)
    block_out, grad_own, grad_got = next(it), next(it), next(it)
    outs = {w: next(it) for w, _ in WEIGHTS}
    outs["small"] = next(it)
    ref = {n: next(it) for n, _ in WEIGHTS}
    ref.update({n: next(it) for n, _, _ in SPACE})
    work = Work(ref)
    got = {
        p: [tuple(next(it) for _ in shapes) for shapes in got_shapes(orders, shard_rows(w), width)]
        for p, (_, _, width, orders, w, _) in REDUCE_PARTS.items()
    }
    stage = {p: next(it) for p in REDUCE_PARTS}
    gather_sems = [next(it) for _ in range(3)]
    reduce_sems = [next(it) for _ in range(3)]
    swap_sems = [next(it) for _ in range(3)]
    vector_sems = next(it)

    vector_loads = [pltpu.make_async_copy(v, ref["in_" + n], vector_sems.at[k]) for k, (n, v) in enumerate(zip(VECTORS, own_vectors))]
    for load in vector_loads:
        load.start()
    here = Place()
    here.meet()
    local["small"] = ref["tile"]
    ref["tile"][...] = jnp.zeros(TILE, F32)
    for k, (n, load) in enumerate(zip(VECTORS, vector_loads)):
        load.wait()
        width = ref["in_" + n].shape[0]
        ref["tile"][k : k + 1, 0:width] = ref["in_" + n][...].astype(F32).reshape(1, width)
    x = here.x
    grids = {w: ref[w].reshape(GRID + (NX * shard_rows(w), ref[w].shape[1])) for w, _ in WEIGHTS}
    grids["spare"] = ref["spare"].reshape(GRID + (NX * shard_rows("w_down"), SPARE))
    grids["small"] = ref["tiles"].reshape(GRID + (NX * TILE[0], TILE[1]))
    into, back = {}, {}
    for n, (p, (w, first, width, orders)) in enumerate(GATHER_PARTS.items()):
        into[p] = Gather(here, n, local[w], grids[w], pl.ds(first, width), orders, gather_sems)
    for n, (p, (a, first, width, orders, w, at)) in enumerate(REDUCE_PARTS.items()):
        out = outs[w].at[ALL, pl.ds(at, width)]
        back[p] = Reduce(here, n, grids[a], pl.ds(first, width), orders, got[p], stage[p], out, reduce_sems)

    def halves(r):
        return r.reshape(HALF)

    grad_low = halves(work.df).at[0]
    own, other = pl.ds(x * SHARE, SHARE), pl.ds((1 - x) * SHARE, SHARE)
    swap = {
        "tok": Swap(here, 0, tok.at[other], halves(work.x).at[:, x], tok.at[own], halves(work.x).at[:, x], swap_sems),
        "cot": Swap(here, 1, cot.at[other], halves(work.cot).at[:, x], cot.at[own], halves(work.cot).at[:, x], swap_sems),
        "proj": Swap(here, 2, proj_in, work.proj.at[x], proj_in, work.proj.at[x], swap_sems),
        "y": Swap(here, 3, halves(work.y).at[:, 1 - x], block_out.at[own], halves(work.y).at[:, x], block_out.at[own], swap_sems),
        "grad": Swap(here, 4, grad_low, grad_got, halves(work.dr).at[:, x], grad_own, swap_sems),
    }

    vectors = [getattr(work, n) for n in VECTORS]
    totals = [getattr(work, "d_" + n) for n in VECTORS]

    def setup():
        work.setup(work.proj, [seg[pl.ds(SHARE * x + b, 1), :].astype(F32) for b in range(SHARE)])

    def lower():
        def block(b):
            grad_low[b] = halves(work.dr)[b, 1 - x].astype(BF)

        blocks_of(SHARE, block)

    stages = {
        "setup": (1, setup),
        "spread": (1, lambda: spread_small(ref["tiles"], vectors)),
        "qkv": (3, work.qkv_block),
        "att": (2 * PAIRS, work.attend),
        "branch": (1, work.branch),
        "upb": (12, work.up_block),
        "down": (3, work.down_block),
        "ln2": (1, work.second_norm),
        "sums": (1, work.second_sums),
        "dz": (3, work.down_back),
        "uback": (2, work.up_back),
        "flip0": (1, partial(work.turn, "h1")),
        "gup": (6, work.up_grad),
        "nback": (1, work.first_norm_back),
        "datt": (3, work.att_back),
        "flip1": (1, partial(work.turn, "att")),
        "gout": (1, work.out_grad),
        "attb": (2 * PAIRS, work.attend_back),
        "tback": (2, work.tokens_back),
        "lower": (1, lower),
        "flip2": (1, partial(work.turn, "x")),
        "gqkv": (3, work.qkv_grad),
        "collect": (1, lambda: collect_small(ref["tiles"], totals)),
    }
    for p, (a, first, width, _, w, at) in REDUCE_PARTS.items():
        if w == "w_down":
            into_part = ref[a].at[ALL, pl.ds(first, width)]
            stages["g" + p] = (4, partial(work.down_grad, into_part, slice(at, at + width)))

    def act(steps, token):
        if token[-1] == "!":
            swap[token[:-1]].start()
        elif token[-1] == "?":
            swap[token[:-1]].arrive()
        else:
            steps[token[:-1]].step(int(token[-1]))

    def play(tokens, steps):
        tokens = [t.split("*") for t in tokens]
        tokens = [(t[0], int(t[1]) if len(t) > 1 else 1) for t in tokens]
        while tokens:
            name, _ = tokens[0]
            if name not in stages:
                act(steps, name)
                tokens.pop(0)
                continue
            count, body = stages[name]
            n, then = 0, []
            while n < count:
                token, times = tokens.pop(0)
                if token == name:
                    n += times
                else:
                    then.append((n - 1, partial(act, steps, token)))
            if count > 1:
                blocks_of(count, body, then)
            else:
                body()

    play(FORWARD, into)
    for part in into.values():
        part.drain()
    play(BACKWARD, back)
    swap["grad"].arrive()
    swap["y"].arrive()
    for each in swap.values():
        each.there.wait_send()
    for part in back.values():
        part.drain()


QUARTER = (SHARE, ROWS // SHARE // NX, D)
SPACE = (
    (("x", (ROWS, D), BF), ("cot", (ROWS, D), BF), ("y", (ROWS, D), BF), ("proj", (NX, DH, FEATS // NX), BF))
    + (("spare", (FF, SPARE), BF), ("tile", TILE, F32))
    + tuple(("in_" + n, (w // N_DEV,), BF) for n, w in zip(VECTORS, WIDTHS))
    + (("tiles", (N_DEV * TILE[0], TILE[1]), F32),)
    + tuple((n, (1, w), F32) for n, w in zip(VECTORS, WIDTHS))
    + tuple(("d_" + n, (1, w), F32) for n, w in zip(VECTORS, WIDTHS))
    + SPACE
)


def layer(tok, cot, weights, vectors, proj, seg):
    anywhere = pl.BlockSpec(memory_space=pl.ANY)
    vmem = pl.BlockSpec(memory_space=pltpu.VMEM)
    shape, dma = jax.ShapeDtypeStruct, pltpu.SemaphoreType.DMA
    received, stages = [], []
    for _, _, width, orders, w, _ in REDUCE_PARTS.values():
        kind = F32 if w == "small" else BF
        received += [pltpu.VMEM(s, kind) for shapes in got_shapes(orders, shard_rows(w), width) for s in shapes]
        stages.append(pltpu.VMEM((shard_rows(w), width), F32))
    there, back = len(GATHER_PARTS), len(REDUCE_PARTS)
    return pl.pallas_call(
        layer_kernel,
        out_shape=[shape(tok.shape, BF), shape(QUARTER, F32), shape(QUARTER, BF)]
        + [shape(w.shape, F32) for w in weights] + [shape(TILE, F32)],
        in_specs=[anywhere] * 15 + [vmem],
        out_specs=[anywhere] * 8,
        scratch_shapes=[pltpu.VMEM(s, BF) for _, s in WEIGHTS] + [pltpu.VMEM(s, d) for _, s, d in SPACE] + received + stages
        + [dma((there, 8)), dma((there, 8)), dma((there,)), dma((back, 9)), dma((back, 9)), dma((back,))]
        + [dma((5,)), dma((5,)), dma((5,)), dma((len(VECTORS),))],
        compiler_params=pltpu.CompilerParams(collective_id=0, has_side_effects=True, vmem_limit_bytes=63 << 20),
        name="layer",
    )(tok, cot, *weights, *vectors, proj, seg)


def finish_kernel(count, *refs):
    it = iter(refs)
    ins, own, got, tile = [next(it) for _ in range(count)], next(it), next(it), next(it)
    outs, grad = [next(it) for _ in range(count)], next(it)
    rows = [next(it) for _ in WIDTHS]
    spaces, got_space, grad_space, sems = [next(it) for _ in range(count)], next(it), next(it), next(it)
    x = lax.axis_index("feat")
    here, there = pl.ds(x * SHARE, SHARE), pl.ds((1 - x) * SHARE, SHARE)
    loads = [pltpu.make_async_copy(got, got_space, sems.at[0, count]), pltpu.make_async_copy(own, grad_space.at[here], sems.at[0, count + 1])]
    loads += [pltpu.make_async_copy(a, b, sems.at[0, n]) for n, (a, b) in enumerate(zip(ins, spaces))]
    stores = [pltpu.make_async_copy(a, b, sems.at[1, n]) for n, (a, b) in enumerate(zip(spaces, outs))]
    halves = [pltpu.make_async_copy(grad_space.at[h], grad.at[h], sems.at[1, count + n]) for n, h in enumerate((there, here))]
    for load in loads:
        load.start()
    for n, row in enumerate(rows):
        row[...] = tile[n, 0 : row.shape[0]]
    loads[0].wait()
    grad_space[there] = got_space[...].astype(F32)
    halves[0].start()
    loads[1].wait()
    halves[1].start()
    for load, store in zip(loads[2:], stores):
        load.wait()
        store.start()
    for store in stores + halves:
        store.wait()


def finish(arrays, own, got, tile):
    anywhere = pl.BlockSpec(memory_space=pl.ANY)
    vmem = pl.BlockSpec(memory_space=pltpu.VMEM)
    count = len(arrays)
    whole = (MICRO,) + own.shape[1:]
    return pl.pallas_call(
        partial(finish_kernel, count),
        out_shape=[jax.ShapeDtypeStruct(a.shape, a.dtype) for a in arrays] + [jax.ShapeDtypeStruct(whole, F32)]
        + [jax.ShapeDtypeStruct((w // N_DEV,), F32) for w in WIDTHS],
        in_specs=[anywhere] * (count + 2) + [vmem],
        out_specs=[anywhere] * (count + 1) + [vmem] * len(WIDTHS),
        scratch_shapes=[pltpu.VMEM(a.shape, a.dtype) for a in arrays]
        + [pltpu.VMEM(got.shape, BF), pltpu.VMEM(whole, F32), pltpu.SemaphoreType.DMA((2, count + 2))],
        name="finish",
    )(*arrays, own, got, tile)


def fast_device(
    tokens_in, out_cotangent, segment_ids, feature_proj,
    w_qkv, b_qkv, w_out, b_out, ln1_gain, ln1_bias, w_up, b_up, w_down, b_down, ln2_gain, ln2_bias,
):
    out, own, got, *sums, tile = layer(
        tokens_in, out_cotangent, [w_qkv, w_out, w_up, w_down],
        [b_qkv, b_out, ln1_gain, ln1_bias, b_up, b_down, ln2_gain, ln2_bias], feature_proj.T, segment_ids,
    )
    out, g_qkv, g_out, g_up, g_down, grad_tok, *vec = finish([out, *sums], own, got, tile)
    return out, grad_tok, g_qkv, vec[0], g_out, vec[1], vec[2], vec[3], g_up, vec[4], g_down, vec[5], vec[6], vec[7]


def solution(mesh):
    return jax.shard_map(
        fast_device if fits(mesh) else on_device,
        mesh=mesh,
        in_specs=(
            P(None, ("dp", "feat"), None),
            P(None, ("dp", "feat"), None),
            P(None, "dp"),
            P("feat", None),
            P(("dp", "feat"), None),
            P(("dp", "feat")),
            P(("dp", "feat"), None),
            P(("dp", "feat")),
            P(("dp", "feat")),
            P(("dp", "feat")),
            P(("dp", "feat"), None),
            P(("dp", "feat")),
            P(("dp", "feat"), None),
            P(("dp", "feat")),
            P(("dp", "feat")),
            P(("dp", "feat")),
        ),
        out_specs=(
            P(None, ("dp", "feat"), None),
            P(None, ("dp", "feat"), None),
            P(("dp", "feat"), None),
            P(("dp", "feat")),
            P(("dp", "feat"), None),
            P(("dp", "feat")),
            P(("dp", "feat")),
            P(("dp", "feat")),
            P(("dp", "feat"), None),
            P(("dp", "feat")),
            P(("dp", "feat"), None),
            P(("dp", "feat")),
            P(("dp", "feat")),
            P(("dp", "feat")),
        ),
        check_vma=False,
    )
```

```python
from functools import partial

import jax
import jax.numpy as jnp
from jax import lax
from jax.experimental import pallas as pl
from jax.experimental.pallas import tpu as pltpu
from jax.sharding import PartitionSpec as P

D = 768
H = 12
DH = 64
FEATS = 256
MICRO = 4
SEGS = 4


EPSILON = 1e-05


def layer_norm(residual, norm_gain, norm_shift):
    center = residual - jnp.mean(residual, -1, keepdims=True)
    spread = jnp.mean(center * center, -1, keepdims=True)
    return center * lax.rsqrt(spread + EPSILON) * norm_gain + norm_shift


def cross_dot(left_op, right_op):
    return lax.dot_general(
        left_op, right_op, (((0,), (0,)), ((), ())), preferred_element_type=jnp.float32
    )


def back_dot(left_op, right_op):
    return lax.dot_general(
        left_op, right_op, (((1,), (1,)), ((), ())), preferred_element_type=jnp.float32
    )


def fetch_weights(
    w_qkv, b_qkv, w_out, b_out, ln1_gain, ln1_bias, w_up, b_up, w_down, b_down, ln2_gain, ln2_bias
):
    return (
        lax.all_gather(w_qkv, ("dp", "feat"), axis=0, tiled=True),
        lax.all_gather(b_qkv, ("dp", "feat"), axis=0, tiled=True),
        lax.all_gather(w_out, ("dp", "feat"), axis=0, tiled=True),
        lax.all_gather(b_out, ("dp", "feat"), axis=0, tiled=True),
        lax.all_gather(ln1_gain, ("dp", "feat"), axis=0, tiled=True),
        lax.all_gather(ln1_bias, ("dp", "feat"), axis=0, tiled=True),
        lax.all_gather(w_up, ("dp", "feat"), axis=0, tiled=True),
        lax.all_gather(b_up, ("dp", "feat"), axis=0, tiled=True),
        lax.all_gather(w_down, ("dp", "feat"), axis=0, tiled=True),
        lax.all_gather(b_down, ("dp", "feat"), axis=0, tiled=True),
        lax.all_gather(ln2_gain, ("dp", "feat"), axis=0, tiled=True),
        lax.all_gather(ln2_bias, ("dp", "feat"), axis=0, tiled=True),
    )


def feature_map(head_rows, feat_proj):
    feat_scale = DH ** (-0.25)
    proj_arg = feat_scale * jnp.einsum(
        "ghd,md->ghm", head_rows, feat_proj, preferred_element_type=jnp.float32
    )
    squares = jnp.einsum("ghd,ghd->gh", head_rows, head_rows, preferred_element_type=jnp.float32)
    proj_arg = proj_arg - 0.5 * feat_scale * feat_scale * squares[:, :, None]
    return jnp.exp(proj_arg) * FEATS ** (-0.5)


def feature_back(head_rows, feat_proj, grad_arg):
    feat_scale = DH ** (-0.25)
    proj_back = feat_scale * jnp.einsum(
        "ghm,md->ghd", grad_arg, feat_proj, preferred_element_type=jnp.float32
    )
    arg_total = jnp.sum(grad_arg.astype(jnp.float32), -1, keepdims=True)
    return proj_back - feat_scale * feat_scale * head_rows.astype(jnp.float32) * arg_total


def spread_segments(phi_low, member):
    tok_count, head_count, feat_width = phi_low.shape
    return (phi_low[:, :, None, :] * member[:, None, :, None]).reshape(
        tok_count, head_count, SEGS * feat_width
    )


def fold_segments(grad_wide, member_f):
    tok_count, head_count, wide_dim = grad_wide.shape
    shaped = grad_wide.reshape(tok_count, head_count, SEGS, wide_dim // SEGS)
    return jnp.sum(shaped * member_f[:, None, :, None], 2)


def micro_step(tokens, cotangent, seg_row, feat_proj, weights):
    (
        w_qkv,
        b_qkv,
        w_out,
        b_out,
        ln1_gain,
        ln1_bias,
        w_up,
        b_up,
        w_down,
        b_down,
        ln2_gain,
        ln2_bias,
    ) = weights
    tok_count = tokens.shape[0]
    qkv_rows = jnp.dot(tokens, w_qkv, preferred_element_type=jnp.float32) + b_qkv.astype(
        jnp.float32
    )
    qkv_low = qkv_rows.astype(jnp.bfloat16)
    grouped = lax.all_gather(qkv_low, "feat", axis=0, tiled=True)
    group_rows = grouped.shape[0]
    query_h = grouped[:, :D].reshape(group_rows, H, DH)
    key_h = grouped[:, D : 2 * D].reshape(group_rows, H, DH)
    value_h = grouped[:, 2 * D :].reshape(group_rows, H, DH)
    phi_q = feature_map(query_h, feat_proj)
    phi_k = feature_map(key_h, feat_proj)
    member_f = (seg_row[:, None] == jnp.arange(SEGS, dtype=jnp.int32)[None, :]).astype(jnp.float32)
    member = member_f.astype(jnp.bfloat16)
    wide_q = spread_segments(phi_q.astype(jnp.bfloat16), member)
    wide_k = spread_segments(phi_k.astype(jnp.bfloat16), member)
    ones_col = jnp.ones((group_rows,), jnp.bfloat16)
    kv_part = jnp.einsum("gha,ghe->hae", wide_k, value_h, preferred_element_type=jnp.float32)
    z_part = jnp.einsum("gha,g->ha", wide_k, ones_col, preferred_element_type=jnp.float32)
    kv_low = kv_part.astype(jnp.bfloat16)
    z_low = z_part.astype(jnp.bfloat16)
    numer_part = jnp.einsum(
        "gha,hae->ghe", wide_q, kv_low, preferred_element_type=jnp.float32
    ).reshape(group_rows, D)
    denom_part = jnp.einsum("gha,ha->gh", wide_q, z_low, preferred_element_type=jnp.float32)
    numer_sum, denom_sum = (
        lax.psum_scatter(numer_part, "feat", scatter_dimension=0, tiled=True),
        lax.psum_scatter(denom_part, "feat", scatter_dimension=0, tiled=True),
    )
    numer_h = numer_sum.reshape(tok_count, H, DH)
    att_low = (numer_h / denom_sum[:, :, None]).reshape(tok_count, D).astype(jnp.bfloat16)
    branch = jnp.dot(att_low, w_out, preferred_element_type=jnp.float32) + b_out.astype(jnp.float32)
    hidden_one, ln1_back = jax.vjp(
        layer_norm,
        tokens.astype(jnp.float32) + branch,
        ln1_gain.astype(jnp.float32),
        ln1_bias.astype(jnp.float32),
    )
    hid_low = hidden_one.astype(jnp.bfloat16)
    pre_act = jnp.dot(hid_low, w_up, preferred_element_type=jnp.float32) + b_up.astype(jnp.float32)
    act_val, gelu_back = jax.vjp(partial(jax.nn.gelu, approximate=False), pre_act)
    act_low = act_val.astype(jnp.bfloat16)
    ffn_out = jnp.dot(act_low, w_down, preferred_element_type=jnp.float32) + b_down.astype(
        jnp.float32
    )
    result, ln2_back = jax.vjp(
        layer_norm, hidden_one + ffn_out, ln2_gain.astype(jnp.float32), ln2_bias.astype(jnp.float32)
    )
    grad_r2, grad_gain2, grad_bias2 = ln2_back(cotangent.astype(jnp.float32))
    grad_ffn = grad_r2.astype(jnp.bfloat16)
    grad_bdown = jnp.sum(grad_ffn.astype(jnp.float32), 0)
    grad_wdown = cross_dot(act_low, grad_ffn)
    (grad_act,) = gelu_back(back_dot(grad_ffn, w_down))
    grad_pre = grad_act.astype(jnp.bfloat16)
    grad_bup = jnp.sum(grad_pre.astype(jnp.float32), 0)
    grad_wup = cross_dot(hid_low, grad_pre)
    grad_h1 = grad_r2 + back_dot(grad_pre, w_up)
    grad_r1, grad_gain1, grad_bias1 = ln1_back(grad_h1)
    grad_branch = grad_r1.astype(jnp.bfloat16)
    grad_bout = jnp.sum(grad_branch.astype(jnp.float32), 0)
    grad_wout = cross_dot(att_low, grad_branch)
    grad_att = back_dot(grad_branch, w_out).reshape(tok_count, H, DH)
    grad_num = (grad_att / denom_sum[:, :, None]).reshape(tok_count, D).astype(jnp.bfloat16)
    grad_den = (-jnp.sum(grad_att * numer_h, -1) / (denom_sum * denom_sum)).astype(jnp.bfloat16)
    group_num, group_den = (
        lax.all_gather(grad_num, "feat", axis=0, tiled=True),
        lax.all_gather(grad_den, "feat", axis=0, tiled=True),
    )
    group_num_h = group_num.reshape(group_rows, H, DH)
    grad_kv_part = jnp.einsum(
        "gha,ghe->hae", wide_q, group_num_h, preferred_element_type=jnp.float32
    )
    grad_z_part = jnp.einsum("gha,gh->ha", wide_q, group_den, preferred_element_type=jnp.float32)
    grad_kv = grad_kv_part.astype(jnp.bfloat16)
    grad_z = grad_z_part.astype(jnp.bfloat16)
    wide_gq = jnp.einsum("ghe,hae->gha", group_num_h, kv_low, preferred_element_type=jnp.float32)
    wide_gq = wide_gq + group_den[:, :, None].astype(jnp.float32) * z_low[None].astype(jnp.float32)
    grad_arg_q = (fold_segments(wide_gq, member_f) * phi_q).astype(jnp.bfloat16)
    wide_gk = jnp.einsum(
        "ghe,hae->gha", value_h, grad_kv, preferred_element_type=jnp.float32
    ) + grad_z[None].astype(jnp.float32)
    grad_arg_k = (fold_segments(wide_gk, member_f) * phi_k).astype(jnp.bfloat16)
    grad_value = jnp.einsum("gha,hae->ghe", wide_k, grad_kv, preferred_element_type=jnp.float32)
    grad_query = feature_back(query_h, feat_proj, grad_arg_q)
    grad_key = feature_back(key_h, feat_proj, grad_arg_k)
    grad_group = jnp.concatenate(
        [
            grad_query.reshape(group_rows, D),
            grad_key.reshape(group_rows, D),
            grad_value.reshape(group_rows, D),
        ],
        1,
    )
    grad_qkv = lax.psum_scatter(
        grad_group.astype(jnp.bfloat16), "feat", scatter_dimension=0, tiled=True
    )
    grad_bqkv = jnp.sum(grad_qkv.astype(jnp.float32), 0)
    grad_wqkv = cross_dot(tokens, grad_qkv)
    grad_tokens = grad_r1 + back_dot(grad_qkv, w_qkv)
    grads_now = (
        grad_wqkv,
        grad_bqkv,
        grad_wout,
        grad_bout,
        grad_gain1,
        grad_bias1,
        grad_wup,
        grad_bup,
        grad_wdown,
        grad_bdown,
        grad_gain2,
        grad_bias2,
    )
    return (result.astype(jnp.bfloat16), grad_tokens, grads_now)


def on_device(
    tokens_in,
    out_cotangent,
    segment_ids,
    feature_proj,
    w_qkv,
    b_qkv,
    w_out,
    b_out,
    ln1_gain,
    ln1_bias,
    w_up,
    b_up,
    w_down,
    b_down,
    ln2_gain,
    ln2_bias,
):
    totals = None
    outputs = []
    grad_inputs = []
    for micro_idx in range(MICRO):
        gathered = fetch_weights(
            w_qkv,
            b_qkv,
            w_out,
            b_out,
            ln1_gain,
            ln1_bias,
            w_up,
            b_up,
            w_down,
            b_down,
            ln2_gain,
            ln2_bias,
        )
        result, grad_tokens, grads_now = micro_step(
            tokens_in[micro_idx],
            out_cotangent[micro_idx],
            segment_ids[micro_idx],
            feature_proj,
            gathered,
        )
        outputs.append(result)
        grad_inputs.append(grad_tokens)
        totals = grads_now if totals is None else jax.tree.map(jnp.add, totals, grads_now)
    (
        grad_wqkv,
        grad_bqkv,
        grad_wout,
        grad_bout,
        grad_gain1,
        grad_bias1,
        grad_wup,
        grad_bup,
        grad_wdown,
        grad_bdown,
        grad_gain2,
        grad_bias2,
    ) = totals
    summed = (
        lax.psum_scatter(grad_wqkv, ("dp", "feat"), scatter_dimension=0, tiled=True),
        lax.psum_scatter(grad_bqkv, ("dp", "feat"), scatter_dimension=0, tiled=True),
        lax.psum_scatter(grad_wout, ("dp", "feat"), scatter_dimension=0, tiled=True),
        lax.psum_scatter(grad_bout, ("dp", "feat"), scatter_dimension=0, tiled=True),
        lax.psum_scatter(grad_gain1, ("dp", "feat"), scatter_dimension=0, tiled=True),
        lax.psum_scatter(grad_bias1, ("dp", "feat"), scatter_dimension=0, tiled=True),
        lax.psum_scatter(grad_wup, ("dp", "feat"), scatter_dimension=0, tiled=True),
        lax.psum_scatter(grad_bup, ("dp", "feat"), scatter_dimension=0, tiled=True),
        lax.psum_scatter(grad_wdown, ("dp", "feat"), scatter_dimension=0, tiled=True),
        lax.psum_scatter(grad_bdown, ("dp", "feat"), scatter_dimension=0, tiled=True),
        lax.psum_scatter(grad_gain2, ("dp", "feat"), scatter_dimension=0, tiled=True),
        lax.psum_scatter(grad_bias2, ("dp", "feat"), scatter_dimension=0, tiled=True),
    )
    return (
        jnp.stack(outputs),
        jnp.stack(grad_inputs),
        summed[0],
        summed[1],
        summed[2],
        summed[3],
        summed[4],
        summed[5],
        summed[6],
        summed[7],
        summed[8],
        summed[9],
        summed[10],
        summed[11],
    )


NZ, NY, NC, NX = 4, 2, 2, 2
N_DEV = NZ * NY * NC * NX
MESH_ID = pl.DeviceIdType.MESH
BF = jnp.bfloat16
F32 = jnp.float32
SHARE = MICRO // NX
GRID = (NZ, NY, NC)
ALL = slice(None)


def fits(mesh):
    return mesh.shape["dp"] == NZ * NY * NC and mesh.shape["feat"] == NX


class Place:
    def __init__(self):
        i = lax.axis_index("dp")
        self.z, self.y, self.c, self.x = i // (NY * NC), (i // NC) % NY, i % NC, lax.axis_index("feat")
        self.sibling = self.device(c=1 - self.c)
        self.over = {"x": self.device(x=1 - self.x), "y": self.device(y=1 - self.y)}
        z = self.z
        self.to = {1: z <= 2, -1: z >= 1, 2: z <= 1, -2: z >= 2}
        self.had = {1: z >= 1, -1: z <= 2, 2: z >= 2, -2: z <= 1}

    def device(self, **other):
        z, y, c, x = (other.get(n, getattr(self, n)) for n in "zycx")
        return (z * (NY * NC) + y * NC + c, x)

    def meet(self):
        barrier = pltpu.get_barrier_semaphore()
        peers = [self.sibling, self.over["x"], self.over["y"]] + [self.device(z=lax.rem(self.z + k, NZ)) for k in (1, 2, 3)]
        for peer in peers:
            pl.semaphore_signal(barrier, inc=1, device_id=peer, device_id_type=MESH_ID)
        pl.semaphore_wait(barrier, len(peers))

    def per_class(self, orders, act):
        if orders[0] == orders[1]:
            act(orders[0])
            return
        for c in range(NC):

            @pl.when(self.c == c)
            def _(order=orders[c]):
                act(order)

    def rows(self, grid, x):
        share = grid.shape[3] // NX
        return pl.ds(pl.multiple_of(x * share, 8), share)

    def view(self, grid, cols, spread=(), **at):
        index = [ALL if n in spread else at.get(n, getattr(self, n)) for n in "zyc"]
        rows = ALL if "x" in spread else self.rows(grid, at.get("x", self.x))
        return grid.at[(*index, rows, cols)]


class Copies:
    def __init__(self, send_sems, recv_sems):
        self.send_sems, self.recv_sems = send_sems, recv_sems

    def copy(self, slot, src, dst, peer, sent=None):
        return pltpu.make_async_remote_copy(
            src_ref=src, dst_ref=dst, send_sem=self.send_sems.at[slot if sent is None else sent],
            recv_sem=self.recv_sems.at[slot], device_id=peer, device_id_type=MESH_ID,
        )


MOVES = (1, -1, 2, -2)


def stretch(order):
    return "".join("zZ" if n == "z" else n for n in order)


class Gather(Copies):
    def __init__(self, here, part, src, grid, cols, orders, sems):
        super().__init__(sems[0].at[part], sems[1].at[part])
        self.here, self.grid, self.cols, self.orders = here, grid, cols, tuple(stretch(o) for o in orders)
        self.src = src.at[ALL, cols]
        self.local = pltpu.make_async_copy(self.src, here.view(grid, cols), sems[2].at[part])

    def phase(self, order, n):
        here, dim = self.here, order[n]
        mine = here.view(self.grid, self.cols, order[:n].replace("Z", "").replace("z", "" if dim == "Z" else "z"))
        src = self.src if n == 0 else mine
        if dim == "z":
            return [
                (here.to[k], here.had[k], self.copy(s, src, mine, here.device(z=lax.rem(here.z + k + NZ, NZ))))
                for s, k in enumerate(MOVES)
            ]
        if dim == "Z":
            inner = (here.z == 1) | (here.z == 2)
            outer = (here.z == 0) | (here.z == 3)
            far = here.view(self.grid, self.cols, order[: n - 1], z=jnp.where(inner, 6 - 3 * here.z, 3 - here.z))
            return [(inner, outer, self.copy(4, far, far, here.device(z=jnp.where(inner, 3 * here.z - 3, 3 - here.z))))]
        return [(None, None, self.copy(5 + "xy".index(dim), src, mine, here.over[dim]))]

    def to_sibling(self):
        mine = self.here.view(self.grid, self.cols, "zyx")
        return self.copy(7, mine, mine, self.here.sibling)

    def step(self, n):
        here, last = self.here, len(self.orders[0])
        if n == 0:
            self.local.start()
            here.per_class(self.orders, lambda order: run_all("start", self.phase(order, 0)))
        elif n <= last:
            here.per_class(self.orders, lambda order: run_all("wait_recv", self.phase(order, n - 1)))
            if n == 1:
                self.local.wait()
            if n < last:
                here.per_class(self.orders, lambda order: run_all("start", self.phase(order, n)))
            else:
                self.to_sibling().start()
        else:
            self.to_sibling().wait_recv()

    def drain(self):
        for n in range(len(self.orders[0])):
            self.here.per_class(self.orders, lambda order, n=n: run_all("wait_send", self.phase(order, n)))
        self.to_sibling().wait_send()


def run_all(what, copies):
    for sends, gets, copy in copies:
        when(gets if what == "wait_recv" else sends, getattr(copy, what))


def when(condition, act):
    if condition is None:
        act()
        return

    @pl.when(condition)
    def _():
        act()


class Reduce(Copies):
    def __init__(self, here, part, grid, cols, orders, got, stage, out, sems):
        super().__init__(sems[0].at[part], sems[1].at[part])
        self.here, self.grid, self.cols, self.orders = here, grid, cols, tuple(stretch(o) for o in orders)
        self.got, self.stage = got, stage
        self.out = pltpu.make_async_copy(stage, out, sems[2].at[part])

    def from_sibling(self):
        here = self.here
        theirs = here.view(self.grid, self.cols, "zyx", c=1 - here.c)
        return self.copy(0, theirs, self.got[0][0], here.sibling)

    def received(self, order, n):
        at = order.replace("Z", "").index(order[n].lower()) + 1
        return self.got[at][self.orders.index(order) % len(self.got[at])]

    def phase(self, order, n):
        here, dim, rest = self.here, order[n], order[n + 1 :].replace("Z", "")
        got, z = self.received(order, n), here.z
        if dim == "z":
            aim = {1: z + 1, -1: z - 1, 2: 2, -2: 1}
            ends = {1: here.to[1], -1: here.to[-1], 2: z == 0, -2: z == 3}
            copies = [
                (ends[k], None, self.copy(3 + s, here.view(self.grid, self.cols, rest, z=aim[k]), got.at[s], here.device(z=aim[k])))
                for s, k in enumerate(MOVES)
            ]
            near = {2: (z == 0, 3, 1), -2: (z == 3, 0, 2)}
            first = [
                (near[k][0], None, self.copy(
                    3 + s, here.view(self.grid, self.cols, rest, z=near[k][1]), got.at[s], here.device(z=near[k][2]), 5 + s
                ))
                for s, k in enumerate(MOVES) if k in near
            ]
            return first + copies
        if dim == "Z":
            end = {2: (z == 1, 3), -2: (z == 2, 0)}
            return [
                (end[k][0], None, self.copy(3 + s, here.view(self.grid, self.cols, rest, z=end[k][1]), got.at[s], here.device(z=end[k][1])))
                for s, k in enumerate(MOVES) if k in end
            ]
        place = {dim: 1 - getattr(here, dim)}
        return [(None, None, self.copy(1 + "xy".index(dim), here.view(self.grid, self.cols, rest, **place), got, here.over[dim]))]

    def arrivals(self, order, n):
        here, got = self.here, self.received(order, n)
        if order[n] != "Z":
            (_, _, copy), = self.phase(order, n)
            return [(None, copy.wait_recv, got)]
        mine = here.view(self.grid, self.cols, order[n + 1 :])
        return [
            (here.had[k], self.copy(3 + s, mine, got.at[s], here.sibling).wait_recv, got.at[s]) for s, k in enumerate(MOVES)
        ]

    def spot(self, spread, q, z=None):
        here, index, inner = self.here, {} if z is None else {"z": z}, {}
        if "y" in spread:
            index["y"] = inner["y"] = q % NY
            q = q // NY
        if "z" in spread:
            index["z"] = inner["z"] = q
        rows = ALL if "x" in spread else here.rows(self.grid, here.x)
        return tuple(index.get(n, getattr(here, n)) for n in "zyc") + (rows, self.cols), tuple(inner[n] for n in "zy" if n in inner)

    def add(self, got, spread, z=None):
        def one(q):
            index, inner = self.spot(spread, q, z)
            self.grid[index] = self.grid[index] + got[inner + (ALL, ALL)]

        count = (NZ if "z" in spread else 1) * (NY if "y" in spread else 1)
        blocks_of(count, one) if count > 1 else one(0)

    def take(self, order, n):
        if order[n] == "z":
            return
        here, final = self.here, n == len(order) - 1
        if final:
            self.stage[...] = self.grid[self.spot((), 0)[0]].astype(F32)
        for condition, wait, got in self.arrivals(order, n):

            def one(wait=wait, got=got):
                wait()
                if final:
                    self.stage[...] += got[...].astype(F32)
                else:
                    self.add(got, order[n + 1 :].replace("Z", ""))

            when(condition, one)

    def send(self, order, n):
        copies = self.phase(order, n)
        if order[n] == "Z":
            got, rest = self.received(order, n), order[n + 1 :]
            for (condition, _, copy), (slot, end) in zip(copies, ((2, 3), (3, 0)), strict=True):

                def pass_on(copy=copy, slot=slot, end=end):
                    copy.wait_recv()
                    self.add(got.at[slot], rest, z=end)
                    copy.start()

                when(condition, pass_on)
        else:
            run_all("start", copies)

    def step(self, n):
        here, last = self.here, len(self.orders[0])
        if n == 0:
            self.from_sibling().start()
        elif n == 1:
            self.from_sibling().wait_recv()
            self.add(self.got[0][0], "zyx")
        else:
            here.per_class(self.orders, lambda order: self.take(order, n - 2))
        if 0 < n <= last:
            here.per_class(self.orders, lambda order: self.send(order, n - 1))
        elif n > last:
            self.out.start()

    def drain(self):
        self.from_sibling().wait_send()
        for n in range(len(self.orders[0])):
            self.here.per_class(self.orders, lambda order, n=n: run_all("wait_send", self.phase(order, n)))
        self.out.wait()


def got_shapes(orders, rows, width):
    first, second = (order_shapes(order, rows, width) for order in orders)
    return [(a,) if a == b else (a, b) for a, b in zip(first, second, strict=True)]


def order_shapes(order, rows, width):

    def block(spread):
        return tuple(dict(z=NZ, y=NY)[n] for n in "zy" if n in spread) + (rows * (NX if "x" in spread else 1), width)

    shapes = [block("zyx")]
    for n, dim in enumerate(order):
        shapes.append(((len(MOVES),) if dim == "z" else ()) + block(order[n + 1 :]))
    return shapes


def blocks_of(count, body, then=()):
    def step(j, carry):
        body(j)
        for at in sorted({at for at, _ in then}):

            @pl.when(j == at)
            def _(at=at):
                for when, act in then:
                    if when == at:
                        act()

        return carry

    lax.fori_loop(0, count, step, 0)


ROWS = 512
BLK = 256
PAIRS = D // 128
FF = 4 * D
WIDE = 2 * FEATS
SCALE = DH ** (-0.25)


def dot(a, b, ca=1, cb=0):
    return lax.dot_general(a, b, (((ca,), (cb,)), ((), ())), preferred_element_type=F32)


def half_masks(width):
    lane = lax.broadcasted_iota(jnp.int32, (1, width), 1) % 128
    first = (lane < DH).astype(F32)
    return first.astype(BF), (1.0 - first).astype(BF)


def lanes(j, width):
    return pl.ds(pl.multiple_of(j * width, width), width)


class Work:
    def __init__(self, refs):
        self.__dict__.update(refs)

    def setup(self, proj, seg_rows):
        row = lax.broadcasted_iota(jnp.int32, (DH, 128), 0)
        col = lax.broadcasted_iota(jnp.int32, (DH, 128), 1)
        for h in range(2):
            place_in = (col == row + h * DH).astype(BF)
            for n in range(NX):
                self.table[pl.ds(h * FEATS + n * 128, 128), 0:128] = dot(proj[n], place_in, 0, 0).astype(BF)
        feat = lax.broadcasted_iota(jnp.int32, (WIDE, 128), 0) // FEATS
        half = lax.broadcasted_iota(jnp.int32, (WIDE, 128), 1) // DH
        same = (feat == half).astype(F32).astype(BF)
        self.table[:, 128:256] = same
        self.flip[D:, :] = jnp.ones((16, ROWS), BF)
        for b in range(2):
            across = jnp.broadcast_to(seg_rows[b], (BLK, BLK))
            self.mask[b] = (across == jnp.transpose(across)).astype(F32).astype(BF)

    def features(self, rows):
        wide = rows.astype(F32)
        squares = wide * wide
        high = squares.astype(BF)
        low = (squares - high.astype(F32)).astype(BF)
        same = self.table[:, 128:256]
        norm = dot(high, same, 1, 1) + dot(low, same, 1, 1)
        arg = SCALE * dot(rows, self.table[:, 0:128], 1, 1) - (0.5 * SCALE * SCALE) * norm
        return (jnp.exp(arg) * FEATS ** (-0.5)).astype(BF)

    def qkv_block(self, j):
        col = lanes(j, D)
        full = dot(self.x[...], self.w_qkv[:, col]) + self.b_qkv[:, col]
        self.qkv[:, col] = full.astype(BF)

    def pair(self, i):
        b, p = i // PAIRS, i % PAIRS
        rows = pl.ds(pl.multiple_of(b * BLK, BLK), BLK)
        cols = [pl.ds(pl.multiple_of(n * D + p * 128, 128), 128) for n in range(3)]
        return b, rows, cols

    def attend(self, i):
        b, rows, cols = self.pair(i)
        mask = self.mask[b]
        m0, m1 = half_masks(128)
        phi_q = self.features(self.qkv[rows, cols[0]])
        phi_k = self.features(self.qkv[rows, cols[1]])
        self.phi_q[i] = phi_q
        self.phi_k[i] = phi_k
        v = self.qkv[rows, cols[2]]
        one = jnp.ones((BLK, 128), BF)
        res = None
        for h, m in enumerate((m0, m1)):
            part = slice(h * FEATS, (h + 1) * FEATS)
            score = dot(phi_q[:, part], phi_k[:, part], 1, 1).astype(BF) * mask
            term = dot(score, jnp.concatenate([v * m, one * m], 1))
            res = term if res is None else res + term
        inv = 1.0 / res[:, 128:]
        self.inv[rows, cols[0]] = inv
        self.att[rows, cols[0]] = (res[:, :128] * inv).astype(BF)

    def normalize(self, r):
        center = r - jnp.mean(r, -1, keepdims=True)
        scale = lax.rsqrt(jnp.mean(center * center, -1, keepdims=True) + EPSILON)
        return center * scale, scale

    def normalize_back(self, dy, n, scale, gain):
        g = dy * gain
        return (g - jnp.mean(g, -1, keepdims=True) - n * jnp.mean(g * n, -1, keepdims=True)) * scale

    def branch(self):
        for j in range(3):
            col = lanes(j, 256)
            self.n1[:, col] = dot(self.att[...], self.w_out[:, col]) + self.b_out[:, col] + self.x[:, col].astype(F32)

        def rows_of(j):
            row = pl.ds(pl.multiple_of(j * 128, 128), 128)
            n1, s1 = self.normalize(self.n1[row, :])
            self.n1[row, :] = n1
            self.s1[row, :] = s1
            self.h1[row, :] = (n1 * self.g1[...] + self.b1[...]).astype(BF)

        blocks_of(ROWS // 128, rows_of)

    def up_block(self, j):
        col = lanes(j, 256)
        for r in range(0, ROWS, 128):
            row = slice(r, r + 128)
            a = dot(self.h1[row, :], self.w_up[:, col]) + self.b_up[:, col]
            cdf = 0.5 * (1.0 + lax.erf(a * 2**-0.5))
            self.z[row, col] = (a * cdf).astype(BF)
            self.slope[row, col] = (cdf + a * jnp.exp(-0.5 * a * a) * (0.5 / 3.141592653589793) ** 0.5).astype(BF)

    def down_block(self, j):
        col = lanes(j, 256)
        back = self.n1[:, col] * self.g1[:, col] + self.b1[:, col]
        self.dr[:, col] = dot(self.z[...], self.w_down[:, col]) + self.b_down[:, col] + back

    def second_norm(self):
        self.d_g2[...] = jnp.zeros_like(self.d_g2)

        def rows_of(j):
            row = pl.ds(pl.multiple_of(j * 128, 128), 128)
            n2, s2 = self.normalize(self.dr[row, :])
            self.y[row, :] = (n2 * self.g2[...] + self.b2[...]).astype(BF)
            dy = self.cot[row, :].astype(F32)
            dr2 = self.normalize_back(dy, n2, s2, self.g2[...])
            self.dr[row, :] = dr2
            self.df[row, :] = dr2.astype(BF)
            self.d_g2[...] += jnp.sum(dy * n2, 0, keepdims=True)

        blocks_of(ROWS // 128, rows_of)

    def second_sums(self):
        ones = self.flip[D:, :]
        self.d_b2[...] = dot(ones, self.cot[...])[0:1]
        self.d_b_down[...] = dot(ones, self.df[...])[0:1]

    def down_back(self, j):
        col = lanes(j, 1024)
        dz = dot(self.df[...], self.w_down[col, :], 1, 1)
        self.slope[:, col] = (dz * self.slope[:, col].astype(F32)).astype(BF)

    def down_grad(self, into, part, j):
        col = lanes(j, D)
        into[col, :] = dot(self.z[:, col], self.df[:, part], 0, 0).astype(BF)

    def up_back(self, j):
        col = lanes(j, 384)
        self.dr[:, col] += dot(self.slope[...], self.w_up[col, :], 1, 1)

    def turn(self, name):
        self.flip[0:D, :] = jnp.transpose(getattr(self, name)[...])

    def weight_grad(self, weight, bias, col, grad):
        full = dot(self.flip[...], grad)
        weight[:, col] = full[0:D].astype(BF)
        bias[:, col] = full[D : D + 1]

    def up_grad(self, j):
        col = lanes(j, 512)
        self.weight_grad(self.w_up, self.d_b_up, col, self.slope[:, col])

    def first_norm_back(self):
        for ref in (self.d_g1, self.d_b1):
            ref[...] = jnp.zeros_like(ref)

        def rows_of(j):
            row = pl.ds(pl.multiple_of(j * 128, 128), 128)
            dh1, n1 = self.dr[row, :], self.n1[row, :]
            dr1 = self.normalize_back(dh1, n1, self.s1[row, :], self.g1[...])
            self.dr[row, :] = dr1
            self.df[row, :] = dr1.astype(BF)
            self.d_g1[...] += jnp.sum(dh1 * n1, 0, keepdims=True)
            self.d_b1[...] += jnp.sum(dh1, 0, keepdims=True)

        blocks_of(ROWS // 128, rows_of)

    def att_back(self, j):
        head_r = lax.broadcasted_iota(jnp.int32, (256, 256), 0) // DH
        head_c = lax.broadcasted_iota(jnp.int32, (256, 256), 1) // DH
        same = (head_r == head_c).astype(F32).astype(BF)
        col = lanes(j, 256)
        datt = dot(self.df[...], self.w_out[col, :], 1, 1)
        inv = self.inv[:, col]
        self.cot[:, col] = (datt * inv).astype(BF)
        prod = datt * self.att[:, col].astype(F32)
        high = prod.astype(BF)
        low = (prod - high.astype(F32)).astype(BF)
        total = dot(high, same) + dot(low, same)
        self.h1[:, col] = (-total * inv).astype(BF)

    def out_grad(self):
        col = slice(0, D)
        self.weight_grad(self.w_out, self.d_b_out, col, self.df[:, col])

    def attend_back(self, i):
        b, rows, cols = self.pair(i)
        mask = self.mask[b]
        m0, m1 = half_masks(256)
        q, k, v = (self.qkv[rows, c] for c in cols)
        dnum, dden = self.cot[rows, cols[0]], self.h1[rows, cols[0]]
        left = jnp.concatenate([dnum, dden * (1.0 / DH)], 1)
        right = jnp.concatenate([v, jnp.ones((BLK, 128), BF)], 1)
        back_q, back_k, dv = None, None, None
        for h, m in enumerate((m0, m1)):
            part = slice(h * FEATS, (h + 1) * FEATS)
            phi_q, phi_k = self.phi_q[i, :, part], self.phi_k[i, :, part]
            mine = left * m
            dscore = dot(mine, right, 1, 1).astype(BF) * mask
            flipped = dot(right, mine, 1, 1).astype(BF) * mask
            darg_q = (dot(dscore, phi_k) * phi_q.astype(F32)).astype(BF)
            darg_k = (dot(flipped, phi_q) * phi_k.astype(F32)).astype(BF)
            score = dot(phi_k, phi_q, 1, 1).astype(BF) * mask
            table = self.table[part, :]
            terms = dot(darg_q, table), dot(darg_k, table), dot(score, mine[:, :128])
            if h == 0:
                back_q, back_k, dv = terms
            else:
                back_q, back_k, dv = back_q + terms[0], back_k + terms[1], dv + terms[2]
        for n, (rows_in, back) in enumerate(((q, back_q), (k, back_k))):
            grad = SCALE * back[:, :128] - (SCALE * SCALE) * rows_in.astype(F32) * back[:, 128:]
            self.qkv[rows, cols[n]] = grad.astype(BF)
        self.qkv[rows, cols[2]] = dv.astype(BF)

    def tokens_back(self, j):
        col = lanes(j, 384)
        self.dr[:, col] += dot(self.qkv[...], self.w_qkv[col, :], 1, 1)

    def qkv_grad(self, j):
        col = lanes(j, D)
        self.weight_grad(self.w_qkv, self.d_b_qkv, col, self.qkv[:, col])


VECTORS = ("b_qkv", "b_out", "g1", "b1", "b_up", "b_down", "g2", "b2")
WIDTHS = (3 * D, D, D, D, FF, D, D, D)
SPACE = (
    ("qkv", (ROWS, 3 * D), BF), ("phi_q", (2 * PAIRS, BLK, WIDE), BF), ("phi_k", (2 * PAIRS, BLK, WIDE), BF),
    ("att", (ROWS, D), BF), ("inv", (ROWS, D), F32), ("n1", (ROWS, D), F32), ("s1", (ROWS, 1), F32),
    ("h1", (ROWS, D), BF), ("z", (ROWS, FF), BF), ("slope", (ROWS, FF), BF), ("dr", (ROWS, D), F32),
    ("df", (ROWS, D), BF), ("flip", (D + 16, ROWS), BF),
    ("table", (WIDE, 256), BF), ("mask", (2, BLK, BLK), BF),
)


GATHER_PARTS = {
    "small": ("small", 0, 128, ("zyx", "zxy")),
    "q": ("w_qkv", 0, 768, ("zyx", "zxy")),
    "k": ("w_qkv", 768, 768, ("zxy", "zxy")),
    "v": ("w_qkv", 1536, 768, ("zxy", "zxy")),
    "out": ("w_out", 0, 768, ("xzy", "yzx")),
    "up0": ("w_up", 0, 1024, ("zyx", "zxy")),
    "up1": ("w_up", 1024, 1024, ("xzy", "yzx")),
    "up2": ("w_up", 2048, 1024, ("xzy", "yzx")),
    "dn0": ("w_down", 0, 256, ("xyz", "xyz")),
    "dn1": ("w_down", 256, 256, ("zyx", "zxy")),
    "dn2": ("w_down", 512, 256, ("xzy", "yzx")),
}
REDUCE_PARTS = {
    "small": ("small", 0, 128, ("xyz", "yxz"), "small", 0),
    "q": ("w_qkv", 0, 768, ("xyz", "yxz"), "w_qkv", 0),
    "k": ("w_qkv", 768, 768, ("xyz", "yxz"), "w_qkv", 768),
    "v": ("w_qkv", 1536, 768, ("xyz", "yxz"), "w_qkv", 1536),
    "out": ("w_out", 0, 768, ("yxz", "yxz"), "w_out", 0),
    "up0": ("w_up", 0, 1536, ("yxz", "yxz"), "w_up", 0),
    "up1": ("w_up", 1536, 1536, ("xyz", "xyz"), "w_up", 1536),
    "dn0": ("spare", 0, 384, ("yzx", "xzy"), "w_down", 0),
    "dn1": ("w_down", 384, 384, ("yzx", "xzy"), "w_down", 384),
}
FORWARD = (
    "proj!", "small0", "tok!", "q0", "out0", "up10", "k0", "v0", "small1", "proj?", "setup", "q1", "k1", "small2",
    "up00", "q2", "dn10", "v1", "k2", "up20", "out1", "up11", "small3", "up01", "q3", "v2", "dn11", "dn20", "k3",
    "small4", "up21", "small5", "dn00", "spread", "q4", "out2", "q5", "cot!", "v3", "up02", "tok?", "qkv", "dn21",
    "dn12", "dn01", "k4", "up12", "k5", "qkv", "out3", "v4", "up22", "v5", "qkv", "att", "up03", "att", "up13",
    "dn13", "dn02", "att", "up23", "att", "dn22", "att", "out4", "att*3", "out5", "att", "up04", "att*3", "up05",
    "branch", "up14", "dn23", "upb*2", "dn03", "upb*2", "dn14", "up15", "upb*4", "dn15", "up24", "dn04", "up25",
    "upb*2", "dn24", "upb", "dn05", "upb", "down*2", "dn25", "down", "cot?", "ln2",
)
BACKWARD = (
    "y!", "gdn0*4", "dn00", "sums", "dz*3", "gdn1*2", "dn01", "gdn1*2", "dn10", "uback*2", "flip0", "gup*2", "dn11",
    "gup", "up00", "gup*3", "up10", "nback", "dn02", "datt", "up01", "datt", "up11", "datt", "flip1", "gout", "out0",
    "dn12", "attb*3", "out1", "attb*2", "dn03", "attb*5", "up02", "attb*2", "up12", "tback*2", "dn13", "lower",
    "flip2", "gqkv", "out2", "q0", "gqkv", "dn04", "k0", "up03", "gqkv", "v0", "q1", "dn14", "k1", "out3", "up13",
    "dn05", "v1", "collect", "up04", "small0", "q2", "dn15", "out4", "small1", "k2", "up14", "v2", "up05", "q3",
    "out5", "small2", "grad!", "k3", "up15", "small3", "v3", "q4", "k4", "small4", "v4", "q5", "k5", "small5", "v5",
)
WEIGHTS = (("w_qkv", (D, 3 * D)), ("w_out", (D, D)), ("w_up", (D, FF)), ("w_down", (FF, D)))
TILE = (8, 128)
SPARE = 384
HALF = (SHARE, NX, ROWS // SHARE // NX, D)


def shard_rows(weight):
    return TILE[0] if weight == "small" else dict(WEIGHTS)[weight][0] // N_DEV


class Swap:
    def __init__(self, here, n, theirs, target, mine, home, sems):
        self.there = pltpu.make_async_remote_copy(
            src_ref=theirs, dst_ref=target, send_sem=sems[0].at[n], recv_sem=sems[1].at[n],
            device_id=here.over["x"], device_id_type=MESH_ID,
        )
        self.here = None if home is None else pltpu.make_async_copy(mine, home, sems[2].at[n])

    def start(self):
        self.there.start()
        if self.here is not None:
            self.here.start()

    def arrive(self):
        self.there.wait_recv()
        if self.here is not None:
            self.here.wait()


def one_hot(width, count):
    at = lax.broadcasted_iota(jnp.int32, (1, count), 1).astype(F32)
    owner = jnp.floor((at + 0.5) * (1.0 / width))
    lane = at - owner * width
    lanes_hot = (lax.broadcasted_iota(jnp.int32, (128, count), 0).astype(F32) == lane).astype(F32).astype(BF)
    owner_hot = (lax.broadcasted_iota(jnp.int32, (N_DEV, count), 0).astype(F32) == owner).astype(F32)
    return lanes_hot, owner_hot


def spread_small(tiles, vectors):
    for width in sorted({v.shape[1] // N_DEV for v in vectors}):
        hot, owner = one_hot(width, width * N_DEV)
        for n, vector in enumerate(vectors):
            if vector.shape[1] == width * N_DEV:
                rows = tiles[pl.ds(n, N_DEV, stride=TILE[0]), :].astype(BF)
                vector[...] = jnp.sum(dot(rows, hot) * owner, 0, keepdims=True)


def collect_small(tiles, vectors):
    for width in sorted({v.shape[1] // N_DEV for v in vectors}):
        hot, owner = one_hot(width, width * N_DEV)
        for n, vector in enumerate(vectors):
            if vector.shape[1] == width * N_DEV:
                full = owner * vector[...]
                high = full.astype(BF)
                low = (full - high.astype(F32)).astype(BF)
                tiles[pl.ds(n, N_DEV, stride=TILE[0]), :] = dot(high, hot, 1, 1) + dot(low, hot, 1, 1)


def layer_kernel(*refs):
    it = iter(refs)
    tok, cot = next(it), next(it)
    local = {w: next(it) for w, _ in WEIGHTS}
    own_vectors = [next(it) for _ in VECTORS]
    proj_in, seg = next(it), next(it)
    block_out, grad_own, grad_got = next(it), next(it), next(it)
    outs = {w: next(it) for w, _ in WEIGHTS}
    outs["small"] = next(it)
    ref = {n: next(it) for n, _ in WEIGHTS}
    ref.update({n: next(it) for n, _, _ in SPACE})
    work = Work(ref)
    got = {
        p: [tuple(next(it) for _ in shapes) for shapes in got_shapes(orders, shard_rows(w), width)]
        for p, (_, _, width, orders, w, _) in REDUCE_PARTS.items()
    }
    stage = {p: next(it) for p in REDUCE_PARTS}
    gather_sems = [next(it) for _ in range(3)]
    reduce_sems = [next(it) for _ in range(3)]
    swap_sems = [next(it) for _ in range(3)]
    vector_sems = next(it)

    vector_loads = [pltpu.make_async_copy(v, ref["in_" + n], vector_sems.at[k]) for k, (n, v) in enumerate(zip(VECTORS, own_vectors))]
    for load in vector_loads:
        load.start()
    here = Place()
    here.meet()
    local["small"] = ref["tile"]
    ref["tile"][...] = jnp.zeros(TILE, F32)
    for k, (n, load) in enumerate(zip(VECTORS, vector_loads)):
        load.wait()
        width = ref["in_" + n].shape[0]
        ref["tile"][k : k + 1, 0:width] = ref["in_" + n][...].astype(F32).reshape(1, width)
    x = here.x
    grids = {w: ref[w].reshape(GRID + (NX * shard_rows(w), ref[w].shape[1])) for w, _ in WEIGHTS}
    grids["spare"] = ref["spare"].reshape(GRID + (NX * shard_rows("w_down"), SPARE))
    grids["small"] = ref["tiles"].reshape(GRID + (NX * TILE[0], TILE[1]))
    into, back = {}, {}
    for n, (p, (w, first, width, orders)) in enumerate(GATHER_PARTS.items()):
        into[p] = Gather(here, n, local[w], grids[w], pl.ds(first, width), orders, gather_sems)
    for n, (p, (a, first, width, orders, w, at)) in enumerate(REDUCE_PARTS.items()):
        out = outs[w].at[ALL, pl.ds(at, width)]
        back[p] = Reduce(here, n, grids[a], pl.ds(first, width), orders, got[p], stage[p], out, reduce_sems)

    def halves(r):
        return r.reshape(HALF)

    grad_low = halves(work.df).at[0]
    own, other = pl.ds(x * SHARE, SHARE), pl.ds((1 - x) * SHARE, SHARE)
    swap = {
        "tok": Swap(here, 0, tok.at[other], halves(work.x).at[:, x], tok.at[own], halves(work.x).at[:, x], swap_sems),
        "cot": Swap(here, 1, cot.at[other], halves(work.cot).at[:, x], cot.at[own], halves(work.cot).at[:, x], swap_sems),
        "proj": Swap(here, 2, proj_in, work.proj.at[x], proj_in, work.proj.at[x], swap_sems),
        "y": Swap(here, 3, halves(work.y).at[:, 1 - x], block_out.at[own], halves(work.y).at[:, x], block_out.at[own], swap_sems),
        "grad": Swap(here, 4, grad_low, grad_got, halves(work.dr).at[:, x], grad_own, swap_sems),
    }

    vectors = [getattr(work, n) for n in VECTORS]
    totals = [getattr(work, "d_" + n) for n in VECTORS]

    def setup():
        work.setup(work.proj, [seg[pl.ds(SHARE * x + b, 1), :].astype(F32) for b in range(SHARE)])

    def lower():
        def block(b):
            grad_low[b] = halves(work.dr)[b, 1 - x].astype(BF)

        blocks_of(SHARE, block)

    stages = {
        "setup": (1, setup),
        "spread": (1, lambda: spread_small(ref["tiles"], vectors)),
        "qkv": (3, work.qkv_block),
        "att": (2 * PAIRS, work.attend),
        "branch": (1, work.branch),
        "upb": (12, work.up_block),
        "down": (3, work.down_block),
        "ln2": (1, work.second_norm),
        "sums": (1, work.second_sums),
        "dz": (3, work.down_back),
        "uback": (2, work.up_back),
        "flip0": (1, partial(work.turn, "h1")),
        "gup": (6, work.up_grad),
        "nback": (1, work.first_norm_back),
        "datt": (3, work.att_back),
        "flip1": (1, partial(work.turn, "att")),
        "gout": (1, work.out_grad),
        "attb": (2 * PAIRS, work.attend_back),
        "tback": (2, work.tokens_back),
        "lower": (1, lower),
        "flip2": (1, partial(work.turn, "x")),
        "gqkv": (3, work.qkv_grad),
        "collect": (1, lambda: collect_small(ref["tiles"], totals)),
    }
    for p, (a, first, width, _, w, at) in REDUCE_PARTS.items():
        if w == "w_down":
            into_part = ref[a].at[ALL, pl.ds(first, width)]
            stages["g" + p] = (4, partial(work.down_grad, into_part, slice(at, at + width)))

    def act(steps, token):
        if token[-1] == "!":
            swap[token[:-1]].start()
        elif token[-1] == "?":
            swap[token[:-1]].arrive()
        else:
            steps[token[:-1]].step(int(token[-1]))

    def play(tokens, steps):
        tokens = [t.split("*") for t in tokens]
        tokens = [(t[0], int(t[1]) if len(t) > 1 else 1) for t in tokens]
        while tokens:
            name, _ = tokens[0]
            if name not in stages:
                act(steps, name)
                tokens.pop(0)
                continue
            count, body = stages[name]
            n, then = 0, []
            while n < count:
                token, times = tokens.pop(0)
                if token == name:
                    n += times
                else:
                    then.append((n - 1, partial(act, steps, token)))
            if count > 1:
                blocks_of(count, body, then)
            else:
                body()

    play(FORWARD, into)
    for part in into.values():
        part.drain()
    play(BACKWARD, back)
    swap["grad"].arrive()
    swap["y"].arrive()
    for each in swap.values():
        each.there.wait_send()
    for part in back.values():
        part.drain()


QUARTER = (SHARE, ROWS // SHARE // NX, D)
SPACE = (
    (("x", (ROWS, D), BF), ("cot", (ROWS, D), BF), ("y", (ROWS, D), BF), ("proj", (NX, DH, FEATS // NX), BF))
    + (("spare", (FF, SPARE), BF), ("tile", TILE, F32))
    + tuple(("in_" + n, (w // N_DEV,), BF) for n, w in zip(VECTORS, WIDTHS))
    + (("tiles", (N_DEV * TILE[0], TILE[1]), F32),)
    + tuple((n, (1, w), F32) for n, w in zip(VECTORS, WIDTHS))
    + tuple(("d_" + n, (1, w), F32) for n, w in zip(VECTORS, WIDTHS))
    + SPACE
)


def layer(tok, cot, weights, vectors, proj, seg):
    anywhere = pl.BlockSpec(memory_space=pl.ANY)
    vmem = pl.BlockSpec(memory_space=pltpu.VMEM)
    shape, dma = jax.ShapeDtypeStruct, pltpu.SemaphoreType.DMA
    received, stages = [], []
    for _, _, width, orders, w, _ in REDUCE_PARTS.values():
        kind = F32 if w == "small" else BF
        received += [pltpu.VMEM(s, kind) for shapes in got_shapes(orders, shard_rows(w), width) for s in shapes]
        stages.append(pltpu.VMEM((shard_rows(w), width), F32))
    there, back = len(GATHER_PARTS), len(REDUCE_PARTS)
    return pl.pallas_call(
        layer_kernel,
        out_shape=[shape(tok.shape, BF), shape(QUARTER, F32), shape(QUARTER, BF)]
        + [shape(w.shape, F32) for w in weights] + [shape(TILE, F32)],
        in_specs=[anywhere] * 15 + [vmem],
        out_specs=[anywhere] * 8,
        scratch_shapes=[pltpu.VMEM(s, BF) for _, s in WEIGHTS] + [pltpu.VMEM(s, d) for _, s, d in SPACE] + received + stages
        + [dma((there, 8)), dma((there, 8)), dma((there,)), dma((back, 9)), dma((back, 9)), dma((back,))]
        + [dma((5,)), dma((5,)), dma((5,)), dma((len(VECTORS),))],
        compiler_params=pltpu.CompilerParams(collective_id=0, has_side_effects=True, vmem_limit_bytes=63 << 20),
        name="layer",
    )(tok, cot, *weights, *vectors, proj, seg)


def finish_kernel(count, *refs):
    it = iter(refs)
    ins, own, got, tile = [next(it) for _ in range(count)], next(it), next(it), next(it)
    outs, grad = [next(it) for _ in range(count)], next(it)
    rows = [next(it) for _ in WIDTHS]
    spaces, got_space, grad_space, sems = [next(it) for _ in range(count)], next(it), next(it), next(it)
    x = lax.axis_index("feat")
    here, there = pl.ds(x * SHARE, SHARE), pl.ds((1 - x) * SHARE, SHARE)
    loads = [pltpu.make_async_copy(got, got_space, sems.at[0, count]), pltpu.make_async_copy(own, grad_space.at[here], sems.at[0, count + 1])]
    loads += [pltpu.make_async_copy(a, b, sems.at[0, n]) for n, (a, b) in enumerate(zip(ins, spaces))]
    stores = [pltpu.make_async_copy(a, b, sems.at[1, n]) for n, (a, b) in enumerate(zip(spaces, outs))]
    halves = [pltpu.make_async_copy(grad_space.at[h], grad.at[h], sems.at[1, count + n]) for n, h in enumerate((there, here))]
    for load in loads:
        load.start()
    for n, row in enumerate(rows):
        row[...] = tile[n, 0 : row.shape[0]]
    loads[0].wait()
    grad_space[there] = got_space[...].astype(F32)
    halves[0].start()
    loads[1].wait()
    halves[1].start()
    for load, store in zip(loads[2:], stores):
        load.wait()
        store.start()
    for store in stores + halves:
        store.wait()


def finish(arrays, own, got, tile):
    anywhere = pl.BlockSpec(memory_space=pl.ANY)
    vmem = pl.BlockSpec(memory_space=pltpu.VMEM)
    count = len(arrays)
    whole = (MICRO,) + own.shape[1:]
    return pl.pallas_call(
        partial(finish_kernel, count),
        out_shape=[jax.ShapeDtypeStruct(a.shape, a.dtype) for a in arrays] + [jax.ShapeDtypeStruct(whole, F32)]
        + [jax.ShapeDtypeStruct((w // N_DEV,), F32) for w in WIDTHS],
        in_specs=[anywhere] * (count + 2) + [vmem],
        out_specs=[anywhere] * (count + 1) + [vmem] * len(WIDTHS),
        scratch_shapes=[pltpu.VMEM(a.shape, a.dtype) for a in arrays]
        + [pltpu.VMEM(got.shape, BF), pltpu.VMEM(whole, F32), pltpu.SemaphoreType.DMA((2, count + 2))],
        name="finish",
    )(*arrays, own, got, tile)


def fast_device(
    tokens_in, out_cotangent, segment_ids, feature_proj,
    w_qkv, b_qkv, w_out, b_out, ln1_gain, ln1_bias, w_up, b_up, w_down, b_down, ln2_gain, ln2_bias,
):
    out, own, got, *sums, tile = layer(
        tokens_in, out_cotangent, [w_qkv, w_out, w_up, w_down],
        [b_qkv, b_out, ln1_gain, ln1_bias, b_up, b_down, ln2_gain, ln2_bias], feature_proj.T, segment_ids,
    )
    out, g_qkv, g_out, g_up, g_down, grad_tok, *vec = finish([out, *sums], own, got, tile)
    return out, grad_tok, g_qkv, vec[0], g_out, vec[1], vec[2], vec[3], g_up, vec[4], g_down, vec[5], vec[6], vec[7]


def solution(mesh):
    return jax.shard_map(
        fast_device if fits(mesh) else on_device,
        mesh=mesh,
        in_specs=(
            P(None, ("dp", "feat"), None),
            P(None, ("dp", "feat"), None),
            P(None, "dp"),
            P("feat", None),
            P(("dp", "feat"), None),
            P(("dp", "feat")),
            P(("dp", "feat"), None),
            P(("dp", "feat")),
            P(("dp", "feat")),
            P(("dp", "feat")),
            P(("dp", "feat"), None),
            P(("dp", "feat")),
            P(("dp", "feat"), None),
            P(("dp", "feat")),
            P(("dp", "feat")),
            P(("dp", "feat")),
        ),
        out_specs=(
            P(None, ("dp", "feat"), None),
            P(None, ("dp", "feat"), None),
            P(("dp", "feat"), None),
            P(("dp", "feat")),
            P(("dp", "feat"), None),
            P(("dp", "feat")),
            P(("dp", "feat")),
            P(("dp", "feat")),
            P(("dp", "feat"), None),
            P(("dp", "feat")),
            P(("dp", "feat"), None),
            P(("dp", "feat")),
            P(("dp", "feat")),
            P(("dp", "feat")),
        ),
        check_vma=False,
    )
```

```python
from functools import partial

import jax
import jax.numpy as jnp
from jax import lax
from jax.experimental import pallas as pl
from jax.experimental.pallas import tpu as pltpu
from jax.sharding import PartitionSpec as P

D = 768
H = 12
DH = 64
FEATS = 256
MICRO = 4
SEGS = 4


EPSILON = 1e-05


def layer_norm(residual, norm_gain, norm_shift):
    center = residual - jnp.mean(residual, -1, keepdims=True)
    spread = jnp.mean(center * center, -1, keepdims=True)
    return center * lax.rsqrt(spread + EPSILON) * norm_gain + norm_shift


def cross_dot(left_op, right_op):
    return lax.dot_general(
        left_op, right_op, (((0,), (0,)), ((), ())), preferred_element_type=jnp.float32
    )


def back_dot(left_op, right_op):
    return lax.dot_general(
        left_op, right_op, (((1,), (1,)), ((), ())), preferred_element_type=jnp.float32
    )


def fetch_weights(
    w_qkv, b_qkv, w_out, b_out, ln1_gain, ln1_bias, w_up, b_up, w_down, b_down, ln2_gain, ln2_bias
):
    return (
        lax.all_gather(w_qkv, ("dp", "feat"), axis=0, tiled=True),
        lax.all_gather(b_qkv, ("dp", "feat"), axis=0, tiled=True),
        lax.all_gather(w_out, ("dp", "feat"), axis=0, tiled=True),
        lax.all_gather(b_out, ("dp", "feat"), axis=0, tiled=True),
        lax.all_gather(ln1_gain, ("dp", "feat"), axis=0, tiled=True),
        lax.all_gather(ln1_bias, ("dp", "feat"), axis=0, tiled=True),
        lax.all_gather(w_up, ("dp", "feat"), axis=0, tiled=True),
        lax.all_gather(b_up, ("dp", "feat"), axis=0, tiled=True),
        lax.all_gather(w_down, ("dp", "feat"), axis=0, tiled=True),
        lax.all_gather(b_down, ("dp", "feat"), axis=0, tiled=True),
        lax.all_gather(ln2_gain, ("dp", "feat"), axis=0, tiled=True),
        lax.all_gather(ln2_bias, ("dp", "feat"), axis=0, tiled=True),
    )


def feature_map(head_rows, feat_proj):
    feat_scale = DH ** (-0.25)
    proj_arg = feat_scale * jnp.einsum(
        "ghd,md->ghm", head_rows, feat_proj, preferred_element_type=jnp.float32
    )
    squares = jnp.einsum("ghd,ghd->gh", head_rows, head_rows, preferred_element_type=jnp.float32)
    proj_arg = proj_arg - 0.5 * feat_scale * feat_scale * squares[:, :, None]
    return jnp.exp(proj_arg) * FEATS ** (-0.5)


def feature_back(head_rows, feat_proj, grad_arg):
    feat_scale = DH ** (-0.25)
    proj_back = feat_scale * jnp.einsum(
        "ghm,md->ghd", grad_arg, feat_proj, preferred_element_type=jnp.float32
    )
    arg_total = jnp.sum(grad_arg.astype(jnp.float32), -1, keepdims=True)
    return proj_back - feat_scale * feat_scale * head_rows.astype(jnp.float32) * arg_total


def spread_segments(phi_low, member):
    tok_count, head_count, feat_width = phi_low.shape
    return (phi_low[:, :, None, :] * member[:, None, :, None]).reshape(
        tok_count, head_count, SEGS * feat_width
    )


def fold_segments(grad_wide, member_f):
    tok_count, head_count, wide_dim = grad_wide.shape
    shaped = grad_wide.reshape(tok_count, head_count, SEGS, wide_dim // SEGS)
    return jnp.sum(shaped * member_f[:, None, :, None], 2)


def micro_step(tokens, cotangent, seg_row, feat_proj, weights):
    (
        w_qkv,
        b_qkv,
        w_out,
        b_out,
        ln1_gain,
        ln1_bias,
        w_up,
        b_up,
        w_down,
        b_down,
        ln2_gain,
        ln2_bias,
    ) = weights
    tok_count = tokens.shape[0]
    qkv_rows = jnp.dot(tokens, w_qkv, preferred_element_type=jnp.float32) + b_qkv.astype(
        jnp.float32
    )
    qkv_low = qkv_rows.astype(jnp.bfloat16)
    grouped = lax.all_gather(qkv_low, "feat", axis=0, tiled=True)
    group_rows = grouped.shape[0]
    query_h = grouped[:, :D].reshape(group_rows, H, DH)
    key_h = grouped[:, D : 2 * D].reshape(group_rows, H, DH)
    value_h = grouped[:, 2 * D :].reshape(group_rows, H, DH)
    phi_q = feature_map(query_h, feat_proj)
    phi_k = feature_map(key_h, feat_proj)
    member_f = (seg_row[:, None] == jnp.arange(SEGS, dtype=jnp.int32)[None, :]).astype(jnp.float32)
    member = member_f.astype(jnp.bfloat16)
    wide_q = spread_segments(phi_q.astype(jnp.bfloat16), member)
    wide_k = spread_segments(phi_k.astype(jnp.bfloat16), member)
    ones_col = jnp.ones((group_rows,), jnp.bfloat16)
    kv_part = jnp.einsum("gha,ghe->hae", wide_k, value_h, preferred_element_type=jnp.float32)
    z_part = jnp.einsum("gha,g->ha", wide_k, ones_col, preferred_element_type=jnp.float32)
    kv_low = kv_part.astype(jnp.bfloat16)
    z_low = z_part.astype(jnp.bfloat16)
    numer_part = jnp.einsum(
        "gha,hae->ghe", wide_q, kv_low, preferred_element_type=jnp.float32
    ).reshape(group_rows, D)
    denom_part = jnp.einsum("gha,ha->gh", wide_q, z_low, preferred_element_type=jnp.float32)
    numer_sum, denom_sum = (
        lax.psum_scatter(numer_part, "feat", scatter_dimension=0, tiled=True),
        lax.psum_scatter(denom_part, "feat", scatter_dimension=0, tiled=True),
    )
    numer_h = numer_sum.reshape(tok_count, H, DH)
    att_low = (numer_h / denom_sum[:, :, None]).reshape(tok_count, D).astype(jnp.bfloat16)
    branch = jnp.dot(att_low, w_out, preferred_element_type=jnp.float32) + b_out.astype(jnp.float32)
    hidden_one, ln1_back = jax.vjp(
        layer_norm,
        tokens.astype(jnp.float32) + branch,
        ln1_gain.astype(jnp.float32),
        ln1_bias.astype(jnp.float32),
    )
    hid_low = hidden_one.astype(jnp.bfloat16)
    pre_act = jnp.dot(hid_low, w_up, preferred_element_type=jnp.float32) + b_up.astype(jnp.float32)
    act_val, gelu_back = jax.vjp(partial(jax.nn.gelu, approximate=False), pre_act)
    act_low = act_val.astype(jnp.bfloat16)
    ffn_out = jnp.dot(act_low, w_down, preferred_element_type=jnp.float32) + b_down.astype(
        jnp.float32
    )
    result, ln2_back = jax.vjp(
        layer_norm, hidden_one + ffn_out, ln2_gain.astype(jnp.float32), ln2_bias.astype(jnp.float32)
    )
    grad_r2, grad_gain2, grad_bias2 = ln2_back(cotangent.astype(jnp.float32))
    grad_ffn = grad_r2.astype(jnp.bfloat16)
    grad_bdown = jnp.sum(grad_ffn.astype(jnp.float32), 0)
    grad_wdown = cross_dot(act_low, grad_ffn)
    (grad_act,) = gelu_back(back_dot(grad_ffn, w_down))
    grad_pre = grad_act.astype(jnp.bfloat16)
    grad_bup = jnp.sum(grad_pre.astype(jnp.float32), 0)
    grad_wup = cross_dot(hid_low, grad_pre)
    grad_h1 = grad_r2 + back_dot(grad_pre, w_up)
    grad_r1, grad_gain1, grad_bias1 = ln1_back(grad_h1)
    grad_branch = grad_r1.astype(jnp.bfloat16)
    grad_bout = jnp.sum(grad_branch.astype(jnp.float32), 0)
    grad_wout = cross_dot(att_low, grad_branch)
    grad_att = back_dot(grad_branch, w_out).reshape(tok_count, H, DH)
    grad_num = (grad_att / denom_sum[:, :, None]).reshape(tok_count, D).astype(jnp.bfloat16)
    grad_den = (-jnp.sum(grad_att * numer_h, -1) / (denom_sum * denom_sum)).astype(jnp.bfloat16)
    group_num, group_den = (
        lax.all_gather(grad_num, "feat", axis=0, tiled=True),
        lax.all_gather(grad_den, "feat", axis=0, tiled=True),
    )
    group_num_h = group_num.reshape(group_rows, H, DH)
    grad_kv_part = jnp.einsum(
        "gha,ghe->hae", wide_q, group_num_h, preferred_element_type=jnp.float32
    )
    grad_z_part = jnp.einsum("gha,gh->ha", wide_q, group_den, preferred_element_type=jnp.float32)
    grad_kv = grad_kv_part.astype(jnp.bfloat16)
    grad_z = grad_z_part.astype(jnp.bfloat16)
    wide_gq = jnp.einsum("ghe,hae->gha", group_num_h, kv_low, preferred_element_type=jnp.float32)
    wide_gq = wide_gq + group_den[:, :, None].astype(jnp.float32) * z_low[None].astype(jnp.float32)
    grad_arg_q = (fold_segments(wide_gq, member_f) * phi_q).astype(jnp.bfloat16)
    wide_gk = jnp.einsum(
        "ghe,hae->gha", value_h, grad_kv, preferred_element_type=jnp.float32
    ) + grad_z[None].astype(jnp.float32)
    grad_arg_k = (fold_segments(wide_gk, member_f) * phi_k).astype(jnp.bfloat16)
    grad_value = jnp.einsum("gha,hae->ghe", wide_k, grad_kv, preferred_element_type=jnp.float32)
    grad_query = feature_back(query_h, feat_proj, grad_arg_q)
    grad_key = feature_back(key_h, feat_proj, grad_arg_k)
    grad_group = jnp.concatenate(
        [
            grad_query.reshape(group_rows, D),
            grad_key.reshape(group_rows, D),
            grad_value.reshape(group_rows, D),
        ],
        1,
    )
    grad_qkv = lax.psum_scatter(
        grad_group.astype(jnp.bfloat16), "feat", scatter_dimension=0, tiled=True
    )
    grad_bqkv = jnp.sum(grad_qkv.astype(jnp.float32), 0)
    grad_wqkv = cross_dot(tokens, grad_qkv)
    grad_tokens = grad_r1 + back_dot(grad_qkv, w_qkv)
    grads_now = (
        grad_wqkv,
        grad_bqkv,
        grad_wout,
        grad_bout,
        grad_gain1,
        grad_bias1,
        grad_wup,
        grad_bup,
        grad_wdown,
        grad_bdown,
        grad_gain2,
        grad_bias2,
    )
    return (result.astype(jnp.bfloat16), grad_tokens, grads_now)


def on_device(
    tokens_in,
    out_cotangent,
    segment_ids,
    feature_proj,
    w_qkv,
    b_qkv,
    w_out,
    b_out,
    ln1_gain,
    ln1_bias,
    w_up,
    b_up,
    w_down,
    b_down,
    ln2_gain,
    ln2_bias,
):
    totals = None
    outputs = []
    grad_inputs = []
    for micro_idx in range(MICRO):
        gathered = fetch_weights(
            w_qkv,
            b_qkv,
            w_out,
            b_out,
            ln1_gain,
            ln1_bias,
            w_up,
            b_up,
            w_down,
            b_down,
            ln2_gain,
            ln2_bias,
        )
        result, grad_tokens, grads_now = micro_step(
            tokens_in[micro_idx],
            out_cotangent[micro_idx],
            segment_ids[micro_idx],
            feature_proj,
            gathered,
        )
        outputs.append(result)
        grad_inputs.append(grad_tokens)
        totals = grads_now if totals is None else jax.tree.map(jnp.add, totals, grads_now)
    (
        grad_wqkv,
        grad_bqkv,
        grad_wout,
        grad_bout,
        grad_gain1,
        grad_bias1,
        grad_wup,
        grad_bup,
        grad_wdown,
        grad_bdown,
        grad_gain2,
        grad_bias2,
    ) = totals
    summed = (
        lax.psum_scatter(grad_wqkv, ("dp", "feat"), scatter_dimension=0, tiled=True),
        lax.psum_scatter(grad_bqkv, ("dp", "feat"), scatter_dimension=0, tiled=True),
        lax.psum_scatter(grad_wout, ("dp", "feat"), scatter_dimension=0, tiled=True),
        lax.psum_scatter(grad_bout, ("dp", "feat"), scatter_dimension=0, tiled=True),
        lax.psum_scatter(grad_gain1, ("dp", "feat"), scatter_dimension=0, tiled=True),
        lax.psum_scatter(grad_bias1, ("dp", "feat"), scatter_dimension=0, tiled=True),
        lax.psum_scatter(grad_wup, ("dp", "feat"), scatter_dimension=0, tiled=True),
        lax.psum_scatter(grad_bup, ("dp", "feat"), scatter_dimension=0, tiled=True),
        lax.psum_scatter(grad_wdown, ("dp", "feat"), scatter_dimension=0, tiled=True),
        lax.psum_scatter(grad_bdown, ("dp", "feat"), scatter_dimension=0, tiled=True),
        lax.psum_scatter(grad_gain2, ("dp", "feat"), scatter_dimension=0, tiled=True),
        lax.psum_scatter(grad_bias2, ("dp", "feat"), scatter_dimension=0, tiled=True),
    )
    return (
        jnp.stack(outputs),
        jnp.stack(grad_inputs),
        summed[0],
        summed[1],
        summed[2],
        summed[3],
        summed[4],
        summed[5],
        summed[6],
        summed[7],
        summed[8],
        summed[9],
        summed[10],
        summed[11],
    )


NZ, NY, NC, NX = 4, 2, 2, 2
N_DEV = NZ * NY * NC * NX
MESH_ID = pl.DeviceIdType.MESH
BF = jnp.bfloat16
F32 = jnp.float32
SHARE = MICRO // NX
GRID = (NZ, NY, NC)
ALL = slice(None)


def fits(mesh):
    return mesh.shape["dp"] == NZ * NY * NC and mesh.shape["feat"] == NX


class Place:
    def __init__(self):
        i = lax.axis_index("dp")
        self.z, self.y, self.c, self.x = i // (NY * NC), (i // NC) % NY, i % NC, lax.axis_index("feat")
        self.sibling = self.device(c=1 - self.c)
        self.over = {"x": self.device(x=1 - self.x), "y": self.device(y=1 - self.y)}
        z = self.z
        self.to = {1: z <= 2, -1: z >= 1, 2: z <= 1, -2: z >= 2}
        self.had = {1: z >= 1, -1: z <= 2, 2: z >= 2, -2: z <= 1}

    def device(self, **other):
        z, y, c, x = (other.get(n, getattr(self, n)) for n in "zycx")
        return (z * (NY * NC) + y * NC + c, x)

    def meet(self):
        barrier = pltpu.get_barrier_semaphore()
        peers = [self.sibling, self.over["x"], self.over["y"]] + [self.device(z=lax.rem(self.z + k, NZ)) for k in (1, 2, 3)]
        for peer in peers:
            pl.semaphore_signal(barrier, inc=1, device_id=peer, device_id_type=MESH_ID)
        pl.semaphore_wait(barrier, len(peers))

    def per_class(self, orders, act):
        if orders[0] == orders[1]:
            act(orders[0])
            return
        for c in range(NC):

            @pl.when(self.c == c)
            def _(order=orders[c]):
                act(order)

    def rows(self, grid, x):
        share = grid.shape[3] // NX
        return pl.ds(pl.multiple_of(x * share, 8), share)

    def view(self, grid, cols, spread=(), **at):
        index = [ALL if n in spread else at.get(n, getattr(self, n)) for n in "zyc"]
        rows = ALL if "x" in spread else self.rows(grid, at.get("x", self.x))
        return grid.at[(*index, rows, cols)]


class Copies:
    def __init__(self, send_sems, recv_sems):
        self.send_sems, self.recv_sems = send_sems, recv_sems

    def copy(self, slot, src, dst, peer, sent=None):
        return pltpu.make_async_remote_copy(
            src_ref=src, dst_ref=dst, send_sem=self.send_sems.at[slot if sent is None else sent],
            recv_sem=self.recv_sems.at[slot], device_id=peer, device_id_type=MESH_ID,
        )


MOVES = (1, -1, 2, -2)


def stretch(order):
    return "".join("zZ" if n == "z" else n for n in order)


class Gather(Copies):
    def __init__(self, here, part, src, grid, cols, orders, sems):
        super().__init__(sems[0].at[part], sems[1].at[part])
        self.here, self.grid, self.cols, self.orders = here, grid, cols, tuple(stretch(o) for o in orders)
        self.src = src.at[ALL, cols]
        self.local = pltpu.make_async_copy(self.src, here.view(grid, cols), sems[2].at[part])

    def phase(self, order, n):
        here, dim = self.here, order[n]
        mine = here.view(self.grid, self.cols, order[:n].replace("Z", "").replace("z", "" if dim == "Z" else "z"))
        src = self.src if n == 0 else mine
        if dim == "z":
            return [
                (here.to[k], here.had[k], self.copy(s, src, mine, here.device(z=lax.rem(here.z + k + NZ, NZ))))
                for s, k in enumerate(MOVES)
            ]
        if dim == "Z":
            inner = (here.z == 1) | (here.z == 2)
            outer = (here.z == 0) | (here.z == 3)
            far = here.view(self.grid, self.cols, order[: n - 1], z=jnp.where(inner, 6 - 3 * here.z, 3 - here.z))
            return [(inner, outer, self.copy(4, far, far, here.device(z=jnp.where(inner, 3 * here.z - 3, 3 - here.z))))]
        return [(None, None, self.copy(5 + "xy".index(dim), src, mine, here.over[dim]))]

    def to_sibling(self):
        mine = self.here.view(self.grid, self.cols, "zyx")
        return self.copy(7, mine, mine, self.here.sibling)

    def step(self, n):
        here, last = self.here, len(self.orders[0])
        if n == 0:
            self.local.start()
            here.per_class(self.orders, lambda order: run_all("start", self.phase(order, 0)))
        elif n <= last:
            here.per_class(self.orders, lambda order: run_all("wait_recv", self.phase(order, n - 1)))
            if n == 1:
                self.local.wait()
            if n < last:
                here.per_class(self.orders, lambda order: run_all("start", self.phase(order, n)))
            else:
                self.to_sibling().start()
        else:
            self.to_sibling().wait_recv()

    def drain(self):
        for n in range(len(self.orders[0])):
            self.here.per_class(self.orders, lambda order, n=n: run_all("wait_send", self.phase(order, n)))
        self.to_sibling().wait_send()


def run_all(what, copies):
    for sends, gets, copy in copies:
        when(gets if what == "wait_recv" else sends, getattr(copy, what))


def when(condition, act):
    if condition is None:
        act()
        return

    @pl.when(condition)
    def _():
        act()


class Reduce(Copies):
    def __init__(self, here, part, grid, cols, orders, got, stage, out, sems):
        super().__init__(sems[0].at[part], sems[1].at[part])
        self.here, self.grid, self.cols, self.orders = here, grid, cols, tuple(stretch(o) for o in orders)
        self.got, self.stage = got, stage
        self.out = pltpu.make_async_copy(stage, out, sems[2].at[part])

    def from_sibling(self):
        here = self.here
        theirs = here.view(self.grid, self.cols, "zyx", c=1 - here.c)
        return self.copy(0, theirs, self.got[0][0], here.sibling)

    def received(self, order, n):
        at = order.replace("Z", "").index(order[n].lower()) + 1
        return self.got[at][self.orders.index(order) % len(self.got[at])]

    def phase(self, order, n):
        here, dim, rest = self.here, order[n], order[n + 1 :].replace("Z", "")
        got, z = self.received(order, n), here.z
        if dim == "z":
            aim = {1: z + 1, -1: z - 1, 2: 2, -2: 1}
            ends = {1: here.to[1], -1: here.to[-1], 2: z == 0, -2: z == 3}
            copies = [
                (ends[k], None, self.copy(3 + s, here.view(self.grid, self.cols, rest, z=aim[k]), got.at[s], here.device(z=aim[k])))
                for s, k in enumerate(MOVES)
            ]
            near = {2: (z == 0, 3, 1), -2: (z == 3, 0, 2)}
            first = [
                (near[k][0], None, self.copy(
                    3 + s, here.view(self.grid, self.cols, rest, z=near[k][1]), got.at[s], here.device(z=near[k][2]), 5 + s
                ))
                for s, k in enumerate(MOVES) if k in near
            ]
            return first + copies
        if dim == "Z":
            end = {2: (z == 1, 3), -2: (z == 2, 0)}
            return [
                (end[k][0], None, self.copy(3 + s, here.view(self.grid, self.cols, rest, z=end[k][1]), got.at[s], here.device(z=end[k][1])))
                for s, k in enumerate(MOVES) if k in end
            ]
        place = {dim: 1 - getattr(here, dim)}
        return [(None, None, self.copy(1 + "xy".index(dim), here.view(self.grid, self.cols, rest, **place), got, here.over[dim]))]

    def arrivals(self, order, n):
        here, got = self.here, self.received(order, n)
        if order[n] != "Z":
            (_, _, copy), = self.phase(order, n)
            return [(None, copy.wait_recv, got)]
        mine = here.view(self.grid, self.cols, order[n + 1 :])
        return [
            (here.had[k], self.copy(3 + s, mine, got.at[s], here.sibling).wait_recv, got.at[s]) for s, k in enumerate(MOVES)
        ]

    def spot(self, spread, q, z=None):
        here, index, inner = self.here, {} if z is None else {"z": z}, {}
        if "y" in spread:
            index["y"] = inner["y"] = q % NY
            q = q // NY
        if "z" in spread:
            index["z"] = inner["z"] = q
        rows = ALL if "x" in spread else here.rows(self.grid, here.x)
        return tuple(index.get(n, getattr(here, n)) for n in "zyc") + (rows, self.cols), tuple(inner[n] for n in "zy" if n in inner)

    def add(self, got, spread, z=None):
        def one(q):
            index, inner = self.spot(spread, q, z)
            self.grid[index] = self.grid[index] + got[inner + (ALL, ALL)]

        count = (NZ if "z" in spread else 1) * (NY if "y" in spread else 1)
        blocks_of(count, one) if count > 1 else one(0)

    def take(self, order, n):
        if order[n] == "z":
            return
        here, final = self.here, n == len(order) - 1
        if final:
            self.stage[...] = self.grid[self.spot((), 0)[0]].astype(F32)
        for condition, wait, got in self.arrivals(order, n):

            def one(wait=wait, got=got):
                wait()
                if final:
                    self.stage[...] += got[...].astype(F32)
                else:
                    self.add(got, order[n + 1 :].replace("Z", ""))

            when(condition, one)

    def send(self, order, n):
        copies = self.phase(order, n)
        if order[n] == "Z":
            got, rest = self.received(order, n), order[n + 1 :]
            for (condition, _, copy), (slot, end) in zip(copies, ((2, 3), (3, 0)), strict=True):

                def pass_on(copy=copy, slot=slot, end=end):
                    copy.wait_recv()
                    self.add(got.at[slot], rest, z=end)
                    copy.start()

                when(condition, pass_on)
        else:
            run_all("start", copies)

    def step(self, n):
        here, last = self.here, len(self.orders[0])
        if n == 0:
            self.from_sibling().start()
        elif n == 1:
            self.from_sibling().wait_recv()
            self.add(self.got[0][0], "zyx")
        else:
            here.per_class(self.orders, lambda order: self.take(order, n - 2))
        if 0 < n <= last:
            here.per_class(self.orders, lambda order: self.send(order, n - 1))
        elif n > last:
            self.out.start()

    def drain(self):
        self.from_sibling().wait_send()
        for n in range(len(self.orders[0])):
            self.here.per_class(self.orders, lambda order, n=n: run_all("wait_send", self.phase(order, n)))
        self.out.wait()


def got_shapes(orders, rows, width):
    first, second = (order_shapes(order, rows, width) for order in orders)
    return [(a,) if a == b else (a, b) for a, b in zip(first, second, strict=True)]


def order_shapes(order, rows, width):

    def block(spread):
        return tuple(dict(z=NZ, y=NY)[n] for n in "zy" if n in spread) + (rows * (NX if "x" in spread else 1), width)

    shapes = [block("zyx")]
    for n, dim in enumerate(order):
        shapes.append(((len(MOVES),) if dim == "z" else ()) + block(order[n + 1 :]))
    return shapes


def blocks_of(count, body, then=()):
    def step(j, carry):
        body(j)
        for at in sorted({at for at, _ in then}):

            @pl.when(j == at)
            def _(at=at):
                for when, act in then:
                    if when == at:
                        act()

        return carry

    lax.fori_loop(0, count, step, 0)


ROWS = 512
BLK = 256
PAIRS = D // 128
FF = 4 * D
WIDE = 2 * FEATS
SCALE = DH ** (-0.25)


def dot(a, b, ca=1, cb=0):
    return lax.dot_general(a, b, (((ca,), (cb,)), ((), ())), preferred_element_type=F32)


def half_masks(width):
    lane = lax.broadcasted_iota(jnp.int32, (1, width), 1) % 128
    first = (lane < DH).astype(F32)
    return first.astype(BF), (1.0 - first).astype(BF)


def lanes(j, width):
    return pl.ds(pl.multiple_of(j * width, width), width)


class Work:
    def __init__(self, refs):
        self.__dict__.update(refs)

    def setup(self, proj, seg_rows):
        row = lax.broadcasted_iota(jnp.int32, (DH, 128), 0)
        col = lax.broadcasted_iota(jnp.int32, (DH, 128), 1)
        for h in range(2):
            place_in = (col == row + h * DH).astype(BF)
            for n in range(NX):
                self.table[pl.ds(h * FEATS + n * 128, 128), 0:128] = dot(proj[n], place_in, 0, 0).astype(BF)
        feat = lax.broadcasted_iota(jnp.int32, (WIDE, 128), 0) // FEATS
        half = lax.broadcasted_iota(jnp.int32, (WIDE, 128), 1) // DH
        same = (feat == half).astype(F32).astype(BF)
        self.table[:, 128:256] = same
        self.flip[D:, :] = jnp.ones((16, ROWS), BF)
        for b in range(2):
            across = jnp.broadcast_to(seg_rows[b], (BLK, BLK))
            self.mask[b] = (across == jnp.transpose(across)).astype(F32).astype(BF)

    def features(self, rows):
        wide = rows.astype(F32)
        squares = wide * wide
        high = squares.astype(BF)
        low = (squares - high.astype(F32)).astype(BF)
        same = self.table[:, 128:256]
        norm = dot(high, same, 1, 1) + dot(low, same, 1, 1)
        arg = SCALE * dot(rows, self.table[:, 0:128], 1, 1) - (0.5 * SCALE * SCALE) * norm
        return (jnp.exp(arg) * FEATS ** (-0.5)).astype(BF)

    def qkv_block(self, j):
        col = lanes(j, D)
        full = dot(self.x[...], self.w_qkv[:, col]) + self.b_qkv[:, col]
        self.qkv[:, col] = full.astype(BF)

    def pair(self, i):
        b, p = i // PAIRS, i % PAIRS
        rows = pl.ds(pl.multiple_of(b * BLK, BLK), BLK)
        cols = [pl.ds(pl.multiple_of(n * D + p * 128, 128), 128) for n in range(3)]
        return b, rows, cols

    def attend(self, i):
        b, rows, cols = self.pair(i)
        mask = self.mask[b]
        m0, m1 = half_masks(128)
        phi_q = self.features(self.qkv[rows, cols[0]])
        phi_k = self.features(self.qkv[rows, cols[1]])
        self.phi_q[i] = phi_q
        self.phi_k[i] = phi_k
        v = self.qkv[rows, cols[2]]
        one = jnp.ones((BLK, 128), BF)
        res = None
        for h, m in enumerate((m0, m1)):
            part = slice(h * FEATS, (h + 1) * FEATS)
            score = dot(phi_q[:, part], phi_k[:, part], 1, 1).astype(BF) * mask
            term = dot(score, jnp.concatenate([v * m, one * m], 1))
            res = term if res is None else res + term
        inv = 1.0 / res[:, 128:]
        self.inv[rows, cols[0]] = inv
        self.att[rows, cols[0]] = (res[:, :128] * inv).astype(BF)

    def normalize(self, r):
        center = r - jnp.mean(r, -1, keepdims=True)
        scale = lax.rsqrt(jnp.mean(center * center, -1, keepdims=True) + EPSILON)
        return center * scale, scale

    def normalize_back(self, dy, n, scale, gain):
        g = dy * gain
        return (g - jnp.mean(g, -1, keepdims=True) - n * jnp.mean(g * n, -1, keepdims=True)) * scale

    def branch(self):
        for j in range(3):
            col = lanes(j, 256)
            self.n1[:, col] = dot(self.att[...], self.w_out[:, col]) + self.b_out[:, col] + self.x[:, col].astype(F32)

        def rows_of(j):
            row = pl.ds(pl.multiple_of(j * 128, 128), 128)
            n1, s1 = self.normalize(self.n1[row, :])
            self.n1[row, :] = n1
            self.s1[row, :] = s1
            self.h1[row, :] = (n1 * self.g1[...] + self.b1[...]).astype(BF)

        blocks_of(ROWS // 128, rows_of)

    def up_block(self, j):
        col = lanes(j, 256)
        for r in range(0, ROWS, 128):
            row = slice(r, r + 128)
            a = dot(self.h1[row, :], self.w_up[:, col]) + self.b_up[:, col]
            cdf = 0.5 * (1.0 + lax.erf(a * 2**-0.5))
            self.z[row, col] = (a * cdf).astype(BF)
            self.slope[row, col] = (cdf + a * jnp.exp(-0.5 * a * a) * (0.5 / 3.141592653589793) ** 0.5).astype(BF)

    def down_block(self, j):
        col = lanes(j, 256)
        back = self.n1[:, col] * self.g1[:, col] + self.b1[:, col]
        self.dr[:, col] = dot(self.z[...], self.w_down[:, col]) + self.b_down[:, col] + back

    def second_norm(self):
        self.d_g2[...] = jnp.zeros_like(self.d_g2)

        def rows_of(j):
            row = pl.ds(pl.multiple_of(j * 128, 128), 128)
            n2, s2 = self.normalize(self.dr[row, :])
            self.y[row, :] = (n2 * self.g2[...] + self.b2[...]).astype(BF)
            dy = self.cot[row, :].astype(F32)
            dr2 = self.normalize_back(dy, n2, s2, self.g2[...])
            self.dr[row, :] = dr2
            self.df[row, :] = dr2.astype(BF)
            self.d_g2[...] += jnp.sum(dy * n2, 0, keepdims=True)

        blocks_of(ROWS // 128, rows_of)

    def second_sums(self):
        ones = self.flip[D:, :]
        self.d_b2[...] = dot(ones, self.cot[...])[0:1]
        self.d_b_down[...] = dot(ones, self.df[...])[0:1]

    def down_back(self, j):
        col = lanes(j, 1024)
        dz = dot(self.df[...], self.w_down[col, :], 1, 1)
        self.slope[:, col] = (dz * self.slope[:, col].astype(F32)).astype(BF)

    def down_grad(self, into, part, j):
        col = lanes(j, D)
        into[col, :] = dot(self.z[:, col], self.df[:, part], 0, 0).astype(BF)

    def up_back(self, j):
        col = lanes(j, 384)
        self.dr[:, col] += dot(self.slope[...], self.w_up[col, :], 1, 1)

    def turn(self, name):
        self.flip[0:D, :] = jnp.transpose(getattr(self, name)[...])

    def weight_grad(self, weight, bias, col, grad):
        full = dot(self.flip[...], grad)
        weight[:, col] = full[0:D].astype(BF)
        bias[:, col] = full[D : D + 1]

    def up_grad(self, j):
        col = lanes(j, 512)
        self.weight_grad(self.w_up, self.d_b_up, col, self.slope[:, col])

    def first_norm_back(self):
        for ref in (self.d_g1, self.d_b1):
            ref[...] = jnp.zeros_like(ref)

        def rows_of(j):
            row = pl.ds(pl.multiple_of(j * 128, 128), 128)
            dh1, n1 = self.dr[row, :], self.n1[row, :]
            dr1 = self.normalize_back(dh1, n1, self.s1[row, :], self.g1[...])
            self.dr[row, :] = dr1
            self.df[row, :] = dr1.astype(BF)
            self.d_g1[...] += jnp.sum(dh1 * n1, 0, keepdims=True)
            self.d_b1[...] += jnp.sum(dh1, 0, keepdims=True)

        blocks_of(ROWS // 128, rows_of)

    def att_back(self, j):
        head_r = lax.broadcasted_iota(jnp.int32, (256, 256), 0) // DH
        head_c = lax.broadcasted_iota(jnp.int32, (256, 256), 1) // DH
        same = (head_r == head_c).astype(F32).astype(BF)
        col = lanes(j, 256)
        datt = dot(self.df[...], self.w_out[col, :], 1, 1)
        inv = self.inv[:, col]
        self.cot[:, col] = (datt * inv).astype(BF)
        prod = datt * self.att[:, col].astype(F32)
        high = prod.astype(BF)
        low = (prod - high.astype(F32)).astype(BF)
        total = dot(high, same) + dot(low, same)
        self.h1[:, col] = (-total * inv).astype(BF)

    def out_grad(self):
        col = slice(0, D)
        self.weight_grad(self.w_out, self.d_b_out, col, self.df[:, col])

    def attend_back(self, i):
        b, rows, cols = self.pair(i)
        mask = self.mask[b]
        m0, m1 = half_masks(256)
        q, k, v = (self.qkv[rows, c] for c in cols)
        dnum, dden = self.cot[rows, cols[0]], self.h1[rows, cols[0]]
        left = jnp.concatenate([dnum, dden * (1.0 / DH)], 1)
        right = jnp.concatenate([v, jnp.ones((BLK, 128), BF)], 1)
        back_q, back_k, dv = None, None, None
        for h, m in enumerate((m0, m1)):
            part = slice(h * FEATS, (h + 1) * FEATS)
            phi_q, phi_k = self.phi_q[i, :, part], self.phi_k[i, :, part]
            mine = left * m
            dscore = dot(mine, right, 1, 1).astype(BF) * mask
            flipped = dot(right, mine, 1, 1).astype(BF) * mask
            darg_q = (dot(dscore, phi_k) * phi_q.astype(F32)).astype(BF)
            darg_k = (dot(flipped, phi_q) * phi_k.astype(F32)).astype(BF)
            score = dot(phi_k, phi_q, 1, 1).astype(BF) * mask
            table = self.table[part, :]
            terms = dot(darg_q, table), dot(darg_k, table), dot(score, mine[:, :128])
            if h == 0:
                back_q, back_k, dv = terms
            else:
                back_q, back_k, dv = back_q + terms[0], back_k + terms[1], dv + terms[2]
        for n, (rows_in, back) in enumerate(((q, back_q), (k, back_k))):
            grad = SCALE * back[:, :128] - (SCALE * SCALE) * rows_in.astype(F32) * back[:, 128:]
            self.qkv[rows, cols[n]] = grad.astype(BF)
        self.qkv[rows, cols[2]] = dv.astype(BF)

    def tokens_back(self, j):
        col = lanes(j, 384)
        self.dr[:, col] += dot(self.qkv[...], self.w_qkv[col, :], 1, 1)

    def qkv_grad(self, j):
        col = lanes(j, D)
        self.weight_grad(self.w_qkv, self.d_b_qkv, col, self.qkv[:, col])


VECTORS = ("b_qkv", "b_out", "g1", "b1", "b_up", "b_down", "g2", "b2")
WIDTHS = (3 * D, D, D, D, FF, D, D, D)
SPACE = (
    ("qkv", (ROWS, 3 * D), BF), ("phi_q", (2 * PAIRS, BLK, WIDE), BF), ("phi_k", (2 * PAIRS, BLK, WIDE), BF),
    ("att", (ROWS, D), BF), ("inv", (ROWS, D), F32), ("n1", (ROWS, D), F32), ("s1", (ROWS, 1), F32),
    ("h1", (ROWS, D), BF), ("z", (ROWS, FF), BF), ("slope", (ROWS, FF), BF), ("dr", (ROWS, D), F32),
    ("df", (ROWS, D), BF), ("flip", (D + 16, ROWS), BF),
    ("table", (WIDE, 256), BF), ("mask", (2, BLK, BLK), BF),
)


GATHER_PARTS = {
    "small": ("small", 0, 128, ("zyx", "zxy")),
    "q": ("w_qkv", 0, 768, ("zyx", "zxy")),
    "k": ("w_qkv", 768, 768, ("zxy", "zxy")),
    "v": ("w_qkv", 1536, 768, ("zxy", "zxy")),
    "out": ("w_out", 0, 768, ("xzy", "yzx")),
    "up0": ("w_up", 0, 1024, ("zyx", "zxy")),
    "up1": ("w_up", 1024, 1024, ("xzy", "yzx")),
    "up2": ("w_up", 2048, 1024, ("xzy", "yzx")),
    "dn0": ("w_down", 0, 256, ("xyz", "xyz")),
    "dn1": ("w_down", 256, 256, ("zyx", "zxy")),
    "dn2": ("w_down", 512, 256, ("xzy", "yzx")),
}
REDUCE_PARTS = {
    "small": ("small", 0, 128, ("xyz", "yxz"), "small", 0),
    "q": ("w_qkv", 0, 768, ("xyz", "yxz"), "w_qkv", 0),
    "k": ("w_qkv", 768, 768, ("xyz", "yxz"), "w_qkv", 768),
    "v": ("w_qkv", 1536, 768, ("xyz", "yxz"), "w_qkv", 1536),
    "out": ("w_out", 0, 768, ("yxz", "yxz"), "w_out", 0),
    "up0": ("w_up", 0, 1536, ("yxz", "yxz"), "w_up", 0),
    "up1": ("w_up", 1536, 1536, ("xyz", "xyz"), "w_up", 1536),
    "dn0": ("spare", 0, 384, ("yzx", "xzy"), "w_down", 0),
    "dn1": ("w_down", 384, 384, ("yzx", "xzy"), "w_down", 384),
}
FORWARD = (
    "proj!", "small0", "tok!", "q0", "out0", "up10", "k0", "v0", "small1", "proj?", "setup", "q1", "k1", "small2",
    "up00", "q2", "dn10", "v1", "k2", "up20", "out1", "up11", "small3", "up01", "q3", "v2", "dn11", "dn20", "k3",
    "small4", "up21", "small5", "dn00", "spread", "q4", "out2", "q5", "cot!", "v3", "up02", "tok?", "qkv", "dn21",
    "dn12", "dn01", "k4", "up12", "k5", "qkv", "out3", "v4", "up22", "v5", "qkv", "att", "up03", "att", "up13",
    "dn13", "dn02", "att", "up23", "att", "dn22", "att", "out4", "att*3", "out5", "att", "up04", "att*3", "up05",
    "branch", "up14", "dn23", "upb*2", "dn03", "upb*2", "dn14", "up15", "upb*4", "dn15", "up24", "dn04", "up25",
    "upb*2", "dn24", "upb", "dn05", "upb", "down*2", "dn25", "down", "cot?", "ln2",
)
BACKWARD = (
    "y!", "gdn0*4", "dn00", "sums", "dz*3", "gdn1", "dn01", "gdn1*3", "dn10", "uback*2", "flip0", "gup*2", "dn11",
    "gup", "up00", "gup*3", "dn02", "up10", "nback", "up01", "datt*2", "up11", "datt", "dn12", "flip1", "gout",
    "out0", "attb*3", "out1", "dn03", "attb*6", "up02", "attb", "up12", "attb", "dn13", "attb", "tback", "out2",
    "dn04", "tback", "lower", "flip2", "gqkv", "up03", "q0", "dn14", "gqkv", "k0", "out3", "up13", "dn05", "q1",
    "dn15", "k1", "gqkv", "up04", "v0", "collect", "out4", "small0", "v1", "q2", "small1", "k2", "up14", "up05", "v2",
    "out5", "q3", "small2", "up15", "k3", "grad!", "v3", "small3", "q4", "k4", "v4", "small4", "q5", "k5", "v5",
    "small5",
)
WEIGHTS = (("w_qkv", (D, 3 * D)), ("w_out", (D, D)), ("w_up", (D, FF)), ("w_down", (FF, D)))
TILE = (8, 128)
SPARE = 384
HALF = (SHARE, NX, ROWS // SHARE // NX, D)


def shard_rows(weight):
    return TILE[0] if weight == "small" else dict(WEIGHTS)[weight][0] // N_DEV


class Swap:
    def __init__(self, here, n, theirs, target, mine, home, sems):
        self.there = pltpu.make_async_remote_copy(
            src_ref=theirs, dst_ref=target, send_sem=sems[0].at[n], recv_sem=sems[1].at[n],
            device_id=here.over["x"], device_id_type=MESH_ID,
        )
        self.here = None if home is None else pltpu.make_async_copy(mine, home, sems[2].at[n])

    def start(self):
        self.there.start()
        if self.here is not None:
            self.here.start()

    def arrive(self):
        self.there.wait_recv()
        if self.here is not None:
            self.here.wait()


def one_hot(width, count):
    at = lax.broadcasted_iota(jnp.int32, (1, count), 1).astype(F32)
    owner = jnp.floor((at + 0.5) * (1.0 / width))
    lane = at - owner * width
    lanes_hot = (lax.broadcasted_iota(jnp.int32, (128, count), 0).astype(F32) == lane).astype(F32).astype(BF)
    owner_hot = (lax.broadcasted_iota(jnp.int32, (N_DEV, count), 0).astype(F32) == owner).astype(F32)
    return lanes_hot, owner_hot


def spread_small(tiles, vectors):
    for width in sorted({v.shape[1] // N_DEV for v in vectors}):
        hot, owner = one_hot(width, width * N_DEV)
        for n, vector in enumerate(vectors):
            if vector.shape[1] == width * N_DEV:
                rows = tiles[pl.ds(n, N_DEV, stride=TILE[0]), :].astype(BF)
                vector[...] = jnp.sum(dot(rows, hot) * owner, 0, keepdims=True)


def collect_small(tiles, vectors):
    for width in sorted({v.shape[1] // N_DEV for v in vectors}):
        hot, owner = one_hot(width, width * N_DEV)
        for n, vector in enumerate(vectors):
            if vector.shape[1] == width * N_DEV:
                full = owner * vector[...]
                high = full.astype(BF)
                low = (full - high.astype(F32)).astype(BF)
                tiles[pl.ds(n, N_DEV, stride=TILE[0]), :] = dot(high, hot, 1, 1) + dot(low, hot, 1, 1)


def layer_kernel(*refs):
    it = iter(refs)
    tok, cot = next(it), next(it)
    local = {w: next(it) for w, _ in WEIGHTS}
    own_vectors = [next(it) for _ in VECTORS]
    proj_in, seg = next(it), next(it)
    block_out, grad_own, grad_got = next(it), next(it), next(it)
    outs = {w: next(it) for w, _ in WEIGHTS}
    outs["small"] = next(it)
    ref = {n: next(it) for n, _ in WEIGHTS}
    ref.update({n: next(it) for n, _, _ in SPACE})
    work = Work(ref)
    got = {
        p: [tuple(next(it) for _ in shapes) for shapes in got_shapes(orders, shard_rows(w), width)]
        for p, (_, _, width, orders, w, _) in REDUCE_PARTS.items()
    }
    stage = {p: next(it) for p in REDUCE_PARTS}
    gather_sems = [next(it) for _ in range(3)]
    reduce_sems = [next(it) for _ in range(3)]
    swap_sems = [next(it) for _ in range(3)]
    vector_sems = next(it)

    vector_loads = [pltpu.make_async_copy(v, ref["in_" + n], vector_sems.at[k]) for k, (n, v) in enumerate(zip(VECTORS, own_vectors))]
    for load in vector_loads:
        load.start()
    here = Place()
    here.meet()
    local["small"] = ref["tile"]
    ref["tile"][...] = jnp.zeros(TILE, F32)
    for k, (n, load) in enumerate(zip(VECTORS, vector_loads)):
        load.wait()
        width = ref["in_" + n].shape[0]
        ref["tile"][k : k + 1, 0:width] = ref["in_" + n][...].astype(F32).reshape(1, width)
    x = here.x
    grids = {w: ref[w].reshape(GRID + (NX * shard_rows(w), ref[w].shape[1])) for w, _ in WEIGHTS}
    grids["spare"] = ref["spare"].reshape(GRID + (NX * shard_rows("w_down"), SPARE))
    grids["small"] = ref["tiles"].reshape(GRID + (NX * TILE[0], TILE[1]))
    into, back = {}, {}
    for n, (p, (w, first, width, orders)) in enumerate(GATHER_PARTS.items()):
        into[p] = Gather(here, n, local[w], grids[w], pl.ds(first, width), orders, gather_sems)
    for n, (p, (a, first, width, orders, w, at)) in enumerate(REDUCE_PARTS.items()):
        out = outs[w].at[ALL, pl.ds(at, width)]
        back[p] = Reduce(here, n, grids[a], pl.ds(first, width), orders, got[p], stage[p], out, reduce_sems)

    def halves(r):
        return r.reshape(HALF)

    grad_low = halves(work.df).at[0]
    own, other = pl.ds(x * SHARE, SHARE), pl.ds((1 - x) * SHARE, SHARE)
    swap = {
        "tok": Swap(here, 0, tok.at[other], halves(work.x).at[:, x], tok.at[own], halves(work.x).at[:, x], swap_sems),
        "cot": Swap(here, 1, cot.at[other], halves(work.cot).at[:, x], cot.at[own], halves(work.cot).at[:, x], swap_sems),
        "proj": Swap(here, 2, proj_in, work.proj.at[x], proj_in, work.proj.at[x], swap_sems),
        "y": Swap(here, 3, halves(work.y).at[:, 1 - x], block_out.at[own], halves(work.y).at[:, x], block_out.at[own], swap_sems),
        "grad": Swap(here, 4, grad_low, grad_got, halves(work.dr).at[:, x], grad_own, swap_sems),
    }

    vectors = [getattr(work, n) for n in VECTORS]
    totals = [getattr(work, "d_" + n) for n in VECTORS]

    def setup():
        work.setup(work.proj, [seg[pl.ds(SHARE * x + b, 1), :].astype(F32) for b in range(SHARE)])

    def lower():
        def block(b):
            grad_low[b] = halves(work.dr)[b, 1 - x].astype(BF)

        blocks_of(SHARE, block)

    stages = {
        "setup": (1, setup),
        "spread": (1, lambda: spread_small(ref["tiles"], vectors)),
        "qkv": (3, work.qkv_block),
        "att": (2 * PAIRS, work.attend),
        "branch": (1, work.branch),
        "upb": (12, work.up_block),
        "down": (3, work.down_block),
        "ln2": (1, work.second_norm),
        "sums": (1, work.second_sums),
        "dz": (3, work.down_back),
        "uback": (2, work.up_back),
        "flip0": (1, partial(work.turn, "h1")),
        "gup": (6, work.up_grad),
        "nback": (1, work.first_norm_back),
        "datt": (3, work.att_back),
        "flip1": (1, partial(work.turn, "att")),
        "gout": (1, work.out_grad),
        "attb": (2 * PAIRS, work.attend_back),
        "tback": (2, work.tokens_back),
        "lower": (1, lower),
        "flip2": (1, partial(work.turn, "x")),
        "gqkv": (3, work.qkv_grad),
        "collect": (1, lambda: collect_small(ref["tiles"], totals)),
    }
    for p, (a, first, width, _, w, at) in REDUCE_PARTS.items():
        if w == "w_down":
            into_part = ref[a].at[ALL, pl.ds(first, width)]
            stages["g" + p] = (4, partial(work.down_grad, into_part, slice(at, at + width)))

    def act(steps, token):
        if token[-1] == "!":
            swap[token[:-1]].start()
        elif token[-1] == "?":
            swap[token[:-1]].arrive()
        else:
            steps[token[:-1]].step(int(token[-1]))

    def play(tokens, steps):
        tokens = [t.split("*") for t in tokens]
        tokens = [(t[0], int(t[1]) if len(t) > 1 else 1) for t in tokens]
        while tokens:
            name, _ = tokens[0]
            if name not in stages:
                act(steps, name)
                tokens.pop(0)
                continue
            count, body = stages[name]
            n, then = 0, []
            while n < count:
                token, times = tokens.pop(0)
                if token == name:
                    n += times
                else:
                    then.append((n - 1, partial(act, steps, token)))
            if count > 1:
                blocks_of(count, body, then)
            else:
                body()

    play(FORWARD, into)
    for part in into.values():
        part.drain()
    play(BACKWARD, back)
    swap["grad"].arrive()
    swap["y"].arrive()
    for each in swap.values():
        each.there.wait_send()
    for part in back.values():
        part.drain()


QUARTER = (SHARE, ROWS // SHARE // NX, D)
SPACE = (
    (("x", (ROWS, D), BF), ("cot", (ROWS, D), BF), ("y", (ROWS, D), BF), ("proj", (NX, DH, FEATS // NX), BF))
    + (("spare", (FF, SPARE), BF), ("tile", TILE, F32))
    + tuple(("in_" + n, (w // N_DEV,), BF) for n, w in zip(VECTORS, WIDTHS))
    + (("tiles", (N_DEV * TILE[0], TILE[1]), F32),)
    + tuple((n, (1, w), F32) for n, w in zip(VECTORS, WIDTHS))
    + tuple(("d_" + n, (1, w), F32) for n, w in zip(VECTORS, WIDTHS))
    + SPACE
)


def layer(tok, cot, weights, vectors, proj, seg):
    anywhere = pl.BlockSpec(memory_space=pl.ANY)
    vmem = pl.BlockSpec(memory_space=pltpu.VMEM)
    shape, dma = jax.ShapeDtypeStruct, pltpu.SemaphoreType.DMA
    received, stages = [], []
    for _, _, width, orders, w, _ in REDUCE_PARTS.values():
        kind = F32 if w == "small" else BF
        received += [pltpu.VMEM(s, kind) for shapes in got_shapes(orders, shard_rows(w), width) for s in shapes]
        stages.append(pltpu.VMEM((shard_rows(w), width), F32))
    there, back = len(GATHER_PARTS), len(REDUCE_PARTS)
    return pl.pallas_call(
        layer_kernel,
        out_shape=[shape(tok.shape, BF), shape(QUARTER, F32), shape(QUARTER, BF)]
        + [shape(w.shape, F32) for w in weights] + [shape(TILE, F32)],
        in_specs=[anywhere] * 15 + [vmem],
        out_specs=[anywhere] * 8,
        scratch_shapes=[pltpu.VMEM(s, BF) for _, s in WEIGHTS] + [pltpu.VMEM(s, d) for _, s, d in SPACE] + received + stages
        + [dma((there, 8)), dma((there, 8)), dma((there,)), dma((back, 9)), dma((back, 9)), dma((back,))]
        + [dma((5,)), dma((5,)), dma((5,)), dma((len(VECTORS),))],
        compiler_params=pltpu.CompilerParams(collective_id=0, has_side_effects=True, vmem_limit_bytes=63 << 20),
        name="layer",
    )(tok, cot, *weights, *vectors, proj, seg)


def finish_kernel(count, *refs):
    it = iter(refs)
    ins, own, got, tile = [next(it) for _ in range(count)], next(it), next(it), next(it)
    outs, grad = [next(it) for _ in range(count)], next(it)
    rows = [next(it) for _ in WIDTHS]
    spaces, got_space, grad_space, sems = [next(it) for _ in range(count)], next(it), next(it), next(it)
    x = lax.axis_index("feat")
    here, there = pl.ds(x * SHARE, SHARE), pl.ds((1 - x) * SHARE, SHARE)
    loads = [pltpu.make_async_copy(got, got_space, sems.at[0, count]), pltpu.make_async_copy(own, grad_space.at[here], sems.at[0, count + 1])]
    loads += [pltpu.make_async_copy(a, b, sems.at[0, n]) for n, (a, b) in enumerate(zip(ins, spaces))]
    stores = [pltpu.make_async_copy(a, b, sems.at[1, n]) for n, (a, b) in enumerate(zip(spaces, outs))]
    halves = [pltpu.make_async_copy(grad_space.at[h], grad.at[h], sems.at[1, count + n]) for n, h in enumerate((there, here))]
    for load in loads:
        load.start()
    for n, row in enumerate(rows):
        row[...] = tile[n, 0 : row.shape[0]]
    loads[0].wait()
    grad_space[there] = got_space[...].astype(F32)
    halves[0].start()
    loads[1].wait()
    halves[1].start()
    for load, store in zip(loads[2:], stores):
        load.wait()
        store.start()
    for store in stores + halves:
        store.wait()


def finish(arrays, own, got, tile):
    anywhere = pl.BlockSpec(memory_space=pl.ANY)
    vmem = pl.BlockSpec(memory_space=pltpu.VMEM)
    count = len(arrays)
    whole = (MICRO,) + own.shape[1:]
    return pl.pallas_call(
        partial(finish_kernel, count),
        out_shape=[jax.ShapeDtypeStruct(a.shape, a.dtype) for a in arrays] + [jax.ShapeDtypeStruct(whole, F32)]
        + [jax.ShapeDtypeStruct((w // N_DEV,), F32) for w in WIDTHS],
        in_specs=[anywhere] * (count + 2) + [vmem],
        out_specs=[anywhere] * (count + 1) + [vmem] * len(WIDTHS),
        scratch_shapes=[pltpu.VMEM(a.shape, a.dtype) for a in arrays]
        + [pltpu.VMEM(got.shape, BF), pltpu.VMEM(whole, F32), pltpu.SemaphoreType.DMA((2, count + 2))],
        name="finish",
    )(*arrays, own, got, tile)


def fast_device(
    tokens_in, out_cotangent, segment_ids, feature_proj,
    w_qkv, b_qkv, w_out, b_out, ln1_gain, ln1_bias, w_up, b_up, w_down, b_down, ln2_gain, ln2_bias,
):
    out, own, got, *sums, tile = layer(
        tokens_in, out_cotangent, [w_qkv, w_out, w_up, w_down],
        [b_qkv, b_out, ln1_gain, ln1_bias, b_up, b_down, ln2_gain, ln2_bias], feature_proj.T, segment_ids,
    )
    out, g_qkv, g_out, g_up, g_down, grad_tok, *vec = finish([out, *sums], own, got, tile)
    return out, grad_tok, g_qkv, vec[0], g_out, vec[1], vec[2], vec[3], g_up, vec[4], g_down, vec[5], vec[6], vec[7]


def solution(mesh):
    return jax.shard_map(
        fast_device if fits(mesh) else on_device,
        mesh=mesh,
        in_specs=(
            P(None, ("dp", "feat"), None),
            P(None, ("dp", "feat"), None),
            P(None, "dp"),
            P("feat", None),
            P(("dp", "feat"), None),
            P(("dp", "feat")),
            P(("dp", "feat"), None),
            P(("dp", "feat")),
            P(("dp", "feat")),
            P(("dp", "feat")),
            P(("dp", "feat"), None),
            P(("dp", "feat")),
            P(("dp", "feat"), None),
            P(("dp", "feat")),
            P(("dp", "feat")),
            P(("dp", "feat")),
        ),
        out_specs=(
            P(None, ("dp", "feat"), None),
            P(None, ("dp", "feat"), None),
            P(("dp", "feat"), None),
            P(("dp", "feat")),
            P(("dp", "feat"), None),
            P(("dp", "feat")),
            P(("dp", "feat")),
            P(("dp", "feat")),
            P(("dp", "feat"), None),
            P(("dp", "feat")),
            P(("dp", "feat"), None),
            P(("dp", "feat")),
            P(("dp", "feat")),
            P(("dp", "feat")),
        ),
        check_vma=False,
    )
```
